32 devices in a mesh: fsdp: 32 (over z, y, x, core).
Axes of the slice: x: 2, y: 2, z: 4, core: 2. Of those that a mesh axis runs over, the one named last changes fastest.
Arguments:
- hidden_in: bfloat16 [8192, 2048], P('fsdp'), may hold values from -6 to 6
- out_cotangent: bfloat16 [8192, 2048], P('fsdp'), may hold values from -6 to 6
- segment_number: int32 [8192], P('fsdp'), may hold values from 0 to 34, as said below
- expert_routes: int32 [8192, 8], P('fsdp'), may hold values from 0 to 15, all different within a row
- pair_order: int32 [32, 2048], P('fsdp'), may hold values from 0 to 2047, each once within a row
- norm_gain: bfloat16 [2048], P('fsdp'), may hold values from 0.5 to 1.5
- query_weight: bfloat16 [2048, 2048], P('fsdp'), may hold values from -0.125 to 0.125
- key_weight: bfloat16 [2048, 2048], P('fsdp'), may hold values from -0.125 to 0.125
- value_weight: bfloat16 [2048, 2048], P('fsdp'), may hold values from -0.125 to 0.125
- output_weight: bfloat16 [2048, 2048], P('fsdp'), may hold values from -0.5 to 0.5
- query_gain: bfloat16 [128], P('fsdp'), may hold values from 0.796875 to 1.796875
- key_gain: bfloat16 [128], P('fsdp'), may hold values from 0.796875 to 1.796875
- ffn_norm_gain: bfloat16 [2048], P('fsdp'), may hold values from 0.5 to 1.5
- router_weight: bfloat16 [2048, 16], P('fsdp'), may hold values from -0.0625 to 0.0625
- expert_gate: bfloat16 [32, 2048, 512], P('fsdp'), may hold values from -0.125 to 0.125
- expert_up: bfloat16 [32, 2048, 512], P('fsdp'), may hold values from -0.125 to 0.125
- expert_down: bfloat16 [32, 512, 2048], P('fsdp'), may hold values from -0.75 to 0.75
Outputs:
- layer_out: bfloat16 [8192, 2048], P('fsdp')
- grad_hidden: float32 [8192, 2048], P('fsdp')
- grad_norm_gain: float32 [2048], P('fsdp')
- grad_query_weight: float32 [2048, 2048], P('fsdp')
- grad_key_weight: float32 [2048, 2048], P('fsdp')
- grad_value_weight: float32 [2048, 2048], P('fsdp')
- grad_output_weight: float32 [2048, 2048], P('fsdp')
- grad_query_gain: float32 [128], P('fsdp')
- grad_key_gain: float32 [128], P('fsdp')
- grad_ffn_gain: float32 [2048], P('fsdp')
- grad_router: float32 [2048, 16], P('fsdp')
- grad_expert_gate: float32 [32, 2048, 512], P('fsdp')
- grad_expert_up: float32 [32, 2048, 512], P('fsdp')
- grad_expert_down: float32 [32, 512, 2048], P('fsdp')
The draws below stay inside these ranges and needn't reach their ends.
Inputs may be any that keep to these rules, and one draw needn't show every extreme that they name: `segment_number`: segment numbers start at 0 in every sequence of 2048 tokens and never fall along it; every document but a sequence's last has 60 to 800 tokens; some document has exactly 800 tokens and some sequence reaches the largest number. `expert_routes`: each token names 8 different experts. `pair_order`: row b lists each of the 2048 pairs of device index b once.
All inputs are finite; a program needn't handle non-finite values.
Results may differ from the reference program's by a relative error of at most 0.023.
Values may be sent and summed in bfloat16 or wider, within the bound.
No kernel may reach another device: no remote copies, remote signals or barrier semaphores. Data moves between devices by JAX's collectives and lax.ppermute only.
A program may use at most 384 MiB of HBM per device.

```python
import math
import jax
import jax.numpy as jnp
from jax import lax

D = 2048
HD = 128
FF = 1024
TOPK = 8
TOK_DEV = 256
DOC_MIN = 60
DOC_MAX = 800
EXPERTS = 16
SEQ_LEN = 2048
TOKENS = 8192
SEQS = 4
PAIRS = 2048
CAP = 128
N_FSDP = 32


def draw_segment_number(key, part):
    doc_slots = SEQ_LEN // DOC_MIN + 1
    doc_lengths = jax.random.randint(key, (SEQS, doc_slots), DOC_MIN, DOC_MAX + 1, dtype=jnp.int32)
    chosen = jax.random.randint(jax.random.fold_in(key, 7), (), 0, SEQS, dtype=jnp.int32)
    seq_rows = jnp.arange(SEQS, dtype=jnp.int32)[:, None]
    doc_lengths = jnp.where(seq_rows == chosen, jnp.int32(DOC_MIN), doc_lengths).astype(jnp.int32)
    longest_row = ((chosen + 1) % SEQS).astype(jnp.int32)
    doc_lengths = doc_lengths.at[longest_row, 0].set(DOC_MAX)
    doc_ends = jnp.cumsum(doc_lengths, axis=1).astype(jnp.int32)
    positions = jnp.arange(SEQ_LEN, dtype=jnp.int32)
    numbers = jnp.sum((doc_ends[:, None, :] <= positions[None, :, None]).astype(jnp.int32), axis=2)
    return numbers.reshape(-1).astype(jnp.int32)


def strengthened(array, own_key, source, target, parts, factor):
    owner, partner = [(jnp.arange(array.shape[axis_at]) // (array.shape[axis_at] // parts)).reshape([-1 if axis == axis_at else 1 for axis in range(array.ndim)]) for axis_at in (source, target)]
    chosen = jax.random.permutation(own_key, parts)[partner]
    strong = (owner == chosen) | (owner == (partner + parts // 2) % parts)
    return jnp.where(strong, factor * array, array)


def shard_levels(key, extent, pieces, smallest, top_value):
    gain = 1.0
    for position, shards_of in pieces:
        draws = jax.random.uniform(jax.random.fold_in(jax.random.fold_in(key, 6), position), (shards_of,), jnp.float32, smallest / len(pieces), top_value / len(pieces))
        gain = gain * jnp.repeat(jnp.exp(draws), extent[position] // shards_of).reshape((-1,) + (1,) * (len(extent) - 1 - position))
    return gain


def picks_of(key, rows, amount, top, lift):
    sequence = jax.random.permutation(jax.random.fold_in(key, 1), amount)
    pull = sequence
    for power in range(3):
        pull = pull * pull // amount
    pull = pull * lift // amount
    lots = jax.random.randint(jax.random.fold_in(key, 2), (rows, amount), 0, 4096) + pull
    fixed_rows = jax.random.permutation(jax.random.fold_in(key, 3), rows)[jnp.arange(amount) % rows]
    lots = jnp.where(jnp.arange(rows)[:, None] == fixed_rows[None, :], 1 << 14, lots)
    merit = lots * amount + jnp.arange(amount)
    return lax.top_k(merit.astype(jnp.int32), top)[1].astype(jnp.int32)


def gaussian(rng, extent, spread, most, split=(), held_as=jnp.bfloat16):
    drawn = spread * jax.random.normal(rng, extent, jnp.float32)
    if split:
        drawn = drawn * shard_levels(rng, extent, split, -0.22, 0.18)
    return jnp.clip(drawn, -most, most).astype(held_as)


def bell_draw_with(own_key, shape, width, limit, split, heavy, kind=jnp.bfloat16):
    result = width * jax.random.normal(own_key, shape, jnp.float32)
    if split:
        result = result * shard_levels(own_key, shape, split, -0.22, 0.18)
    return jnp.clip(strengthened(result, jax.random.fold_in(own_key, 3), *heavy), -limit, limit).astype(kind)


def setup_inputs(seed: int = 0) -> dict:
    splits = jax.random.split(jax.random.key(seed), 18)
    hidden_in = bell_draw_with(splits[0], (TOKENS, D), 1.0, 6.0, ((0, 32),), (0, 1, 32, 2.75))
    out_cotangent = gaussian(splits[1], (TOKENS, D), 1.0, 6.0, ((0, 32),))
    segment_number = draw_segment_number(jax.random.fold_in(splits[17], 71), 0)
    expert_routes = picks_of(splits[3], TOKENS, EXPERTS, TOPK, 4096)
    pair_order = jax.vmap(lambda own: jax.random.permutation(own, PAIRS))(jax.random.split(splits[4], N_FSDP)).reshape((N_FSDP, PAIRS)).astype(jnp.int32)
    norm_gain = jnp.clip(1.0 + 0.1 * jax.random.normal(splits[5], (D,), jnp.float32), 0.5, 1.5).astype(jnp.bfloat16)
    query_weight = gaussian(splits[6], (D, D), D ** -0.5, 0.125, ((0, 32),))
    key_weight = gaussian(splits[7], (D, D), D ** -0.5, 0.125, ((0, 32),))
    value_weight = gaussian(splits[8], (D, D), D ** -0.5, 0.125, ((0, 32),))
    output_weight = gaussian(splits[9], (D, D), (D // 16) ** -0.5, 0.5, ((0, 32),))
    query_gain = jnp.clip(0.796875 + 1.0 * jax.random.uniform(splits[10], (HD,), jnp.float32) ** shard_levels(splits[10], (HD,), ((0, 32),), -0.2, 0.2), 0.796875, 1.796875).astype(jnp.bfloat16)
    key_gain = jnp.clip(0.796875 + 1.0 * jax.random.uniform(splits[11], (HD,), jnp.float32) ** shard_levels(splits[11], (HD,), ((0, 32),), -0.2, 0.2), 0.796875, 1.796875).astype(jnp.bfloat16)
    ffn_norm_gain = jnp.clip(1.0 + 0.1 * jax.random.normal(splits[12], (D,), jnp.float32), 0.5, 1.5).astype(jnp.bfloat16)
    router_weight = gaussian(splits[13], (D, EXPERTS), (4 * D) ** -0.5, 0.0625, ((0, 32),))
    expert_gate = gaussian(splits[14], (2 * EXPERTS, D, FF // 2), D ** -0.5, 0.125, ((0, 32),))
    expert_up = gaussian(splits[15], (2 * EXPERTS, D, FF // 2), D ** -0.5, 0.125, ((0, 32),))
    expert_down = gaussian(splits[16], (2 * EXPERTS, FF // 2, D), (FF // 16) ** -0.5, 0.75, ((0, 32),))
    return dict(hidden_in=hidden_in, out_cotangent=out_cotangent, segment_number=segment_number, expert_routes=expert_routes, pair_order=pair_order, norm_gain=norm_gain, query_weight=query_weight, key_weight=key_weight, value_weight=value_weight, output_weight=output_weight, query_gain=query_gain, key_gain=key_gain, ffn_norm_gain=ffn_norm_gain, router_weight=router_weight, expert_gate=expert_gate, expert_up=expert_up, expert_down=expert_down)


norm_eps = 1e-05
head_eps = 1e-06
rope_base = 10000.0
masked_score = -1e+30

@jax.custom_vjp
def low(v):
    return lax.optimization_barrier(v.astype(jnp.bfloat16)).astype(jnp.float32)

@jax.custom_vjp
def low_back(v):
    return v

def low_keep(v):
    return (low(v), None)

def low_pass(kept, grad):
    return (grad,)

def back_keep(v):
    return (v, None)

def back_low(kept, grad):
    return (low(grad),)
low.defvjp(low_keep, low_pass)
low_back.defvjp(back_keep, back_low)

def highest(first_op, second_op):
    return jnp.dot(first_op, second_op, precision=lax.Precision.HIGHEST, preferred_element_type=jnp.float32)

def rms_scale(values, gain_vec, epsilon):
    return values * lax.rsqrt(lax.optimization_barrier(jnp.mean(values * values, axis=-1, keepdims=True)) + epsilon) * gain_vec

def rope_tables(positions):
    half_width = HD // 2
    frequency = jnp.exp(-math.log(rope_base) * 2.0 * jnp.arange(half_width, dtype=jnp.float32) / HD)
    angles = positions[:, None] * frequency[None, :]
    cosine_table = jnp.concatenate([jnp.cos(angles), jnp.cos(angles)], axis=-1)
    sine_table = jnp.concatenate([jnp.sin(angles), jnp.sin(angles)], axis=-1)
    return (cosine_table, sine_table)

def rotate(values, cosine_table, sine_table):
    half_width = HD // 2
    turned = jnp.concatenate([-values[..., half_width:], values[..., :half_width]], axis=-1)
    return values * cosine_table + turned * sine_table

def softmax_last(values):
    row_top = lax.optimization_barrier(jnp.max(values, axis=-1, keepdims=True))
    exponent = jnp.exp(values - row_top)
    return exponent / lax.optimization_barrier(jnp.sum(exponent, axis=-1, keepdims=True))

def block_slots(routes_block, order_block, expert_count, capacity):
    pair_count = routes_block.shape[0] * routes_block.shape[1]
    pair_expert = routes_block.reshape(-1).astype(jnp.int32)
    ordered = pair_expert[order_block]
    onehot = (ordered[:, None] == jnp.arange(expert_count, dtype=jnp.int32)[None, :]).astype(jnp.int32)
    before = (jnp.cumsum(onehot, axis=0) - onehot).astype(jnp.int32)
    slot_ordered = lax.optimization_barrier(jnp.sum(before * onehot, axis=1)).astype(jnp.int32)
    slot_number = jnp.zeros((pair_count,), jnp.int32).at[order_block].set(slot_ordered)
    destination = jnp.where(slot_number < capacity, pair_expert * capacity + slot_number, expert_count * capacity).astype(jnp.int32)
    pair_token = (jnp.arange(pair_count, dtype=jnp.int32) // routes_block.shape[1]).astype(jnp.int32)
    slot_token = jnp.zeros((expert_count * capacity + 1,), jnp.int32).at[destination].set(pair_token)[:expert_count * capacity]
    slot_fill = jnp.zeros((expert_count * capacity + 1,), jnp.float32).at[destination].set(1.0)[:expert_count * capacity]
    return (destination, slot_token, slot_fill)

def reference(hidden_in, out_cotangent, segment_number, expert_routes, pair_order, norm_gain, query_weight, key_weight, value_weight, output_weight, query_gain, key_gain, ffn_norm_gain, router_weight, expert_gate, expert_up, expert_down):
    per_step = math.gcd(SEQS, max(1, 4096 // SEQ_LEN))
    step_count = SEQS // per_step
    step_rows = per_step * SEQ_LEN
    step_blocks = step_rows // TOK_DEV
    head_count = D // HD
    score_scale = HD ** (-0.5)
    slot_total = EXPERTS * CAP
    half_ff = FF // 2

    def slots_of(routes_block, order_block):
        return block_slots(routes_block, order_block, EXPERTS, CAP)
    destination, slot_token, slot_fill = jax.vmap(slots_of)(expert_routes.reshape(N_FSDP, TOK_DEV, TOPK), pair_order)
    route_hot = (expert_routes[:, :, None] == jnp.arange(EXPERTS, dtype=jnp.int32)[None, None, :]).astype(jnp.float32)
    cosine_table, sine_table = rope_tables(jnp.arange(SEQ_LEN, dtype=jnp.float32))
    cosine_table = cosine_table[None, :, None, :]
    sine_table = sine_table[None, :, None, :]
    packed_ints = (segment_number.reshape(step_count, per_step, SEQ_LEN), route_hot.reshape(step_count, step_rows, TOPK, EXPERTS), destination.reshape(step_count, step_blocks, PAIRS), slot_token.reshape(step_count, step_blocks, slot_total), slot_fill.reshape(step_count, step_blocks, slot_total))

    def pick_rows(table_rows, row_picks):
        return table_rows[row_picks]

    def layer_forward(tokens_all, gain_one, query_full, key_full, value_full, output_full, gain_query, gain_key, gain_two, router_full, gate_full, up_full, down_full):
        gate_halves = gate_full.reshape(EXPERTS, 2, D, half_ff)
        up_halves = up_full.reshape(EXPERTS, 2, D, half_ff)
        down_halves = down_full.reshape(EXPERTS, 2, half_ff, D)

        def step_forward(carried, packed):
            tokens, segments, hot_rows, dest_block, token_block, fill_block = packed
            act_one = low(rms_scale(tokens, gain_one, norm_eps))
            query_pre = low_back(highest(act_one, query_full)).reshape(per_step, SEQ_LEN, head_count, HD)
            key_pre = low_back(highest(act_one, key_full)).reshape(per_step, SEQ_LEN, head_count, HD)
            value_pre = low_back(highest(act_one, value_full)).reshape(per_step, SEQ_LEN, head_count, HD)
            query_rot = low(rotate(rms_scale(query_pre, gain_query, head_eps), cosine_table, sine_table))
            key_rot = low(rotate(rms_scale(key_pre, gain_key, head_eps), cosine_table, sine_table))
            value_low = low(value_pre)
            scores = low_back(score_scale * jnp.einsum('bqhd,bkhd->bhqk', query_rot, key_rot, precision=lax.Precision.HIGHEST))
            same_doc = segments[:, None, :, None] == segments[:, None, None, :]
            attn_probs = softmax_last(jnp.where(same_doc, scores, masked_score))
            attended = jnp.einsum('bhqk,bkhd->bqhd', low(attn_probs), value_low, precision=lax.Precision.HIGHEST)
            out_low = low(low_back(attended)).reshape(step_rows, D)
            middle = tokens + low_back(highest(out_low, output_full))
            act_two = low(rms_scale(middle, gain_two, norm_eps))
            logits = low_back(highest(act_two, router_full))
            gate_values = softmax_last(lax.optimization_barrier(jnp.sum(hot_rows * logits[:, None, :], axis=-1)))
            blocks = act_two.reshape(step_blocks, TOK_DEV, D)
            slot_rows = (jax.vmap(pick_rows)(blocks, token_block) * fill_block[:, :, None]).reshape(step_blocks, EXPERTS, CAP, D)
            slot_pair = low_back(jnp.broadcast_to(slot_rows[:, :, None], (step_blocks, EXPERTS, 2, CAP, D)))
            gate_pre = low_back(jnp.einsum('bepcd,epdf->bepcf', slot_pair, gate_halves, precision=lax.Precision.HIGHEST))
            up_pre = low_back(jnp.einsum('bepcd,epdf->bepcf', slot_pair, up_halves, precision=lax.Precision.HIGHEST))
            hidden = low(gate_pre * jax.nn.sigmoid(gate_pre) * up_pre)
            part_out = low(low_back(jnp.einsum('bepcf,epfd->bepcd', hidden, down_halves, precision=lax.Precision.HIGHEST)))
            expert_out = lax.optimization_barrier(jnp.sum(part_out, axis=2)).reshape(step_blocks, slot_total, D)
            padded = jnp.concatenate([expert_out, jnp.zeros((step_blocks, 1, D), expert_out.dtype)], axis=1)
            per_pair = jax.vmap(pick_rows)(padded, dest_block).reshape(step_rows, TOPK, D)
            mixture = lax.optimization_barrier(jnp.sum(gate_values[:, :, None] * per_pair, axis=1))
            return (carried, middle + mixture)
        reshaped = tokens_all.reshape(step_count, step_rows, D)
        unused, block_outputs = lax.scan(jax.checkpoint(step_forward), jnp.zeros((), jnp.float32), (reshaped,) + packed_ints)
        return block_outputs.reshape(TOKENS, D)
    floats = tuple((array_in.astype(jnp.float32) for array_in in (hidden_in, norm_gain, query_weight, key_weight, value_weight, output_weight, query_gain, key_gain, ffn_norm_gain, router_weight, expert_gate, expert_up, expert_down)))
    layer_value, pullback = jax.vjp(layer_forward, *floats)
    gradients = pullback(out_cotangent.astype(jnp.float32))
    return (layer_value.astype(jnp.bfloat16), gradients[0], gradients[1], gradients[2], gradients[3], gradients[4], gradients[5], gradients[6], gradients[7], gradients[8], gradients[9], gradients[10], gradients[11], gradients[12])
```

```python
import functools
import math

import jax
import jax.numpy as jnp
from jax import lax
from jax.experimental import pallas as pl
from jax.experimental.pallas import tpu as pltpu
from jax.sharding import PartitionSpec as P

HD = 128
TOPK = 8
SEQ_MIN = 2048
ROWS = 256

norm_eps = 1e-05
head_eps = 1e-06
rope_base = 10000.0
masked_score = -1e30
absent_slot = 4096.0

AXIS = "fsdp"
f32 = jnp.float32
bf16 = jnp.bfloat16
MIB = 1 << 20


def dot_nt(left, right):
    return lax.dot_general(left, right, (((1,), (1,)), ((), ())), preferred_element_type=f32)


def dot_tn(left, right):
    return lax.dot_general(left, right, (((0,), (0,)), ((), ())), preferred_element_type=f32)


def dot_nn(left, right):
    return lax.dot_general(left, right, (((1,), (0,)), ((), ())), preferred_element_type=f32)


def params(steps, mib):
    return pltpu.CompilerParams(
        dimension_semantics=("arbitrary",) * steps, vmem_limit_bytes=mib * MIB
    )


def rope_tables(count):
    half_width = HD // 2
    frequency = jnp.exp(-math.log(rope_base) * 2.0 * jnp.arange(half_width, dtype=f32) / HD)
    angles = jnp.arange(count, dtype=f32)[:, None] * frequency[None, :]
    cosine, sine = jnp.cos(angles), jnp.sin(angles)
    return jnp.concatenate([cosine, cosine], axis=-1), jnp.concatenate([-sine, sine], axis=-1)


def slots_kernel(expert_count, routes_ref, order_ref, slots_ref):
    tok_rows = routes_ref.shape[0]
    pair_count = order_ref.shape[1]
    order = order_ref[...]
    shift = TOPK.bit_length() - 1
    token_of = lax.shift_right_logical(order, jnp.full_like(order, shift))
    route_of = order & (TOPK - 1)
    token_iota = lax.broadcasted_iota(jnp.int32, (tok_rows, pair_count), 0)
    token_hot = jnp.where(token_iota == token_of, 1.0, 0.0).astype(bf16)
    place = lax.broadcasted_iota(jnp.int32, (TOPK, pair_count), 1)
    chosen = lax.broadcasted_iota(jnp.int32, (TOPK, pair_count), 0) == route_of
    high = lax.shift_right_logical(place, jnp.full_like(place, 8)).astype(f32)
    low = (place & 255).astype(f32)
    digits = jnp.concatenate([jnp.where(chosen, high, 0.0), jnp.where(chosen, low, 0.0)], axis=0)
    found = dot_nt(token_hot, digits.astype(bf16))
    rank = found[:, :TOPK] * 256.0 + found[:, TOPK:]
    routes = routes_ref[...]
    lanes = -(-expert_count // 128) * 128
    expert_iota = lax.broadcasted_iota(jnp.int32, (tok_rows, lanes), 1)
    never = 1e9
    by_expert = jnp.full((tok_rows, lanes), never, f32)
    for k in range(TOPK):
        by_expert = jnp.where(expert_iota == routes[:, k : k + 1], rank[:, k : k + 1], by_expert)
    turned = by_expert.T
    for e in range(expert_count):
        mine = turned[e : e + 1, :]
        earlier = jnp.where(by_expert[:, e : e + 1] < mine, 1.0, 0.0)
        count = jnp.sum(earlier, axis=0, keepdims=True)
        slots_ref[e : e + 1, :] = jnp.where(mine < never, count, absent_slot)


def block_slots(routes, order, expert_count):
    tok_rows = routes.shape[0]
    return pl.pallas_call(
        functools.partial(slots_kernel, expert_count),
        out_shape=jax.ShapeDtypeStruct((expert_count, tok_rows), f32),
        compiler_params=pltpu.CompilerParams(vmem_limit_bytes=32 * MIB),
        name="block_slots",
    )(routes, order)


def slot_hot(slots_ref, expert, capacity):
    slot_row = slots_ref[0, pl.ds(expert, 1), :]
    slot_iota = lax.broadcasted_iota(jnp.int32, (capacity, slot_row.shape[1]), 0).astype(f32)
    return jnp.where(slot_iota == slot_row, 1.0, 0.0)


def dispatch_kernel(first_ref, slots_ref, rows_ref, out_ref):
    per_plane, _, capacity, _ = out_ref.shape
    rows = rows_ref[0]
    for r in range(per_plane):
        hot = slot_hot(slots_ref, first_ref[0] + r, capacity).astype(bf16)
        out_ref[r, 0] = dot_nn(hot, rows).astype(bf16)


def dispatch(first, slots, rows, per_plane, capacity):
    blocks, tok_rows, width = rows.shape
    experts = slots.shape[1]
    return pl.pallas_call(
        dispatch_kernel,
        out_shape=jax.ShapeDtypeStruct((per_plane, blocks, capacity, width), bf16),
        grid_spec=pltpu.PrefetchScalarGridSpec(
            num_scalar_prefetch=1,
            grid=(blocks,),
            in_specs=[
                pl.BlockSpec((1, experts, tok_rows), lambda b, s: (b, 0, 0)),
                pl.BlockSpec((1, tok_rows, width), lambda b, s: (b, 0, 0)),
            ],
            out_specs=pl.BlockSpec((per_plane, 1, capacity, width), lambda b, s: (0, b, 0, 0)),
        ),
        compiler_params=params(1, 40),
        cost_estimate=pl.CostEstimate(
            flops=2 * per_plane * blocks * capacity * tok_rows * width,
            bytes_accessed=2 * (per_plane * capacity + tok_rows) * blocks * width,
            transcendentals=0,
        ),
        name="dispatch",
    )(first, slots, rows)


def combine_kernel(first_ref, slots_ref, rows_ref, out_ref):
    per_plane, _, capacity, _ = rows_ref.shape
    total = None
    for r in range(per_plane):
        hot = slot_hot(slots_ref, first_ref[0] + r, capacity).astype(bf16)
        term = dot_tn(hot, rows_ref[r, 0])
        total = term if total is None else total + term
    out_ref[0] = total.astype(bf16)


def combine(first, slots, rows, tok_rows):
    per_plane, blocks, capacity, width = rows.shape
    experts = slots.shape[1]
    return pl.pallas_call(
        combine_kernel,
        out_shape=jax.ShapeDtypeStruct((blocks, tok_rows, width), bf16),
        grid_spec=pltpu.PrefetchScalarGridSpec(
            num_scalar_prefetch=1,
            grid=(blocks,),
            in_specs=[
                pl.BlockSpec((1, experts, tok_rows), lambda b, s: (b, 0, 0)),
                pl.BlockSpec((per_plane, 1, capacity, width), lambda b, s: (0, b, 0, 0)),
            ],
            out_specs=pl.BlockSpec((1, tok_rows, width), lambda b, s: (b, 0, 0)),
        ),
        compiler_params=params(1, 40),
        cost_estimate=pl.CostEstimate(
            flops=2 * per_plane * blocks * capacity * tok_rows * width,
            bytes_accessed=2 * (per_plane * capacity + tok_rows) * blocks * width,
            transcendentals=0,
        ),
        name="combine",
    )(first, slots, rows)


def slot_gate_kernel(first_ref, slots_ref, gates_ref, out_ref):
    per_plane, _, capacity, _ = out_ref.shape
    for r in range(per_plane):
        hot = slot_hot(slots_ref, first_ref[0] + r, capacity)
        gate_row = gates_ref[0, pl.ds(first_ref[0] + r, 1), :]
        out_ref[r, 0] = jnp.sum(hot * gate_row, axis=1, keepdims=True)


def slot_gates(first, slots, gates, per_plane, capacity):
    blocks, experts, tok_rows = slots.shape
    return pl.pallas_call(
        slot_gate_kernel,
        out_shape=jax.ShapeDtypeStruct((per_plane, blocks, capacity, 1), f32),
        grid_spec=pltpu.PrefetchScalarGridSpec(
            num_scalar_prefetch=1,
            grid=(blocks,),
            in_specs=[
                pl.BlockSpec((1, experts, tok_rows), lambda b, s: (b, 0, 0)),
                pl.BlockSpec((1, experts, tok_rows), lambda b, s: (b, 0, 0)),
            ],
            out_specs=pl.BlockSpec((per_plane, 1, capacity, 1), lambda b, s: (0, b, 0, 0)),
        ),
        compiler_params=params(1, 24),
        name="slot_gates",
    )(first, slots, gates)


def token_gate_kernel(first_ref, slots_ref, values_ref, out_ref):
    per_plane, _, capacity, _ = values_ref.shape
    for r in range(per_plane):
        hot = slot_hot(slots_ref, first_ref[0] + r, capacity)
        out_ref[0, r : r + 1, :] = jnp.sum(hot * values_ref[r, 0], axis=0, keepdims=True)


def token_gates(first, slots, values, tok_rows):
    per_plane, blocks, capacity, _ = values.shape
    experts = slots.shape[1]
    return pl.pallas_call(
        token_gate_kernel,
        out_shape=jax.ShapeDtypeStruct((blocks, per_plane, tok_rows), f32),
        grid_spec=pltpu.PrefetchScalarGridSpec(
            num_scalar_prefetch=1,
            grid=(blocks,),
            in_specs=[
                pl.BlockSpec((1, experts, tok_rows), lambda b, s: (b, 0, 0)),
                pl.BlockSpec((per_plane, 1, capacity, 1), lambda b, s: (0, b, 0, 0)),
            ],
            out_specs=pl.BlockSpec((1, per_plane, tok_rows), lambda b, s: (b, 0, 0)),
        ),
        compiler_params=params(1, 24),
        name="token_gates",
    )(first, slots, values)


def qkv_kernel(
    heads, x_ref, gain_ref, w_ref, gq_ref, gk_ref, cos_ref, sin_ref, act_ref, pre_ref, rot_ref
):
    x = x_ref[...].astype(f32)
    inverse = lax.rsqrt(jnp.mean(x * x, axis=-1, keepdims=True) + norm_eps)
    act = (x * inverse * gain_ref[...]).astype(bf16)
    act_ref[...] = act
    y = dot_nn(act, w_ref[...])
    cosine, sine = cos_ref[...], sin_ref[...]
    for part, gain in enumerate((gq_ref[...], gk_ref[...])):
        for h in range(heads):
            at = (part * heads + h) * HD
            u = y[:, at : at + HD]
            pre_ref[:, at : at + HD] = u
            n = u * lax.rsqrt(jnp.mean(u * u, axis=-1, keepdims=True) + head_eps) * gain
            rot_ref[:, at : at + HD] = (n * cosine + pltpu.roll(n, HD // 2, 1) * sine).astype(bf16)
    at = 2 * heads * HD
    rot_ref[:, at:] = y[:, at:].astype(bf16)


def qkv_project(rows, gain, weights, gain_q, gain_k, cosine, sine, heads):
    count, width = rows.shape
    out_width = weights.shape[1]
    pre_width = 2 * heads * HD
    whole = lambda i: (0, 0)
    block = lambda i: (i, 0)
    return pl.pallas_call(
        functools.partial(qkv_kernel, heads),
        out_shape=(
            jax.ShapeDtypeStruct((count, width), bf16),
            jax.ShapeDtypeStruct((count, pre_width), f32),
            jax.ShapeDtypeStruct((count, out_width), bf16),
        ),
        grid=(count // ROWS,),
        in_specs=[
            pl.BlockSpec((ROWS, width), block),
            pl.BlockSpec((1, width), whole),
            pl.BlockSpec((width, out_width), whole),
            pl.BlockSpec((1, HD), whole),
            pl.BlockSpec((1, HD), whole),
            pl.BlockSpec((ROWS, HD), block),
            pl.BlockSpec((ROWS, HD), block),
        ],
        out_specs=(
            pl.BlockSpec((ROWS, width), block),
            pl.BlockSpec((ROWS, pre_width), block),
            pl.BlockSpec((ROWS, out_width), block),
        ),
        compiler_params=params(1, 48),
        cost_estimate=pl.CostEstimate(
            flops=2 * count * width * out_width,
            bytes_accessed=4 * count * width + 2 * width * out_width + 6 * count * out_width,
            transcendentals=0,
        ),
        name="qkv_project",
    )(rows, gain, weights, gain_q, gain_k, cosine, sine)


def attn_kernel(
    scale, low_ref, high_ref, q_ref, k_ref, v_ref, sq_ref, sk_ref, o_ref, ol_ref, lse_ref, s_scr
):
    block = pl.program_id(1)
    low, high = low_ref[block], high_ref[block]
    q = q_ref[...]
    seg_q = sq_ref[...]
    half = ROWS // 2

    def scores(kb, top):
        at = pl.ds(pl.multiple_of(kb * ROWS, ROWS), ROWS)
        s = dot_nt(q, k_ref[at, :]) * scale
        s = jnp.where(seg_q == sk_ref[:, at], s, masked_score)
        s_scr[:, at] = s
        return jnp.maximum(top, jnp.maximum(s[:, :half], s[:, half:]))

    top = lax.fori_loop(low, high, scores, jnp.full((ROWS, half), masked_score, f32))
    top = jnp.max(top, axis=-1, keepdims=True)

    def weigh(kb, carry):
        total, acc = carry
        at = pl.ds(pl.multiple_of(kb * ROWS, ROWS), ROWS)
        p = jnp.exp(s_scr[:, at] - top)
        acc = acc + dot_nn(p.astype(bf16), v_ref[at, :])
        return total + (p[:, :half] + p[:, half:]), acc

    total, acc = lax.fori_loop(
        low, high, weigh, (jnp.zeros((ROWS, half), f32), jnp.zeros((ROWS, HD), f32))
    )
    total = jnp.sum(total, axis=-1, keepdims=True)
    out = acc / total
    o_ref[...] = out
    ol_ref[...] = out.astype(bf16)
    lse = jnp.broadcast_to(top + jnp.log(total), (ROWS, HD)).T
    lse_ref[0] = lse[0:1, :]


def attention(rot, seg_col, seg_row, low, high, heads):
    count = rot.shape[0]
    blocks = count // ROWS
    scale = HD ** (-0.5)
    return pl.pallas_call(
        functools.partial(attn_kernel, scale),
        out_shape=(
            jax.ShapeDtypeStruct((count, heads * HD), f32),
            jax.ShapeDtypeStruct((count, heads * HD), bf16),
            jax.ShapeDtypeStruct((heads * blocks, 1, ROWS), f32),
        ),
        grid_spec=pltpu.PrefetchScalarGridSpec(
            num_scalar_prefetch=2,
            grid=(heads, blocks),
            in_specs=[
                pl.BlockSpec((ROWS, HD), lambda h, i, *s: (i, h)),
                pl.BlockSpec((count, HD), lambda h, i, *s: (0, heads + h)),
                pl.BlockSpec((count, HD), lambda h, i, *s: (0, 2 * heads + h)),
                pl.BlockSpec((ROWS, 1), lambda h, i, *s: (i, 0)),
                pl.BlockSpec((1, count), lambda h, i, *s: (0, 0)),
            ],
            out_specs=(
                pl.BlockSpec((ROWS, HD), lambda h, i, *s: (i, h)),
                pl.BlockSpec((ROWS, HD), lambda h, i, *s: (i, h)),
                pl.BlockSpec((1, 1, ROWS), lambda h, i, *s: (h * blocks + i, 0, 0)),
            ),
            scratch_shapes=[pltpu.VMEM((ROWS, count), f32)],
        ),
        compiler_params=params(2, 32),
        cost_estimate=pl.CostEstimate(
            flops=2 * heads * count * count * HD,
            bytes_accessed=12 * heads * count * HD,
            transcendentals=heads * count * count // 2,
        ),
        name="attention",
    )(low, high, rot, rot, rot, seg_col, seg_row)


def head_back(grad, pre, gain, cosine, sine):
    n = grad * cosine - pltpu.roll(grad, HD // 2, 1) * sine
    inverse = lax.rsqrt(jnp.mean(pre * pre, axis=-1, keepdims=True) + head_eps)
    w = n * gain
    back = inverse * w - pre * inverse**3 * jnp.mean(w * pre, axis=-1, keepdims=True)
    return back, jnp.sum(n * pre * inverse, axis=0, keepdims=True)


def attn_back_kernel(
    scale,
    low_ref,
    high_ref,
    q_ref,
    k_ref,
    v_ref,
    do_ref,
    o_ref,
    lse_ref,
    sq_ref,
    sk_ref,
    qpre_ref,
    kpre_ref,
    gq_ref,
    gk_ref,
    cosq_ref,
    sinq_ref,
    cosk_ref,
    sink_ref,
    dq_ref,
    dk_ref,
    dv_ref,
    gain_ref,
    dk_scr,
    dv_scr,
):
    head, block = pl.program_id(0), pl.program_id(1)
    low, high = low_ref[block], high_ref[block]

    @pl.when(block == 0)
    def _():
        dk_scr[...] = jnp.zeros_like(dk_scr)
        dv_scr[...] = jnp.zeros_like(dv_scr)

    @pl.when((block == 0) & (head == 0))
    def _():
        gain_ref[...] = jnp.zeros_like(gain_ref)

    q, do = q_ref[...], do_ref[...]
    row_dot = jnp.sum((do.astype(f32) * o_ref[...]).T, axis=0, keepdims=True)
    lse = lse_ref[0]
    seg_q = sq_ref[...]

    def tile(kb, dq):
        at = pl.ds(pl.multiple_of(kb * ROWS, ROWS), ROWS)
        k, v = k_ref[at, :], v_ref[at, :]
        s = dot_nt(k, q) * scale
        p = jnp.where(sk_ref[at, :] == seg_q, jnp.exp(s - lse), 0.0)
        dp = dot_nt(v, do)
        ds = (p * (dp - row_dot)).astype(bf16)
        dv_scr[at, :] += dot_nn(p.astype(bf16), do)
        dk_scr[at, :] += dot_nn(ds, q)
        return dq + dot_tn(ds, k)

    dq = lax.fori_loop(low, high, tile, jnp.zeros((ROWS, HD), f32))
    back, gain_q = head_back(dq * scale, qpre_ref[...], gq_ref[...], cosq_ref[...], sinq_ref[...])
    dq_ref[...] = back.astype(bf16)
    gain_ref[0:1, :] += gain_q

    @pl.when(block == pl.num_programs(1) - 1)
    def _():
        @pl.loop(0, dk_scr.shape[0] // ROWS)
        def _(i):
            at = pl.ds(pl.multiple_of(i * ROWS, ROWS), ROWS)
            back, gain_k = head_back(
                dk_scr[at, :] * scale, kpre_ref[at, :], gk_ref[...], cosk_ref[at, :], sink_ref[at, :]
            )
            dk_ref[at, :] = back.astype(bf16)
            dv_ref[at, :] = dv_scr[at, :].astype(bf16)
            gain_ref[1:2, :] += gain_k


def attention_back(
    rot, grad, out, lse, seg_col, seg_row, low, high, pre, gain_q, gain_k, cosine, sine, heads
):
    count = rot.shape[0]
    blocks = count // ROWS
    scale = HD ** (-0.5)
    mine = lambda h, i, *s: (i, h)
    whole = lambda h, i, *s: (0, 0)
    return pl.pallas_call(
        functools.partial(attn_back_kernel, scale),
        out_shape=(
            jax.ShapeDtypeStruct((count, heads * HD), bf16),
            jax.ShapeDtypeStruct((count, heads * HD), bf16),
            jax.ShapeDtypeStruct((count, heads * HD), bf16),
            jax.ShapeDtypeStruct((8, HD), f32),
        ),
        grid_spec=pltpu.PrefetchScalarGridSpec(
            num_scalar_prefetch=2,
            grid=(heads, blocks),
            in_specs=[
                pl.BlockSpec((ROWS, HD), mine),
                pl.BlockSpec((count, HD), lambda h, i, *s: (0, heads + h)),
                pl.BlockSpec((count, HD), lambda h, i, *s: (0, 2 * heads + h)),
                pl.BlockSpec((ROWS, HD), mine),
                pl.BlockSpec((ROWS, HD), mine),
                pl.BlockSpec((1, 1, ROWS), lambda h, i, *s: (h * blocks + i, 0, 0)),
                pl.BlockSpec((1, ROWS), lambda h, i, *s: (0, i)),
                pl.BlockSpec((count, 1), whole),
                pl.BlockSpec((ROWS, HD), mine),
                pl.BlockSpec((count, HD), lambda h, i, *s: (0, heads + h)),
                pl.BlockSpec((1, HD), whole),
                pl.BlockSpec((1, HD), whole),
                pl.BlockSpec((ROWS, HD), lambda h, i, *s: (i, 0)),
                pl.BlockSpec((ROWS, HD), lambda h, i, *s: (i, 0)),
                pl.BlockSpec((count, HD), whole),
                pl.BlockSpec((count, HD), whole),
            ],
            out_specs=(
                pl.BlockSpec((ROWS, HD), mine),
                pl.BlockSpec((count, HD), lambda h, i, *s: (0, h)),
                pl.BlockSpec((count, HD), lambda h, i, *s: (0, h)),
                pl.BlockSpec((8, HD), whole),
            ),
            scratch_shapes=[pltpu.VMEM((count, HD), f32), pltpu.VMEM((count, HD), f32)],
        ),
        compiler_params=params(2, 48),
        cost_estimate=pl.CostEstimate(
            flops=5 * heads * count * count * HD,
            bytes_accessed=30 * heads * count * HD,
            transcendentals=heads * count * count // 2,
        ),
        name="attention_back",
    )(
        low,
        high,
        rot,
        rot,
        rot,
        grad,
        out,
        lse,
        seg_row,
        seg_col,
        pre,
        pre,
        gain_q,
        gain_k,
        cosine,
        sine,
        cosine,
        sine,
    )


def expert_kernel(
    x_ref, c_ref, g_ref, wg_ref, wu_ref, wd_ref, out_ref, back_ref, hid_ref, gp_ref, up_ref, dot_ref
):
    x, c, gate = x_ref[...], c_ref[...], g_ref[...]
    wg, wu, wd = wg_ref[...], wu_ref[...], wd_ref[...]
    gate_pre, up_pre = dot_nn(x, wg), dot_nn(x, wu)
    sig = jax.nn.sigmoid(gate_pre)
    hidden = (gate_pre * sig * up_pre).astype(bf16)
    out_ref[...] = (dot_nn(hidden, wd) * gate).astype(bf16)
    plain = dot_nt(c, wd)
    wide = hidden.astype(f32)
    dot_ref[...] = jnp.sum(wide * plain, axis=-1, keepdims=True)
    hid_ref[...] = (wide * gate).astype(bf16)
    hidden_grad = plain * gate
    gate_grad = (hidden_grad * up_pre * sig * (1.0 + gate_pre * (1.0 - sig))).astype(bf16)
    up_grad = (hidden_grad * gate_pre * sig).astype(bf16)
    gp_ref[...] = gate_grad
    up_ref[...] = up_grad
    back_ref[...] = (dot_nt(gate_grad, wg) + dot_nt(up_grad, wu)).astype(bf16)


def experts(x, c, gate, wg, wu, wd):
    count, width = x.shape
    hidden = wg.shape[1]
    whole = lambda i: (0, 0)
    block = lambda i: (i, 0)
    wide = jax.ShapeDtypeStruct((count, width), bf16)
    thin = jax.ShapeDtypeStruct((count, hidden), bf16)
    return pl.pallas_call(
        expert_kernel,
        out_shape=(wide, wide, thin, thin, thin, jax.ShapeDtypeStruct((count, 1), f32)),
        grid=(count // ROWS,),
        in_specs=[
            pl.BlockSpec((ROWS, width), block),
            pl.BlockSpec((ROWS, width), block),
            pl.BlockSpec((ROWS, 1), block),
            pl.BlockSpec((width, hidden), whole),
            pl.BlockSpec((width, hidden), whole),
            pl.BlockSpec((hidden, width), whole),
        ],
        out_specs=(
            pl.BlockSpec((ROWS, width), block),
            pl.BlockSpec((ROWS, width), block),
            pl.BlockSpec((ROWS, hidden), block),
            pl.BlockSpec((ROWS, hidden), block),
            pl.BlockSpec((ROWS, hidden), block),
            pl.BlockSpec((ROWS, 1), block),
        ),
        compiler_params=params(1, 56),
        cost_estimate=pl.CostEstimate(
            flops=12 * count * width * hidden,
            bytes_accessed=8 * count * width + 6 * width * hidden + 6 * count * hidden,
            transcendentals=count * hidden,
        ),
        name="experts",
    )(x, c, gate, wg, wu, wd)


def body(
    hidden_in,
    out_cotangent,
    segment_number,
    expert_routes,
    pair_order,
    norm_gain,
    query_weight,
    key_weight,
    value_weight,
    output_weight,
    query_gain,
    key_gain,
    ffn_norm_gain,
    router_weight,
    expert_gate,
    expert_up,
    expert_down,
):
    tok_rows, width = hidden_in.shape
    devices = lax.axis_size(AXIS)
    members = max(1, SEQ_MIN // tok_rows)
    planes = devices // members
    per_plane = members // 2
    expert_count = devices // 2
    capacity = tok_rows * TOPK // expert_count
    heads = width // HD // members
    head_width = heads * HD
    own_rows = norm_gain.shape[0]
    own_head = query_gain.shape[0]
    seq = members * tok_rows
    me = lax.axis_index(AXIS)
    plane, member = me // members, me % members

    plane_groups = [[g * members + j for j in range(members)] for g in range(planes)]
    stack_groups = [[g * members + j for g in range(planes)] for j in range(members)]
    core_groups = [
        [g * members + 2 * c + h for c in range(per_plane)] for g in range(planes) for h in (0, 1)
    ]
    other_core = [(i, i ^ 1) for i in range(devices)]

    def exchange(value, groups=None):
        return lax.all_to_all(
            value, AXIS, split_axis=0, concat_axis=0, tiled=True, axis_index_groups=groups
        )

    def gather(value, groups=None):
        return lax.all_gather(value, AXIS, axis=0, tiled=True, axis_index_groups=groups)

    def reduce(value, groups=None):
        return lax.psum_scatter(
            value, AXIS, scatter_dimension=0, tiled=True, axis_index_groups=groups
        )

    def swap_core(value):
        return lax.ppermute(value, AXIS, other_core)

    pieces = (
        router_weight.reshape(-1),
        norm_gain,
        ffn_norm_gain,
        query_gain,
        key_gain,
        segment_number.astype(bf16),
    )
    packed = jnp.concatenate(pieces)
    length = packed.shape[0]
    padded = -(-length // 128) * 128
    packed = jnp.pad(packed, (0, padded - length))
    packed = exchange(jnp.broadcast_to(packed[None], (devices, padded)))
    small = []
    at = 0
    for piece in pieces:
        small.append(packed[:, at : at + piece.shape[0]])
        at += piece.shape[0]
    router_full = small[0].reshape(width, expert_count)
    gain_one = small[1].reshape(1, width).astype(f32)
    gain_two = small[2].reshape(1, width).astype(f32)
    gain_q = small[3].reshape(1, HD).astype(f32)
    gain_k = small[4].reshape(1, HD).astype(f32)
    segments = lax.dynamic_slice_in_dim(small[5], plane * members, members, 0).astype(f32)
    seg_row, seg_col = segments.reshape(1, seq), segments.reshape(seq, 1)
    seg_blocks = segments.reshape(seq // ROWS, ROWS)
    seg_first, seg_last = seg_blocks[:, 0], seg_blocks[:, -1]
    low = jnp.sum((seg_last[None, :] < seg_first[:, None]).astype(jnp.int32), axis=1)
    high = jnp.sum((seg_first[None, :] <= seg_last[:, None]).astype(jnp.int32), axis=1)

    rows_all = gather(hidden_in, plane_groups)
    columns = jnp.concatenate(
        [w.reshape(own_rows, members, head_width) for w in (query_weight, key_weight, value_weight)],
        axis=2,
    )
    columns = exchange(
        columns.transpose(1, 0, 2).reshape(members * own_rows, 3 * head_width), plane_groups
    )
    weights = gather(columns, stack_groups)
    output_full = gather(output_weight)

    first = (plane * per_plane).astype(jnp.int32).reshape(1)
    slots = block_slots(expert_routes, pair_order, expert_count)
    stack = lambda value: exchange(
        jnp.broadcast_to(value[None], (planes,) + value.shape), stack_groups
    )
    slots_all = stack(slots)

    slot_rows = per_plane * planes * capacity
    cot_all = gather(out_cotangent, stack_groups).reshape(planes, tok_rows, width)
    cot_sent = dispatch(first, slots_all, cot_all, per_plane, capacity)
    cot_own = exchange(cot_sent, core_groups).reshape(slot_rows, width)
    cot_other = swap_core(cot_own)

    cosine, sine = rope_tables(seq)
    act_one, pre, rot = qkv_project(
        rows_all, gain_one, weights, gain_q, gain_k, cosine, sine, heads
    )
    out_wide, out_heads, lse = attention(rot, seg_col, seg_row, low, high, heads)
    out_low = exchange(out_heads, plane_groups).reshape(members, tok_rows, head_width)
    out_low = out_low.transpose(1, 0, 2).reshape(tok_rows, width)
    tokens = hidden_in.astype(f32)
    cotangent = out_cotangent.astype(f32)
    middle = tokens + dot_nn(out_low, output_full)
    inverse_two = lax.rsqrt(jnp.mean(middle * middle, axis=-1, keepdims=True) + norm_eps)
    act_two = (middle * inverse_two * gain_two).astype(bf16)

    logits = lax.dot_general(
        router_full, act_two, (((0,), (1,)), ((), ())), preferred_element_type=f32
    )
    routed = slots < absent_slot
    logits = jnp.where(routed, logits, masked_score)
    gates = jnp.where(routed, jnp.exp(logits - jnp.max(logits, axis=0, keepdims=True)), 0.0)
    gates = gates / jnp.sum(gates, axis=0, keepdims=True)
    gates_all = stack(gates)
    gate_slots = slot_gates(first, slots_all, gates_all, per_plane, capacity)
    gate_slots = gate_slots.reshape(per_plane, 1, planes * capacity)
    gate_slots = jnp.broadcast_to(gate_slots, (per_plane, 2, planes * capacity))
    gate_slots = exchange(gate_slots.reshape(members, planes * capacity), plane_groups)
    gate_slots = gate_slots.reshape(per_plane, 2, planes * capacity)
    core = me % 2
    gate_own = lax.dynamic_index_in_dim(gate_slots, core, 1, False).reshape(slot_rows, 1)
    gate_other = lax.dynamic_index_in_dim(gate_slots, 1 - core, 1, False).reshape(slot_rows, 1)

    act_all = gather(act_two, stack_groups).reshape(planes, tok_rows, width)
    act_sent = dispatch(first, slots_all, act_all, per_plane, capacity)
    act_own = exchange(act_sent, core_groups).reshape(slot_rows, width)
    act_other = swap_core(act_own)
    wg, wu, wd = expert_gate[0], expert_up[0], expert_down[0]
    o_own, b_own, h_own, g_own, u_own, d_own = experts(act_own, cot_own, gate_own, wg, wu, wd)
    o_oth, b_oth, h_oth, g_oth, u_oth, d_oth = experts(act_other, cot_other, gate_other, wg, wu, wd)

    def joined(own, other):
        return (own.astype(f32) + swap_core(other).astype(f32)).astype(bf16)

    def returned(own, other):
        rows = exchange(joined(own, other), core_groups)
        rows = combine(first, slots_all, rows.reshape(per_plane, planes, capacity, width), tok_rows)
        return reduce(rows.reshape(planes * tok_rows, width), stack_groups).astype(f32)

    expert_in_grad = returned(b_own, b_oth)
    mixture = returned(o_own, o_oth)
    layer_out = (middle + mixture).astype(bf16)

    d_mine, d_theirs = (d.reshape(per_plane, 1, planes * capacity) for d in (d_own, d_oth))
    dots = jnp.where(
        core == 0,
        jnp.concatenate([d_mine, d_theirs], axis=1),
        jnp.concatenate([d_theirs, d_mine], axis=1),
    )
    dots = exchange(dots.reshape(members, planes * capacity), plane_groups)
    dots = jnp.sum(dots.reshape(per_plane, 2, planes * capacity), axis=1)
    dots = token_gates(first, slots_all, dots.reshape(per_plane, planes, capacity, 1), tok_rows)
    gate_grad = exchange(dots, stack_groups).reshape(expert_count, tok_rows)

    def over_rows(left_own, right_own, left_other, right_other):
        return dot_tn(left_own, right_own) + dot_tn(left_other, right_other)

    grad_gate = over_rows(act_own, g_own, act_other, g_oth)
    grad_up = over_rows(act_own, u_own, act_other, u_oth)
    grad_down = over_rows(h_own, cot_own, h_oth, cot_other)

    select_grad = gates * (gate_grad - jnp.sum(gates * gate_grad, axis=0, keepdims=True))
    logit_grad = select_grad.astype(bf16)
    grad_router = lax.dot_general(
        act_two, logit_grad, (((0,), (1,)), ((), ())), preferred_element_type=f32
    )
    act_two_grad = expert_in_grad + lax.dot_general(
        logit_grad, router_full, (((0,), (1,)), ((), ())), preferred_element_type=f32
    )
    weighted = act_two_grad * gain_two
    grad_gain_two = jnp.sum(act_two_grad * middle * inverse_two, axis=0)
    middle_grad = (
        cotangent
        + inverse_two * weighted
        - middle * inverse_two**3 * jnp.mean(weighted * middle, axis=-1, keepdims=True)
    )
    middle_low = middle_grad.astype(bf16)

    out_grad = dot_nt(middle_low, output_full).astype(bf16)
    out_grad = out_grad.reshape(tok_rows, members, head_width).transpose(1, 0, 2)
    out_grad = exchange(out_grad.reshape(seq, head_width), plane_groups)
    dq, dk, dv, grad_gains = attention_back(
        rot,
        out_grad,
        out_wide,
        lse,
        seg_col,
        seg_row,
        low,
        high,
        pre,
        gain_q,
        gain_k,
        cosine,
        sine,
        heads,
    )
    dqkv = jnp.concatenate([dq, dk, dv], axis=1)
    act_one_part = dot_nt(dqkv, weights).astype(bf16)
    act_one_grad = reduce(act_one_part, plane_groups).astype(f32)
    part = dot_tn(act_one, dqkv).astype(bf16)
    part = reduce(part, stack_groups)
    part = exchange(part, plane_groups).reshape(members, own_rows, 3, head_width)
    part = part.transpose(2, 1, 0, 3).reshape(3, own_rows, width).astype(f32)
    grad_query, grad_key, grad_value = part[0], part[1], part[2]

    middle_all = gather(middle_low, plane_groups)
    output_part = dot_tn(out_heads, middle_all).astype(bf16)
    output_part = reduce(output_part, stack_groups)
    to_owner = [
        (g * members + j, j * planes + g) for g in range(planes) for j in range(members)
    ]
    grad_output = lax.ppermute(output_part, AXIS, to_owner).astype(f32)

    inverse_one = lax.rsqrt(jnp.mean(tokens * tokens, axis=-1, keepdims=True) + norm_eps)
    weighted = act_one_grad * gain_one
    grad_hidden = (
        middle_grad
        + inverse_one * weighted
        - tokens * inverse_one**3 * jnp.mean(weighted * tokens, axis=-1, keepdims=True)
    )
    grad_gain_one = (
        jnp.sum(
            grad_query * query_weight.astype(f32)
            + grad_key * key_weight.astype(f32)
            + grad_value * value_weight.astype(f32),
            axis=1,
        )
        / norm_gain.astype(f32)
    )

    sums = (
        grad_router.reshape(devices, -1),
        grad_gain_two.reshape(devices, -1),
        grad_gains[0].reshape(devices, -1),
        grad_gains[1].reshape(devices, -1),
    )
    packed = jnp.concatenate(sums, axis=1)
    length = packed.shape[1]
    padded = -(-length // 128) * 128
    packed = jnp.sum(exchange(jnp.pad(packed, ((0, 0), (0, padded - length)))), axis=0)
    at, tiny = 0, []
    for piece in sums:
        tiny.append(packed[at : at + piece.shape[1]])
        at += piece.shape[1]

    return (
        layer_out,
        grad_hidden,
        grad_gain_one,
        grad_query,
        grad_key,
        grad_value,
        grad_output,
        tiny[2],
        tiny[3],
        tiny[1],
        tiny[0].reshape(own_rows, expert_count),
        grad_gate[None],
        grad_up[None],
        grad_down[None],
    )


def solution(mesh):
    row, mat, cube = P(AXIS), P(AXIS, None), P(AXIS, None, None)
    return jax.shard_map(
        body,
        mesh=mesh,
        in_specs=(mat, mat, row, mat, mat, row, mat, mat, mat, mat, row, row, row, mat)
        + (cube,) * 3,
        out_specs=(mat, mat, row, mat, mat, mat, mat, row, row, row, mat) + (cube,) * 3,
        check_vma=False,
    )
```

```python
import functools
import math

import jax
import jax.numpy as jnp
from jax import lax
from jax.experimental import pallas as pl
from jax.experimental.pallas import tpu as pltpu
from jax.sharding import PartitionSpec as P

HD = 128
TOPK = 8
SEQ_MIN = 2048
ROWS = 256

norm_eps = 1e-05
head_eps = 1e-06
rope_base = 10000.0
masked_score = -1e30
absent_slot = 4096.0

AXIS = "fsdp"
f32 = jnp.float32
bf16 = jnp.bfloat16
MIB = 1 << 20


def dot_nt(left, right):
    return lax.dot_general(left, right, (((1,), (1,)), ((), ())), preferred_element_type=f32)


def dot_tn(left, right):
    return lax.dot_general(left, right, (((0,), (0,)), ((), ())), preferred_element_type=f32)


def dot_nn(left, right):
    return lax.dot_general(left, right, (((1,), (0,)), ((), ())), preferred_element_type=f32)


def params(steps, mib):
    return pltpu.CompilerParams(
        dimension_semantics=("arbitrary",) * steps, vmem_limit_bytes=mib * MIB
    )


def rope_tables(count):
    half_width = HD // 2
    frequency = jnp.exp(-math.log(rope_base) * 2.0 * jnp.arange(half_width, dtype=f32) / HD)
    angles = jnp.arange(count, dtype=f32)[:, None] * frequency[None, :]
    cosine, sine = jnp.cos(angles), jnp.sin(angles)
    return jnp.concatenate([cosine, cosine], axis=-1), jnp.concatenate([-sine, sine], axis=-1)


def slots_kernel(expert_count, routes_ref, order_ref, slots_ref):
    tok_rows = routes_ref.shape[0]
    pair_count = order_ref.shape[1]
    order = order_ref[...]
    shift = TOPK.bit_length() - 1
    token_of = lax.shift_right_logical(order, jnp.full_like(order, shift))
    route_of = order & (TOPK - 1)
    token_iota = lax.broadcasted_iota(jnp.int32, (tok_rows, pair_count), 0)
    token_hot = jnp.where(token_iota == token_of, 1.0, 0.0).astype(bf16)
    place = lax.broadcasted_iota(jnp.int32, (TOPK, pair_count), 1)
    chosen = lax.broadcasted_iota(jnp.int32, (TOPK, pair_count), 0) == route_of
    high = lax.shift_right_logical(place, jnp.full_like(place, 8)).astype(f32)
    low = (place & 255).astype(f32)
    digits = jnp.concatenate([jnp.where(chosen, high, 0.0), jnp.where(chosen, low, 0.0)], axis=0)
    found = dot_nt(token_hot, digits.astype(bf16))
    rank = found[:, :TOPK] * 256.0 + found[:, TOPK:]
    routes = routes_ref[...]
    lanes = -(-expert_count // 128) * 128
    expert_iota = lax.broadcasted_iota(jnp.int32, (tok_rows, lanes), 1)
    never = 1e9
    by_expert = jnp.full((tok_rows, lanes), never, f32)
    for k in range(TOPK):
        by_expert = jnp.where(expert_iota == routes[:, k : k + 1], rank[:, k : k + 1], by_expert)
    turned = by_expert.T
    for e in range(expert_count):
        mine = turned[e : e + 1, :]
        earlier = jnp.where(by_expert[:, e : e + 1] < mine, 1.0, 0.0)
        count = jnp.sum(earlier, axis=0, keepdims=True)
        slots_ref[e : e + 1, :] = jnp.where(mine < never, count, absent_slot)


def block_slots(routes, order, expert_count):
    tok_rows = routes.shape[0]
    return pl.pallas_call(
        functools.partial(slots_kernel, expert_count),
        out_shape=jax.ShapeDtypeStruct((expert_count, tok_rows), f32),
        compiler_params=pltpu.CompilerParams(vmem_limit_bytes=32 * MIB),
        name="block_slots",
    )(routes, order)


def slot_hot(slots_ref, expert, capacity):
    slot_row = slots_ref[pl.ds(expert, 1), :]
    slot_iota = lax.broadcasted_iota(jnp.int32, (capacity, slot_row.shape[1]), 0).astype(f32)
    return jnp.where(slot_iota == slot_row, 1.0, 0.0).astype(bf16)


def dispatch_kernel(experts_ref, slots_ref, rows_ref, *out_refs):
    capacity = out_refs[0].shape[0]
    hot = [slot_hot(slots_ref, experts_ref[r], capacity) for r in range(len(out_refs))]
    rows = dot_nn(jnp.concatenate(hot, axis=0), rows_ref[...])
    for r, out_ref in enumerate(out_refs):
        out_ref[...] = rows[r * capacity : (r + 1) * capacity].astype(bf16)


def dispatch(targets, slots, rows, per_plane, capacity):
    tok_rows, width = rows.shape
    vmem = pl.BlockSpec(memory_space=pltpu.VMEM)
    return pl.pallas_call(
        dispatch_kernel,
        out_shape=(jax.ShapeDtypeStruct((capacity, width), bf16),) * per_plane,
        in_specs=[pl.BlockSpec(memory_space=pltpu.SMEM), vmem, vmem],
        out_specs=(vmem,) * per_plane,
        compiler_params=pltpu.CompilerParams(vmem_limit_bytes=32 * MIB),
        cost_estimate=pl.CostEstimate(
            flops=2 * per_plane * capacity * tok_rows * width,
            bytes_accessed=2 * (per_plane * capacity + tok_rows) * width,
            transcendentals=0,
        ),
        name="dispatch",
    )(targets, slots, rows)


def combine_kernel(experts_ref, slots_ref, *refs):
    row_refs, out_ref = refs[:-1], refs[-1]
    capacity = row_refs[0].shape[0]
    hot = [slot_hot(slots_ref, experts_ref[r], capacity) for r in range(len(row_refs))]
    rows = jnp.concatenate([ref[...] for ref in row_refs], axis=0)
    out_ref[...] = dot_tn(jnp.concatenate(hot, axis=0), rows).astype(bf16)


def combine(targets, slots, rows, block, tok_rows):
    per_plane = len(rows)
    capacity, width = rows[0].shape[-2:]
    if block is None:
        spec = pl.BlockSpec((capacity, width), lambda i, s: (0, 0))
    else:
        spec = pl.BlockSpec((None, capacity, width), lambda i, s: (block, 0, 0))
    return pl.pallas_call(
        combine_kernel,
        out_shape=jax.ShapeDtypeStruct((tok_rows, width), bf16),
        grid_spec=pltpu.PrefetchScalarGridSpec(
            num_scalar_prefetch=1,
            grid=(1,),
            in_specs=[pl.BlockSpec(slots.shape, lambda i, s: (0, 0))] + [spec] * per_plane,
            out_specs=pl.BlockSpec((tok_rows, width), lambda i, s: (0, 0)),
        ),
        compiler_params=params(1, 32),
        cost_estimate=pl.CostEstimate(
            flops=2 * per_plane * capacity * tok_rows * width,
            bytes_accessed=2 * (per_plane * capacity + tok_rows) * width,
            transcendentals=0,
        ),
        name="combine",
    )(targets, slots, *rows)


def qkv_kernel(heads, planes, at_ref, x_ref, gain_ref, *refs):
    w_refs = refs[:planes]
    gq_ref, gk_ref, cos_ref, sin_ref, act_ref, pre_ref, rot_ref = refs[planes:]
    x = x_ref[...].astype(f32)
    inverse = lax.rsqrt(jnp.mean(x * x, axis=-1, keepdims=True) + norm_eps)
    act = (x * inverse * gain_ref[...]).astype(bf16)
    act_ref[...] = act
    y = None
    depth = w_refs[0].shape[0]
    for d in range(planes):
        columns = pl.ds(pl.multiple_of(at_ref[d] * depth, depth), depth)
        term = dot_nn(act_ref[:, columns], w_refs[d][...])
        y = term if y is None else y + term
    cosine, sine = cos_ref[...], sin_ref[...]
    for part, gain in enumerate((gq_ref[...], gk_ref[...])):
        for h in range(heads):
            at = (part * heads + h) * HD
            u = y[:, at : at + HD]
            pre_ref[:, at : at + HD] = u
            n = u * lax.rsqrt(jnp.mean(u * u, axis=-1, keepdims=True) + head_eps) * gain
            rot_ref[:, at : at + HD] = (n * cosine + pltpu.roll(n, HD // 2, 1) * sine).astype(bf16)
    at = 2 * heads * HD
    rot_ref[:, at:] = y[:, at:].astype(bf16)


def qkv_project(places, rows, gain, weights, gain_q, gain_k, cosine, sine, heads):
    count, width = rows.shape
    planes = len(weights)
    depth, out_width = weights[0].shape
    pre_width = 2 * heads * HD
    whole = lambda i, s: (0, 0)
    block = lambda i, s: (i, 0)
    return pl.pallas_call(
        functools.partial(qkv_kernel, heads, planes),
        out_shape=(
            jax.ShapeDtypeStruct((count, width), bf16),
            jax.ShapeDtypeStruct((count, pre_width), f32),
            jax.ShapeDtypeStruct((count, out_width), bf16),
        ),
        grid_spec=pltpu.PrefetchScalarGridSpec(
            num_scalar_prefetch=1,
            grid=(count // ROWS,),
            in_specs=[
                pl.BlockSpec((ROWS, width), block),
                pl.BlockSpec((1, width), whole),
            ]
            + [pl.BlockSpec((depth, out_width), whole)] * planes
            + [
                pl.BlockSpec((1, HD), whole),
                pl.BlockSpec((1, HD), whole),
                pl.BlockSpec((ROWS, HD), block),
                pl.BlockSpec((ROWS, HD), block),
            ],
            out_specs=(
                pl.BlockSpec((ROWS, width), block),
                pl.BlockSpec((ROWS, pre_width), block),
                pl.BlockSpec((ROWS, out_width), block),
            ),
        ),
        compiler_params=params(1, 48),
        cost_estimate=pl.CostEstimate(
            flops=2 * count * width * out_width,
            bytes_accessed=4 * count * width + 2 * width * out_width + 6 * count * out_width,
            transcendentals=0,
        ),
        name="qkv_project",
    )(places, rows, gain, *weights, gain_q, gain_k, cosine, sine)


def attn_kernel(
    scale, low_ref, high_ref, q_ref, k_ref, v_ref, sq_ref, sk_ref, o_ref, ol_ref, lse_ref, s_scr
):
    block = pl.program_id(1)
    low, high = low_ref[block], high_ref[block]
    q = q_ref[...]
    seg_q = sq_ref[...]
    half = ROWS // 2

    def scores(kb, top):
        at = pl.ds(pl.multiple_of(kb * ROWS, ROWS), ROWS)
        s = dot_nt(q, k_ref[at, :]) * scale
        s = jnp.where(seg_q == sk_ref[:, at], s, masked_score)
        s_scr[:, at] = s
        return jnp.maximum(top, jnp.maximum(s[:, :half], s[:, half:]))

    top = lax.fori_loop(low, high, scores, jnp.full((ROWS, half), masked_score, f32))
    top = jnp.max(top, axis=-1, keepdims=True)

    def weigh(kb, carry):
        total, acc = carry
        at = pl.ds(pl.multiple_of(kb * ROWS, ROWS), ROWS)
        p = jnp.exp(s_scr[:, at] - top)
        acc = acc + dot_nn(p.astype(bf16), v_ref[at, :])
        return total + (p[:, :half] + p[:, half:]), acc

    total, acc = lax.fori_loop(
        low, high, weigh, (jnp.zeros((ROWS, half), f32), jnp.zeros((ROWS, HD), f32))
    )
    total = jnp.sum(total, axis=-1, keepdims=True)
    out = acc / total
    o_ref[...] = out
    ol_ref[...] = out.astype(bf16)
    lse = jnp.broadcast_to(top + jnp.log(total), (ROWS, HD)).T
    lse_ref[0] = lse[0:1, :]


def attention(rot, seg_col, seg_row, low, high, heads):
    count = rot.shape[0]
    blocks = count // ROWS
    scale = HD ** (-0.5)
    return pl.pallas_call(
        functools.partial(attn_kernel, scale),
        out_shape=(
            jax.ShapeDtypeStruct((count, heads * HD), f32),
            jax.ShapeDtypeStruct((count, heads * HD), bf16),
            jax.ShapeDtypeStruct((heads * blocks, 1, ROWS), f32),
        ),
        grid_spec=pltpu.PrefetchScalarGridSpec(
            num_scalar_prefetch=2,
            grid=(heads, blocks),
            in_specs=[
                pl.BlockSpec((ROWS, HD), lambda h, i, *s: (i, h)),
                pl.BlockSpec((count, HD), lambda h, i, *s: (0, heads + h)),
                pl.BlockSpec((count, HD), lambda h, i, *s: (0, 2 * heads + h)),
                pl.BlockSpec((ROWS, 1), lambda h, i, *s: (i, 0)),
                pl.BlockSpec((1, count), lambda h, i, *s: (0, 0)),
            ],
            out_specs=(
                pl.BlockSpec((ROWS, HD), lambda h, i, *s: (i, h)),
                pl.BlockSpec((ROWS, HD), lambda h, i, *s: (i, h)),
                pl.BlockSpec((1, 1, ROWS), lambda h, i, *s: (h * blocks + i, 0, 0)),
            ),
            scratch_shapes=[pltpu.VMEM((ROWS, count), f32)],
        ),
        compiler_params=params(2, 32),
        cost_estimate=pl.CostEstimate(
            flops=2 * heads * count * count * HD,
            bytes_accessed=12 * heads * count * HD,
            transcendentals=heads * count * count // 2,
        ),
        name="attention",
    )(low, high, rot, rot, rot, seg_col, seg_row)


def head_back(grad, pre, gain, cosine, sine):
    n = grad * cosine - pltpu.roll(grad, HD // 2, 1) * sine
    inverse = lax.rsqrt(jnp.mean(pre * pre, axis=-1, keepdims=True) + head_eps)
    w = n * gain
    back = inverse * w - pre * inverse**3 * jnp.mean(w * pre, axis=-1, keepdims=True)
    return back, jnp.sum(n * pre * inverse, axis=0, keepdims=True)


def attn_back_kernel(
    scale,
    low_ref,
    high_ref,
    q_ref,
    k_ref,
    v_ref,
    do_ref,
    o_ref,
    lse_ref,
    sq_ref,
    sk_ref,
    qpre_ref,
    kpre_ref,
    gq_ref,
    gk_ref,
    cosq_ref,
    sinq_ref,
    cosk_ref,
    sink_ref,
    dq_ref,
    dk_ref,
    dv_ref,
    gain_ref,
    dk_scr,
    dv_scr,
):
    head, block = pl.program_id(0), pl.program_id(1)
    low, high = low_ref[block], high_ref[block]

    @pl.when(block == 0)
    def _():
        dk_scr[...] = jnp.zeros_like(dk_scr)
        dv_scr[...] = jnp.zeros_like(dv_scr)

    @pl.when((block == 0) & (head == 0))
    def _():
        gain_ref[...] = jnp.zeros_like(gain_ref)

    q, do = q_ref[...], do_ref[...]
    row_dot = jnp.sum((do.astype(f32) * o_ref[...]).T, axis=0, keepdims=True)
    lse = lse_ref[0]
    seg_q = sq_ref[...]

    def tile(kb, dq):
        at = pl.ds(pl.multiple_of(kb * ROWS, ROWS), ROWS)
        k, v = k_ref[at, :], v_ref[at, :]
        s = dot_nt(k, q) * scale
        p = jnp.where(sk_ref[at, :] == seg_q, jnp.exp(s - lse), 0.0)
        dp = dot_nt(v, do)
        ds = (p * (dp - row_dot)).astype(bf16)
        dv_scr[at, :] += dot_nn(p.astype(bf16), do)
        dk_scr[at, :] += dot_nn(ds, q)
        return dq + dot_tn(ds, k)

    dq = lax.fori_loop(low, high, tile, jnp.zeros((ROWS, HD), f32))
    back, gain_q = head_back(dq * scale, qpre_ref[...], gq_ref[...], cosq_ref[...], sinq_ref[...])
    dq_ref[...] = back.astype(bf16)
    gain_ref[0:1, :] += gain_q

    @pl.when(block == pl.num_programs(1) - 1)
    def _():
        @pl.loop(0, dk_scr.shape[0] // ROWS)
        def _(i):
            at = pl.ds(pl.multiple_of(i * ROWS, ROWS), ROWS)
            back, gain_k = head_back(
                dk_scr[at, :] * scale, kpre_ref[at, :], gk_ref[...], cosk_ref[at, :], sink_ref[at, :]
            )
            dk_ref[at, :] = back.astype(bf16)
            dv_ref[at, :] = dv_scr[at, :].astype(bf16)
            gain_ref[1:2, :] += gain_k


def attention_back(
    rot, grad, out, lse, seg_col, seg_row, low, high, pre, gain_q, gain_k, cosine, sine, heads
):
    count = rot.shape[0]
    blocks = count // ROWS
    scale = HD ** (-0.5)
    mine = lambda h, i, *s: (i, h)
    whole = lambda h, i, *s: (0, 0)
    return pl.pallas_call(
        functools.partial(attn_back_kernel, scale),
        out_shape=(
            jax.ShapeDtypeStruct((count, heads * HD), bf16),
            jax.ShapeDtypeStruct((count, heads * HD), bf16),
            jax.ShapeDtypeStruct((count, heads * HD), bf16),
            jax.ShapeDtypeStruct((8, HD), f32),
        ),
        grid_spec=pltpu.PrefetchScalarGridSpec(
            num_scalar_prefetch=2,
            grid=(heads, blocks),
            in_specs=[
                pl.BlockSpec((ROWS, HD), mine),
                pl.BlockSpec((count, HD), lambda h, i, *s: (0, heads + h)),
                pl.BlockSpec((count, HD), lambda h, i, *s: (0, 2 * heads + h)),
                pl.BlockSpec((ROWS, HD), mine),
                pl.BlockSpec((ROWS, HD), mine),
                pl.BlockSpec((1, 1, ROWS), lambda h, i, *s: (h * blocks + i, 0, 0)),
                pl.BlockSpec((1, ROWS), lambda h, i, *s: (0, i)),
                pl.BlockSpec((count, 1), whole),
                pl.BlockSpec((ROWS, HD), mine),
                pl.BlockSpec((count, HD), lambda h, i, *s: (0, heads + h)),
                pl.BlockSpec((1, HD), whole),
                pl.BlockSpec((1, HD), whole),
                pl.BlockSpec((ROWS, HD), lambda h, i, *s: (i, 0)),
                pl.BlockSpec((ROWS, HD), lambda h, i, *s: (i, 0)),
                pl.BlockSpec((count, HD), whole),
                pl.BlockSpec((count, HD), whole),
            ],
            out_specs=(
                pl.BlockSpec((ROWS, HD), mine),
                pl.BlockSpec((count, HD), lambda h, i, *s: (0, h)),
                pl.BlockSpec((count, HD), lambda h, i, *s: (0, h)),
                pl.BlockSpec((8, HD), whole),
            ),
            scratch_shapes=[pltpu.VMEM((count, HD), f32), pltpu.VMEM((count, HD), f32)],
        ),
        compiler_params=params(2, 48),
        cost_estimate=pl.CostEstimate(
            flops=5 * heads * count * count * HD,
            bytes_accessed=30 * heads * count * HD,
            transcendentals=heads * count * count // 2,
        ),
        name="attention_back",
    )(
        low,
        high,
        rot,
        rot,
        rot,
        grad,
        out,
        lse,
        seg_row,
        seg_col,
        pre,
        pre,
        gain_q,
        gain_k,
        cosine,
        sine,
        cosine,
        sine,
    )


def expert_kernel(per_plane, count, carried, mine_ref, *refs):
    x_refs, refs = refs[:per_plane], refs[per_plane:]
    c_refs, refs = refs[:per_plane], refs[per_plane:]
    wg_ref, wu_ref, wd_ref = refs[:3]
    refs = refs[3 + carried :]
    back_refs, refs = refs[:per_plane], refs[per_plane:]
    out_refs, refs = refs[:per_plane], refs[per_plane:]
    xs_ref, cs_ref, hid_ref, gp_ref, up_ref, out_acc, back_acc, gate_scr, dot_scr = refs
    step = pl.program_id(0)
    capacity = x_refs[0].shape[0]
    width = c_refs[0].shape[1]
    extra = x_refs[0].shape[1] - width
    rows = per_plane * capacity
    lane = lax.broadcasted_iota(jnp.int32, (rows, extra), 1)
    high, low = lane == mine_ref[0], lane == mine_ref[0] + count

    @pl.when(step == 0)
    def _():
        for r in range(per_plane):
            at = slice(r * capacity, (r + 1) * capacity)
            xs_ref[at, :] = x_refs[r][:, :width]
            cs_ref[at, :] = c_refs[r][...]
            gates = x_refs[r][:, width:].astype(f32)
            picked = jnp.where(high[at] | low[at], gates, 0.0)
            gate_scr[at, :] = jnp.sum(picked, axis=-1, keepdims=True)
        out_acc[...] = jnp.zeros_like(out_acc)
        back_acc[...] = jnp.zeros_like(back_acc)
        dot_scr[...] = jnp.zeros_like(dot_scr)

    x, c, gate = xs_ref[...], cs_ref[...], gate_scr[...]
    wg, wu, wd = wg_ref[...], wu_ref[...], wd_ref[...]
    gate_pre, up_pre = dot_nn(x, wg), dot_nn(x, wu)
    sig = jax.nn.sigmoid(gate_pre)
    hidden = (gate_pre * sig * up_pre).astype(bf16)
    out_acc[...] += dot_nn(hidden, wd)
    plain = dot_nt(c, wd)
    wide = hidden.astype(f32)
    dot_scr[...] += jnp.sum(wide * plain, axis=-1, keepdims=True)
    hid_ref[...] = (wide * gate).astype(bf16)
    hidden_grad = plain * gate
    gate_grad = (hidden_grad * up_pre * sig * (1.0 + gate_pre * (1.0 - sig))).astype(bf16)
    up_grad = (hidden_grad * gate_pre * sig).astype(bf16)
    gp_ref[...] = gate_grad
    up_ref[...] = up_grad
    back_acc[...] += dot_nt(gate_grad, wg) + dot_nt(up_grad, wu)

    @pl.when(step == pl.num_programs(0) - 1)
    def _():
        dots = dot_scr[...]
        coarse = dots.astype(bf16).astype(f32)
        lanes = jnp.where(high, coarse, jnp.where(low, dots - coarse, 0.0)).astype(bf16)
        for r in range(per_plane):
            at = slice(r * capacity, (r + 1) * capacity)
            back_refs[r][:, :width] = back_acc[at, :].astype(bf16)
            back_refs[r][:, width:] = lanes[at]
            out_refs[r][...] = (out_acc[at, :] * gate[at]).astype(bf16)


def experts(mine, x, c, wg, wu, wd, block, blocks, count, kept):
    per_plane = len(x)
    capacity, wide = x[0].shape
    width = c[0].shape[1]
    halves, _, hidden = wg.shape
    rows = per_plane * capacity
    fixed = pl.BlockSpec((capacity, wide), lambda f, s: (0, 0))
    stacked = pl.BlockSpec((None, capacity, width), lambda f, s: (block, 0, 0))
    narrow = pl.BlockSpec((capacity, width), lambda f, s: (0, 0))
    back = jax.ShapeDtypeStruct((capacity, wide), bf16)
    out = jax.ShapeDtypeStruct((blocks, capacity, width), bf16)
    saved = jax.ShapeDtypeStruct((blocks * rows, width), bf16)
    thin = jax.ShapeDtypeStruct((blocks * rows, halves * hidden), bf16)
    saved_spec = pl.BlockSpec((rows, width), lambda f, s: (block, 0))
    thin_spec = pl.BlockSpec((rows, hidden), lambda f, s: (block, f))
    carried = 0 if kept is None else len(kept)
    inputs = 1 + 2 * per_plane + 3
    result = pl.pallas_call(
        functools.partial(expert_kernel, per_plane, count, carried),
        out_shape=(back,) * per_plane + (out,) * per_plane + (saved, saved, thin, thin, thin),
        grid_spec=pltpu.PrefetchScalarGridSpec(
            num_scalar_prefetch=1,
            grid=(halves,),
            in_specs=[fixed] * per_plane
            + [narrow] * per_plane
            + [
                pl.BlockSpec((None, width, hidden), lambda f, s: (f, 0, 0)),
                pl.BlockSpec((None, width, hidden), lambda f, s: (f, 0, 0)),
                pl.BlockSpec((None, hidden, width), lambda f, s: (f, 0, 0)),
            ]
            + [pl.BlockSpec(memory_space=pl.ANY)] * carried,
            out_specs=(fixed,) * per_plane
            + (stacked,) * per_plane
            + (saved_spec, saved_spec, thin_spec, thin_spec, thin_spec),
            scratch_shapes=[
                pltpu.VMEM((rows, width), f32),
                pltpu.VMEM((rows, width), f32),
                pltpu.VMEM((rows, 1), f32),
                pltpu.VMEM((rows, 1), f32),
            ],
        ),
        input_output_aliases={inputs + i: per_plane + i for i in range(carried)},
        compiler_params=params(1, 60),
        cost_estimate=pl.CostEstimate(
            flops=12 * rows * width * hidden * halves,
            bytes_accessed=12 * rows * width + 6 * width * hidden * halves,
            transcendentals=rows * hidden * halves,
        ),
        name="experts",
    )(mine, *x, *c, wg, wu, wd, *(kept or ()))
    return result[:per_plane], result[per_plane:]


def after(value, *others):
    return lax.optimization_barrier((value,) + others)[0]


def body(
    hidden_in,
    out_cotangent,
    segment_number,
    expert_routes,
    pair_order,
    norm_gain,
    query_weight,
    key_weight,
    value_weight,
    output_weight,
    query_gain,
    key_gain,
    ffn_norm_gain,
    router_weight,
    expert_gate,
    expert_up,
    expert_down,
):
    tok_rows, width = hidden_in.shape
    devices = lax.axis_size(AXIS)
    members = max(1, SEQ_MIN // tok_rows)
    planes = devices // members
    per_plane = members // 2
    expert_count = devices // 2
    capacity = tok_rows * TOPK // expert_count
    heads = width // HD // members
    head_width = heads * HD
    own_rows = norm_gain.shape[0]
    seq = members * tok_rows
    me = lax.axis_index(AXIS)
    plane, member = me // members, me % members
    mine = (me // 2).astype(jnp.int32).reshape(1)
    chips = jnp.arange(per_plane, dtype=jnp.int32)
    targets = (plane * per_plane + ((member // 2) ^ chips)).astype(jnp.int32)
    places = (plane ^ jnp.arange(planes, dtype=jnp.int32)).astype(jnp.int32)

    plane_groups = [[g * members + j for j in range(members)] for g in range(planes)]
    stack_groups = [[g * members + j for g in range(planes)] for j in range(members)]

    def exchange(value, groups=None):
        return lax.all_to_all(
            value, AXIS, split_axis=0, concat_axis=0, tiled=True, axis_index_groups=groups
        )

    def gather(value, groups=None):
        return lax.all_gather(value, AXIS, axis=0, tiled=True, axis_index_groups=groups)

    def reduce(value, groups=None):
        return lax.psum_scatter(
            value, AXIS, scatter_dimension=0, tiled=True, axis_index_groups=groups
        )

    def flip(value, bits):
        if bits == 0:
            return value
        return lax.ppermute(value, AXIS, [(i, i ^ bits) for i in range(devices)])

    def to_core(value):
        return flip(value, 1)

    def to_chip(values):
        return [flip(value, 2 * r) for r, value in enumerate(values)]

    def to_plane(value, d):
        return flip(value, members * d)

    columns = jnp.concatenate(
        [w.reshape(own_rows, members, head_width) for w in (query_weight, key_weight, value_weight)],
        axis=2,
    )
    columns = exchange(
        columns.transpose(1, 0, 2).reshape(members * own_rows, 3 * head_width), plane_groups
    )
    weights = [to_plane(columns, d) for d in range(planes)]
    rows_all = gather(hidden_in, plane_groups)

    pieces = (
        router_weight.reshape(-1),
        norm_gain,
        ffn_norm_gain,
        query_gain,
        key_gain,
        segment_number.astype(bf16),
    )
    packed = jnp.concatenate(pieces)
    length = packed.shape[0]
    padded = -(-length // 128) * 128
    packed = after(jnp.pad(packed, (0, padded - length)), columns)
    packed = exchange(jnp.broadcast_to(packed[None], (devices, padded)))
    small = []
    at = 0
    for piece in pieces:
        small.append(packed[:, at : at + piece.shape[0]])
        at += piece.shape[0]
    router_full = small[0].reshape(width, expert_count)
    gain_one = small[1].reshape(1, width).astype(f32)
    gain_two = small[2].reshape(1, width).astype(f32)
    gain_q = small[3].reshape(1, HD).astype(f32)
    gain_k = small[4].reshape(1, HD).astype(f32)
    segments = lax.dynamic_slice_in_dim(small[5], plane * members, members, 0).astype(f32)
    seg_row, seg_col = segments.reshape(1, seq), segments.reshape(seq, 1)
    seg_blocks = segments.reshape(seq // ROWS, ROWS)
    seg_first, seg_last = seg_blocks[:, 0], seg_blocks[:, -1]
    low = jnp.sum((seg_last[None, :] < seg_first[:, None]).astype(jnp.int32), axis=1)
    high = jnp.sum((seg_first[None, :] <= seg_last[:, None]).astype(jnp.int32), axis=1)
    output_full = gather(output_weight)

    halves = lambda w: jnp.concatenate([w, to_core(w)], axis=0)
    wg, wu, wd = halves(expert_gate), halves(expert_up), halves(expert_down)

    slots = block_slots(expert_routes, pair_order, expert_count)
    slots = [to_plane(slots, d) for d in range(planes)]
    cot = []
    for d in range(planes):
        rows = to_plane(after(out_cotangent, *weights), d)
        sent = dispatch(targets, slots[d], rows, per_plane, capacity)
        cot.append(to_chip(sent))

    cosine, sine = rope_tables(seq)
    act_one, pre, rot = qkv_project(
        places, rows_all, gain_one, weights, gain_q, gain_k, cosine, sine, heads
    )
    out_wide, out_heads, lse = attention(rot, seg_col, seg_row, low, high, heads)
    out_low = exchange(out_heads, plane_groups).reshape(members, tok_rows, head_width)
    out_low = out_low.transpose(1, 0, 2).reshape(tok_rows, width)
    tokens = hidden_in.astype(f32)
    cotangent = out_cotangent.astype(f32)
    middle = tokens + dot_nn(out_low, output_full)
    inverse_two = lax.rsqrt(jnp.mean(middle * middle, axis=-1, keepdims=True) + norm_eps)
    act_two = (middle * inverse_two * gain_two).astype(bf16)

    logits = dot_nn(act_two, router_full)
    expert_ids = jnp.arange(expert_count, dtype=jnp.int32)
    routed = jnp.any(expert_routes[:, :, None] == expert_ids[None, None, :], axis=1)
    logits = jnp.where(routed, logits, masked_score)
    gates = jnp.where(routed, jnp.exp(logits - jnp.max(logits, axis=1, keepdims=True)), 0.0)
    gates = gates / jnp.sum(gates, axis=1, keepdims=True)
    coarse = lax.reduce_precision(gates, 8, 7)
    extra = -(-2 * expert_count // 128) * 128
    act_wide = jnp.concatenate(
        [
            act_two,
            coarse.astype(bf16),
            (gates - coarse).astype(bf16),
            jnp.zeros((tok_rows, extra - 2 * expert_count), bf16),
        ],
        axis=1,
    )

    act_sent = []
    for d in range(planes):
        rows = to_plane(act_wide, d)
        act_sent.append(to_chip(dispatch(targets, slots[d], rows, per_plane, capacity)))
    kept = None
    backs = []
    for d in range(planes):
        back, kept = experts(
            mine,
            act_sent[d],
            cot[d],
            wg,
            wu,
            wd,
            d,
            planes,
            expert_count,
            kept,
        )
        back = combine(targets, slots[d], to_chip(back), None, tok_rows)
        backs.append(to_plane(back, d))
    outs, (x_all, c_all, hid_all, gp_all, up_all) = kept[:per_plane], kept[per_plane:]
    back_sum = sum(back.astype(f32) for back in backs)
    expert_in_grad = back_sum[:, :width]
    gate_grad = (
        back_sum[:, width : width + expert_count]
        + back_sum[:, width + expert_count : width + 2 * expert_count]
    )

    outs = to_chip([after(out, *backs) for out in outs])
    mixture = sum(
        to_plane(combine(targets, slots[d], outs, d, tok_rows), d).astype(f32)
        for d in range(planes)
    )
    layer_out = (middle + mixture).astype(bf16)

    hidden = expert_gate.shape[2]

    grad_gate = dot_tn(x_all, gp_all[:, :hidden]) + to_core(dot_tn(x_all, gp_all[:, hidden:]))
    grad_up = dot_tn(x_all, up_all[:, :hidden]) + to_core(dot_tn(x_all, up_all[:, hidden:]))
    grad_down = dot_tn(hid_all[:, :hidden], c_all) + to_core(dot_tn(hid_all[:, hidden:], c_all))

    select_grad = gates * (gate_grad - jnp.sum(gates * gate_grad, axis=1, keepdims=True))
    logit_grad = select_grad.astype(bf16)
    grad_router = dot_tn(act_two, logit_grad)
    act_two_grad = expert_in_grad + dot_nt(logit_grad, router_full)
    weighted = act_two_grad * gain_two
    grad_gain_two = jnp.sum(act_two_grad * middle * inverse_two, axis=0)
    middle_grad = (
        cotangent
        + inverse_two * weighted
        - middle * inverse_two**3 * jnp.mean(weighted * middle, axis=-1, keepdims=True)
    )
    middle_low = middle_grad.astype(bf16)

    out_grad = dot_nt(middle_low, output_full).astype(bf16)
    out_grad = out_grad.reshape(tok_rows, members, head_width).transpose(1, 0, 2)
    out_grad = exchange(out_grad.reshape(seq, head_width), plane_groups)
    dq, dk, dv, grad_gains = attention_back(
        rot,
        out_grad,
        out_wide,
        lse,
        seg_col,
        seg_row,
        low,
        high,
        pre,
        gain_q,
        gain_k,
        cosine,
        sine,
        heads,
    )
    dqkv = jnp.concatenate([dq, dk, dv], axis=1)
    depth = members * own_rows
    ordered = jnp.zeros((width, 3 * head_width), bf16)
    for d in range(planes):
        ordered = lax.dynamic_update_slice_in_dim(ordered, weights[d], places[d] * depth, 0)
    act_one_part = dot_nt(dqkv, ordered).astype(bf16)
    act_one_grad = reduce(act_one_part, plane_groups).astype(f32)
    part = dot_tn(act_one, dqkv).astype(bf16)
    part = reduce(part, stack_groups)
    part = exchange(part, plane_groups).reshape(members, own_rows, 3, head_width)
    part = part.transpose(2, 1, 0, 3).reshape(3, own_rows, width).astype(f32)
    grad_query, grad_key, grad_value = part[0], part[1], part[2]

    middle_all = gather(middle_low, plane_groups)
    output_part = dot_tn(out_heads, middle_all).astype(bf16)
    output_part = reduce(output_part, stack_groups)
    to_owner = [
        (g * members + j, j * planes + g) for g in range(planes) for j in range(members)
    ]
    grad_output = lax.ppermute(output_part, AXIS, to_owner).astype(f32)

    inverse_one = lax.rsqrt(jnp.mean(tokens * tokens, axis=-1, keepdims=True) + norm_eps)
    weighted = act_one_grad * gain_one
    grad_hidden = (
        middle_grad
        + inverse_one * weighted
        - tokens * inverse_one**3 * jnp.mean(weighted * tokens, axis=-1, keepdims=True)
    )
    grad_gain_one = (
        jnp.sum(
            grad_query * query_weight.astype(f32)
            + grad_key * key_weight.astype(f32)
            + grad_value * value_weight.astype(f32),
            axis=1,
        )
        / norm_gain.astype(f32)
    )

    sums = (
        grad_router.reshape(devices, -1),
        grad_gain_two.reshape(devices, -1),
        grad_gains[0].reshape(devices, -1),
        grad_gains[1].reshape(devices, -1),
    )
    packed = jnp.concatenate(sums, axis=1)
    length = packed.shape[1]
    padded = -(-length // 128) * 128
    packed = jnp.sum(exchange(jnp.pad(packed, ((0, 0), (0, padded - length)))), axis=0)
    at, tiny = 0, []
    for piece in sums:
        tiny.append(packed[at : at + piece.shape[1]])
        at += piece.shape[1]

    return (
        layer_out,
        grad_hidden,
        grad_gain_one,
        grad_query,
        grad_key,
        grad_value,
        grad_output,
        tiny[2],
        tiny[3],
        tiny[1],
        tiny[0].reshape(own_rows, expert_count),
        grad_gate[None],
        grad_up[None],
        grad_down[None],
    )


def solution(mesh):
    row, mat, cube = P(AXIS), P(AXIS, None), P(AXIS, None, None)
    return jax.shard_map(
        body,
        mesh=mesh,
        in_specs=(mat, mat, row, mat, mat, row, mat, mat, mat, mat, row, row, row, mat)
        + (cube,) * 3,
        out_specs=(mat, mat, row, mat, mat, mat, mat, row, row, row, mat) + (cube,) * 3,
        check_vma=False,
    )
```

```python
import functools
import math

import jax
import jax.numpy as jnp
from jax import lax
from jax.experimental import pallas as pl
from jax.experimental.pallas import tpu as pltpu
from jax.sharding import PartitionSpec as P

HD = 128
TOPK = 8
SEQ_MIN = 2048
ROWS = 256

norm_eps = 1e-05
head_eps = 1e-06
rope_base = 10000.0
masked_score = -1e30
absent_slot = 4096.0

AXIS = "fsdp"
f32 = jnp.float32
bf16 = jnp.bfloat16
MIB = 1 << 20


def dot_nt(left, right):
    return lax.dot_general(left, right, (((1,), (1,)), ((), ())), preferred_element_type=f32)


def dot_tn(left, right):
    return lax.dot_general(left, right, (((0,), (0,)), ((), ())), preferred_element_type=f32)


def dot_nn(left, right):
    return lax.dot_general(left, right, (((1,), (0,)), ((), ())), preferred_element_type=f32)


def params(steps, mib):
    return pltpu.CompilerParams(
        dimension_semantics=("arbitrary",) * steps, vmem_limit_bytes=mib * MIB
    )


def rope_tables(count):
    half_width = HD // 2
    frequency = jnp.exp(-math.log(rope_base) * 2.0 * jnp.arange(half_width, dtype=f32) / HD)
    angles = jnp.arange(count, dtype=f32)[:, None] * frequency[None, :]
    cosine, sine = jnp.cos(angles), jnp.sin(angles)
    return jnp.concatenate([cosine, cosine], axis=-1), jnp.concatenate([-sine, sine], axis=-1)


def slots_kernel(expert_count, routes_ref, order_ref, slots_ref):
    tok_rows = routes_ref.shape[0]
    pair_count = order_ref.shape[1]
    order = order_ref[...]
    shift = TOPK.bit_length() - 1
    token_of = lax.shift_right_logical(order, jnp.full_like(order, shift))
    route_of = order & (TOPK - 1)
    token_iota = lax.broadcasted_iota(jnp.int32, (tok_rows, pair_count), 0)
    token_hot = jnp.where(token_iota == token_of, 1.0, 0.0).astype(bf16)
    place = lax.broadcasted_iota(jnp.int32, (TOPK, pair_count), 1)
    chosen = lax.broadcasted_iota(jnp.int32, (TOPK, pair_count), 0) == route_of
    high = lax.shift_right_logical(place, jnp.full_like(place, 8)).astype(f32)
    low = (place & 255).astype(f32)
    digits = jnp.concatenate([jnp.where(chosen, high, 0.0), jnp.where(chosen, low, 0.0)], axis=0)
    found = dot_nt(token_hot, digits.astype(bf16))
    rank = found[:, :TOPK] * 256.0 + found[:, TOPK:]
    routes = routes_ref[...]
    lanes = -(-expert_count // 128) * 128
    expert_iota = lax.broadcasted_iota(jnp.int32, (tok_rows, lanes), 1)
    never = 1e9
    by_expert = jnp.full((tok_rows, lanes), never, f32)
    for k in range(TOPK):
        by_expert = jnp.where(expert_iota == routes[:, k : k + 1], rank[:, k : k + 1], by_expert)
    turned = by_expert.T
    for e in range(expert_count):
        mine = turned[e : e + 1, :]
        earlier = jnp.where(by_expert[:, e : e + 1] < mine, 1.0, 0.0)
        count = jnp.sum(earlier, axis=0, keepdims=True)
        slots_ref[e : e + 1, :] = jnp.where(mine < never, count, absent_slot)


def block_slots(routes, order, expert_count):
    tok_rows = routes.shape[0]
    return pl.pallas_call(
        functools.partial(slots_kernel, expert_count),
        out_shape=jax.ShapeDtypeStruct((expert_count, tok_rows), f32),
        compiler_params=pltpu.CompilerParams(vmem_limit_bytes=32 * MIB),
        name="block_slots",
    )(routes, order)


def slot_hot(slots_ref, expert, capacity):
    slot_row = slots_ref[pl.ds(expert, 1), :]
    slot_iota = lax.broadcasted_iota(jnp.int32, (capacity, slot_row.shape[1]), 0).astype(f32)
    return jnp.where(slot_iota == slot_row, 1.0, 0.0).astype(bf16)


def dispatch_kernel(experts_ref, slots_ref, rows_ref, *out_refs):
    capacity = out_refs[0].shape[0]
    hot = [slot_hot(slots_ref, experts_ref[r], capacity) for r in range(len(out_refs))]
    rows = dot_nn(jnp.concatenate(hot, axis=0), rows_ref[...])
    for r, out_ref in enumerate(out_refs):
        out_ref[...] = rows[r * capacity : (r + 1) * capacity].astype(bf16)


def dispatch(targets, slots, rows, per_plane, capacity):
    tok_rows, width = rows.shape
    vmem = pl.BlockSpec(memory_space=pltpu.VMEM)
    return pl.pallas_call(
        dispatch_kernel,
        out_shape=(jax.ShapeDtypeStruct((capacity, width), bf16),) * per_plane,
        in_specs=[pl.BlockSpec(memory_space=pltpu.SMEM), vmem, vmem],
        out_specs=(vmem,) * per_plane,
        compiler_params=pltpu.CompilerParams(vmem_limit_bytes=32 * MIB),
        cost_estimate=pl.CostEstimate(
            flops=2 * per_plane * capacity * tok_rows * width,
            bytes_accessed=2 * (per_plane * capacity + tok_rows) * width,
            transcendentals=0,
        ),
        name="dispatch",
    )(targets, slots, rows)


def combine_kernel(experts_ref, slots_ref, *refs):
    row_refs, out_ref = refs[:-1], refs[-1]
    capacity = row_refs[0].shape[0]
    hot = [slot_hot(slots_ref, experts_ref[r], capacity) for r in range(len(row_refs))]
    rows = jnp.concatenate([ref[...] for ref in row_refs], axis=0)
    out_ref[...] = dot_tn(jnp.concatenate(hot, axis=0), rows).astype(bf16)


def combine(targets, slots, rows, block, tok_rows):
    per_plane = len(rows)
    capacity, width = rows[0].shape[-2:]
    if block is None:
        spec = pl.BlockSpec((capacity, width), lambda i, s: (0, 0))
    else:
        spec = pl.BlockSpec((None, capacity, width), lambda i, s: (block, 0, 0))
    return pl.pallas_call(
        combine_kernel,
        out_shape=jax.ShapeDtypeStruct((tok_rows, width), bf16),
        grid_spec=pltpu.PrefetchScalarGridSpec(
            num_scalar_prefetch=1,
            grid=(1,),
            in_specs=[pl.BlockSpec(slots.shape, lambda i, s: (0, 0))] + [spec] * per_plane,
            out_specs=pl.BlockSpec((tok_rows, width), lambda i, s: (0, 0)),
        ),
        compiler_params=params(1, 32),
        cost_estimate=pl.CostEstimate(
            flops=2 * per_plane * capacity * tok_rows * width,
            bytes_accessed=2 * (per_plane * capacity + tok_rows) * width,
            transcendentals=0,
        ),
        name="combine",
    )(targets, slots, *rows)


def qkv_kernel(heads, planes, at_ref, x_ref, gain_ref, *refs):
    w_refs = refs[:planes]
    gq_ref, gk_ref, cos_ref, sin_ref, act_ref, pre_ref, rot_ref = refs[planes:]
    x = x_ref[...].astype(f32)
    inverse = lax.rsqrt(jnp.mean(x * x, axis=-1, keepdims=True) + norm_eps)
    act = (x * inverse * gain_ref[...]).astype(bf16)
    act_ref[...] = act
    y = None
    depth = w_refs[0].shape[0]
    for d in range(planes):
        columns = pl.ds(pl.multiple_of(at_ref[d] * depth, depth), depth)
        term = dot_nn(act_ref[:, columns], w_refs[d][...])
        y = term if y is None else y + term
    cosine, sine = cos_ref[...], sin_ref[...]
    for part, gain in enumerate((gq_ref[...], gk_ref[...])):
        for h in range(heads):
            at = (part * heads + h) * HD
            u = y[:, at : at + HD]
            pre_ref[:, at : at + HD] = u
            n = u * lax.rsqrt(jnp.mean(u * u, axis=-1, keepdims=True) + head_eps) * gain
            rot_ref[:, at : at + HD] = (n * cosine + pltpu.roll(n, HD // 2, 1) * sine).astype(bf16)
    at = 2 * heads * HD
    rot_ref[:, at:] = y[:, at:].astype(bf16)


def qkv_project(places, rows, gain, weights, gain_q, gain_k, cosine, sine, heads):
    count, width = rows.shape
    planes = len(weights)
    depth, out_width = weights[0].shape
    pre_width = 2 * heads * HD
    whole = lambda i, s: (0, 0)
    block = lambda i, s: (i, 0)
    return pl.pallas_call(
        functools.partial(qkv_kernel, heads, planes),
        out_shape=(
            jax.ShapeDtypeStruct((count, width), bf16),
            jax.ShapeDtypeStruct((count, pre_width), f32),
            jax.ShapeDtypeStruct((count, out_width), bf16),
        ),
        grid_spec=pltpu.PrefetchScalarGridSpec(
            num_scalar_prefetch=1,
            grid=(count // ROWS,),
            in_specs=[
                pl.BlockSpec((ROWS, width), block),
                pl.BlockSpec((1, width), whole),
            ]
            + [pl.BlockSpec((depth, out_width), whole)] * planes
            + [
                pl.BlockSpec((1, HD), whole),
                pl.BlockSpec((1, HD), whole),
                pl.BlockSpec((ROWS, HD), block),
                pl.BlockSpec((ROWS, HD), block),
            ],
            out_specs=(
                pl.BlockSpec((ROWS, width), block),
                pl.BlockSpec((ROWS, pre_width), block),
                pl.BlockSpec((ROWS, out_width), block),
            ),
        ),
        compiler_params=params(1, 48),
        cost_estimate=pl.CostEstimate(
            flops=2 * count * width * out_width,
            bytes_accessed=4 * count * width + 2 * width * out_width + 6 * count * out_width,
            transcendentals=0,
        ),
        name="qkv_project",
    )(places, rows, gain, *weights, gain_q, gain_k, cosine, sine)


def attn_kernel(
    scale, low_ref, high_ref, q_ref, k_ref, v_ref, sq_ref, sk_ref, o_ref, ol_ref, lse_ref, s_scr
):
    block = pl.program_id(1)
    low, high = low_ref[block], high_ref[block]
    q = q_ref[...]
    seg_q = sq_ref[...]
    half = ROWS // 2

    def scores(kb, top):
        at = pl.ds(pl.multiple_of(kb * ROWS, ROWS), ROWS)
        s = dot_nt(q, k_ref[at, :]) * scale
        s = jnp.where(seg_q == sk_ref[:, at], s, masked_score)
        s_scr[:, at] = s
        return jnp.maximum(top, jnp.maximum(s[:, :half], s[:, half:]))

    top = lax.fori_loop(low, high, scores, jnp.full((ROWS, half), masked_score, f32))
    top = jnp.max(top, axis=-1, keepdims=True)

    def weigh(kb, carry):
        total, acc = carry
        at = pl.ds(pl.multiple_of(kb * ROWS, ROWS), ROWS)
        p = jnp.exp(s_scr[:, at] - top)
        acc = acc + dot_nn(p.astype(bf16), v_ref[at, :])
        return total + (p[:, :half] + p[:, half:]), acc

    total, acc = lax.fori_loop(
        low, high, weigh, (jnp.zeros((ROWS, half), f32), jnp.zeros((ROWS, HD), f32))
    )
    total = jnp.sum(total, axis=-1, keepdims=True)
    out = acc / total
    o_ref[...] = out
    ol_ref[...] = out.astype(bf16)
    lse = jnp.broadcast_to(top + jnp.log(total), (ROWS, HD)).T
    lse_ref[0] = lse[0:1, :]


def attention(rot, seg_col, seg_row, low, high, heads):
    count = rot.shape[0]
    blocks = count // ROWS
    scale = HD ** (-0.5)
    return pl.pallas_call(
        functools.partial(attn_kernel, scale),
        out_shape=(
            jax.ShapeDtypeStruct((count, heads * HD), f32),
            jax.ShapeDtypeStruct((count, heads * HD), bf16),
            jax.ShapeDtypeStruct((heads * blocks, 1, ROWS), f32),
        ),
        grid_spec=pltpu.PrefetchScalarGridSpec(
            num_scalar_prefetch=2,
            grid=(heads, blocks),
            in_specs=[
                pl.BlockSpec((ROWS, HD), lambda h, i, *s: (i, h)),
                pl.BlockSpec((count, HD), lambda h, i, *s: (0, heads + h)),
                pl.BlockSpec((count, HD), lambda h, i, *s: (0, 2 * heads + h)),
                pl.BlockSpec((ROWS, 1), lambda h, i, *s: (i, 0)),
                pl.BlockSpec((1, count), lambda h, i, *s: (0, 0)),
            ],
            out_specs=(
                pl.BlockSpec((ROWS, HD), lambda h, i, *s: (i, h)),
                pl.BlockSpec((ROWS, HD), lambda h, i, *s: (i, h)),
                pl.BlockSpec((1, 1, ROWS), lambda h, i, *s: (h * blocks + i, 0, 0)),
            ),
            scratch_shapes=[pltpu.VMEM((ROWS, count), f32)],
        ),
        compiler_params=params(2, 32),
        cost_estimate=pl.CostEstimate(
            flops=2 * heads * count * count * HD,
            bytes_accessed=12 * heads * count * HD,
            transcendentals=heads * count * count // 2,
        ),
        name="attention",
    )(low, high, rot, rot, rot, seg_col, seg_row)


def head_back(grad, pre, gain, cosine, sine):
    n = grad * cosine - pltpu.roll(grad, HD // 2, 1) * sine
    inverse = lax.rsqrt(jnp.mean(pre * pre, axis=-1, keepdims=True) + head_eps)
    w = n * gain
    back = inverse * w - pre * inverse**3 * jnp.mean(w * pre, axis=-1, keepdims=True)
    return back, jnp.sum(n * pre * inverse, axis=0, keepdims=True)


def attn_back_kernel(
    scale,
    low_ref,
    high_ref,
    q_ref,
    k_ref,
    v_ref,
    do_ref,
    o_ref,
    lse_ref,
    sq_ref,
    sk_ref,
    qpre_ref,
    kpre_ref,
    gq_ref,
    gk_ref,
    cosq_ref,
    sinq_ref,
    cosk_ref,
    sink_ref,
    dq_ref,
    dk_ref,
    dv_ref,
    gain_ref,
    dk_scr,
    dv_scr,
):
    block = pl.program_id(0)
    low, high = low_ref[block], high_ref[block]

    @pl.when(block == 0)
    def _():
        dk_scr[...] = jnp.zeros_like(dk_scr)
        dv_scr[...] = jnp.zeros_like(dv_scr)
        gain_ref[...] = jnp.zeros_like(gain_ref)

    q, do = q_ref[...], do_ref[...]
    row_dot = jnp.sum((do.astype(f32) * o_ref[...]).T, axis=0, keepdims=True)
    lse = lse_ref[0]
    seg_q = sq_ref[...]

    def tile(kb, dq):
        at = pl.ds(pl.multiple_of(kb * ROWS, ROWS), ROWS)
        k, v = k_ref[at, :], v_ref[at, :]
        s = dot_nt(k, q) * scale
        p = jnp.where(sk_ref[at, :] == seg_q, jnp.exp(s - lse), 0.0)
        dp = dot_nt(v, do)
        ds = (p * (dp - row_dot)).astype(bf16)
        dv_scr[at, :] += dot_nn(p.astype(bf16), do)
        dk_scr[at, :] += dot_nn(ds, q)
        return dq + dot_tn(ds, k)

    dq = lax.fori_loop(low, high, tile, jnp.zeros((ROWS, HD), f32))
    back, gain_q = head_back(dq * scale, qpre_ref[...], gq_ref[...], cosq_ref[...], sinq_ref[...])
    dq_ref[...] = back.astype(bf16)
    gain_ref[0:1, :] += gain_q

    @pl.when(block == pl.num_programs(0) - 1)
    def _():
        @pl.loop(0, dk_scr.shape[0] // ROWS)
        def _(i):
            at = pl.ds(pl.multiple_of(i * ROWS, ROWS), ROWS)
            back, gain_k = head_back(
                dk_scr[at, :] * scale, kpre_ref[at, :], gk_ref[...], cosk_ref[at, :], sink_ref[at, :]
            )
            dk_ref[at, :] = back.astype(bf16)
            dv_ref[at, :] = dv_scr[at, :].astype(bf16)
            gain_ref[1:2, :] += gain_k


def attention_back(
    head, rot, grad, out, lse, seg_col, seg_row, low, high, pre, gain_q, gain_k, cosine, sine, heads
):
    count = rot.shape[0]
    blocks = count // ROWS
    scale = HD ** (-0.5)
    mine = lambda i, *s: (i, head)
    first = lambda i, *s: (i, 0)
    whole = lambda i, *s: (0, 0)
    result = jax.ShapeDtypeStruct((count, HD), bf16)
    return pl.pallas_call(
        functools.partial(attn_back_kernel, scale),
        out_shape=(result, result, result, jax.ShapeDtypeStruct((8, HD), f32)),
        grid_spec=pltpu.PrefetchScalarGridSpec(
            num_scalar_prefetch=2,
            grid=(blocks,),
            in_specs=[
                pl.BlockSpec((ROWS, HD), mine),
                pl.BlockSpec((count, HD), lambda i, *s: (0, heads + head)),
                pl.BlockSpec((count, HD), lambda i, *s: (0, 2 * heads + head)),
                pl.BlockSpec((ROWS, HD), mine),
                pl.BlockSpec((ROWS, HD), mine),
                pl.BlockSpec((1, 1, ROWS), lambda i, *s: (head * blocks + i, 0, 0)),
                pl.BlockSpec((1, ROWS), lambda i, *s: (0, i)),
                pl.BlockSpec((count, 1), whole),
                pl.BlockSpec((ROWS, HD), mine),
                pl.BlockSpec((count, HD), lambda i, *s: (0, heads + head)),
                pl.BlockSpec((1, HD), whole),
                pl.BlockSpec((1, HD), whole),
                pl.BlockSpec((ROWS, HD), first),
                pl.BlockSpec((ROWS, HD), first),
                pl.BlockSpec((count, HD), whole),
                pl.BlockSpec((count, HD), whole),
            ],
            out_specs=(
                pl.BlockSpec((ROWS, HD), first),
                pl.BlockSpec((count, HD), whole),
                pl.BlockSpec((count, HD), whole),
                pl.BlockSpec((8, HD), whole),
            ),
            scratch_shapes=[pltpu.VMEM((count, HD), f32), pltpu.VMEM((count, HD), f32)],
        ),
        compiler_params=params(1, 48),
        cost_estimate=pl.CostEstimate(
            flops=5 * count * count * HD,
            bytes_accessed=30 * count * HD,
            transcendentals=count * count // 2,
        ),
        name="attention_back",
    )(
        low, high, rot, rot, rot, grad, out, lse, seg_row, seg_col, pre, pre, gain_q, gain_k,
        cosine, sine, cosine, sine,
    )


def expert_kernel(per_plane, count, carried, mine_ref, *refs):
    x_refs, refs = refs[:per_plane], refs[per_plane:]
    c_refs, refs = refs[:per_plane], refs[per_plane:]
    wg_ref, wu_ref, wd_ref = refs[:3]
    refs = refs[3 + carried :]
    back_refs, refs = refs[:per_plane], refs[per_plane:]
    out_refs, refs = refs[:per_plane], refs[per_plane:]
    xs_ref, cs_ref, hid_ref, gp_ref, up_ref, out_acc, back_acc, gate_scr, dot_scr = refs
    step = pl.program_id(0)
    capacity = x_refs[0].shape[0]
    width = c_refs[0].shape[1]
    extra = x_refs[0].shape[1] - width
    rows = per_plane * capacity
    lane = lax.broadcasted_iota(jnp.int32, (rows, extra), 1)
    high, low = lane == mine_ref[0], lane == mine_ref[0] + count

    @pl.when(step == 0)
    def _():
        for r in range(per_plane):
            at = slice(r * capacity, (r + 1) * capacity)
            xs_ref[at, :] = x_refs[r][:, :width]
            cs_ref[at, :] = c_refs[r][...]
            gates = x_refs[r][:, width:].astype(f32)
            picked = jnp.where(high[at] | low[at], gates, 0.0)
            gate_scr[at, :] = jnp.sum(picked, axis=-1, keepdims=True)
        out_acc[...] = jnp.zeros_like(out_acc)
        back_acc[...] = jnp.zeros_like(back_acc)
        dot_scr[...] = jnp.zeros_like(dot_scr)

    x, c, gate = xs_ref[...], cs_ref[...], gate_scr[...]
    wg, wu, wd = wg_ref[...], wu_ref[...], wd_ref[...]
    gate_pre, up_pre = dot_nn(x, wg), dot_nn(x, wu)
    sig = jax.nn.sigmoid(gate_pre)
    hidden = (gate_pre * sig * up_pre).astype(bf16)
    out_acc[...] += dot_nn(hidden, wd)
    plain = dot_nt(c, wd)
    wide = hidden.astype(f32)
    dot_scr[...] += jnp.sum(wide * plain, axis=-1, keepdims=True)
    hid_ref[...] = (wide * gate).astype(bf16)
    hidden_grad = plain * gate
    gate_grad = (hidden_grad * up_pre * sig * (1.0 + gate_pre * (1.0 - sig))).astype(bf16)
    up_grad = (hidden_grad * gate_pre * sig).astype(bf16)
    gp_ref[...] = gate_grad
    up_ref[...] = up_grad
    back_acc[...] += dot_nt(gate_grad, wg) + dot_nt(up_grad, wu)

    @pl.when(step == pl.num_programs(0) - 1)
    def _():
        dots = dot_scr[...]
        coarse = dots.astype(bf16).astype(f32)
        lanes = jnp.where(high, coarse, jnp.where(low, dots - coarse, 0.0)).astype(bf16)
        for r in range(per_plane):
            at = slice(r * capacity, (r + 1) * capacity)
            back_refs[r][:, :width] = back_acc[at, :].astype(bf16)
            back_refs[r][:, width:] = lanes[at]
            out_refs[r][...] = (out_acc[at, :] * gate[at]).astype(bf16)


def experts(mine, x, c, wg, wu, wd, block, blocks, count, kept):
    per_plane = len(x)
    capacity, wide = x[0].shape
    width = c[0].shape[1]
    halves, _, hidden = wg.shape
    rows = per_plane * capacity
    fixed = pl.BlockSpec((capacity, wide), lambda f, s: (0, 0))
    stacked = pl.BlockSpec((None, capacity, width), lambda f, s: (block, 0, 0))
    narrow = pl.BlockSpec((capacity, width), lambda f, s: (0, 0))
    back = jax.ShapeDtypeStruct((capacity, wide), bf16)
    out = jax.ShapeDtypeStruct((blocks, capacity, width), bf16)
    saved = jax.ShapeDtypeStruct((blocks * rows, width), bf16)
    thin = jax.ShapeDtypeStruct((blocks * rows, halves * hidden), bf16)
    saved_spec = pl.BlockSpec((rows, width), lambda f, s: (block, 0))
    thin_spec = pl.BlockSpec((rows, hidden), lambda f, s: (block, f))
    carried = 0 if kept is None else len(kept)
    inputs = 1 + 2 * per_plane + 3
    result = pl.pallas_call(
        functools.partial(expert_kernel, per_plane, count, carried),
        out_shape=(back,) * per_plane + (out,) * per_plane + (saved, saved, thin, thin, thin),
        grid_spec=pltpu.PrefetchScalarGridSpec(
            num_scalar_prefetch=1,
            grid=(halves,),
            in_specs=[fixed] * per_plane
            + [narrow] * per_plane
            + [
                pl.BlockSpec((None, width, hidden), lambda f, s: (f, 0, 0)),
                pl.BlockSpec((None, width, hidden), lambda f, s: (f, 0, 0)),
                pl.BlockSpec((None, hidden, width), lambda f, s: (f, 0, 0)),
            ]
            + [pl.BlockSpec(memory_space=pl.ANY)] * carried,
            out_specs=(fixed,) * per_plane
            + (stacked,) * per_plane
            + (saved_spec, saved_spec, thin_spec, thin_spec, thin_spec),
            scratch_shapes=[
                pltpu.VMEM((rows, width), f32),
                pltpu.VMEM((rows, width), f32),
                pltpu.VMEM((rows, 1), f32),
                pltpu.VMEM((rows, 1), f32),
            ],
        ),
        input_output_aliases={inputs + i: per_plane + i for i in range(carried)},
        compiler_params=params(1, 60),
        cost_estimate=pl.CostEstimate(
            flops=12 * rows * width * hidden * halves,
            bytes_accessed=12 * rows * width + 6 * width * hidden * halves,
            transcendentals=rows * hidden * halves,
        ),
        name="experts",
    )(mine, *x, *c, wg, wu, wd, *(kept or ()))
    return result[:per_plane], result[per_plane:]


def after(value, *others):
    return lax.optimization_barrier((value,) + others)[0]


def body(
    hidden_in,
    out_cotangent,
    segment_number,
    expert_routes,
    pair_order,
    norm_gain,
    query_weight,
    key_weight,
    value_weight,
    output_weight,
    query_gain,
    key_gain,
    ffn_norm_gain,
    router_weight,
    expert_gate,
    expert_up,
    expert_down,
):
    tok_rows, width = hidden_in.shape
    devices = lax.axis_size(AXIS)
    members = max(1, SEQ_MIN // tok_rows)
    planes = devices // members
    per_plane = members // 2
    expert_count = devices // 2
    capacity = tok_rows * TOPK // expert_count
    heads = width // HD // members
    head_width = heads * HD
    own_rows = norm_gain.shape[0]
    seq = members * tok_rows
    me = lax.axis_index(AXIS)
    plane, member = me // members, me % members
    mine = (me // 2).astype(jnp.int32).reshape(1)
    chips = jnp.arange(per_plane, dtype=jnp.int32)
    targets = (plane * per_plane + ((member // 2) ^ chips)).astype(jnp.int32)
    places = (plane ^ jnp.arange(planes, dtype=jnp.int32)).astype(jnp.int32)

    plane_groups = [[g * members + j for j in range(members)] for g in range(planes)]
    stack_groups = [[g * members + j for g in range(planes)] for j in range(members)]

    def exchange(value, groups=None):
        return lax.all_to_all(
            value, AXIS, split_axis=0, concat_axis=0, tiled=True, axis_index_groups=groups
        )

    def gather(value, groups=None):
        return lax.all_gather(value, AXIS, axis=0, tiled=True, axis_index_groups=groups)

    def reduce(value, groups=None):
        return lax.psum_scatter(
            value, AXIS, scatter_dimension=0, tiled=True, axis_index_groups=groups
        )

    def flip(value, bits):
        if bits == 0:
            return value
        return lax.ppermute(value, AXIS, [(i, i ^ bits) for i in range(devices)])

    def to_core(value):
        return flip(value, 1)

    def to_chip(values):
        return [flip(value, 2 * r) for r, value in enumerate(values)]

    def to_plane(value, d):
        return flip(value, members * d)

    upward = [(i, i + members) for i in range(devices - members)]
    downward = [(i + members, i) for i in range(devices - members)]

    def spread(value, start=None):
        start = value if start is None else start
        below, above = [start], [start]
        for _ in range(planes - 1):
            below.append(lax.ppermute(below[-1], AXIS, upward))
            above.append(lax.ppermute(above[-1], AXIS, downward))
        found = [value]
        for d in range(1, planes):
            wanted = {}
            for g in range(planes):
                wanted.setdefault((g ^ d) - g, []).append(g)
            chosen = None
            for away, at in wanted.items():
                from_there = above[away] if away > 0 else below[-away]
                if chosen is None:
                    chosen = from_there
                else:
                    here = functools.reduce(lambda x, y: x | y, [plane == g for g in at])
                    chosen = jnp.where(here, from_there, chosen)
            found.append(chosen)
        return found

    def in_order(values):
        rows = values[0].shape[0]
        joined = jnp.zeros((planes * rows,) + values[0].shape[1:], values[0].dtype)
        for d, value in enumerate(values):
            joined = lax.dynamic_update_slice_in_dim(joined, value, places[d] * rows, 0)
        return joined

    columns = jnp.concatenate(
        [w.reshape(own_rows, members, head_width) for w in (query_weight, key_weight, value_weight)],
        axis=2,
    )
    columns = exchange(
        columns.transpose(1, 0, 2).reshape(members * own_rows, 3 * head_width), plane_groups
    )
    weights = spread(columns)
    rows_all = gather(hidden_in, plane_groups)

    pieces = (
        router_weight.reshape(-1),
        norm_gain,
        ffn_norm_gain,
        query_gain,
        key_gain,
        segment_number.astype(bf16),
    )
    packed = jnp.concatenate(pieces)
    length = packed.shape[0]
    padded = -(-length // 128) * 128
    packed = after(jnp.pad(packed, (0, padded - length)), columns)
    packed = exchange(jnp.broadcast_to(packed[None], (devices, padded)))
    small = []
    at = 0
    for piece in pieces:
        small.append(packed[:, at : at + piece.shape[0]])
        at += piece.shape[0]
    router_full = small[0].reshape(width, expert_count)
    gain_one = small[1].reshape(1, width).astype(f32)
    gain_two = small[2].reshape(1, width).astype(f32)
    gain_q = small[3].reshape(1, HD).astype(f32)
    gain_k = small[4].reshape(1, HD).astype(f32)
    segments = lax.dynamic_slice_in_dim(small[5], plane * members, members, 0).astype(f32)
    seg_row, seg_col = segments.reshape(1, seq), segments.reshape(seq, 1)
    seg_blocks = segments.reshape(seq // ROWS, ROWS)
    seg_first, seg_last = seg_blocks[:, 0], seg_blocks[:, -1]
    low = jnp.sum((seg_last[None, :] < seg_first[:, None]).astype(jnp.int32), axis=1)
    high = jnp.sum((seg_first[None, :] <= seg_last[:, None]).astype(jnp.int32), axis=1)
    output_full = gather(in_order(spread(output_weight)), plane_groups)

    halves = lambda w: jnp.concatenate([w, to_core(w)], axis=0)
    wg, wu, wd = halves(expert_gate), halves(expert_up), halves(expert_down)

    slots = block_slots(expert_routes, pair_order, expert_count)
    slots = [to_plane(slots, d) for d in range(planes)]
    cot = []
    for d, rows in enumerate(spread(out_cotangent, after(out_cotangent, *weights))):
        cot.append(to_chip(dispatch(targets, slots[d], rows, per_plane, capacity)))

    cosine, sine = rope_tables(seq)
    act_one, pre, rot = qkv_project(
        places, rows_all, gain_one, weights, gain_q, gain_k, cosine, sine, heads
    )
    out_wide, out_heads, lse = attention(rot, seg_col, seg_row, low, high, heads)
    out_low = exchange(out_heads, plane_groups).reshape(members, tok_rows, head_width)
    out_low = out_low.transpose(1, 0, 2).reshape(tok_rows, planes, members, own_rows)
    out_low = out_low.transpose(0, 2, 1, 3).reshape(tok_rows, width)
    tokens = hidden_in.astype(f32)
    cotangent = out_cotangent.astype(f32)
    middle = tokens + dot_nn(out_low, output_full)
    inverse_two = lax.rsqrt(jnp.mean(middle * middle, axis=-1, keepdims=True) + norm_eps)
    act_two = (middle * inverse_two * gain_two).astype(bf16)

    logits = dot_nn(act_two, router_full)
    expert_ids = jnp.arange(expert_count, dtype=jnp.int32)
    routed = jnp.any(expert_routes[:, :, None] == expert_ids[None, None, :], axis=1)
    logits = jnp.where(routed, logits, masked_score)
    gates = jnp.where(routed, jnp.exp(logits - jnp.max(logits, axis=1, keepdims=True)), 0.0)
    gates = gates / jnp.sum(gates, axis=1, keepdims=True)
    coarse = lax.reduce_precision(gates, 8, 7)
    extra = -(-2 * expert_count // 128) * 128
    act_wide = jnp.concatenate(
        [
            act_two,
            coarse.astype(bf16),
            (gates - coarse).astype(bf16),
            jnp.zeros((tok_rows, extra - 2 * expert_count), bf16),
        ],
        axis=1,
    )

    rows = spread(act_wide)
    act_sent, backs, kept, came = [], [], None, []

    def send(d, *others):
        act_sent.append(to_chip(dispatch(targets, slots[d], after(rows[d], *others), per_plane, capacity)))

    def sum_up(d, *others):
        first_row = after(came[d][0], *others)
        back = combine(targets, slots[d], [first_row] + came[d][1:], None, tok_rows)
        backs.append(to_plane(back, d))

    send(0)
    if planes > 1:
        send(1)
    for d in range(planes):
        own = act_sent[d][0]
        if d + 1 < planes:
            own = after(own, act_sent[d + 1][0])
        back, kept = experts(
            mine, [own] + act_sent[d][1:], cot[d], wg, wu, wd, d, planes, expert_count, kept
        )
        if d + 2 < planes:
            send(d + 2, back[0])
        came.append(to_chip(back))
        if d > 0:
            sum_up(d - 1, back[0])
    sum_up(planes - 1)
    outs, (x_all, c_all, hid_all, gp_all, up_all) = kept[:per_plane], kept[per_plane:]
    outs = to_chip([after(out, *came[-1]) for out in outs])

    hidden = expert_gate.shape[2]

    grad_gate = dot_tn(x_all, gp_all[:, :hidden]) + to_core(dot_tn(x_all, gp_all[:, hidden:]))
    grad_up = dot_tn(x_all, up_all[:, :hidden]) + to_core(dot_tn(x_all, up_all[:, hidden:]))
    grad_down = dot_tn(hid_all[:, :hidden], c_all) + to_core(dot_tn(hid_all[:, hidden:], c_all))

    backs[-1] = after(backs[-1], grad_gate, grad_up, grad_down)
    back_sum = sum(back.astype(f32) for back in backs)
    expert_in_grad = back_sum[:, :width]
    gate_grad = (
        back_sum[:, width : width + expert_count]
        + back_sum[:, width + expert_count : width + 2 * expert_count]
    )
    select_grad = gates * (gate_grad - jnp.sum(gates * gate_grad, axis=1, keepdims=True))
    logit_grad = select_grad.astype(bf16)
    grad_router = dot_tn(act_two, logit_grad)
    act_two_grad = expert_in_grad + dot_nt(logit_grad, router_full)
    weighted = act_two_grad * gain_two
    grad_gain_two = jnp.sum(act_two_grad * middle * inverse_two, axis=0)
    middle_grad = (
        cotangent
        + inverse_two * weighted
        - middle * inverse_two**3 * jnp.mean(weighted * middle, axis=-1, keepdims=True)
    )
    middle_low = middle_grad.astype(bf16)

    out_grad = dot_nt(middle_low, output_full).astype(bf16)
    out_grad = out_grad.reshape(tok_rows, members, planes, own_rows).transpose(0, 2, 1, 3)
    out_grad = out_grad.reshape(tok_rows, members, head_width).transpose(1, 0, 2)
    out_grad = exchange(out_grad.reshape(seq, head_width), plane_groups)
    middle_all = gather(middle_low, plane_groups)
    grads, parts, mixture = [], [], None
    for head in range(heads):
        tied = out_grad
        if head == heads - 1:
            sent = [
                combine(
                    targets, slots[d], [after(outs[0], *grads)] + outs[1:], d, tok_rows
                )
                for d in range(planes)
            ]
            tied = after(out_grad, *sent)
            mixture = [to_plane(value, d) for d, value in enumerate(sent)]
        dq, dk, dv, gains = attention_back(
            head,
            rot,
            tied,
            out_wide,
            lse,
            seg_col,
            seg_row,
            low,
            high,
            pre,
            gain_q,
            gain_k,
            cosine,
            sine,
            heads,
        )
        grads.append(jnp.concatenate([dq, dk, dv], axis=1))
        parts.append(gains)
    grad_gains = sum(parts)
    layer_out = middle + sum(value.astype(f32) for value in mixture)
    layer_out = layer_out.astype(bf16)

    taken = []
    for grad in grads:
        part = reduce(dot_tn(act_one, grad).astype(bf16), stack_groups)
        taken.append(exchange(part, plane_groups).reshape(members, own_rows, 3, 1, HD))
    part = jnp.concatenate(taken, axis=3)
    part = part.transpose(2, 1, 0, 3, 4).reshape(3, own_rows, width).astype(f32)
    grad_query, grad_key, grad_value = part[0], part[1], part[2]

    core, chip = me % 2, member // 2
    ordered = in_order(weights).reshape(width, 3, heads, HD)
    tall = [grad.reshape(per_plane, 2, tok_rows, 3 * HD) for grad in grads]

    def for_core(which):
        total = None
        for head, grad in enumerate(tall):
            rows_in = lax.dynamic_index_in_dim(grad, which, 1, False)
            rows_in = rows_in.reshape(per_plane * tok_rows, 3 * HD)
            term = dot_nt(rows_in, ordered[:, :, head].reshape(width, 3 * HD))
            total = term if total is None else total + term
        return total

    theirs = to_core(for_core(1 - core).astype(bf16))
    pair_sum = (for_core(core) + theirs.astype(f32)).astype(bf16)
    pair_sum = pair_sum.reshape(per_plane, tok_rows, width)
    act_one_grad = sum(
        flip(lax.dynamic_index_in_dim(pair_sum, chip ^ r, 0, False), 2 * r).astype(f32)
        for r in range(per_plane)
    )

    output_part = dot_tn(out_heads, middle_all).astype(bf16)
    output_part = output_part.reshape(planes, head_width // planes, width)
    output_part = sum(
        to_plane(lax.dynamic_index_in_dim(output_part, places[d], 0, False), d).astype(f32)
        for d in range(planes)
    )
    to_owner = [
        (g * members + j, j * planes + g) for g in range(planes) for j in range(members)
    ]
    grad_output = lax.ppermute(output_part, AXIS, to_owner)

    inverse_one = lax.rsqrt(jnp.mean(tokens * tokens, axis=-1, keepdims=True) + norm_eps)
    weighted = act_one_grad * gain_one
    grad_hidden = (
        middle_grad
        + inverse_one * weighted
        - tokens * inverse_one**3 * jnp.mean(weighted * tokens, axis=-1, keepdims=True)
    )
    grad_gain_one = (
        jnp.sum(
            grad_query * query_weight.astype(f32)
            + grad_key * key_weight.astype(f32)
            + grad_value * value_weight.astype(f32),
            axis=1,
        )
        / norm_gain.astype(f32)
    )

    sums = (
        grad_router.reshape(devices, -1),
        grad_gain_two.reshape(devices, -1),
        grad_gains[0].reshape(devices, -1),
        grad_gains[1].reshape(devices, -1),
    )
    packed = jnp.concatenate(sums, axis=1)
    length = packed.shape[1]
    padded = -(-length // 128) * 128
    packed = jnp.sum(exchange(jnp.pad(packed, ((0, 0), (0, padded - length)))), axis=0)
    at, tiny = 0, []
    for piece in sums:
        tiny.append(packed[at : at + piece.shape[1]])
        at += piece.shape[1]

    return (
        layer_out,
        grad_hidden,
        grad_gain_one,
        grad_query,
        grad_key,
        grad_value,
        grad_output,
        tiny[2],
        tiny[3],
        tiny[1],
        tiny[0].reshape(own_rows, expert_count),
        grad_gate[None],
        grad_up[None],
        grad_down[None],
    )


def solution(mesh):
    row, mat, cube = P(AXIS), P(AXIS, None), P(AXIS, None, None)
    return jax.shard_map(
        body,
        mesh=mesh,
        in_specs=(mat, mat, row, mat, mat, row, mat, mat, mat, mat, row, row, row, mat)
        + (cube,) * 3,
        out_specs=(mat, mat, row, mat, mat, mat, mat, row, row, row, mat) + (cube,) * 3,
        check_vma=False,
    )
```

```python
import functools
import math

import jax
import jax.numpy as jnp
from jax import lax
from jax.experimental import pallas as pl
from jax.experimental.pallas import tpu as pltpu
from jax.sharding import PartitionSpec as P

HD = 128
TOPK = 8
SEQ_MIN = 2048
ROWS = 256
SHARE = 32

norm_eps = 1e-05
head_eps = 1e-06
rope_base = 10000.0
masked_score = -1e30
absent_slot = 4096.0

AXIS = "fsdp"
f32 = jnp.float32
bf16 = jnp.bfloat16
MIB = 1 << 20


def dot_nt(left, right):
    return lax.dot_general(left, right, (((1,), (1,)), ((), ())), preferred_element_type=f32)


def dot_tn(left, right):
    return lax.dot_general(left, right, (((0,), (0,)), ((), ())), preferred_element_type=f32)


def dot_nn(left, right):
    return lax.dot_general(left, right, (((1,), (0,)), ((), ())), preferred_element_type=f32)


def params(steps, mib):
    return pltpu.CompilerParams(
        dimension_semantics=("arbitrary",) * steps, vmem_limit_bytes=mib * MIB
    )


def estimate(flops, bytes_accessed, transcendentals):
    return pl.CostEstimate(
        flops=flops // SHARE, bytes_accessed=bytes_accessed // SHARE, transcendentals=transcendentals // SHARE
    )


def rope_tables(count):
    half_width = HD // 2
    frequency = jnp.exp(-math.log(rope_base) * 2.0 * jnp.arange(half_width, dtype=f32) / HD)
    angles = jnp.arange(count, dtype=f32)[:, None] * frequency[None, :]
    cosine, sine = jnp.cos(angles), jnp.sin(angles)
    return jnp.concatenate([cosine, cosine], axis=-1), jnp.concatenate([-sine, sine], axis=-1)


def slots_kernel(expert_count, routes_ref, order_ref, slots_ref):
    tok_rows = routes_ref.shape[0]
    pair_count = order_ref.shape[1]
    order = order_ref[...]
    shift = TOPK.bit_length() - 1
    token_of = lax.shift_right_logical(order, jnp.full_like(order, shift))
    route_of = order & (TOPK - 1)
    token_iota = lax.broadcasted_iota(jnp.int32, (tok_rows, pair_count), 0)
    token_hot = jnp.where(token_iota == token_of, 1.0, 0.0).astype(bf16)
    place = lax.broadcasted_iota(jnp.int32, (TOPK, pair_count), 1)
    chosen = lax.broadcasted_iota(jnp.int32, (TOPK, pair_count), 0) == route_of
    high = lax.shift_right_logical(place, jnp.full_like(place, 8)).astype(f32)
    low = (place & 255).astype(f32)
    digits = jnp.concatenate([jnp.where(chosen, high, 0.0), jnp.where(chosen, low, 0.0)], axis=0)
    found = dot_nt(token_hot, digits.astype(bf16))
    rank = found[:, :TOPK] * 256.0 + found[:, TOPK:]
    routes = routes_ref[...]
    lanes = -(-expert_count // 128) * 128
    expert_iota = lax.broadcasted_iota(jnp.int32, (tok_rows, lanes), 1)
    never = 1e9
    by_expert = jnp.full((tok_rows, lanes), never, f32)
    for k in range(TOPK):
        by_expert = jnp.where(expert_iota == routes[:, k : k + 1], rank[:, k : k + 1], by_expert)
    turned = by_expert.T
    for e in range(expert_count):
        mine = turned[e : e + 1, :]
        earlier = jnp.where(by_expert[:, e : e + 1] < mine, 1.0, 0.0)
        count = jnp.sum(earlier, axis=0, keepdims=True)
        slots_ref[e : e + 1, :] = jnp.where(mine < never, count, absent_slot)


def block_slots(routes, order, expert_count):
    tok_rows = routes.shape[0]
    return pl.pallas_call(
        functools.partial(slots_kernel, expert_count),
        out_shape=jax.ShapeDtypeStruct((expert_count, tok_rows), f32),
        compiler_params=pltpu.CompilerParams(vmem_limit_bytes=32 * MIB),
        name="block_slots",
    )(routes, order)


def slot_hot(slots_ref, expert, capacity):
    slot_row = slots_ref[pl.ds(expert, 1), :]
    slot_iota = lax.broadcasted_iota(jnp.int32, (capacity, slot_row.shape[1]), 0).astype(f32)
    return jnp.where(slot_iota == slot_row, 1.0, 0.0).astype(bf16)


def dispatch_kernel(per_plane, at_ref, slots_ref, rows_ref, out_ref):
    capacity = out_ref.shape[0] // per_plane
    hot = [slot_hot(slots_ref, at_ref[0] + r, capacity) for r in range(per_plane)]
    out_ref[...] = dot_nn(jnp.concatenate(hot, axis=0), rows_ref[...]).astype(bf16)


def dispatch(at, slots, rows, per_plane, capacity):
    _, tok_rows, width = rows.shape
    slot_rows = per_plane * capacity
    return pl.pallas_call(
        functools.partial(dispatch_kernel, per_plane),
        out_shape=jax.ShapeDtypeStruct((slot_rows, width), bf16),
        grid_spec=pltpu.PrefetchScalarGridSpec(
            num_scalar_prefetch=1,
            grid=(1,),
            in_specs=[
                pl.BlockSpec(slots.shape, lambda i, s: (0, 0)),
                pl.BlockSpec((None, tok_rows, width), lambda i, s: (s[1], 0, 0)),
            ],
            out_specs=pl.BlockSpec((slot_rows, width), lambda i, s: (0, 0)),
        ),
        compiler_params=params(1, 32),
        cost_estimate=estimate(
            flops=2 * slot_rows * tok_rows * width,
            bytes_accessed=2 * (slot_rows + tok_rows) * width,
            transcendentals=0,
        ),
        name="dispatch",
    )(at, slots, rows)


def combine_kernel(per_plane, carried, at_ref, slots_ref, rows_ref, *refs):
    out_ref = refs[carried]
    capacity = rows_ref.shape[0] // per_plane
    hot = [slot_hot(slots_ref, at_ref[0] + r, capacity) for r in range(per_plane)]
    out_ref[...] = dot_tn(jnp.concatenate(hot, axis=0), rows_ref[...]).astype(bf16)


def combine(at, slots, rows, per_plane, tok_rows, blocks=1, kept=None):
    slot_rows, width = rows.shape
    carried = 0 if kept is None else 1
    return pl.pallas_call(
        functools.partial(combine_kernel, per_plane, carried),
        out_shape=jax.ShapeDtypeStruct((blocks, tok_rows, width), bf16),
        grid_spec=pltpu.PrefetchScalarGridSpec(
            num_scalar_prefetch=1,
            grid=(1,),
            in_specs=[
                pl.BlockSpec(slots.shape, lambda i, s: (0, 0)),
                pl.BlockSpec((slot_rows, width), lambda i, s: (0, 0)),
            ]
            + [pl.BlockSpec(memory_space=pl.ANY)] * carried,
            out_specs=pl.BlockSpec((None, tok_rows, width), lambda i, s: (s[1], 0, 0)),
        ),
        input_output_aliases={3: 0} if carried else {},
        compiler_params=params(1, 32),
        cost_estimate=estimate(
            flops=2 * slot_rows * tok_rows * width,
            bytes_accessed=2 * (slot_rows + tok_rows) * width,
            transcendentals=0,
        ),
        name="combine",
    )(at, slots, rows, *(() if kept is None else (kept,)))


def qkv_kernel(heads, planes, at_ref, x_ref, gain_ref, *refs):
    w_refs = refs[:planes]
    gq_ref, gk_ref, cos_ref, sin_ref, act_ref, pre_ref, rot_ref = refs[planes:]
    x = x_ref[...].astype(f32)
    inverse = lax.rsqrt(jnp.mean(x * x, axis=-1, keepdims=True) + norm_eps)
    act = (x * inverse * gain_ref[...]).astype(bf16)
    act_ref[...] = act
    y = None
    depth = w_refs[0].shape[0]
    for d in range(planes):
        columns = pl.ds(pl.multiple_of(at_ref[d] * depth, depth), depth)
        term = dot_nn(act_ref[:, columns], w_refs[d][...])
        y = term if y is None else y + term
    cosine, sine = cos_ref[...], sin_ref[...]
    for part, gain in enumerate((gq_ref[...], gk_ref[...])):
        for h in range(heads):
            at = (part * heads + h) * HD
            u = y[:, at : at + HD]
            pre_ref[:, at : at + HD] = u
            n = u * lax.rsqrt(jnp.mean(u * u, axis=-1, keepdims=True) + head_eps) * gain
            rot_ref[:, at : at + HD] = (n * cosine + pltpu.roll(n, HD // 2, 1) * sine).astype(bf16)
    at = 2 * heads * HD
    rot_ref[:, at:] = y[:, at:].astype(bf16)


def qkv_project(places, rows, gain, weights, gain_q, gain_k, cosine, sine, heads):
    count, width = rows.shape
    planes = len(weights)
    depth, out_width = weights[0].shape
    pre_width = 2 * heads * HD
    whole = lambda i, s: (0, 0)
    block = lambda i, s: (i, 0)
    return pl.pallas_call(
        functools.partial(qkv_kernel, heads, planes),
        out_shape=(
            jax.ShapeDtypeStruct((count, width), bf16),
            jax.ShapeDtypeStruct((count, pre_width), f32),
            jax.ShapeDtypeStruct((count, out_width), bf16),
        ),
        grid_spec=pltpu.PrefetchScalarGridSpec(
            num_scalar_prefetch=1,
            grid=(count // ROWS,),
            in_specs=[
                pl.BlockSpec((ROWS, width), block),
                pl.BlockSpec((1, width), whole),
            ]
            + [pl.BlockSpec((depth, out_width), whole)] * planes
            + [
                pl.BlockSpec((1, HD), whole),
                pl.BlockSpec((1, HD), whole),
                pl.BlockSpec((ROWS, HD), block),
                pl.BlockSpec((ROWS, HD), block),
            ],
            out_specs=(
                pl.BlockSpec((ROWS, width), block),
                pl.BlockSpec((ROWS, pre_width), block),
                pl.BlockSpec((ROWS, out_width), block),
            ),
        ),
        compiler_params=params(1, 48),
        cost_estimate=estimate(
            flops=2 * count * width * out_width,
            bytes_accessed=4 * count * width + 2 * width * out_width + 6 * count * out_width,
            transcendentals=0,
        ),
        name="qkv_project",
    )(places, rows, gain, *weights, gain_q, gain_k, cosine, sine)


def attn_kernel(
    scale, low_ref, high_ref, q_ref, k_ref, v_ref, sq_ref, sk_ref, o_ref, ol_ref, lse_ref, s_scr
):
    block = pl.program_id(1)
    low, high = low_ref[block], high_ref[block]
    q = q_ref[...]
    seg_q = sq_ref[...]
    half = ROWS // 2

    def scores(kb, top):
        at = pl.ds(pl.multiple_of(kb * ROWS, ROWS), ROWS)
        s = dot_nt(q, k_ref[at, :]) * scale
        s = jnp.where(seg_q == sk_ref[:, at], s, masked_score)
        s_scr[:, at] = s
        return jnp.maximum(top, jnp.maximum(s[:, :half], s[:, half:]))

    top = lax.fori_loop(low, high, scores, jnp.full((ROWS, half), masked_score, f32))
    top = jnp.max(top, axis=-1, keepdims=True)

    def weigh(kb, carry):
        total, acc = carry
        at = pl.ds(pl.multiple_of(kb * ROWS, ROWS), ROWS)
        p = jnp.exp(s_scr[:, at] - top)
        acc = acc + dot_nn(p.astype(bf16), v_ref[at, :])
        return total + (p[:, :half] + p[:, half:]), acc

    total, acc = lax.fori_loop(
        low, high, weigh, (jnp.zeros((ROWS, half), f32), jnp.zeros((ROWS, HD), f32))
    )
    total = jnp.sum(total, axis=-1, keepdims=True)
    out = acc / total
    o_ref[...] = out
    ol_ref[...] = out.astype(bf16)
    lse = jnp.broadcast_to(top + jnp.log(total), (ROWS, HD)).T
    lse_ref[0] = lse[0:1, :]


def attention(rot, seg_col, seg_row, low, high, heads):
    count = rot.shape[0]
    blocks = count // ROWS
    scale = HD ** (-0.5)
    return pl.pallas_call(
        functools.partial(attn_kernel, scale),
        out_shape=(
            jax.ShapeDtypeStruct((count, heads * HD), f32),
            jax.ShapeDtypeStruct((count, heads * HD), bf16),
            jax.ShapeDtypeStruct((heads * blocks, 1, ROWS), f32),
        ),
        grid_spec=pltpu.PrefetchScalarGridSpec(
            num_scalar_prefetch=2,
            grid=(heads, blocks),
            in_specs=[
                pl.BlockSpec((ROWS, HD), lambda h, i, *s: (i, h)),
                pl.BlockSpec((count, HD), lambda h, i, *s: (0, heads + h)),
                pl.BlockSpec((count, HD), lambda h, i, *s: (0, 2 * heads + h)),
                pl.BlockSpec((ROWS, 1), lambda h, i, *s: (i, 0)),
                pl.BlockSpec((1, count), lambda h, i, *s: (0, 0)),
            ],
            out_specs=(
                pl.BlockSpec((ROWS, HD), lambda h, i, *s: (i, h)),
                pl.BlockSpec((ROWS, HD), lambda h, i, *s: (i, h)),
                pl.BlockSpec((1, 1, ROWS), lambda h, i, *s: (h * blocks + i, 0, 0)),
            ),
            scratch_shapes=[pltpu.VMEM((ROWS, count), f32)],
        ),
        compiler_params=params(2, 32),
        cost_estimate=estimate(
            flops=2 * heads * count * count * HD,
            bytes_accessed=12 * heads * count * HD,
            transcendentals=heads * count * count // 2,
        ),
        name="attention",
    )(low, high, rot, rot, rot, seg_col, seg_row)


def head_back(grad, pre, gain, cosine, sine):
    n = grad * cosine - pltpu.roll(grad, HD // 2, 1) * sine
    inverse = lax.rsqrt(jnp.mean(pre * pre, axis=-1, keepdims=True) + head_eps)
    w = n * gain
    back = inverse * w - pre * inverse**3 * jnp.mean(w * pre, axis=-1, keepdims=True)
    return back, jnp.sum(n * pre * inverse, axis=0, keepdims=True)


def attn_back_kernel(
    scale,
    low_ref,
    high_ref,
    q_ref,
    k_ref,
    v_ref,
    do_ref,
    o_ref,
    lse_ref,
    sq_ref,
    sk_ref,
    qpre_ref,
    kpre_ref,
    gq_ref,
    gk_ref,
    cosq_ref,
    sinq_ref,
    cosk_ref,
    sink_ref,
    dq_ref,
    dk_ref,
    dv_ref,
    gain_ref,
    dk_scr,
    dv_scr,
):
    block = pl.program_id(0)
    low, high = low_ref[block], high_ref[block]

    @pl.when(block == 0)
    def _():
        dk_scr[...] = jnp.zeros_like(dk_scr)
        dv_scr[...] = jnp.zeros_like(dv_scr)
        gain_ref[...] = jnp.zeros_like(gain_ref)

    q, do = q_ref[...], do_ref[...]
    row_dot = jnp.sum((do.astype(f32) * o_ref[...]).T, axis=0, keepdims=True)
    lse = lse_ref[0]
    seg_q = sq_ref[...]

    def tile(kb, dq):
        at = pl.ds(pl.multiple_of(kb * ROWS, ROWS), ROWS)
        k, v = k_ref[at, :], v_ref[at, :]
        s = dot_nt(k, q) * scale
        p = jnp.where(sk_ref[at, :] == seg_q, jnp.exp(s - lse), 0.0)
        dp = dot_nt(v, do)
        ds = (p * (dp - row_dot)).astype(bf16)
        dv_scr[at, :] += dot_nn(p.astype(bf16), do)
        dk_scr[at, :] += dot_nn(ds, q)
        return dq + dot_tn(ds, k)

    dq = lax.fori_loop(low, high, tile, jnp.zeros((ROWS, HD), f32))
    back, gain_q = head_back(dq * scale, qpre_ref[...], gq_ref[...], cosq_ref[...], sinq_ref[...])
    dq_ref[...] = back.astype(bf16)
    gain_ref[0:1, :] += gain_q

    @pl.when(block == pl.num_programs(0) - 1)
    def _():
        @pl.loop(0, dk_scr.shape[0] // ROWS)
        def _(i):
            at = pl.ds(pl.multiple_of(i * ROWS, ROWS), ROWS)
            back, gain_k = head_back(
                dk_scr[at, :] * scale, kpre_ref[at, :], gk_ref[...], cosk_ref[at, :], sink_ref[at, :]
            )
            dk_ref[at, :] = back.astype(bf16)
            dv_ref[at, :] = dv_scr[at, :].astype(bf16)
            gain_ref[1:2, :] += gain_k


def attention_back(
    head, rot, grad, out, lse, seg_col, seg_row, low, high, pre, gain_q, gain_k, cosine, sine, heads
):
    count = rot.shape[0]
    blocks = count // ROWS
    scale = HD ** (-0.5)
    mine = lambda i, *s: (i, head)
    first = lambda i, *s: (i, 0)
    whole = lambda i, *s: (0, 0)
    result = jax.ShapeDtypeStruct((count, HD), bf16)
    return pl.pallas_call(
        functools.partial(attn_back_kernel, scale),
        out_shape=(result, result, result, jax.ShapeDtypeStruct((8, HD), f32)),
        grid_spec=pltpu.PrefetchScalarGridSpec(
            num_scalar_prefetch=2,
            grid=(blocks,),
            in_specs=[
                pl.BlockSpec((ROWS, HD), mine),
                pl.BlockSpec((count, HD), lambda i, *s: (0, heads + head)),
                pl.BlockSpec((count, HD), lambda i, *s: (0, 2 * heads + head)),
                pl.BlockSpec((ROWS, HD), mine),
                pl.BlockSpec((ROWS, HD), mine),
                pl.BlockSpec((1, 1, ROWS), lambda i, *s: (head * blocks + i, 0, 0)),
                pl.BlockSpec((1, ROWS), lambda i, *s: (0, i)),
                pl.BlockSpec((count, 1), whole),
                pl.BlockSpec((ROWS, HD), mine),
                pl.BlockSpec((count, HD), lambda i, *s: (0, heads + head)),
                pl.BlockSpec((1, HD), whole),
                pl.BlockSpec((1, HD), whole),
                pl.BlockSpec((ROWS, HD), first),
                pl.BlockSpec((ROWS, HD), first),
                pl.BlockSpec((count, HD), whole),
                pl.BlockSpec((count, HD), whole),
            ],
            out_specs=(
                pl.BlockSpec((ROWS, HD), first),
                pl.BlockSpec((count, HD), whole),
                pl.BlockSpec((count, HD), whole),
                pl.BlockSpec((8, HD), whole),
            ),
            scratch_shapes=[pltpu.VMEM((count, HD), f32), pltpu.VMEM((count, HD), f32)],
        ),
        compiler_params=params(1, 48),
        cost_estimate=estimate(
            flops=5 * count * count * HD,
            bytes_accessed=30 * count * HD,
            transcendentals=count * count // 2,
        ),
        name="attention_back",
    )(
        low, high, rot, rot, rot, grad, out, lse, seg_row, seg_col, pre, pre, gain_q, gain_k,
        cosine, sine, cosine, sine,
    )


def expert_kernel(count, carried, mine_ref, x_ref, c_ref, wg_ref, wu_ref, wd_ref, *refs):
    refs = refs[carried:]
    back_ref, out_ref, xs_ref, cs_ref, hid_ref, gp_ref, up_ref = refs[:7]
    out_acc, back_acc, gate_scr, dot_scr = refs[7:]
    step = pl.program_id(0)
    rows, width = c_ref.shape
    extra = x_ref.shape[1] - width
    lane = lax.broadcasted_iota(jnp.int32, (rows, extra), 1)
    high, low = lane == mine_ref[0], lane == mine_ref[0] + count

    @pl.when(step == 0)
    def _():
        xs_ref[...] = x_ref[:, :width]
        cs_ref[...] = c_ref[...]
        picked = jnp.where(high | low, x_ref[:, width:].astype(f32), 0.0)
        gate_scr[...] = jnp.sum(picked, axis=-1, keepdims=True)
        out_acc[...] = jnp.zeros_like(out_acc)
        back_acc[...] = jnp.zeros_like(back_acc)
        dot_scr[...] = jnp.zeros_like(dot_scr)

    x, c, gate = x_ref[:, :width], c_ref[...], gate_scr[...]
    wg, wu, wd = wg_ref[...], wu_ref[...], wd_ref[...]
    gate_pre, up_pre = dot_nn(x, wg), dot_nn(x, wu)
    sig = jax.nn.sigmoid(gate_pre)
    hidden = (gate_pre * sig * up_pre).astype(bf16)
    out_acc[...] += dot_nn(hidden, wd)
    plain = dot_nt(c, wd)
    wide = hidden.astype(f32)
    dot_scr[...] += jnp.sum(wide * plain, axis=-1, keepdims=True)
    hid_ref[...] = (wide * gate).astype(bf16)
    hidden_grad = plain * gate
    gate_grad = (hidden_grad * up_pre * sig * (1.0 + gate_pre * (1.0 - sig))).astype(bf16)
    up_grad = (hidden_grad * gate_pre * sig).astype(bf16)
    gp_ref[...] = gate_grad
    up_ref[...] = up_grad
    back_acc[...] += dot_nt(gate_grad, wg) + dot_nt(up_grad, wu)

    @pl.when(step == pl.num_programs(0) - 1)
    def _():
        dots = dot_scr[...]
        coarse = dots.astype(bf16).astype(f32)
        lanes = jnp.where(high, coarse, jnp.where(low, dots - coarse, 0.0)).astype(bf16)
        back_ref[:, :width] = back_acc[...].astype(bf16)
        back_ref[:, width:] = lanes
        out_ref[...] = (out_acc[...] * gate).astype(bf16)


def experts(mine, x, c, wg, wu, wd, block, blocks, count, kept):
    rows, wide = x.shape
    width = c.shape[1]
    halves, _, hidden = wg.shape
    whole = lambda f, s: (0, 0)
    saved = jax.ShapeDtypeStruct((blocks * rows, width), bf16)
    thin = jax.ShapeDtypeStruct((blocks * rows, halves * hidden), bf16)
    saved_spec = pl.BlockSpec((rows, width), lambda f, s: (block, 0))
    thin_spec = pl.BlockSpec((rows, hidden), lambda f, s: (block, f))
    carried = 0 if kept is None else len(kept)
    result = pl.pallas_call(
        functools.partial(expert_kernel, count, carried),
        out_shape=(
            jax.ShapeDtypeStruct((rows, wide), bf16),
            jax.ShapeDtypeStruct((rows, width), bf16),
            saved,
            saved,
            thin,
            thin,
            thin,
        ),
        grid_spec=pltpu.PrefetchScalarGridSpec(
            num_scalar_prefetch=1,
            grid=(halves,),
            in_specs=[
                pl.BlockSpec((rows, wide), whole),
                pl.BlockSpec((rows, width), whole),
                pl.BlockSpec((None, width, hidden), lambda f, s: (f, 0, 0)),
                pl.BlockSpec((None, width, hidden), lambda f, s: (f, 0, 0)),
                pl.BlockSpec((None, hidden, width), lambda f, s: (f, 0, 0)),
            ]
            + [pl.BlockSpec(memory_space=pl.ANY)] * carried,
            out_specs=(
                pl.BlockSpec((rows, wide), whole),
                pl.BlockSpec((rows, width), whole),
                saved_spec,
                saved_spec,
                thin_spec,
                thin_spec,
                thin_spec,
            ),
            scratch_shapes=[
                pltpu.VMEM((rows, width), f32),
                pltpu.VMEM((rows, width), f32),
                pltpu.VMEM((rows, 1), f32),
                pltpu.VMEM((rows, 1), f32),
            ],
        ),
        input_output_aliases={6 + i: 2 + i for i in range(carried)},
        compiler_params=params(1, 60),
        cost_estimate=estimate(
            flops=12 * rows * width * hidden * halves,
            bytes_accessed=12 * rows * width + 6 * width * hidden * halves,
            transcendentals=rows * hidden * halves,
        ),
        name="experts",
    )(mine, x, c, wg, wu, wd, *(kept or ()))
    return result[0], result[1], result[2:]


def after(value, *others):
    return lax.optimization_barrier((value,) + others)[0]


def body(
    hidden_in,
    out_cotangent,
    segment_number,
    expert_routes,
    pair_order,
    norm_gain,
    query_weight,
    key_weight,
    value_weight,
    output_weight,
    query_gain,
    key_gain,
    ffn_norm_gain,
    router_weight,
    expert_gate,
    expert_up,
    expert_down,
):
    tok_rows, width = hidden_in.shape
    devices = lax.axis_size(AXIS)
    members = max(1, SEQ_MIN // tok_rows)
    planes = devices // members
    per_plane = members // 2
    expert_count = devices // 2
    capacity = tok_rows * TOPK // expert_count
    heads = width // HD // members
    head_width = heads * HD
    own_rows = norm_gain.shape[0]
    seq = members * tok_rows
    me = lax.axis_index(AXIS)
    plane, member = me // members, me % members
    mine = (me // 2).astype(jnp.int32).reshape(1)
    first = (plane * per_plane).astype(jnp.int32)
    single = jnp.stack([first, jnp.zeros_like(first)])
    places = (plane ^ jnp.arange(planes, dtype=jnp.int32)).astype(jnp.int32)
    stacked = [jnp.stack([first, places[d]]) for d in range(planes)]

    plane_groups = [[g * members + j for j in range(members)] for g in range(planes)]
    stack_groups = [[g * members + j for g in range(planes)] for j in range(members)]
    core_groups = [
        [g * members + 2 * c + h for c in range(per_plane)] for g in range(planes) for h in (0, 1)
    ]

    def exchange(value, groups=None):
        return lax.all_to_all(
            value, AXIS, split_axis=0, concat_axis=0, tiled=True, axis_index_groups=groups
        )

    def gather(value, groups=None):
        return lax.all_gather(value, AXIS, axis=0, tiled=True, axis_index_groups=groups)

    def flip(value, bits):
        if bits == 0:
            return value
        return lax.ppermute(value, AXIS, [(i, i ^ bits) for i in range(devices)])

    def to_core(value):
        return flip(value, 1)

    def to_plane(value, d):
        return flip(value, members * d)

    def in_order(values):
        rows = values[0].shape[0]
        joined = jnp.zeros((planes * rows,) + values[0].shape[1:], values[0].dtype)
        for d, value in enumerate(values):
            joined = lax.dynamic_update_slice_in_dim(joined, value, places[d] * rows, 0)
        return joined

    def over_planes(value):
        value = value.reshape((planes, -1) + value.shape[1:])
        return sum(
            to_plane(lax.dynamic_index_in_dim(value, places[d], 0, False), d).astype(f32)
            for d in range(planes)
        )

    wire, core_op = [], []

    def on_wire(value, groups):
        came = exchange(after(value, *wire[-1:]), groups)
        wire.append(came)
        return came

    def to_chips(value):
        return on_wire(value, core_groups)

    def in_turn(value):
        return after(value, *core_op[-1:])

    def ran(value):
        core_op.append(value)
        return value

    halves = lambda w: jnp.concatenate([w, to_core(w)], axis=0)
    wg, wu, wd = halves(expert_gate), halves(expert_up), halves(expert_down)
    cot_rows = {0: out_cotangent}
    if planes > 1:
        cot_rows[1] = to_plane(out_cotangent, 1)

    columns = jnp.concatenate(
        [w.reshape(own_rows, members, head_width) for w in (query_weight, key_weight, value_weight)],
        axis=2,
    )
    columns = on_wire(
        columns.transpose(1, 0, 2).reshape(members * own_rows, 3 * head_width), plane_groups
    )
    slots = block_slots(expert_routes, pair_order, expert_count)
    slots = [to_plane(slots, d) for d in range(planes)]
    ready = (*cot_rows.values(), wg, wu, wd, *slots)
    weights = [to_plane(after(columns, *ready), d) for d in range(planes)]
    rows_all = gather(after(hidden_in, columns), plane_groups)
    output_full = gather(after(output_weight, columns))

    pieces = (
        router_weight.reshape(-1),
        norm_gain,
        ffn_norm_gain,
        query_gain,
        key_gain,
        segment_number.astype(bf16),
    )
    packed = jnp.concatenate(pieces)
    length = packed.shape[0]
    padded = -(-length // 128) * 128
    packed = jnp.pad(packed, (0, padded - length))
    packed = on_wire(jnp.broadcast_to(packed[None], (devices, padded)), None)
    small = []
    at = 0
    for piece in pieces:
        small.append(packed[:, at : at + piece.shape[0]])
        at += piece.shape[0]
    router_full = small[0].reshape(width, expert_count)
    gain_one = small[1].reshape(1, width).astype(f32)
    gain_two = small[2].reshape(1, width).astype(f32)
    gain_q = small[3].reshape(1, HD).astype(f32)
    gain_k = small[4].reshape(1, HD).astype(f32)
    segments = lax.dynamic_slice_in_dim(small[5], plane * members, members, 0).astype(f32)
    seg_row, seg_col = segments.reshape(1, seq), segments.reshape(seq, 1)
    seg_blocks = segments.reshape(seq // ROWS, ROWS)
    seg_first, seg_last = seg_blocks[:, 0], seg_blocks[:, -1]
    low = jnp.sum((seg_last[None, :] < seg_first[:, None]).astype(jnp.int32), axis=1)
    high = jnp.sum((seg_first[None, :] <= seg_last[:, None]).astype(jnp.int32), axis=1)

    turns = [0] + list(range(2, planes)) + [1] if planes > 1 else [0]
    cot = {}
    for d in turns[1:-1]:
        lowest = d & -d
        if d == lowest:
            cot_rows[d] = to_plane(after(out_cotangent, *weights), d)
        else:
            cot_rows[d] = to_plane(cot_rows[d ^ lowest], lowest)

    def send_cot(d):
        sent = dispatch(single, slots[d], in_turn(cot_rows[d])[None], per_plane, capacity)
        cot[d] = to_chips(ran(sent))

    for d in range(min(2, planes)):
        send_cot(d)

    cosine, sine = rope_tables(seq)
    act_one, pre, rot = qkv_project(
        places, after(rows_all, cot[0]), gain_one, weights, gain_q, gain_k, cosine, sine, heads
    )
    ran(act_one)
    out_wide, out_heads, lse = attention(in_turn(rot), seg_col, seg_row, low, high, heads)
    ran(out_heads)
    out_low = on_wire(out_heads, plane_groups).reshape(members, tok_rows, head_width)
    out_low = after(out_low.transpose(1, 0, 2).reshape(tok_rows, width), *[cot_rows[d] for d in turns[1:2]])
    tokens = hidden_in.astype(f32)
    cotangent = out_cotangent.astype(f32)
    middle = tokens + dot_nn(out_low, output_full)
    inverse_two = lax.rsqrt(jnp.mean(middle * middle, axis=-1, keepdims=True) + norm_eps)
    act_two = (middle * inverse_two * gain_two).astype(bf16)

    logits = dot_nn(act_two, router_full)
    expert_ids = jnp.arange(expert_count, dtype=jnp.int32)
    routed = jnp.any(expert_routes[:, :, None] == expert_ids[None, None, :], axis=1)
    logits = jnp.where(routed, logits, masked_score)
    gates = jnp.where(routed, jnp.exp(logits - jnp.max(logits, axis=1, keepdims=True)), 0.0)
    gates = gates / jnp.sum(gates, axis=1, keepdims=True)
    coarse = lax.reduce_precision(gates, 8, 7)
    extra = -(-2 * expert_count // 128) * 128
    act_wide = jnp.concatenate(
        [
            act_two,
            coarse.astype(bf16),
            (gates - coarse).astype(bf16),
            jnp.zeros((tok_rows, extra - 2 * expert_count), bf16),
        ],
        axis=1,
    )

    act_all = gather(act_wide, stack_groups).reshape(planes, tok_rows, -1)
    act, back, out, kept, backs = {}, {}, {}, None, {}

    def send_act(d):
        rows, at = (act_wide[None], single) if d == 0 else (act_all, stacked[d])
        sent = dispatch(at, slots[d], in_turn(rows), per_plane, capacity)
        act[d] = ran(sent)

    def run_expert(d):
        nonlocal kept
        back[d], out[d], kept = experts(
            mine, in_turn(act[d]), cot[d], wg, wu, wd, d, planes, expert_count, kept
        )
        ran(back[d])

    def sum_up(d):
        rows = combine(single, slots[d], in_turn(back[d]), per_plane, tok_rows)
        backs[d] = to_plane(ran(rows)[0], d)

    send_act(0)
    act[0] = to_chips(act[0])
    for d in range(planes):
        if d not in cot:
            send_cot(d)
    run_expert(0)
    for d in turns[1:]:
        send_act(d)
    for i, d in enumerate(turns[1:]):
        act[d] = to_chips(act[d])
        if i > 0:
            back[turns[i]] = to_chips(back[turns[i]])
        if i + 1 < planes - 1:
            run_expert(d)
            if i > 0:
                sum_up(turns[i])
    rest = [0]
    if planes > 1:
        run_expert(turns[-1])
        rest = [0, turns[-1]]
    if planes > 2:
        sum_up(turns[-2])
    for d in rest:
        back[d] = to_chips(back[d])

    x_all, c_all, hid_all, gp_all, up_all = kept
    hidden = expert_gate.shape[2]
    their_grads = [
        dot_tn(in_turn(x_all), gp_all[:, hidden:]),
        dot_tn(in_turn(x_all), up_all[:, hidden:]),
        dot_tn(hid_all[:, hidden:], in_turn(c_all)),
    ]
    ran(their_grads[-1])
    sum_up(rest[0])
    own_grads = [
        dot_tn(in_turn(x_all), gp_all[:, :hidden]),
        dot_tn(in_turn(x_all), up_all[:, :hidden]),
        dot_tn(hid_all[:, :hidden], in_turn(c_all)),
    ]
    ran(own_grads[-1])
    for d in rest[1:]:
        sum_up(d)
    del rest
    grad_gate, grad_up, grad_down = (
        own + to_core(theirs) for own, theirs in zip(own_grads, their_grads)
    )
    outs = {}
    for d in turns[:2]:
        outs[d] = to_chips(out[d])

    back_sum = sum(value.astype(f32) for value in backs.values())
    expert_in_grad = back_sum[:, :width]
    gate_grad = (
        back_sum[:, width : width + expert_count]
        + back_sum[:, width + expert_count : width + 2 * expert_count]
    )
    select_grad = gates * (gate_grad - jnp.sum(gates * gate_grad, axis=1, keepdims=True))
    logit_grad = select_grad.astype(bf16)
    grad_router = dot_tn(act_two, logit_grad)
    act_two_grad = expert_in_grad + dot_nt(logit_grad, router_full)
    weighted = act_two_grad * gain_two
    grad_gain_two = jnp.sum(act_two_grad * middle * inverse_two, axis=0)
    middle_grad = (
        cotangent
        + inverse_two * weighted
        - middle * inverse_two**3 * jnp.mean(weighted * middle, axis=-1, keepdims=True)
    )
    middle_low = middle_grad.astype(bf16)

    out_grad = dot_nt(middle_low, output_full).astype(bf16)
    out_grad = out_grad.reshape(tok_rows, members, head_width).transpose(1, 0, 2)
    out_grad = on_wire(out_grad.reshape(seq, head_width), plane_groups)
    middle_all = gather(after(middle_low, out_grad), plane_groups)
    for d in turns[2:]:
        outs[d] = to_chips(out[d])
    mixed = None

    def mix(d):
        nonlocal mixed
        mixed = combine(
            stacked[d], slots[d], in_turn(outs[d]), per_plane, tok_rows, planes, mixed
        )
        ran(mixed)

    ran(middle_low)
    for d in turns[:2]:
        mix(d)
    grads, gains, taken = [], [], []
    for head in range(heads):
        dq, dk, dv, gain = attention_back(
            head,
            rot,
            in_turn(out_grad),
            out_wide,
            lse,
            seg_col,
            seg_row,
            low,
            high,
            pre,
            gain_q,
            gain_k,
            cosine,
            sine,
            heads,
        )
        grads.append(jnp.concatenate([dq, dk, dv], axis=1))
        gains.append(gain)
        ran(dq)
        part = dot_tn(in_turn(act_one), grads[-1]).astype(bf16)
        taken.append(over_planes(ran(part)).astype(bf16))
        if head == 0:
            for d in turns[2:]:
                mix(d)
    grad_gains = sum(gains)
    mixture = lax.psum_scatter(
        mixed.reshape(planes * tok_rows, width),
        AXIS,
        scatter_dimension=0,
        tiled=True,
        axis_index_groups=stack_groups,
    )
    layer_out = (middle + mixture.astype(f32)).astype(bf16)

    core = me % 2
    ordered = in_order(weights).reshape(width, 3, heads, HD)
    tall = [grad.reshape(per_plane, 2, tok_rows, 3 * HD) for grad in grads]

    def for_core(which):
        total = None
        for head, grad in enumerate(tall):
            rows_in = lax.dynamic_index_in_dim(grad, which, 1, False)
            rows_in = rows_in.reshape(per_plane * tok_rows, 3 * HD)
            term = dot_nt(rows_in, ordered[:, :, head].reshape(width, 3 * HD))
            total = term if total is None else total + term
        return total

    theirs = to_core(ran(for_core(1 - core).astype(bf16)))
    output_part = dot_tn(out_heads, in_turn(middle_all)).astype(bf16)
    output_part = over_planes(ran(output_part))
    pair_sum = for_core(core) + theirs.astype(f32)
    pair_sum = after(pair_sum.astype(bf16), output_part)

    sums = (
        grad_router.reshape(devices, -1),
        grad_gain_two.reshape(devices, -1),
        grad_gains[0].reshape(devices, -1),
        grad_gains[1].reshape(devices, -1),
    )
    packed = jnp.concatenate(sums, axis=1)
    length = packed.shape[1]
    padded = -(-length // 128) * 128
    packed = on_wire(jnp.pad(packed, ((0, 0), (0, padded - length))), None)

    taken[:-1] = [on_wire(part, plane_groups) for part in taken[:-1]]
    act_one_grad = to_chips(pair_sum).reshape(per_plane, tok_rows, width)
    act_one_grad = jnp.sum(act_one_grad.astype(f32), axis=0)

    to_owner = [
        (g * members + j, j * planes + g) for g in range(planes) for j in range(members)
    ]
    grad_output = lax.ppermute(output_part, AXIS, to_owner)
    taken[-1] = on_wire(taken[-1], plane_groups)
    taken = [part.reshape(members, own_rows, 3, 1, HD) for part in taken]
    part = jnp.concatenate(taken, axis=3)
    part = part.transpose(2, 1, 0, 3, 4).reshape(3, own_rows, width).astype(f32)
    grad_query, grad_key, grad_value = part[0], part[1], part[2]

    inverse_one = lax.rsqrt(jnp.mean(tokens * tokens, axis=-1, keepdims=True) + norm_eps)
    weighted = act_one_grad * gain_one
    grad_hidden = (
        middle_grad
        + inverse_one * weighted
        - tokens * inverse_one**3 * jnp.mean(weighted * tokens, axis=-1, keepdims=True)
    )
    grad_gain_one = (
        jnp.sum(
            grad_query * query_weight.astype(f32)
            + grad_key * key_weight.astype(f32)
            + grad_value * value_weight.astype(f32),
            axis=1,
        )
        / norm_gain.astype(f32)
    )

    summed = jnp.sum(packed, axis=0)
    at, tiny = 0, []
    for piece in sums:
        tiny.append(summed[at : at + piece.shape[1]])
        at += piece.shape[1]

    return (
        layer_out,
        grad_hidden,
        grad_gain_one,
        grad_query,
        grad_key,
        grad_value,
        grad_output,
        tiny[2],
        tiny[3],
        tiny[1],
        tiny[0].reshape(own_rows, expert_count),
        grad_gate[None],
        grad_up[None],
        grad_down[None],
    )


def solution(mesh):
    row, mat, cube = P(AXIS), P(AXIS, None), P(AXIS, None, None)
    return jax.shard_map(
        body,
        mesh=mesh,
        in_specs=(mat, mat, row, mat, mat, row, mat, mat, mat, mat, row, row, row, mat)
        + (cube,) * 3,
        out_specs=(mat, mat, row, mat, mat, mat, mat, row, row, row, mat) + (cube,) * 3,
        check_vma=False,
    )
```

```python
import functools
import math

import jax
import jax.numpy as jnp
from jax import lax
from jax.experimental import pallas as pl
from jax.experimental.pallas import tpu as pltpu
from jax.sharding import PartitionSpec as P

HD = 128
TOPK = 8
SEQ_MIN = 2048
ROWS = 256
SHARE = 32

norm_eps = 1e-05
head_eps = 1e-06
rope_base = 10000.0
masked_score = -1e30
absent_slot = 4096.0

AXIS = "fsdp"
f32 = jnp.float32
bf16 = jnp.bfloat16
MIB = 1 << 20


def dot_nt(left, right):
    return lax.dot_general(left, right, (((1,), (1,)), ((), ())), preferred_element_type=f32)


def dot_tn(left, right):
    return lax.dot_general(left, right, (((0,), (0,)), ((), ())), preferred_element_type=f32)


def dot_nn(left, right):
    return lax.dot_general(left, right, (((1,), (0,)), ((), ())), preferred_element_type=f32)


def params(steps, mib):
    return pltpu.CompilerParams(
        dimension_semantics=("arbitrary",) * steps, vmem_limit_bytes=mib * MIB
    )


def estimate(flops, bytes_accessed, transcendentals):
    return pl.CostEstimate(
        flops=flops // SHARE, bytes_accessed=bytes_accessed // SHARE, transcendentals=transcendentals // SHARE
    )


def rope_tables(count):
    half_width = HD // 2
    frequency = jnp.exp(-math.log(rope_base) * 2.0 * jnp.arange(half_width, dtype=f32) / HD)
    angles = jnp.arange(count, dtype=f32)[:, None] * frequency[None, :]
    cosine, sine = jnp.cos(angles), jnp.sin(angles)
    return jnp.concatenate([cosine, cosine], axis=-1), jnp.concatenate([-sine, sine], axis=-1)


def slots_kernel(expert_count, routes_ref, order_ref, slots_ref):
    tok_rows = routes_ref.shape[0]
    pair_count = order_ref.shape[1]
    order = order_ref[...]
    shift = TOPK.bit_length() - 1
    token_of = lax.shift_right_logical(order, jnp.full_like(order, shift))
    route_of = order & (TOPK - 1)
    token_iota = lax.broadcasted_iota(jnp.int32, (tok_rows, pair_count), 0)
    token_hot = jnp.where(token_iota == token_of, 1.0, 0.0).astype(bf16)
    place = lax.broadcasted_iota(jnp.int32, (TOPK, pair_count), 1)
    chosen = lax.broadcasted_iota(jnp.int32, (TOPK, pair_count), 0) == route_of
    high = lax.shift_right_logical(place, jnp.full_like(place, 8)).astype(f32)
    low = (place & 255).astype(f32)
    digits = jnp.concatenate([jnp.where(chosen, high, 0.0), jnp.where(chosen, low, 0.0)], axis=0)
    found = dot_nt(token_hot, digits.astype(bf16))
    rank = found[:, :TOPK] * 256.0 + found[:, TOPK:]
    routes = routes_ref[...]
    lanes = -(-expert_count // 128) * 128
    expert_iota = lax.broadcasted_iota(jnp.int32, (tok_rows, lanes), 1)
    never = 1e9
    by_expert = jnp.full((tok_rows, lanes), never, f32)
    for k in range(TOPK):
        by_expert = jnp.where(expert_iota == routes[:, k : k + 1], rank[:, k : k + 1], by_expert)
    turned = by_expert.T
    for e in range(expert_count):
        mine = turned[e : e + 1, :]
        earlier = jnp.where(by_expert[:, e : e + 1] < mine, 1.0, 0.0)
        count = jnp.sum(earlier, axis=0, keepdims=True)
        slots_ref[e : e + 1, :] = jnp.where(mine < never, count, absent_slot)


def block_slots(routes, order, expert_count):
    tok_rows = routes.shape[0]
    return pl.pallas_call(
        functools.partial(slots_kernel, expert_count),
        out_shape=jax.ShapeDtypeStruct((expert_count, tok_rows), f32),
        compiler_params=pltpu.CompilerParams(vmem_limit_bytes=32 * MIB),
        name="block_slots",
    )(routes, order)


def slot_hot(slots_ref, expert, capacity):
    slot_row = slots_ref[pl.ds(expert, 1), :]
    slot_iota = lax.broadcasted_iota(jnp.int32, (capacity, slot_row.shape[1]), 0).astype(f32)
    return jnp.where(slot_iota == slot_row, 1.0, 0.0).astype(bf16)


def plane_hot(slots_ref, first, shape):
    return jnp.concatenate([slot_hot(slots_ref, first + r, shape[1]) for r in range(shape[0])])


def dispatch_kernel(at_ref, slots_ref, rows_ref, out_ref):
    hot = plane_hot(slots_ref, at_ref[0], out_ref.shape)
    out_ref[...] = dot_nn(hot, rows_ref[...]).astype(bf16).reshape(out_ref.shape)


def dispatch(at, slots, rows, per_plane, capacity):
    blocks, experts, tok_rows = slots.shape
    width = rows.shape[2]
    slot_rows = per_plane * capacity
    return pl.pallas_call(
        dispatch_kernel,
        out_shape=jax.ShapeDtypeStruct((per_plane, blocks, capacity, width), bf16),
        grid_spec=pltpu.PrefetchScalarGridSpec(
            num_scalar_prefetch=1,
            grid=(blocks,),
            in_specs=[
                pl.BlockSpec((None, experts, tok_rows), lambda i, s: (i, 0, 0)),
                pl.BlockSpec((None, tok_rows, width), lambda i, s: (s[1 + i], 0, 0)),
            ],
            out_specs=pl.BlockSpec((per_plane, None, capacity, width), lambda i, s: (0, i, 0, 0)),
        ),
        compiler_params=params(1, 40),
        cost_estimate=estimate(
            flops=2 * blocks * slot_rows * tok_rows * width,
            bytes_accessed=2 * blocks * (slot_rows + tok_rows) * width,
            transcendentals=0,
        ),
        name="dispatch",
    )(at, slots, rows)


def combine_kernel(carried, at_ref, slots_ref, rows_ref, *refs):
    out_ref = refs[carried]
    hot = plane_hot(slots_ref, at_ref[0], rows_ref.shape)
    rows = rows_ref[...].reshape(hot.shape[0], rows_ref.shape[2])
    out_ref[...] = dot_tn(hot, rows).astype(bf16)


def combine(at, slots, rows, planes, kept=None):
    blocks, experts, tok_rows = slots.shape
    per_plane, _, capacity, width = rows.shape
    slot_rows = per_plane * capacity
    carried = 0 if kept is None else 1
    return pl.pallas_call(
        functools.partial(combine_kernel, carried),
        out_shape=jax.ShapeDtypeStruct((planes, tok_rows, width), bf16),
        grid_spec=pltpu.PrefetchScalarGridSpec(
            num_scalar_prefetch=1,
            grid=(blocks,),
            in_specs=[
                pl.BlockSpec((None, experts, tok_rows), lambda i, s: (i, 0, 0)),
                pl.BlockSpec((per_plane, None, capacity, width), lambda i, s: (0, i, 0, 0)),
            ]
            + [pl.BlockSpec(memory_space=pl.ANY)] * carried,
            out_specs=pl.BlockSpec((None, tok_rows, width), lambda i, s: (s[1 + i], 0, 0)),
        ),
        input_output_aliases={3: 0} if carried else {},
        compiler_params=params(1, 40),
        cost_estimate=estimate(
            flops=2 * blocks * slot_rows * tok_rows * width,
            bytes_accessed=2 * blocks * (slot_rows + tok_rows) * width,
            transcendentals=0,
        ),
        name="combine",
    )(at, slots, rows, *(() if kept is None else (kept,)))


def qkv_kernel(heads, planes, at_ref, x_ref, gain_ref, *refs):
    w_refs = refs[:planes]
    gq_ref, gk_ref, cos_ref, sin_ref, act_ref, pre_ref, rot_ref, all_ref = refs[planes:]
    depth = w_refs[0].shape[0]

    @pl.when(pl.program_id(0) == 0)
    def _():
        for d in range(planes):
            place = pl.ds(pl.multiple_of(at_ref[d] * depth, depth), depth)
            all_ref[place, :] = w_refs[d][...]

    x = x_ref[...].astype(f32)
    inverse = lax.rsqrt(jnp.mean(x * x, axis=-1, keepdims=True) + norm_eps)
    act = (x * inverse * gain_ref[...]).astype(bf16)
    act_ref[...] = act
    y = None
    for d in range(planes):
        columns = pl.ds(pl.multiple_of(at_ref[d] * depth, depth), depth)
        term = dot_nn(act_ref[:, columns], w_refs[d][...])
        y = term if y is None else y + term
    cosine, sine = cos_ref[...], sin_ref[...]
    for part, gain in enumerate((gq_ref[...], gk_ref[...])):
        for h in range(heads):
            at = (part * heads + h) * HD
            u = y[:, at : at + HD]
            pre_ref[:, at : at + HD] = u
            n = u * lax.rsqrt(jnp.mean(u * u, axis=-1, keepdims=True) + head_eps) * gain
            rot_ref[:, at : at + HD] = (n * cosine + pltpu.roll(n, HD // 2, 1) * sine).astype(bf16)
    at = 2 * heads * HD
    rot_ref[:, at:] = y[:, at:].astype(bf16)


def qkv_project(places, rows, gain, weights, gain_q, gain_k, cosine, sine, heads):
    count, width = rows.shape
    planes = len(weights)
    depth, out_width = weights[0].shape
    pre_width = 2 * heads * HD
    whole = lambda i, s: (0, 0)
    block = lambda i, s: (i, 0)
    return pl.pallas_call(
        functools.partial(qkv_kernel, heads, planes),
        out_shape=(
            jax.ShapeDtypeStruct((count, width), bf16),
            jax.ShapeDtypeStruct((count, pre_width), f32),
            jax.ShapeDtypeStruct((count, out_width), bf16),
            jax.ShapeDtypeStruct((width, out_width), bf16),
        ),
        grid_spec=pltpu.PrefetchScalarGridSpec(
            num_scalar_prefetch=1,
            grid=(count // ROWS,),
            in_specs=[
                pl.BlockSpec((ROWS, width), block),
                pl.BlockSpec((1, width), whole),
            ]
            + [pl.BlockSpec((depth, out_width), whole)] * planes
            + [
                pl.BlockSpec((1, HD), whole),
                pl.BlockSpec((1, HD), whole),
                pl.BlockSpec((ROWS, HD), block),
                pl.BlockSpec((ROWS, HD), block),
            ],
            out_specs=(
                pl.BlockSpec((ROWS, width), block),
                pl.BlockSpec((ROWS, pre_width), block),
                pl.BlockSpec((ROWS, out_width), block),
                pl.BlockSpec((width, out_width), whole),
            ),
        ),
        compiler_params=params(1, 56),
        cost_estimate=estimate(
            flops=2 * count * width * out_width,
            bytes_accessed=4 * count * width + 2 * width * out_width + 6 * count * out_width,
            transcendentals=0,
        ),
        name="qkv_project",
    )(places, rows, gain, *weights, gain_q, gain_k, cosine, sine)


def attn_kernel(
    scale, low_ref, high_ref, q_ref, k_ref, v_ref, sq_ref, sk_ref, o_ref, ol_ref, lse_ref, s_scr
):
    block = pl.program_id(1)
    low, high = low_ref[block], high_ref[block]
    q = q_ref[...]
    seg_q = sq_ref[...]
    half = ROWS // 2

    def scores(kb, top):
        at = pl.ds(pl.multiple_of(kb * ROWS, ROWS), ROWS)
        s = dot_nt(q, k_ref[at, :]) * scale
        s = jnp.where(seg_q == sk_ref[:, at], s, masked_score)
        s_scr[:, at] = s
        return jnp.maximum(top, jnp.maximum(s[:, :half], s[:, half:]))

    top = lax.fori_loop(low, high, scores, jnp.full((ROWS, half), masked_score, f32))
    top = jnp.max(top, axis=-1, keepdims=True)

    def weigh(kb, carry):
        total, acc = carry
        at = pl.ds(pl.multiple_of(kb * ROWS, ROWS), ROWS)
        p = jnp.exp(s_scr[:, at] - top)
        acc = acc + dot_nn(p.astype(bf16), v_ref[at, :])
        return total + (p[:, :half] + p[:, half:]), acc

    total, acc = lax.fori_loop(
        low, high, weigh, (jnp.zeros((ROWS, half), f32), jnp.zeros((ROWS, HD), f32))
    )
    total = jnp.sum(total, axis=-1, keepdims=True)
    out = acc / total
    o_ref[...] = out
    ol_ref[...] = out.astype(bf16)
    lse = jnp.broadcast_to(top + jnp.log(total), (ROWS, HD)).T
    lse_ref[0] = lse[0:1, :]


def attention(rot, seg_col, seg_row, low, high, heads):
    count = rot.shape[0]
    blocks = count // ROWS
    scale = HD ** (-0.5)
    return pl.pallas_call(
        functools.partial(attn_kernel, scale),
        out_shape=(
            jax.ShapeDtypeStruct((count, heads * HD), f32),
            jax.ShapeDtypeStruct((count, heads * HD), bf16),
            jax.ShapeDtypeStruct((heads * blocks, 1, ROWS), f32),
        ),
        grid_spec=pltpu.PrefetchScalarGridSpec(
            num_scalar_prefetch=2,
            grid=(heads, blocks),
            in_specs=[
                pl.BlockSpec((ROWS, HD), lambda h, i, *s: (i, h)),
                pl.BlockSpec((count, HD), lambda h, i, *s: (0, heads + h)),
                pl.BlockSpec((count, HD), lambda h, i, *s: (0, 2 * heads + h)),
                pl.BlockSpec((ROWS, 1), lambda h, i, *s: (i, 0)),
                pl.BlockSpec((1, count), lambda h, i, *s: (0, 0)),
            ],
            out_specs=(
                pl.BlockSpec((ROWS, HD), lambda h, i, *s: (i, h)),
                pl.BlockSpec((ROWS, HD), lambda h, i, *s: (i, h)),
                pl.BlockSpec((1, 1, ROWS), lambda h, i, *s: (h * blocks + i, 0, 0)),
            ),
            scratch_shapes=[pltpu.VMEM((ROWS, count), f32)],
        ),
        compiler_params=params(2, 32),
        cost_estimate=estimate(
            flops=2 * heads * count * count * HD,
            bytes_accessed=12 * heads * count * HD,
            transcendentals=heads * count * count // 2,
        ),
        name="attention",
    )(low, high, rot, rot, rot, seg_col, seg_row)


def head_back(grad, pre, gain, cosine, sine):
    n = grad * cosine - pltpu.roll(grad, HD // 2, 1) * sine
    inverse = lax.rsqrt(jnp.mean(pre * pre, axis=-1, keepdims=True) + head_eps)
    w = n * gain
    back = inverse * w - pre * inverse**3 * jnp.mean(w * pre, axis=-1, keepdims=True)
    return back, jnp.sum(n * pre * inverse, axis=0, keepdims=True)


def attn_back_kernel(
    scale,
    low_ref,
    high_ref,
    q_ref,
    k_ref,
    v_ref,
    do_ref,
    o_ref,
    lse_ref,
    sq_ref,
    sk_ref,
    qpre_ref,
    kpre_ref,
    gq_ref,
    gk_ref,
    cosq_ref,
    sinq_ref,
    cosk_ref,
    sink_ref,
    dq_ref,
    dk_ref,
    dv_ref,
    gain_ref,
    dk_scr,
    dv_scr,
):
    head, block = pl.program_id(0), pl.program_id(1)
    low, high = low_ref[block], high_ref[block]

    @pl.when(block == 0)
    def _():
        dk_scr[...] = jnp.zeros_like(dk_scr)
        dv_scr[...] = jnp.zeros_like(dv_scr)

    @pl.when((block == 0) & (head == 0))
    def _():
        gain_ref[...] = jnp.zeros_like(gain_ref)

    q, do = q_ref[...], do_ref[...]
    row_dot = jnp.sum((do.astype(f32) * o_ref[...]).T, axis=0, keepdims=True)
    lse = lse_ref[0]
    seg_q = sq_ref[...]

    def tile(kb, dq):
        at = pl.ds(pl.multiple_of(kb * ROWS, ROWS), ROWS)
        k, v = k_ref[at, :], v_ref[at, :]
        s = dot_nt(k, q) * scale
        p = jnp.where(sk_ref[at, :] == seg_q, jnp.exp(s - lse), 0.0)
        dp = dot_nt(v, do)
        ds = (p * (dp - row_dot)).astype(bf16)
        dv_scr[at, :] += dot_nn(p.astype(bf16), do)
        dk_scr[at, :] += dot_nn(ds, q)
        return dq + dot_tn(ds, k)

    dq = lax.fori_loop(low, high, tile, jnp.zeros((ROWS, HD), f32))
    back, gain_q = head_back(dq * scale, qpre_ref[...], gq_ref[...], cosq_ref[...], sinq_ref[...])
    dq_ref[...] = back.astype(bf16)
    gain_ref[0:1, :] += gain_q

    @pl.when(block == pl.num_programs(1) - 1)
    def _():
        @pl.loop(0, dk_scr.shape[0] // ROWS)
        def _(i):
            at = pl.ds(pl.multiple_of(i * ROWS, ROWS), ROWS)
            back, gain_k = head_back(
                dk_scr[at, :] * scale, kpre_ref[at, :], gk_ref[...], cosk_ref[at, :], sink_ref[at, :]
            )
            dk_ref[at, :] = back.astype(bf16)
            dv_ref[at, :] = dv_scr[at, :].astype(bf16)
            gain_ref[1:2, :] += gain_k


def attention_back(
    rot, grad, out, lse, seg_col, seg_row, low, high, pre, gain_q, gain_k, cosine, sine, heads
):
    count = rot.shape[0]
    blocks = count // ROWS
    scale = HD ** (-0.5)
    mine = lambda h, i, *s: (i, h)
    whole = lambda h, i, *s: (0, 0)
    return pl.pallas_call(
        functools.partial(attn_back_kernel, scale),
        out_shape=(
            jax.ShapeDtypeStruct((count, heads * HD), bf16),
            jax.ShapeDtypeStruct((count, heads * HD), bf16),
            jax.ShapeDtypeStruct((count, heads * HD), bf16),
            jax.ShapeDtypeStruct((8, HD), f32),
        ),
        grid_spec=pltpu.PrefetchScalarGridSpec(
            num_scalar_prefetch=2,
            grid=(heads, blocks),
            in_specs=[
                pl.BlockSpec((ROWS, HD), mine),
                pl.BlockSpec((count, HD), lambda h, i, *s: (0, heads + h)),
                pl.BlockSpec((count, HD), lambda h, i, *s: (0, 2 * heads + h)),
                pl.BlockSpec((ROWS, HD), mine),
                pl.BlockSpec((ROWS, HD), mine),
                pl.BlockSpec((1, 1, ROWS), lambda h, i, *s: (h * blocks + i, 0, 0)),
                pl.BlockSpec((1, ROWS), lambda h, i, *s: (0, i)),
                pl.BlockSpec((count, 1), whole),
                pl.BlockSpec((ROWS, HD), mine),
                pl.BlockSpec((count, HD), lambda h, i, *s: (0, heads + h)),
                pl.BlockSpec((1, HD), whole),
                pl.BlockSpec((1, HD), whole),
                pl.BlockSpec((ROWS, HD), lambda h, i, *s: (i, 0)),
                pl.BlockSpec((ROWS, HD), lambda h, i, *s: (i, 0)),
                pl.BlockSpec((count, HD), whole),
                pl.BlockSpec((count, HD), whole),
            ],
            out_specs=(
                pl.BlockSpec((ROWS, HD), mine),
                pl.BlockSpec((count, HD), lambda h, i, *s: (0, h)),
                pl.BlockSpec((count, HD), lambda h, i, *s: (0, h)),
                pl.BlockSpec((8, HD), whole),
            ),
            scratch_shapes=[pltpu.VMEM((count, HD), f32), pltpu.VMEM((count, HD), f32)],
        ),
        compiler_params=params(2, 48),
        cost_estimate=estimate(
            flops=5 * heads * count * count * HD,
            bytes_accessed=30 * heads * count * HD,
            transcendentals=heads * count * count // 2,
        ),
        name="attention_back",
    )(
        low,
        high,
        rot,
        rot,
        rot,
        grad,
        out,
        lse,
        seg_row,
        seg_col,
        pre,
        pre,
        gain_q,
        gain_k,
        cosine,
        sine,
        cosine,
        sine,
    )


def expert_kernel(base, count, carried, mine_ref, x_ref, *refs):
    near = 1 if base == 0 else 0
    c_refs, refs = refs[: near + 1], refs[near + 1 :]
    wg_ref, wu_ref, wd_ref = refs[:3]
    refs = refs[3 + carried :]
    back_ref, out_ref, xs_ref, c_ref, hid_ref, gp_ref, up_ref = refs[:7]
    out_acc, back_acc, gate_scr, dot_scr = refs[7:]
    step = pl.program_id(1)
    per_plane, capacity, width = c_ref.shape
    rows = per_plane * capacity
    extra = x_ref.shape[2] - width
    lane = lax.broadcasted_iota(jnp.int32, (rows, extra), 1)
    high, low = lane == mine_ref[0], lane == mine_ref[0] + count

    @pl.when(step == 0)
    def _():
        xs_ref[...] = x_ref[:, :, :width]
        if near:

            @pl.when(pl.program_id(0) == 0)
            def _():
                c_ref[...] = c_refs[0][...]

            @pl.when(pl.program_id(0) > 0)
            def _():
                c_ref[...] = c_refs[1][...]

        else:
            c_ref[...] = c_refs[0][...]
        gates = x_ref[:, :, width:].reshape(rows, extra).astype(f32)
        gate_scr[...] = jnp.sum(jnp.where(high | low, gates, 0.0), axis=-1, keepdims=True)
        out_acc[...] = jnp.zeros_like(out_acc)
        back_acc[...] = jnp.zeros_like(back_acc)
        dot_scr[...] = jnp.zeros_like(dot_scr)

    x = x_ref[:, :, :width].reshape(rows, width)
    c = c_ref[...].reshape(rows, width)
    gate = gate_scr[...]
    wg, wu, wd = wg_ref[...], wu_ref[...], wd_ref[...]
    gate_pre, up_pre = dot_nn(x, wg), dot_nn(x, wu)
    sig = jax.nn.sigmoid(gate_pre)
    hidden = (gate_pre * sig * up_pre).astype(bf16)
    out_acc[...] += dot_nn(hidden, wd)
    plain = dot_nt(c, wd)
    wide = hidden.astype(f32)
    dot_scr[...] += jnp.sum(wide * plain, axis=-1, keepdims=True)
    hid_ref[...] = (wide * gate).astype(bf16).reshape(hid_ref.shape)
    hidden_grad = plain * gate
    gate_grad = (hidden_grad * up_pre * sig * (1.0 + gate_pre * (1.0 - sig))).astype(bf16)
    up_grad = (hidden_grad * gate_pre * sig).astype(bf16)
    gp_ref[...] = gate_grad.reshape(gp_ref.shape)
    up_ref[...] = up_grad.reshape(up_ref.shape)
    back_acc[...] += dot_nt(gate_grad, wg) + dot_nt(up_grad, wu)

    @pl.when(step == pl.num_programs(1) - 1)
    def _():
        dots = dot_scr[...]
        coarse = dots.astype(bf16).astype(f32)
        lanes = jnp.where(high, coarse, jnp.where(low, dots - coarse, 0.0)).astype(bf16)
        back_ref[:, :, :width] = back_acc[...].astype(bf16).reshape(c_ref.shape)
        back_ref[:, :, width:] = lanes.reshape(per_plane, capacity, extra)
        out_ref[...] = (out_acc[...] * gate).astype(bf16).reshape(out_ref.shape)


def experts(mine, x, near, far, wg, wu, wd, base, planes, count, kept):
    per_plane, blocks, capacity, wide = x.shape
    width = near.shape[3]
    halves, _, hidden = wg.shape
    rows = per_plane * capacity
    saved = jax.ShapeDtypeStruct((per_plane, planes, capacity, width), bf16)
    thin = jax.ShapeDtypeStruct((per_plane, planes, capacity, halves * hidden), bf16)
    moved = pl.BlockSpec((per_plane, None, capacity, wide), lambda i, f, s: (0, i, 0, 0))
    saved_spec = pl.BlockSpec((per_plane, None, capacity, width), lambda i, f, s: (0, base + i, 0, 0))
    thin_spec = pl.BlockSpec((per_plane, None, capacity, hidden), lambda i, f, s: (0, base + i, 0, f))
    carried = 0 if kept is None else len(kept)
    cots = (near, far) if base == 0 else (far,)
    cot_specs = [
        pl.BlockSpec(
            (per_plane, None, capacity, width), lambda i, f, s: (0, jnp.maximum(base + i - 1, 0), 0, 0)
        )
    ]
    if base == 0:
        cot_specs = [pl.BlockSpec((per_plane, None, capacity, width), lambda i, f, s: (0, 0, 0, 0))] + cot_specs
    result = pl.pallas_call(
        functools.partial(expert_kernel, base, count, carried),
        out_shape=(jax.ShapeDtypeStruct(x.shape, bf16), saved, saved, saved, thin, thin, thin),
        grid_spec=pltpu.PrefetchScalarGridSpec(
            num_scalar_prefetch=1,
            grid=(blocks, halves),
            in_specs=[
                moved,
                *cot_specs,
                pl.BlockSpec((None, width, hidden), lambda i, f, s: (f, 0, 0)),
                pl.BlockSpec((None, width, hidden), lambda i, f, s: (f, 0, 0)),
                pl.BlockSpec((None, hidden, width), lambda i, f, s: (f, 0, 0)),
            ]
            + [pl.BlockSpec(memory_space=pl.ANY)] * carried,
            out_specs=(moved, saved_spec, saved_spec, saved_spec, thin_spec, thin_spec, thin_spec),
            scratch_shapes=[
                pltpu.VMEM((rows, width), f32),
                pltpu.VMEM((rows, width), f32),
                pltpu.VMEM((rows, 1), f32),
                pltpu.VMEM((rows, 1), f32),
            ],
        ),
        input_output_aliases={5 + len(cots) + i: 1 + i for i in range(carried)},
        compiler_params=params(2, 60),
        cost_estimate=estimate(
            flops=12 * blocks * rows * width * hidden * halves,
            bytes_accessed=10 * blocks * rows * width + 6 * blocks * width * hidden * halves,
            transcendentals=blocks * rows * hidden * halves,
        ),
        name="experts",
    )(mine, x, *cots, wg, wu, wd, *(kept or ()))
    return result[0], result[1:]


def after(value, *others):
    return lax.optimization_barrier((value,) + others)[0]


def body(
    hidden_in,
    out_cotangent,
    segment_number,
    expert_routes,
    pair_order,
    norm_gain,
    query_weight,
    key_weight,
    value_weight,
    output_weight,
    query_gain,
    key_gain,
    ffn_norm_gain,
    router_weight,
    expert_gate,
    expert_up,
    expert_down,
):
    tok_rows, width = hidden_in.shape
    devices = lax.axis_size(AXIS)
    members = max(1, SEQ_MIN // tok_rows)
    planes = devices // members
    per_plane = members // 2
    expert_count = devices // 2
    capacity = tok_rows * TOPK // expert_count
    heads = width // HD // members
    head_width = heads * HD
    own_rows = norm_gain.shape[0]
    seq = members * tok_rows
    me = lax.axis_index(AXIS)
    plane, member = me // members, me % members
    mine = (me // 2).astype(jnp.int32).reshape(1)
    first = (plane * per_plane).astype(jnp.int32)
    places = (plane ^ jnp.arange(planes, dtype=jnp.int32)).astype(jnp.int32)
    counted = jnp.concatenate([first[None], jnp.arange(planes, dtype=jnp.int32)])
    halfway = -(-planes // 2)
    chunks = [part for part in (range(halfway), range(halfway, planes)) if len(part)]

    def placed(part):
        return jnp.concatenate([first[None], places[part.start : part.stop]])

    plane_groups = [[g * members + j for j in range(members)] for g in range(planes)]
    stack_groups = [[g * members + j for g in range(planes)] for j in range(members)]
    core_groups = [
        [g * members + 2 * c + h for c in range(per_plane)] for g in range(planes) for h in (0, 1)
    ]

    def exchange(value, groups=None):
        return lax.all_to_all(
            value, AXIS, split_axis=0, concat_axis=0, tiled=True, axis_index_groups=groups
        )

    def gather(value, groups=None):
        return lax.all_gather(value, AXIS, axis=0, tiled=True, axis_index_groups=groups)

    def flip(value, bits):
        if bits == 0:
            return value
        return lax.ppermute(value, AXIS, [(i, i ^ bits) for i in range(devices)])

    def to_core(value):
        return flip(value, 1)

    def to_plane(value, d):
        return flip(value, members * d)

    def over_planes(value):
        value = value.reshape((planes, -1) + value.shape[1:])
        return sum(
            to_plane(lax.dynamic_index_in_dim(value, places[d], 0, False), d).astype(f32)
            for d in range(planes)
        )

    def over_stack(value):
        return lax.psum_scatter(
            value.reshape(planes * tok_rows, -1),
            AXIS,
            scatter_dimension=0,
            tiled=True,
            axis_index_groups=stack_groups,
        )

    wire, core_op = [], []

    def on_wire(value, groups):
        came = exchange(after(value, *wire[-1:]), groups)
        wire.append(came)
        return came

    def to_chips(value):
        return on_wire(value, core_groups)

    def in_turn(value):
        return after(value, *core_op[-1:])

    def ran(value):
        core_op.append(value)
        return value

    columns = jnp.concatenate(
        [w.reshape(own_rows, members, head_width) for w in (query_weight, key_weight, value_weight)],
        axis=2,
    )
    columns = on_wire(
        columns.transpose(1, 0, 2).reshape(members * own_rows, 3 * head_width), plane_groups
    )
    weights = [to_plane(columns, d) for d in range(planes)]
    rows_all = gather(hidden_in, plane_groups)
    output_full = gather(output_weight)

    pieces = (
        router_weight.reshape(-1),
        norm_gain,
        ffn_norm_gain,
        query_gain,
        key_gain,
        segment_number.astype(bf16),
    )
    packed = jnp.concatenate(pieces)
    length = packed.shape[0]
    padded = -(-length // 128) * 128
    packed = jnp.pad(packed, (0, padded - length))
    packed = on_wire(jnp.broadcast_to(packed[None], (devices, padded)), None)
    small = []
    at = 0
    for piece in pieces:
        small.append(packed[:, at : at + piece.shape[0]])
        at += piece.shape[0]
    router_full = small[0].reshape(width, expert_count)
    gain_one = small[1].reshape(1, width).astype(f32)
    gain_two = small[2].reshape(1, width).astype(f32)
    gain_q = small[3].reshape(1, HD).astype(f32)
    gain_k = small[4].reshape(1, HD).astype(f32)
    segments = lax.dynamic_slice_in_dim(small[5], plane * members, members, 0).astype(f32)
    seg_row, seg_col = segments.reshape(1, seq), segments.reshape(seq, 1)
    seg_blocks = segments.reshape(seq // ROWS, ROWS)
    seg_first, seg_last = seg_blocks[:, 0], seg_blocks[:, -1]
    low = jnp.sum((seg_last[None, :] < seg_first[:, None]).astype(jnp.int32), axis=1)
    high = jnp.sum((seg_first[None, :] <= seg_last[:, None]).astype(jnp.int32), axis=1)

    slots = block_slots(expert_routes, pair_order, expert_count)
    cot_own = dispatch(counted, slots[None], out_cotangent[None], per_plane, capacity)
    cot_parts = [to_chips(cot_own)]
    cot_rows = [out_cotangent]
    for d in range(1, planes):
        lowest = d & -d
        start = after(out_cotangent, *weights) if d == lowest else cot_rows[d ^ lowest]
        cot_rows.append(to_plane(start, lowest))
    slots = jnp.stack([to_plane(slots, d) for d in range(planes)])

    halves = lambda w: jnp.concatenate([w, to_core(w)], axis=0)
    wg, wu, wd = halves(expert_gate), halves(expert_up), halves(expert_down)

    cosine, sine = rope_tables(seq)
    act_one, pre, rot, ordered = qkv_project(
        places, after(rows_all, *cot_parts), gain_one, weights, gain_q, gain_k, cosine, sine, heads
    )
    out_wide, out_heads, lse = attention(rot, seg_col, seg_row, low, high, heads)
    early = [cot_rows[d] for d in range(1, planes) if d & (d - 1) == 0]
    out_low = on_wire(after(out_heads, *early), plane_groups)
    out_low = out_low.reshape(members, tok_rows, head_width).transpose(1, 0, 2)
    out_low = after(out_low.reshape(tok_rows, width), wg, wu, wd)
    tokens = hidden_in.astype(f32)
    cotangent = out_cotangent.astype(f32)
    middle = tokens + dot_nn(out_low, output_full)
    inverse_two = lax.rsqrt(jnp.mean(middle * middle, axis=-1, keepdims=True) + norm_eps)
    act_two = (middle * inverse_two * gain_two).astype(bf16)

    logits = dot_nn(act_two, router_full)
    expert_ids = jnp.arange(expert_count, dtype=jnp.int32)
    routed = jnp.any(expert_routes[:, :, None] == expert_ids[None, None, :], axis=1)
    logits = jnp.where(routed, logits, masked_score)
    gates = jnp.where(routed, jnp.exp(logits - jnp.max(logits, axis=1, keepdims=True)), 0.0)
    gates = gates / jnp.sum(gates, axis=1, keepdims=True)
    coarse = lax.reduce_precision(gates, 8, 7)
    extra = -(-2 * expert_count // 128) * 128
    act_wide = jnp.concatenate(
        [
            act_two,
            coarse.astype(bf16),
            (gates - coarse).astype(bf16),
            jnp.zeros((tok_rows, extra - 2 * expert_count), bf16),
        ],
        axis=1,
    )

    act_all = gather(act_wide, stack_groups).reshape(planes, tok_rows, -1)
    if planes > 1:
        far = jnp.stack([after(rows, act_wide) for rows in cot_rows[1:]])
        sent = dispatch(counted[:planes], slots[1:], far, per_plane, capacity)
        cot_parts.append(to_chips(ran(sent)))

    act = []
    for part in chunks:
        own_slots = slots[part.start : part.stop]
        sent = dispatch(placed(part), own_slots, in_turn(act_all), per_plane, capacity)
        act.append(to_chips(ran(sent)))
    kept, back = None, []
    for part, rows in zip(chunks, act):
        sent, kept = experts(
            mine,
            in_turn(rows),
            cot_parts[0],
            cot_parts[-1],
            wg,
            wu,
            wd,
            part.start,
            planes,
            expert_count,
            kept,
        )
        back.append(to_chips(ran(sent)))
    out_all, x_all, c_all, hid_all, gp_all, up_all = kept

    hidden = expert_gate.shape[2]
    flat = lambda value: value.reshape(-1, value.shape[3])
    pairs = (
        (flat(x_all), flat(gp_all), 1),
        (flat(x_all), flat(up_all), 1),
        (flat(hid_all), flat(c_all), 0),
    )

    def half(pair, which):
        left, right, split = pair
        cut = slice(which * hidden, (which + 1) * hidden)
        return dot_tn(left, right[:, cut]) if split else dot_tn(left[:, cut], right)

    theirs = [to_core(ran(half(pair, 1))) for pair in pairs]
    returned = None
    for part, rows in zip(chunks, back):
        own_slots = slots[part.start : part.stop]
        returned = ran(combine(placed(part), own_slots, in_turn(rows), planes, returned))
    back_sum = over_stack(returned)
    grad_gate, grad_up, grad_down = (
        half(pair, 0) + other for pair, other in zip(pairs, theirs)
    )
    outs = to_chips(out_all)

    back_sum = after(back_sum, grad_gate, grad_up, grad_down).astype(f32)
    expert_in_grad = back_sum[:, :width]
    gate_grad = (
        back_sum[:, width : width + expert_count]
        + back_sum[:, width + expert_count : width + 2 * expert_count]
    )
    select_grad = gates * (gate_grad - jnp.sum(gates * gate_grad, axis=1, keepdims=True))
    logit_grad = select_grad.astype(bf16)
    grad_router = dot_tn(act_two, logit_grad)
    act_two_grad = expert_in_grad + dot_nt(logit_grad, router_full)
    weighted = act_two_grad * gain_two
    grad_gain_two = jnp.sum(act_two_grad * middle * inverse_two, axis=0)
    middle_grad = (
        cotangent
        + inverse_two * weighted
        - middle * inverse_two**3 * jnp.mean(weighted * middle, axis=-1, keepdims=True)
    )
    middle_low = middle_grad.astype(bf16)

    out_grad = dot_nt(middle_low, output_full).astype(bf16)
    out_grad = out_grad.reshape(tok_rows, members, head_width).transpose(1, 0, 2)
    out_grad = on_wire(out_grad.reshape(seq, head_width), plane_groups)
    mixed = combine(placed(range(planes)), slots, after(outs, middle_low), planes)
    mixture = over_stack(mixed)
    layer_out = (middle + mixture.astype(f32)).astype(bf16)
    middle_all = gather(after(middle_low, mixed), plane_groups)
    dq, dk, dv, grad_gains = attention_back(
        rot,
        after(out_grad, mixed),
        out_wide,
        lse,
        seg_col,
        seg_row,
        low,
        high,
        pre,
        gain_q,
        gain_k,
        cosine,
        sine,
        heads,
    )
    dqkv = jnp.concatenate([dq, dk, dv], axis=1)

    sums = (
        grad_router.reshape(devices, -1),
        grad_gain_two.reshape(devices, -1),
        grad_gains[0].reshape(devices, -1),
        grad_gains[1].reshape(devices, -1),
    )
    packed = jnp.concatenate(sums, axis=1)
    length = packed.shape[1]
    padded = -(-length // 128) * 128
    packed = on_wire(jnp.pad(packed, ((0, 0), (0, padded - length))), None)

    part = dot_tn(act_one, dqkv).astype(bf16)
    core = me % 2
    tall = after(dqkv, part).reshape(per_plane, 2, tok_rows, 3 * head_width)

    def for_core(which):
        rows_in = lax.dynamic_index_in_dim(tall, which, 1, False)
        return dot_nt(rows_in.reshape(per_plane * tok_rows, 3 * head_width), ordered)

    taken = over_planes(part).astype(bf16)
    given = to_core(for_core(1 - core).astype(bf16))
    act_one_grad = (for_core(core) + given.astype(f32)).astype(bf16)
    act_one_grad, packed = lax.optimization_barrier((act_one_grad, packed))
    act_one_grad = exchange(act_one_grad, core_groups)

    output_part = over_planes(dot_tn(out_heads, middle_all).astype(bf16))
    to_owner = [
        (g * members + j, j * planes + g) for g in range(planes) for j in range(members)
    ]
    grad_output = lax.ppermute(output_part, AXIS, to_owner)
    taken, act_one_grad, grad_output = lax.optimization_barrier((taken, act_one_grad, grad_output))
    part = exchange(taken, plane_groups).reshape(members, own_rows, 3, head_width)
    part = part.transpose(2, 1, 0, 3).reshape(3, own_rows, width).astype(f32)
    grad_query, grad_key, grad_value = part[0], part[1], part[2]
    act_one_grad = act_one_grad.reshape(per_plane, tok_rows, width)
    act_one_grad = jnp.sum(act_one_grad.astype(f32), axis=0)

    inverse_one = lax.rsqrt(jnp.mean(tokens * tokens, axis=-1, keepdims=True) + norm_eps)
    weighted = act_one_grad * gain_one
    grad_hidden = (
        middle_grad
        + inverse_one * weighted
        - tokens * inverse_one**3 * jnp.mean(weighted * tokens, axis=-1, keepdims=True)
    )
    grad_gain_one = (
        jnp.sum(
            grad_query * query_weight.astype(f32)
            + grad_key * key_weight.astype(f32)
            + grad_value * value_weight.astype(f32),
            axis=1,
        )
        / norm_gain.astype(f32)
    )

    summed = jnp.sum(packed, axis=0)
    at, tiny = 0, []
    for piece in sums:
        tiny.append(summed[at : at + piece.shape[1]])
        at += piece.shape[1]

    return (
        layer_out,
        grad_hidden,
        grad_gain_one,
        grad_query,
        grad_key,
        grad_value,
        grad_output,
        tiny[2],
        tiny[3],
        tiny[1],
        tiny[0].reshape(own_rows, expert_count),
        grad_gate[None],
        grad_up[None],
        grad_down[None],
    )


def solution(mesh):
    row, mat, cube = P(AXIS), P(AXIS, None), P(AXIS, None, None)
    return jax.shard_map(
        body,
        mesh=mesh,
        in_specs=(mat, mat, row, mat, mat, row, mat, mat, mat, mat, row, row, row, mat)
        + (cube,) * 3,
        out_specs=(mat, mat, row, mat, mat, mat, mat, row, row, row, mat) + (cube,) * 3,
        check_vma=False,
    )
```

```python
import functools
import math

import jax
import jax.numpy as jnp
from jax import lax
from jax.experimental import pallas as pl
from jax.experimental.pallas import tpu as pltpu
from jax.sharding import PartitionSpec as P

HD = 128
TOPK = 8
SEQ_MIN = 2048
ROWS = 256
SHARE = 32

norm_eps = 1e-05
head_eps = 1e-06
rope_base = 10000.0
masked_score = -1e30
absent_slot = 4096.0

AXIS = "fsdp"
f32 = jnp.float32
bf16 = jnp.bfloat16
MIB = 1 << 20


def dot_nt(left, right):
    return lax.dot_general(left, right, (((1,), (1,)), ((), ())), preferred_element_type=f32)


def dot_tn(left, right):
    return lax.dot_general(left, right, (((0,), (0,)), ((), ())), preferred_element_type=f32)


def dot_nn(left, right):
    return lax.dot_general(left, right, (((1,), (0,)), ((), ())), preferred_element_type=f32)


def params(steps, mib):
    return pltpu.CompilerParams(
        dimension_semantics=("arbitrary",) * steps, vmem_limit_bytes=mib * MIB
    )


def estimate(flops, bytes_accessed, transcendentals):
    return pl.CostEstimate(
        flops=flops // SHARE, bytes_accessed=bytes_accessed // SHARE, transcendentals=transcendentals // SHARE
    )


def rope_tables(count):
    half_width = HD // 2
    frequency = jnp.exp(-math.log(rope_base) * 2.0 * jnp.arange(half_width, dtype=f32) / HD)
    angles = jnp.arange(count, dtype=f32)[:, None] * frequency[None, :]
    cosine, sine = jnp.cos(angles), jnp.sin(angles)
    return jnp.concatenate([cosine, cosine], axis=-1), jnp.concatenate([-sine, sine], axis=-1)


def slots_kernel(expert_count, routes_ref, order_ref, slots_ref):
    tok_rows = routes_ref.shape[0]
    pair_count = order_ref.shape[1]
    order = order_ref[...]
    shift = TOPK.bit_length() - 1
    token_of = lax.shift_right_logical(order, jnp.full_like(order, shift))
    route_of = order & (TOPK - 1)
    token_iota = lax.broadcasted_iota(jnp.int32, (tok_rows, pair_count), 0)
    token_hot = jnp.where(token_iota == token_of, 1.0, 0.0).astype(bf16)
    place = lax.broadcasted_iota(jnp.int32, (TOPK, pair_count), 1)
    chosen = lax.broadcasted_iota(jnp.int32, (TOPK, pair_count), 0) == route_of
    high = lax.shift_right_logical(place, jnp.full_like(place, 8)).astype(f32)
    low = (place & 255).astype(f32)
    digits = jnp.concatenate([jnp.where(chosen, high, 0.0), jnp.where(chosen, low, 0.0)], axis=0)
    found = dot_nt(token_hot, digits.astype(bf16))
    rank = found[:, :TOPK] * 256.0 + found[:, TOPK:]
    routes = routes_ref[...]
    lanes = -(-expert_count // 128) * 128
    expert_iota = lax.broadcasted_iota(jnp.int32, (tok_rows, lanes), 1)
    never = 1e9
    by_expert = jnp.full((tok_rows, lanes), never, f32)
    for k in range(TOPK):
        by_expert = jnp.where(expert_iota == routes[:, k : k + 1], rank[:, k : k + 1], by_expert)
    turned = by_expert.T
    for e in range(expert_count):
        mine = turned[e : e + 1, :]
        earlier = jnp.where(by_expert[:, e : e + 1] < mine, 1.0, 0.0)
        count = jnp.sum(earlier, axis=0, keepdims=True)
        slots_ref[e : e + 1, :] = jnp.where(mine < never, count, absent_slot)


def block_slots(routes, order, expert_count):
    tok_rows = routes.shape[0]
    return pl.pallas_call(
        functools.partial(slots_kernel, expert_count),
        out_shape=jax.ShapeDtypeStruct((expert_count, tok_rows), f32),
        compiler_params=pltpu.CompilerParams(vmem_limit_bytes=32 * MIB),
        name="block_slots",
    )(routes, order)


def slot_hot(slots_ref, expert, capacity):
    slot_row = slots_ref[pl.ds(expert, 1), :]
    slot_iota = lax.broadcasted_iota(jnp.int32, (capacity, slot_row.shape[1]), 0).astype(f32)
    return jnp.where(slot_iota == slot_row, 1.0, 0.0).astype(bf16)


def plane_hot(slots_ref, first, shape):
    return jnp.concatenate([slot_hot(slots_ref, first + r, shape[1]) for r in range(shape[0])])


def dispatch_kernel(at_ref, slots_ref, rows_ref, out_ref):
    hot = plane_hot(slots_ref, at_ref[0], out_ref.shape)
    out_ref[...] = dot_nn(hot, rows_ref[...]).astype(bf16).reshape(out_ref.shape)


def dispatch(at, slots, rows, per_plane, capacity):
    blocks, experts, tok_rows = slots.shape
    width = rows.shape[2]
    slot_rows = per_plane * capacity
    return pl.pallas_call(
        dispatch_kernel,
        out_shape=jax.ShapeDtypeStruct((per_plane, blocks, capacity, width), bf16),
        grid_spec=pltpu.PrefetchScalarGridSpec(
            num_scalar_prefetch=1,
            grid=(blocks,),
            in_specs=[
                pl.BlockSpec((None, experts, tok_rows), lambda i, s: (i, 0, 0)),
                pl.BlockSpec((None, tok_rows, width), lambda i, s: (s[1 + i], 0, 0)),
            ],
            out_specs=pl.BlockSpec((per_plane, None, capacity, width), lambda i, s: (0, i, 0, 0)),
        ),
        compiler_params=params(1, 40),
        cost_estimate=estimate(
            flops=2 * blocks * slot_rows * tok_rows * width,
            bytes_accessed=2 * blocks * (slot_rows + tok_rows) * width,
            transcendentals=0,
        ),
        name="dispatch",
    )(at, slots, rows)


def combine_kernel(carried, at_ref, slots_ref, rows_ref, *refs):
    out_ref = refs[carried]
    hot = plane_hot(slots_ref, at_ref[0], rows_ref.shape)
    rows = rows_ref[...].reshape(hot.shape[0], rows_ref.shape[2])
    out_ref[...] = dot_tn(hot, rows).astype(bf16)


def combine(at, slots, rows, planes, kept=None):
    blocks, experts, tok_rows = slots.shape
    per_plane, _, capacity, width = rows.shape
    slot_rows = per_plane * capacity
    carried = 0 if kept is None else 1
    return pl.pallas_call(
        functools.partial(combine_kernel, carried),
        out_shape=jax.ShapeDtypeStruct((planes, tok_rows, width), bf16),
        grid_spec=pltpu.PrefetchScalarGridSpec(
            num_scalar_prefetch=1,
            grid=(blocks,),
            in_specs=[
                pl.BlockSpec((None, experts, tok_rows), lambda i, s: (i, 0, 0)),
                pl.BlockSpec((per_plane, None, capacity, width), lambda i, s: (0, i, 0, 0)),
            ]
            + [pl.BlockSpec(memory_space=pl.ANY)] * carried,
            out_specs=pl.BlockSpec((None, tok_rows, width), lambda i, s: (s[1 + i], 0, 0)),
        ),
        input_output_aliases={3: 0} if carried else {},
        compiler_params=params(1, 40),
        cost_estimate=estimate(
            flops=2 * blocks * slot_rows * tok_rows * width,
            bytes_accessed=2 * blocks * (slot_rows + tok_rows) * width,
            transcendentals=0,
        ),
        name="combine",
    )(at, slots, rows, *(() if kept is None else (kept,)))


def qkv_kernel(heads, planes, at_ref, x_ref, gain_ref, *refs):
    w_refs = refs[:planes]
    gq_ref, gk_ref, cos_ref, sin_ref, act_ref, pre_ref, rot_ref, all_ref = refs[planes:]
    depth = w_refs[0].shape[0]

    @pl.when(pl.program_id(0) == 0)
    def _():
        for d in range(planes):
            place = pl.ds(pl.multiple_of(at_ref[d] * depth, depth), depth)
            all_ref[place, :] = w_refs[d][...]

    x = x_ref[...].astype(f32)
    inverse = lax.rsqrt(jnp.mean(x * x, axis=-1, keepdims=True) + norm_eps)
    act = (x * inverse * gain_ref[...]).astype(bf16)
    act_ref[...] = act
    y = None
    for d in range(planes):
        columns = pl.ds(pl.multiple_of(at_ref[d] * depth, depth), depth)
        term = dot_nn(act_ref[:, columns], w_refs[d][...])
        y = term if y is None else y + term
    cosine, sine = cos_ref[...], sin_ref[...]
    for part, gain in enumerate((gq_ref[...], gk_ref[...])):
        for h in range(heads):
            at = (part * heads + h) * HD
            u = y[:, at : at + HD]
            pre_ref[:, at : at + HD] = u
            n = u * lax.rsqrt(jnp.mean(u * u, axis=-1, keepdims=True) + head_eps) * gain
            rot_ref[:, at : at + HD] = (n * cosine + pltpu.roll(n, HD // 2, 1) * sine).astype(bf16)
    at = 2 * heads * HD
    rot_ref[:, at:] = y[:, at:].astype(bf16)


def qkv_project(places, rows, gain, weights, gain_q, gain_k, cosine, sine, heads):
    count, width = rows.shape
    planes = len(weights)
    depth, out_width = weights[0].shape
    pre_width = 2 * heads * HD
    whole = lambda i, s: (0, 0)
    block = lambda i, s: (i, 0)
    return pl.pallas_call(
        functools.partial(qkv_kernel, heads, planes),
        out_shape=(
            jax.ShapeDtypeStruct((count, width), bf16),
            jax.ShapeDtypeStruct((count, pre_width), f32),
            jax.ShapeDtypeStruct((count, out_width), bf16),
            jax.ShapeDtypeStruct((width, out_width), bf16),
        ),
        grid_spec=pltpu.PrefetchScalarGridSpec(
            num_scalar_prefetch=1,
            grid=(count // ROWS,),
            in_specs=[
                pl.BlockSpec((ROWS, width), block),
                pl.BlockSpec((1, width), whole),
            ]
            + [pl.BlockSpec((depth, out_width), whole)] * planes
            + [
                pl.BlockSpec((1, HD), whole),
                pl.BlockSpec((1, HD), whole),
                pl.BlockSpec((ROWS, HD), block),
                pl.BlockSpec((ROWS, HD), block),
            ],
            out_specs=(
                pl.BlockSpec((ROWS, width), block),
                pl.BlockSpec((ROWS, pre_width), block),
                pl.BlockSpec((ROWS, out_width), block),
                pl.BlockSpec((width, out_width), whole),
            ),
        ),
        compiler_params=params(1, 56),
        cost_estimate=estimate(
            flops=2 * count * width * out_width,
            bytes_accessed=4 * count * width + 2 * width * out_width + 6 * count * out_width,
            transcendentals=0,
        ),
        name="qkv_project",
    )(places, rows, gain, *weights, gain_q, gain_k, cosine, sine)


def attn_kernel(
    scale, low_ref, high_ref, q_ref, k_ref, v_ref, sq_ref, sk_ref, o_ref, ol_ref, lse_ref, s_scr
):
    block = pl.program_id(1)
    low, high = low_ref[block], high_ref[block]
    q = q_ref[...]
    seg_q = sq_ref[...]
    half = ROWS // 2

    def scores(kb, top):
        at = pl.ds(pl.multiple_of(kb * ROWS, ROWS), ROWS)
        s = dot_nt(q, k_ref[at, :]) * scale
        s = jnp.where(seg_q == sk_ref[:, at], s, masked_score)
        s_scr[:, at] = s
        return jnp.maximum(top, jnp.maximum(s[:, :half], s[:, half:]))

    top = lax.fori_loop(low, high, scores, jnp.full((ROWS, half), masked_score, f32))
    top = jnp.max(top, axis=-1, keepdims=True)

    def weigh(kb, carry):
        total, acc = carry
        at = pl.ds(pl.multiple_of(kb * ROWS, ROWS), ROWS)
        p = jnp.exp(s_scr[:, at] - top)
        acc = acc + dot_nn(p.astype(bf16), v_ref[at, :])
        return total + (p[:, :half] + p[:, half:]), acc

    total, acc = lax.fori_loop(
        low, high, weigh, (jnp.zeros((ROWS, half), f32), jnp.zeros((ROWS, HD), f32))
    )
    total = jnp.sum(total, axis=-1, keepdims=True)
    out = acc / total
    o_ref[...] = out
    ol_ref[...] = out.astype(bf16)
    lse = jnp.broadcast_to(top + jnp.log(total), (ROWS, HD)).T
    lse_ref[0] = lse[0:1, :]


def attention(rot, seg_col, seg_row, low, high, heads):
    count = rot.shape[0]
    blocks = count // ROWS
    scale = HD ** (-0.5)
    return pl.pallas_call(
        functools.partial(attn_kernel, scale),
        out_shape=(
            jax.ShapeDtypeStruct((count, heads * HD), f32),
            jax.ShapeDtypeStruct((count, heads * HD), bf16),
            jax.ShapeDtypeStruct((heads * blocks, 1, ROWS), f32),
        ),
        grid_spec=pltpu.PrefetchScalarGridSpec(
            num_scalar_prefetch=2,
            grid=(heads, blocks),
            in_specs=[
                pl.BlockSpec((ROWS, HD), lambda h, i, *s: (i, h)),
                pl.BlockSpec((count, HD), lambda h, i, *s: (0, heads + h)),
                pl.BlockSpec((count, HD), lambda h, i, *s: (0, 2 * heads + h)),
                pl.BlockSpec((ROWS, 1), lambda h, i, *s: (i, 0)),
                pl.BlockSpec((1, count), lambda h, i, *s: (0, 0)),
            ],
            out_specs=(
                pl.BlockSpec((ROWS, HD), lambda h, i, *s: (i, h)),
                pl.BlockSpec((ROWS, HD), lambda h, i, *s: (i, h)),
                pl.BlockSpec((1, 1, ROWS), lambda h, i, *s: (h * blocks + i, 0, 0)),
            ),
            scratch_shapes=[pltpu.VMEM((ROWS, count), f32)],
        ),
        compiler_params=params(2, 32),
        cost_estimate=estimate(
            flops=2 * heads * count * count * HD,
            bytes_accessed=12 * heads * count * HD,
            transcendentals=heads * count * count // 2,
        ),
        name="attention",
    )(low, high, rot, rot, rot, seg_col, seg_row)


def head_back(grad, pre, gain, cosine, sine):
    n = grad * cosine - pltpu.roll(grad, HD // 2, 1) * sine
    inverse = lax.rsqrt(jnp.mean(pre * pre, axis=-1, keepdims=True) + head_eps)
    w = n * gain
    back = inverse * w - pre * inverse**3 * jnp.mean(w * pre, axis=-1, keepdims=True)
    return back, jnp.sum(n * pre * inverse, axis=0, keepdims=True)


def attn_back_kernel(
    scale,
    low_ref,
    high_ref,
    q_ref,
    k_ref,
    v_ref,
    do_ref,
    o_ref,
    lse_ref,
    sq_ref,
    sk_ref,
    qpre_ref,
    kpre_ref,
    gq_ref,
    gk_ref,
    cosq_ref,
    sinq_ref,
    cosk_ref,
    sink_ref,
    dq_ref,
    dk_ref,
    dv_ref,
    gain_ref,
    dk_scr,
    dv_scr,
):
    head, block = pl.program_id(0), pl.program_id(1)
    low, high = low_ref[block], high_ref[block]

    @pl.when(block == 0)
    def _():
        dk_scr[...] = jnp.zeros_like(dk_scr)
        dv_scr[...] = jnp.zeros_like(dv_scr)

    @pl.when((block == 0) & (head == 0))
    def _():
        gain_ref[...] = jnp.zeros_like(gain_ref)

    q, do = q_ref[...], do_ref[...]
    row_dot = jnp.sum((do.astype(f32) * o_ref[...]).T, axis=0, keepdims=True)
    lse = lse_ref[0]
    seg_q = sq_ref[...]

    def tile(kb, dq):
        at = pl.ds(pl.multiple_of(kb * ROWS, ROWS), ROWS)
        k, v = k_ref[at, :], v_ref[at, :]
        s = dot_nt(k, q) * scale
        p = jnp.where(sk_ref[at, :] == seg_q, jnp.exp(s - lse), 0.0)
        dp = dot_nt(v, do)
        ds = (p * (dp - row_dot)).astype(bf16)
        dv_scr[at, :] += dot_nn(p.astype(bf16), do)
        dk_scr[at, :] += dot_nn(ds, q)
        return dq + dot_tn(ds, k)

    dq = lax.fori_loop(low, high, tile, jnp.zeros((ROWS, HD), f32))
    back, gain_q = head_back(dq * scale, qpre_ref[...], gq_ref[...], cosq_ref[...], sinq_ref[...])
    dq_ref[...] = back.astype(bf16)
    gain_ref[0:1, :] += gain_q

    @pl.when(block == pl.num_programs(1) - 1)
    def _():
        @pl.loop(0, dk_scr.shape[0] // ROWS)
        def _(i):
            at = pl.ds(pl.multiple_of(i * ROWS, ROWS), ROWS)
            back, gain_k = head_back(
                dk_scr[at, :] * scale, kpre_ref[at, :], gk_ref[...], cosk_ref[at, :], sink_ref[at, :]
            )
            dk_ref[at, :] = back.astype(bf16)
            dv_ref[at, :] = dv_scr[at, :].astype(bf16)
            gain_ref[1:2, :] += gain_k


def attention_back(
    rot, grad, out, lse, seg_col, seg_row, low, high, pre, gain_q, gain_k, cosine, sine, heads
):
    count = rot.shape[0]
    blocks = count // ROWS
    scale = HD ** (-0.5)
    mine = lambda h, i, *s: (i, h)
    whole = lambda h, i, *s: (0, 0)
    return pl.pallas_call(
        functools.partial(attn_back_kernel, scale),
        out_shape=(
            jax.ShapeDtypeStruct((count, heads * HD), bf16),
            jax.ShapeDtypeStruct((count, heads * HD), bf16),
            jax.ShapeDtypeStruct((count, heads * HD), bf16),
            jax.ShapeDtypeStruct((8, HD), f32),
        ),
        grid_spec=pltpu.PrefetchScalarGridSpec(
            num_scalar_prefetch=2,
            grid=(heads, blocks),
            in_specs=[
                pl.BlockSpec((ROWS, HD), mine),
                pl.BlockSpec((count, HD), lambda h, i, *s: (0, heads + h)),
                pl.BlockSpec((count, HD), lambda h, i, *s: (0, 2 * heads + h)),
                pl.BlockSpec((ROWS, HD), mine),
                pl.BlockSpec((ROWS, HD), mine),
                pl.BlockSpec((1, 1, ROWS), lambda h, i, *s: (h * blocks + i, 0, 0)),
                pl.BlockSpec((1, ROWS), lambda h, i, *s: (0, i)),
                pl.BlockSpec((count, 1), whole),
                pl.BlockSpec((ROWS, HD), mine),
                pl.BlockSpec((count, HD), lambda h, i, *s: (0, heads + h)),
                pl.BlockSpec((1, HD), whole),
                pl.BlockSpec((1, HD), whole),
                pl.BlockSpec((ROWS, HD), lambda h, i, *s: (i, 0)),
                pl.BlockSpec((ROWS, HD), lambda h, i, *s: (i, 0)),
                pl.BlockSpec((count, HD), whole),
                pl.BlockSpec((count, HD), whole),
            ],
            out_specs=(
                pl.BlockSpec((ROWS, HD), mine),
                pl.BlockSpec((count, HD), lambda h, i, *s: (0, h)),
                pl.BlockSpec((count, HD), lambda h, i, *s: (0, h)),
                pl.BlockSpec((8, HD), whole),
            ),
            scratch_shapes=[pltpu.VMEM((count, HD), f32), pltpu.VMEM((count, HD), f32)],
        ),
        compiler_params=params(2, 48),
        cost_estimate=estimate(
            flops=5 * heads * count * count * HD,
            bytes_accessed=30 * heads * count * HD,
            transcendentals=heads * count * count // 2,
        ),
        name="attention_back",
    )(
        low,
        high,
        rot,
        rot,
        rot,
        grad,
        out,
        lse,
        seg_row,
        seg_col,
        pre,
        pre,
        gain_q,
        gain_k,
        cosine,
        sine,
        cosine,
        sine,
    )


def expert_kernel(base, count, carried, mine_ref, x_ref, *refs):
    near = 1 if base == 0 else 0
    c_refs, refs = refs[: near + 1], refs[near + 1 :]
    wg_ref, wu_ref, wd_ref = refs[:3]
    refs = refs[3 + carried :]
    back_ref, out_ref, xs_ref, c_ref, hid_ref, gp_ref, up_ref = refs[:7]
    out_acc, back_acc, gate_scr, dot_scr = refs[7:]
    step = pl.program_id(1)
    per_plane, capacity, width = c_ref.shape
    rows = per_plane * capacity
    extra = x_ref.shape[2] - width
    lane = lax.broadcasted_iota(jnp.int32, (rows, extra), 1)
    high, low = lane == mine_ref[0], lane == mine_ref[0] + count

    @pl.when(step == 0)
    def _():
        xs_ref[...] = x_ref[:, :, :width]
        if near:

            @pl.when(pl.program_id(0) == 0)
            def _():
                c_ref[...] = c_refs[0][...]

            @pl.when(pl.program_id(0) > 0)
            def _():
                c_ref[...] = c_refs[1][...]

        else:
            c_ref[...] = c_refs[0][...]
        gates = x_ref[:, :, width:].reshape(rows, extra).astype(f32)
        gate_scr[...] = jnp.sum(jnp.where(high | low, gates, 0.0), axis=-1, keepdims=True)
        out_acc[...] = jnp.zeros_like(out_acc)
        back_acc[...] = jnp.zeros_like(back_acc)
        dot_scr[...] = jnp.zeros_like(dot_scr)

    x = x_ref[:, :, :width].reshape(rows, width)
    c = c_ref[...].reshape(rows, width)
    gate = gate_scr[...]
    wg, wu, wd = wg_ref[...], wu_ref[...], wd_ref[...]
    gate_pre, up_pre = dot_nn(x, wg), dot_nn(x, wu)
    sig = jax.nn.sigmoid(gate_pre)
    hidden = (gate_pre * sig * up_pre).astype(bf16)
    out_acc[...] += dot_nn(hidden, wd)
    plain = dot_nt(c, wd)
    wide = hidden.astype(f32)
    dot_scr[...] += jnp.sum(wide * plain, axis=-1, keepdims=True)
    hid_ref[...] = (wide * gate).astype(bf16).reshape(hid_ref.shape)
    hidden_grad = plain * gate
    gate_grad = (hidden_grad * up_pre * sig * (1.0 + gate_pre * (1.0 - sig))).astype(bf16)
    up_grad = (hidden_grad * gate_pre * sig).astype(bf16)
    gp_ref[...] = gate_grad.reshape(gp_ref.shape)
    up_ref[...] = up_grad.reshape(up_ref.shape)
    back_acc[...] += dot_nt(gate_grad, wg) + dot_nt(up_grad, wu)

    @pl.when(step == pl.num_programs(1) - 1)
    def _():
        dots = dot_scr[...]
        coarse = dots.astype(bf16).astype(f32)
        lanes = jnp.where(high, coarse, jnp.where(low, dots - coarse, 0.0)).astype(bf16)
        back_ref[:, :, :width] = back_acc[...].astype(bf16).reshape(c_ref.shape)
        back_ref[:, :, width:] = lanes.reshape(per_plane, capacity, extra)
        out_ref[...] = (out_acc[...] * gate).astype(bf16).reshape(out_ref.shape)


def experts(mine, x, near, far, wg, wu, wd, base, planes, count, kept):
    per_plane, blocks, capacity, wide = x.shape
    width = near.shape[3]
    halves, _, hidden = wg.shape
    rows = per_plane * capacity
    saved = jax.ShapeDtypeStruct((per_plane, planes, capacity, width), bf16)
    thin = jax.ShapeDtypeStruct((per_plane, planes, capacity, halves * hidden), bf16)
    moved = pl.BlockSpec((per_plane, None, capacity, wide), lambda i, f, s: (0, i, 0, 0))
    saved_spec = pl.BlockSpec((per_plane, None, capacity, width), lambda i, f, s: (0, base + i, 0, 0))
    thin_spec = pl.BlockSpec((per_plane, None, capacity, hidden), lambda i, f, s: (0, base + i, 0, f))
    carried = 0 if kept is None else len(kept)
    cots = (near, far) if base == 0 else (far,)
    cot_specs = [
        pl.BlockSpec(
            (per_plane, None, capacity, width), lambda i, f, s: (0, jnp.maximum(base + i - 1, 0), 0, 0)
        )
    ]
    if base == 0:
        cot_specs = [pl.BlockSpec((per_plane, None, capacity, width), lambda i, f, s: (0, 0, 0, 0))] + cot_specs
    result = pl.pallas_call(
        functools.partial(expert_kernel, base, count, carried),
        out_shape=(jax.ShapeDtypeStruct(x.shape, bf16), saved, saved, saved, thin, thin, thin),
        grid_spec=pltpu.PrefetchScalarGridSpec(
            num_scalar_prefetch=1,
            grid=(blocks, halves),
            in_specs=[
                moved,
                *cot_specs,
                pl.BlockSpec((None, width, hidden), lambda i, f, s: (f, 0, 0)),
                pl.BlockSpec((None, width, hidden), lambda i, f, s: (f, 0, 0)),
                pl.BlockSpec((None, hidden, width), lambda i, f, s: (f, 0, 0)),
            ]
            + [pl.BlockSpec(memory_space=pl.ANY)] * carried,
            out_specs=(moved, saved_spec, saved_spec, saved_spec, thin_spec, thin_spec, thin_spec),
            scratch_shapes=[
                pltpu.VMEM((rows, width), f32),
                pltpu.VMEM((rows, width), f32),
                pltpu.VMEM((rows, 1), f32),
                pltpu.VMEM((rows, 1), f32),
            ],
        ),
        input_output_aliases={5 + len(cots) + i: 1 + i for i in range(carried)},
        compiler_params=params(2, 60),
        cost_estimate=estimate(
            flops=12 * blocks * rows * width * hidden * halves,
            bytes_accessed=10 * blocks * rows * width + 6 * blocks * width * hidden * halves,
            transcendentals=blocks * rows * hidden * halves,
        ),
        name="experts",
    )(mine, x, *cots, wg, wu, wd, *(kept or ()))
    return result[0], result[1:]


def gram_kernel(plus, left_ref, right_ref, *refs):
    total = dot_tn(left_ref[...], right_ref[...])
    if plus:
        total = total + refs[0][...]
    refs[-1][...] = total.astype(refs[-1].dtype)


def gram(left, right, left_cols, right_cols, dtype, plus=None):
    rows = left.shape[0]
    left_at, left_count = left_cols
    right_at, right_count = right_cols
    tall = min(left_count, 256)
    wide = min(right_count, 1024)
    out_spec = pl.BlockSpec((tall, wide), lambda j, i: (i, j))
    return pl.pallas_call(
        functools.partial(gram_kernel, plus is not None),
        out_shape=jax.ShapeDtypeStruct((left_count, right_count), dtype),
        grid=(right_count // wide, left_count // tall),
        in_specs=[
            pl.BlockSpec((rows, tall), lambda j, i: (0, left_at // tall + i)),
            pl.BlockSpec((rows, wide), lambda j, i: (0, right_at // wide + j)),
        ]
        + [out_spec] * (plus is not None),
        out_specs=out_spec,
        compiler_params=params(2, 48),
        cost_estimate=estimate(
            flops=2 * rows * left_count * right_count,
            bytes_accessed=2 * rows * (left_count + right_count) + 4 * left_count * right_count,
            transcendentals=0,
        ),
        name="gram",
    )(left, right, *(() if plus is None else (plus,)))


def project_kernel(plus, core_ref, rows_ref, weights_ref, *refs):
    total = dot_nt(rows_ref[...], weights_ref[...])
    if plus:
        total = total + refs[0][...].astype(f32)
    refs[-1][...] = total.astype(bf16)


def project_back(core, rows, weights, tok_rows, plus=None):
    count, depth = rows.shape
    width = weights.shape[0]
    chips = count // tok_rows // 2
    out_spec = pl.BlockSpec((tok_rows, width), lambda i, s: (i, 0))
    return pl.pallas_call(
        functools.partial(project_kernel, plus is not None),
        out_shape=jax.ShapeDtypeStruct((chips * tok_rows, width), bf16),
        grid_spec=pltpu.PrefetchScalarGridSpec(
            num_scalar_prefetch=1,
            grid=(chips,),
            in_specs=[
                pl.BlockSpec((tok_rows, depth), lambda i, s: (2 * i + s[0], 0)),
                pl.BlockSpec((width, depth), lambda i, s: (0, 0)),
            ]
            + [out_spec] * (plus is not None),
            out_specs=out_spec,
        ),
        compiler_params=params(1, 40),
        cost_estimate=estimate(
            flops=count * depth * width,
            bytes_accessed=2 * width * depth + count * depth + count * width,
            transcendentals=0,
        ),
        name="project_back",
    )(core, rows, weights, *(() if plus is None else (plus,)))


def after(value, *others):
    return lax.optimization_barrier((value,) + others)[0]


def body(
    hidden_in,
    out_cotangent,
    segment_number,
    expert_routes,
    pair_order,
    norm_gain,
    query_weight,
    key_weight,
    value_weight,
    output_weight,
    query_gain,
    key_gain,
    ffn_norm_gain,
    router_weight,
    expert_gate,
    expert_up,
    expert_down,
):
    tok_rows, width = hidden_in.shape
    devices = lax.axis_size(AXIS)
    members = max(1, SEQ_MIN // tok_rows)
    planes = devices // members
    per_plane = members // 2
    expert_count = devices // 2
    capacity = tok_rows * TOPK // expert_count
    heads = width // HD // members
    head_width = heads * HD
    own_rows = norm_gain.shape[0]
    seq = members * tok_rows
    me = lax.axis_index(AXIS)
    plane, member = me // members, me % members
    mine = (me // 2).astype(jnp.int32).reshape(1)
    first = (plane * per_plane).astype(jnp.int32)
    places = (plane ^ jnp.arange(planes, dtype=jnp.int32)).astype(jnp.int32)
    counted = jnp.concatenate([first[None], jnp.arange(planes, dtype=jnp.int32)])
    halfway = -(-planes // 2)
    chunks = [part for part in (range(halfway), range(halfway, planes)) if len(part)]

    def placed(part):
        return jnp.concatenate([first[None], places[part.start : part.stop]])

    plane_groups = [[g * members + j for j in range(members)] for g in range(planes)]
    stack_groups = [[g * members + j for g in range(planes)] for j in range(members)]
    core_groups = [
        [g * members + 2 * c + h for c in range(per_plane)] for g in range(planes) for h in (0, 1)
    ]

    def exchange(value, groups=None):
        return lax.all_to_all(
            value, AXIS, split_axis=0, concat_axis=0, tiled=True, axis_index_groups=groups
        )

    def gather(value, groups=None):
        return lax.all_gather(value, AXIS, axis=0, tiled=True, axis_index_groups=groups)

    def flip(value, bits):
        if bits == 0:
            return value
        return lax.ppermute(value, AXIS, [(i, i ^ bits) for i in range(devices)])

    def to_core(value):
        return flip(value, 1)

    def to_plane(value, d):
        return flip(value, members * d)

    def over_planes(value):
        value = value.reshape((planes, -1) + value.shape[1:])
        return sum(
            to_plane(lax.dynamic_index_in_dim(value, places[d], 0, False), d).astype(f32)
            for d in range(planes)
        )

    def over_stack(value):
        return lax.psum_scatter(
            value.reshape(planes * tok_rows, -1),
            AXIS,
            scatter_dimension=0,
            tiled=True,
            axis_index_groups=stack_groups,
        )

    wire, core_op = [], []

    def on_wire(value, groups):
        came = exchange(after(value, *wire[-1:]), groups)
        wire.append(came)
        return came

    def to_chips(value):
        return on_wire(value, core_groups)

    def in_turn(value):
        return after(value, *core_op[-1:])

    def ran(value):
        core_op.append(value)
        return value

    pieces = (
        router_weight.reshape(-1),
        norm_gain,
        ffn_norm_gain,
        query_gain,
        key_gain,
        segment_number.astype(bf16),
    )
    packed = jnp.concatenate(pieces)
    length = packed.shape[0]
    padded = -(-length // 128) * 128
    packed = jnp.pad(packed, (0, padded - length))
    packed = on_wire(jnp.broadcast_to(packed[None], (devices, padded)), None)
    small = []
    at = 0
    for piece in pieces:
        small.append(packed[:, at : at + piece.shape[0]])
        at += piece.shape[0]
    router_full = small[0].reshape(width, expert_count)
    gain_one = small[1].reshape(1, width).astype(f32)
    gain_two = small[2].reshape(1, width).astype(f32)
    gain_q = small[3].reshape(1, HD).astype(f32)
    gain_k = small[4].reshape(1, HD).astype(f32)
    segments = lax.dynamic_slice_in_dim(small[5], plane * members, members, 0).astype(f32)
    seg_row, seg_col = segments.reshape(1, seq), segments.reshape(seq, 1)
    seg_blocks = segments.reshape(seq // ROWS, ROWS)
    seg_first, seg_last = seg_blocks[:, 0], seg_blocks[:, -1]
    low = jnp.sum((seg_last[None, :] < seg_first[:, None]).astype(jnp.int32), axis=1)
    high = jnp.sum((seg_first[None, :] <= seg_last[:, None]).astype(jnp.int32), axis=1)

    columns = jnp.concatenate(
        [w.reshape(own_rows, members, head_width) for w in (query_weight, key_weight, value_weight)],
        axis=2,
    )
    slots = block_slots(expert_routes, pair_order, expert_count)
    columns = on_wire(
        after(columns, slots).transpose(1, 0, 2).reshape(members * own_rows, 3 * head_width), plane_groups
    )
    slots = [to_plane(slots, d) for d in range(planes)]
    weights = [to_plane(after(columns, *slots), d) for d in range(planes)]
    rows_all = gather(hidden_in, plane_groups)
    output_full = gather(output_weight)

    cot_own = dispatch(counted, slots[0][None], out_cotangent[None], per_plane, capacity)
    cot_parts = [to_chips(cot_own)]
    slots = jnp.stack(slots)
    cot_rows = {0: out_cotangent}
    top = planes // 2
    early, late = [], []
    if planes > 1:
        cot_rows[top] = to_plane(after(out_cotangent, *weights), top)
        early.append(cot_rows[top])
    for d in range(1, planes):
        if d != top:
            lowest = d & -d
            start = after(out_cotangent, *early) if d == lowest else cot_rows[d ^ lowest]
            cot_rows[d] = to_plane(start, lowest)
            late.append(cot_rows[d])

    halves = lambda w: jnp.concatenate([w, to_core(w)], axis=0)
    wg, wu, wd = halves(expert_gate), halves(expert_up), halves(expert_down)

    cosine, sine = rope_tables(seq)
    act_one, pre, rot, ordered = qkv_project(
        places, rows_all, gain_one, weights, gain_q, gain_k, cosine, sine, heads
    )
    out_wide, out_heads, lse = attention(rot, seg_col, seg_row, low, high, heads)
    out_low = on_wire(after(out_heads, *early), plane_groups)
    out_low = out_low.reshape(members, tok_rows, head_width).transpose(1, 0, 2)
    out_low = after(out_low.reshape(tok_rows, width), wg, wu, wd)
    tokens = hidden_in.astype(f32)
    cotangent = out_cotangent.astype(f32)
    middle = tokens + dot_nn(out_low, output_full)
    inverse_two = lax.rsqrt(jnp.mean(middle * middle, axis=-1, keepdims=True) + norm_eps)
    act_two = (middle * inverse_two * gain_two).astype(bf16)

    logits = dot_nn(act_two, router_full)
    expert_ids = jnp.arange(expert_count, dtype=jnp.int32)
    routed = jnp.any(expert_routes[:, :, None] == expert_ids[None, None, :], axis=1)
    logits = jnp.where(routed, logits, masked_score)
    gates = jnp.where(routed, jnp.exp(logits - jnp.max(logits, axis=1, keepdims=True)), 0.0)
    gates = gates / jnp.sum(gates, axis=1, keepdims=True)
    coarse = lax.reduce_precision(gates, 8, 7)
    extra = -(-2 * expert_count // 128) * 128
    act_wide = jnp.concatenate(
        [
            act_two,
            coarse.astype(bf16),
            (gates - coarse).astype(bf16),
            jnp.zeros((tok_rows, extra - 2 * expert_count), bf16),
        ],
        axis=1,
    )

    act_wide = after(act_wide, *late)
    act_all = gather(act_wide, stack_groups).reshape(planes, tok_rows, -1)
    if planes > 1:
        far = jnp.stack([after(cot_rows[d], act_wide) for d in range(1, planes)])
        sent = dispatch(counted[:planes], slots[1:], far, per_plane, capacity)
        cot_parts.append(to_chips(ran(sent)))

    act = []
    for part in chunks:
        own_slots = slots[part.start : part.stop]
        sent = dispatch(placed(part), own_slots, in_turn(act_all), per_plane, capacity)
        act.append(to_chips(ran(sent)))
    kept, back = None, []
    for part, rows in zip(chunks, act):
        sent, kept = experts(
            mine,
            in_turn(rows),
            cot_parts[0],
            cot_parts[-1],
            wg,
            wu,
            wd,
            part.start,
            planes,
            expert_count,
            kept,
        )
        back.append(to_chips(ran(sent)))
    out_all, x_all, c_all, hid_all, gp_all, up_all = kept

    hidden = expert_gate.shape[2]
    flat = lambda value: value.reshape(-1, value.shape[3])
    sides = (
        (flat(x_all), flat(gp_all), 1),
        (flat(x_all), flat(up_all), 1),
        (flat(hid_all), flat(c_all), 0),
    )

    def half(side, which, plus=None):
        left, right, split = side
        cut, whole = (which * hidden, hidden), (0, width)
        cols = (whole, cut) if split else (cut, whole)
        return gram(left, right, *cols, f32, plus)

    theirs = [half(side, 1) for side in sides]
    core_op.extend(theirs)
    theirs = [to_core(grad) for grad in theirs]
    returned = None
    for part, rows in zip(chunks, back):
        own_slots = slots[part.start : part.stop]
        rows = after(rows, *core_op[-3:])
        returned = ran(combine(placed(part), own_slots, rows, planes, returned))
    back_sum = over_stack(returned)
    outs = to_chips(out_all)
    grad_gate, grad_up, grad_down = (
        half(side, 0, other) for side, other in zip(sides, theirs)
    )

    back_sum = after(back_sum, grad_gate, grad_up, grad_down).astype(f32)
    expert_in_grad = back_sum[:, :width]
    gate_grad = (
        back_sum[:, width : width + expert_count]
        + back_sum[:, width + expert_count : width + 2 * expert_count]
    )
    select_grad = gates * (gate_grad - jnp.sum(gates * gate_grad, axis=1, keepdims=True))
    logit_grad = select_grad.astype(bf16)
    grad_router = dot_tn(act_two, logit_grad)
    act_two_grad = expert_in_grad + dot_nt(logit_grad, router_full)
    weighted = act_two_grad * gain_two
    grad_gain_two = jnp.sum(act_two_grad * middle * inverse_two, axis=0)
    middle_grad = (
        cotangent
        + inverse_two * weighted
        - middle * inverse_two**3 * jnp.mean(weighted * middle, axis=-1, keepdims=True)
    )
    middle_low = middle_grad.astype(bf16)

    out_grad = dot_nt(middle_low, output_full).astype(bf16)
    out_grad = out_grad.reshape(tok_rows, members, head_width).transpose(1, 0, 2)
    out_grad = on_wire(out_grad.reshape(seq, head_width), plane_groups)
    mixed = combine(placed(range(planes)), slots, after(outs, middle_low), planes)
    mixture = over_stack(mixed)
    layer_out = (middle + mixture.astype(f32)).astype(bf16)
    middle_all = gather(after(middle_low, mixed), plane_groups)
    dq, dk, dv, grad_gains = attention_back(
        rot,
        after(out_grad, mixed),
        out_wide,
        lse,
        seg_col,
        seg_row,
        low,
        high,
        pre,
        gain_q,
        gain_k,
        cosine,
        sine,
        heads,
    )
    dqkv = jnp.concatenate([dq, dk, dv], axis=1)

    sums = (
        grad_router.reshape(devices, -1),
        grad_gain_two.reshape(devices, -1),
        grad_gains[0].reshape(devices, -1),
        grad_gains[1].reshape(devices, -1),
    )
    packed = jnp.concatenate(sums, axis=1)
    length = packed.shape[1]
    padded = -(-length // 128) * 128
    packed = jnp.pad(packed, ((0, 0), (0, padded - length)))

    core = (me % 2).astype(jnp.int32).reshape(1)
    part = gram(act_one, dqkv, (0, width), (0, 3 * head_width), bf16)
    taken = over_planes(part).astype(bf16)
    given = to_core(project_back(1 - core, after(dqkv, part), ordered, tok_rows))
    act_one_grad = project_back(core, dqkv, ordered, tok_rows, given)
    act_one_grad = exchange(act_one_grad, core_groups)

    output_part = gram(out_heads, middle_all, (0, head_width), (0, width), bf16)
    output_part = over_planes(output_part)
    to_owner = [
        (g * members + j, j * planes + g) for g in range(planes) for j in range(members)
    ]
    grad_output = lax.ppermute(output_part, AXIS, to_owner)
    packed, act_one_grad = lax.optimization_barrier((packed, act_one_grad))
    packed = exchange(packed)
    taken, packed, grad_output = lax.optimization_barrier((taken, packed, grad_output))
    part = exchange(taken, plane_groups).reshape(members, own_rows, 3, head_width)
    part = part.transpose(2, 1, 0, 3).reshape(3, own_rows, width).astype(f32)
    grad_query, grad_key, grad_value = part[0], part[1], part[2]
    act_one_grad = act_one_grad.reshape(per_plane, tok_rows, width)
    act_one_grad = jnp.sum(act_one_grad.astype(f32), axis=0)

    inverse_one = lax.rsqrt(jnp.mean(tokens * tokens, axis=-1, keepdims=True) + norm_eps)
    weighted = act_one_grad * gain_one
    grad_hidden = (
        middle_grad
        + inverse_one * weighted
        - tokens * inverse_one**3 * jnp.mean(weighted * tokens, axis=-1, keepdims=True)
    )
    grad_gain_one = (
        jnp.sum(
            grad_query * query_weight.astype(f32)
            + grad_key * key_weight.astype(f32)
            + grad_value * value_weight.astype(f32),
            axis=1,
        )
        / norm_gain.astype(f32)
    )

    summed = jnp.sum(packed, axis=0)
    at, tiny = 0, []
    for piece in sums:
        tiny.append(summed[at : at + piece.shape[1]])
        at += piece.shape[1]

    return (
        layer_out,
        grad_hidden,
        grad_gain_one,
        grad_query,
        grad_key,
        grad_value,
        grad_output,
        tiny[2],
        tiny[3],
        tiny[1],
        tiny[0].reshape(own_rows, expert_count),
        grad_gate[None],
        grad_up[None],
        grad_down[None],
    )


def solution(mesh):
    row, mat, cube = P(AXIS), P(AXIS, None), P(AXIS, None, None)
    return jax.shard_map(
        body,
        mesh=mesh,
        in_specs=(mat, mat, row, mat, mat, row, mat, mat, mat, mat, row, row, row, mat)
        + (cube,) * 3,
        out_specs=(mat, mat, row, mat, mat, mat, mat, row, row, row, mat) + (cube,) * 3,
        check_vma=False,
    )
```

```python
import functools
import math

import jax
import jax.numpy as jnp
from jax import lax
from jax.experimental import pallas as pl
from jax.experimental.pallas import tpu as pltpu
from jax.sharding import PartitionSpec as P

HD = 128
TOPK = 8
SEQ_MIN = 2048
ROWS = 256
SHARE = 32

norm_eps = 1e-05
head_eps = 1e-06
rope_base = 10000.0
masked_score = -1e30
absent_slot = 4096.0

AXIS = "fsdp"
f32 = jnp.float32
bf16 = jnp.bfloat16
MIB = 1 << 20


def dot_nt(left, right):
    return lax.dot_general(left, right, (((1,), (1,)), ((), ())), preferred_element_type=f32)


def dot_tn(left, right):
    return lax.dot_general(left, right, (((0,), (0,)), ((), ())), preferred_element_type=f32)


def dot_nn(left, right):
    return lax.dot_general(left, right, (((1,), (0,)), ((), ())), preferred_element_type=f32)


def params(steps, mib):
    return pltpu.CompilerParams(
        dimension_semantics=("arbitrary",) * steps, vmem_limit_bytes=mib * MIB
    )


def estimate(flops, bytes_accessed, transcendentals):
    return pl.CostEstimate(
        flops=flops // SHARE, bytes_accessed=bytes_accessed // SHARE, transcendentals=transcendentals // SHARE
    )


def rope_tables(count):
    half_width = HD // 2
    frequency = jnp.exp(-math.log(rope_base) * 2.0 * jnp.arange(half_width, dtype=f32) / HD)
    angles = jnp.arange(count, dtype=f32)[:, None] * frequency[None, :]
    cosine, sine = jnp.cos(angles), jnp.sin(angles)
    return jnp.concatenate([cosine, cosine], axis=-1), jnp.concatenate([-sine, sine], axis=-1)


def slots_kernel(expert_count, routes_ref, order_ref, slots_ref):
    tok_rows = routes_ref.shape[0]
    pair_count = order_ref.shape[1]
    order = order_ref[...]
    shift = TOPK.bit_length() - 1
    token_of = lax.shift_right_logical(order, jnp.full_like(order, shift))
    route_of = order & (TOPK - 1)
    token_iota = lax.broadcasted_iota(jnp.int32, (tok_rows, pair_count), 0)
    token_hot = jnp.where(token_iota == token_of, 1.0, 0.0).astype(bf16)
    place = lax.broadcasted_iota(jnp.int32, (TOPK, pair_count), 1)
    chosen = lax.broadcasted_iota(jnp.int32, (TOPK, pair_count), 0) == route_of
    high = lax.shift_right_logical(place, jnp.full_like(place, 8)).astype(f32)
    low = (place & 255).astype(f32)
    digits = jnp.concatenate([jnp.where(chosen, high, 0.0), jnp.where(chosen, low, 0.0)], axis=0)
    found = dot_nt(token_hot, digits.astype(bf16))
    rank = found[:, :TOPK] * 256.0 + found[:, TOPK:]
    routes = routes_ref[...]
    lanes = -(-expert_count // 128) * 128
    expert_iota = lax.broadcasted_iota(jnp.int32, (tok_rows, lanes), 1)
    never = 1e9
    by_expert = jnp.full((tok_rows, lanes), never, f32)
    for k in range(TOPK):
        by_expert = jnp.where(expert_iota == routes[:, k : k + 1], rank[:, k : k + 1], by_expert)
    turned = by_expert.T
    for e in range(expert_count):
        mine = turned[e : e + 1, :]
        earlier = jnp.where(by_expert[:, e : e + 1] < mine, 1.0, 0.0)
        count = jnp.sum(earlier, axis=0, keepdims=True)
        slots_ref[e : e + 1, :] = jnp.where(mine < never, count, absent_slot)


def block_slots(routes, order, expert_count):
    tok_rows = routes.shape[0]
    return pl.pallas_call(
        functools.partial(slots_kernel, expert_count),
        out_shape=jax.ShapeDtypeStruct((expert_count, tok_rows), f32),
        compiler_params=pltpu.CompilerParams(vmem_limit_bytes=32 * MIB),
        name="block_slots",
    )(routes, order)


def slot_hot(slots_ref, expert, capacity):
    slot_row = slots_ref[pl.ds(expert, 1), :]
    slot_iota = lax.broadcasted_iota(jnp.int32, (capacity, slot_row.shape[1]), 0).astype(f32)
    return jnp.where(slot_iota == slot_row, 1.0, 0.0).astype(bf16)


def plane_hot(slots_ref, first, shape):
    return jnp.concatenate([slot_hot(slots_ref, first + r, shape[1]) for r in range(shape[0])])


def dispatch_kernel(at_ref, slots_ref, rows_ref, out_ref):
    hot = plane_hot(slots_ref, at_ref[0], out_ref.shape)
    out_ref[...] = dot_nn(hot, rows_ref[...]).astype(bf16).reshape(out_ref.shape)


def dispatch(at, slots, rows, per_plane, capacity):
    blocks, experts, tok_rows = slots.shape
    width = rows.shape[2]
    slot_rows = per_plane * capacity
    return pl.pallas_call(
        dispatch_kernel,
        out_shape=jax.ShapeDtypeStruct((per_plane, blocks, capacity, width), bf16),
        grid_spec=pltpu.PrefetchScalarGridSpec(
            num_scalar_prefetch=1,
            grid=(blocks,),
            in_specs=[
                pl.BlockSpec((None, experts, tok_rows), lambda i, s: (i, 0, 0)),
                pl.BlockSpec((None, tok_rows, width), lambda i, s: (s[1 + i], 0, 0)),
            ],
            out_specs=pl.BlockSpec((per_plane, None, capacity, width), lambda i, s: (0, i, 0, 0)),
        ),
        compiler_params=params(1, 40),
        cost_estimate=estimate(
            flops=2 * blocks * slot_rows * tok_rows * width,
            bytes_accessed=2 * blocks * (slot_rows + tok_rows) * width,
            transcendentals=0,
        ),
        name="dispatch",
    )(at, slots, rows)


def combine_kernel(carried, at_ref, slots_ref, rows_ref, *refs):
    out_ref = refs[carried]
    hot = plane_hot(slots_ref, at_ref[0], rows_ref.shape)
    rows = rows_ref[...].reshape(hot.shape[0], rows_ref.shape[2])
    out_ref[...] = dot_tn(hot, rows).astype(bf16)


def combine(at, slots, rows, planes, kept=None):
    blocks, experts, tok_rows = slots.shape
    per_plane, _, capacity, width = rows.shape
    slot_rows = per_plane * capacity
    carried = 0 if kept is None else 1
    return pl.pallas_call(
        functools.partial(combine_kernel, carried),
        out_shape=jax.ShapeDtypeStruct((planes, tok_rows, width), bf16),
        grid_spec=pltpu.PrefetchScalarGridSpec(
            num_scalar_prefetch=1,
            grid=(blocks,),
            in_specs=[
                pl.BlockSpec((None, experts, tok_rows), lambda i, s: (i, 0, 0)),
                pl.BlockSpec((per_plane, None, capacity, width), lambda i, s: (0, i, 0, 0)),
            ]
            + [pl.BlockSpec(memory_space=pl.ANY)] * carried,
            out_specs=pl.BlockSpec((None, tok_rows, width), lambda i, s: (s[1 + i], 0, 0)),
        ),
        input_output_aliases={3: 0} if carried else {},
        compiler_params=params(1, 40),
        cost_estimate=estimate(
            flops=2 * blocks * slot_rows * tok_rows * width,
            bytes_accessed=2 * blocks * (slot_rows + tok_rows) * width,
            transcendentals=0,
        ),
        name="combine",
    )(at, slots, rows, *(() if kept is None else (kept,)))


def qkv_kernel(heads, planes, at_ref, x_ref, gain_ref, *refs):
    w_refs = refs[:planes]
    gq_ref, gk_ref, cos_ref, sin_ref, act_ref, pre_ref, rot_ref, all_ref = refs[planes:]
    depth = w_refs[0].shape[0]

    @pl.when(pl.program_id(0) == 0)
    def _():
        for d in range(planes):
            place = pl.ds(pl.multiple_of(at_ref[d] * depth, depth), depth)
            all_ref[place, :] = w_refs[d][...]

    x = x_ref[...].astype(f32)
    inverse = lax.rsqrt(jnp.mean(x * x, axis=-1, keepdims=True) + norm_eps)
    act = (x * inverse * gain_ref[...]).astype(bf16)
    act_ref[...] = act
    y = None
    for d in range(planes):
        columns = pl.ds(pl.multiple_of(at_ref[d] * depth, depth), depth)
        term = dot_nn(act_ref[:, columns], w_refs[d][...])
        y = term if y is None else y + term
    cosine, sine = cos_ref[...], sin_ref[...]
    for part, gain in enumerate((gq_ref[...], gk_ref[...])):
        for h in range(heads):
            at = (part * heads + h) * HD
            u = y[:, at : at + HD]
            pre_ref[:, at : at + HD] = u
            n = u * lax.rsqrt(jnp.mean(u * u, axis=-1, keepdims=True) + head_eps) * gain
            rot_ref[:, at : at + HD] = (n * cosine + pltpu.roll(n, HD // 2, 1) * sine).astype(bf16)
    at = 2 * heads * HD
    rot_ref[:, at:] = y[:, at:].astype(bf16)


def qkv_project(places, rows, gain, weights, gain_q, gain_k, cosine, sine, heads):
    count, width = rows.shape
    planes = len(weights)
    depth, out_width = weights[0].shape
    pre_width = 2 * heads * HD
    whole = lambda i, s: (0, 0)
    block = lambda i, s: (i, 0)
    return pl.pallas_call(
        functools.partial(qkv_kernel, heads, planes),
        out_shape=(
            jax.ShapeDtypeStruct((count, width), bf16),
            jax.ShapeDtypeStruct((count, pre_width), f32),
            jax.ShapeDtypeStruct((count, out_width), bf16),
            jax.ShapeDtypeStruct((width, out_width), bf16),
        ),
        grid_spec=pltpu.PrefetchScalarGridSpec(
            num_scalar_prefetch=1,
            grid=(count // ROWS,),
            in_specs=[
                pl.BlockSpec((ROWS, width), block),
                pl.BlockSpec((1, width), whole),
            ]
            + [pl.BlockSpec((depth, out_width), whole)] * planes
            + [
                pl.BlockSpec((1, HD), whole),
                pl.BlockSpec((1, HD), whole),
                pl.BlockSpec((ROWS, HD), block),
                pl.BlockSpec((ROWS, HD), block),
            ],
            out_specs=(
                pl.BlockSpec((ROWS, width), block),
                pl.BlockSpec((ROWS, pre_width), block),
                pl.BlockSpec((ROWS, out_width), block),
                pl.BlockSpec((width, out_width), whole),
            ),
        ),
        compiler_params=params(1, 56),
        cost_estimate=estimate(
            flops=2 * count * width * out_width,
            bytes_accessed=4 * count * width + 2 * width * out_width + 6 * count * out_width,
            transcendentals=0,
        ),
        name="qkv_project",
    )(places, rows, gain, *weights, gain_q, gain_k, cosine, sine)


def attn_kernel(
    scale, low_ref, high_ref, q_ref, k_ref, v_ref, sq_ref, sk_ref, o_ref, ol_ref, lse_ref, s_scr
):
    block = pl.program_id(1)
    low, high = low_ref[block], high_ref[block]
    q = q_ref[...]
    seg_q = sq_ref[...]
    half = ROWS // 2

    def scores(kb, top):
        at = pl.ds(pl.multiple_of(kb * ROWS, ROWS), ROWS)
        s = dot_nt(q, k_ref[at, :]) * scale
        s = jnp.where(seg_q == sk_ref[:, at], s, masked_score)
        s_scr[:, at] = s
        return jnp.maximum(top, jnp.maximum(s[:, :half], s[:, half:]))

    top = lax.fori_loop(low, high, scores, jnp.full((ROWS, half), masked_score, f32))
    top = jnp.max(top, axis=-1, keepdims=True)

    def weigh(kb, carry):
        total, acc = carry
        at = pl.ds(pl.multiple_of(kb * ROWS, ROWS), ROWS)
        p = jnp.exp(s_scr[:, at] - top)
        acc = acc + dot_nn(p.astype(bf16), v_ref[at, :])
        return total + (p[:, :half] + p[:, half:]), acc

    total, acc = lax.fori_loop(
        low, high, weigh, (jnp.zeros((ROWS, half), f32), jnp.zeros((ROWS, HD), f32))
    )
    total = jnp.sum(total, axis=-1, keepdims=True)
    out = acc / total
    o_ref[...] = out
    ol_ref[...] = out.astype(bf16)
    lse = jnp.broadcast_to(top + jnp.log(total), (ROWS, HD)).T
    lse_ref[0] = lse[0:1, :]


def attention(rot, seg_col, seg_row, low, high, heads):
    count = rot.shape[0]
    blocks = count // ROWS
    scale = HD ** (-0.5)
    return pl.pallas_call(
        functools.partial(attn_kernel, scale),
        out_shape=(
            jax.ShapeDtypeStruct((count, heads * HD), f32),
            jax.ShapeDtypeStruct((count, heads * HD), bf16),
            jax.ShapeDtypeStruct((heads * blocks, 1, ROWS), f32),
        ),
        grid_spec=pltpu.PrefetchScalarGridSpec(
            num_scalar_prefetch=2,
            grid=(heads, blocks),
            in_specs=[
                pl.BlockSpec((ROWS, HD), lambda h, i, *s: (i, h)),
                pl.BlockSpec((count, HD), lambda h, i, *s: (0, heads + h)),
                pl.BlockSpec((count, HD), lambda h, i, *s: (0, 2 * heads + h)),
                pl.BlockSpec((ROWS, 1), lambda h, i, *s: (i, 0)),
                pl.BlockSpec((1, count), lambda h, i, *s: (0, 0)),
            ],
            out_specs=(
                pl.BlockSpec((ROWS, HD), lambda h, i, *s: (i, h)),
                pl.BlockSpec((ROWS, HD), lambda h, i, *s: (i, h)),
                pl.BlockSpec((1, 1, ROWS), lambda h, i, *s: (h * blocks + i, 0, 0)),
            ),
            scratch_shapes=[pltpu.VMEM((ROWS, count), f32)],
        ),
        compiler_params=params(2, 32),
        cost_estimate=estimate(
            flops=2 * heads * count * count * HD,
            bytes_accessed=12 * heads * count * HD,
            transcendentals=heads * count * count // 2,
        ),
        name="attention",
    )(low, high, rot, rot, rot, seg_col, seg_row)


def head_back(grad, pre, gain, cosine, sine):
    n = grad * cosine - pltpu.roll(grad, HD // 2, 1) * sine
    inverse = lax.rsqrt(jnp.mean(pre * pre, axis=-1, keepdims=True) + head_eps)
    w = n * gain
    back = inverse * w - pre * inverse**3 * jnp.mean(w * pre, axis=-1, keepdims=True)
    return back, jnp.sum(n * pre * inverse, axis=0, keepdims=True)


def attn_back_kernel(
    scale,
    low_ref,
    high_ref,
    q_ref,
    k_ref,
    v_ref,
    do_ref,
    o_ref,
    lse_ref,
    sq_ref,
    sk_ref,
    qpre_ref,
    kpre_ref,
    gq_ref,
    gk_ref,
    cosq_ref,
    sinq_ref,
    cosk_ref,
    sink_ref,
    dq_ref,
    dk_ref,
    dv_ref,
    gain_ref,
    dk_scr,
    dv_scr,
):
    head, block = pl.program_id(0), pl.program_id(1)
    low, high = low_ref[block], high_ref[block]

    @pl.when(block == 0)
    def _():
        dk_scr[...] = jnp.zeros_like(dk_scr)
        dv_scr[...] = jnp.zeros_like(dv_scr)

    @pl.when((block == 0) & (head == 0))
    def _():
        gain_ref[...] = jnp.zeros_like(gain_ref)

    q, do = q_ref[...], do_ref[...]
    row_dot = jnp.sum((do.astype(f32) * o_ref[...]).T, axis=0, keepdims=True)
    lse = lse_ref[0]
    seg_q = sq_ref[...]

    def tile(kb, dq):
        at = pl.ds(pl.multiple_of(kb * ROWS, ROWS), ROWS)
        k, v = k_ref[at, :], v_ref[at, :]
        s = dot_nt(k, q) * scale
        p = jnp.where(sk_ref[at, :] == seg_q, jnp.exp(s - lse), 0.0)
        dp = dot_nt(v, do)
        ds = (p * (dp - row_dot)).astype(bf16)
        dv_scr[at, :] += dot_nn(p.astype(bf16), do)
        dk_scr[at, :] += dot_nn(ds, q)
        return dq + dot_tn(ds, k)

    dq = lax.fori_loop(low, high, tile, jnp.zeros((ROWS, HD), f32))
    back, gain_q = head_back(dq * scale, qpre_ref[...], gq_ref[...], cosq_ref[...], sinq_ref[...])
    dq_ref[...] = back.astype(bf16)
    gain_ref[0:1, :] += gain_q

    @pl.when(block == pl.num_programs(1) - 1)
    def _():
        @pl.loop(0, dk_scr.shape[0] // ROWS)
        def _(i):
            at = pl.ds(pl.multiple_of(i * ROWS, ROWS), ROWS)
            back, gain_k = head_back(
                dk_scr[at, :] * scale, kpre_ref[at, :], gk_ref[...], cosk_ref[at, :], sink_ref[at, :]
            )
            dk_ref[at, :] = back.astype(bf16)
            dv_ref[at, :] = dv_scr[at, :].astype(bf16)
            gain_ref[1:2, :] += gain_k


def attention_back(
    rot, grad, out, lse, seg_col, seg_row, low, high, pre, gain_q, gain_k, cosine, sine, heads
):
    count = rot.shape[0]
    blocks = count // ROWS
    scale = HD ** (-0.5)
    mine = lambda h, i, *s: (i, h)
    whole = lambda h, i, *s: (0, 0)
    return pl.pallas_call(
        functools.partial(attn_back_kernel, scale),
        out_shape=(
            jax.ShapeDtypeStruct((count, heads * HD), bf16),
            jax.ShapeDtypeStruct((count, heads * HD), bf16),
            jax.ShapeDtypeStruct((count, heads * HD), bf16),
            jax.ShapeDtypeStruct((8, HD), f32),
        ),
        grid_spec=pltpu.PrefetchScalarGridSpec(
            num_scalar_prefetch=2,
            grid=(heads, blocks),
            in_specs=[
                pl.BlockSpec((ROWS, HD), mine),
                pl.BlockSpec((count, HD), lambda h, i, *s: (0, heads + h)),
                pl.BlockSpec((count, HD), lambda h, i, *s: (0, 2 * heads + h)),
                pl.BlockSpec((ROWS, HD), mine),
                pl.BlockSpec((ROWS, HD), mine),
                pl.BlockSpec((1, 1, ROWS), lambda h, i, *s: (h * blocks + i, 0, 0)),
                pl.BlockSpec((1, ROWS), lambda h, i, *s: (0, i)),
                pl.BlockSpec((count, 1), whole),
                pl.BlockSpec((ROWS, HD), mine),
                pl.BlockSpec((count, HD), lambda h, i, *s: (0, heads + h)),
                pl.BlockSpec((1, HD), whole),
                pl.BlockSpec((1, HD), whole),
                pl.BlockSpec((ROWS, HD), lambda h, i, *s: (i, 0)),
                pl.BlockSpec((ROWS, HD), lambda h, i, *s: (i, 0)),
                pl.BlockSpec((count, HD), whole),
                pl.BlockSpec((count, HD), whole),
            ],
            out_specs=(
                pl.BlockSpec((ROWS, HD), mine),
                pl.BlockSpec((count, HD), lambda h, i, *s: (0, h)),
                pl.BlockSpec((count, HD), lambda h, i, *s: (0, h)),
                pl.BlockSpec((8, HD), whole),
            ),
            scratch_shapes=[pltpu.VMEM((count, HD), f32), pltpu.VMEM((count, HD), f32)],
        ),
        compiler_params=params(2, 48),
        cost_estimate=estimate(
            flops=5 * heads * count * count * HD,
            bytes_accessed=30 * heads * count * HD,
            transcendentals=heads * count * count // 2,
        ),
        name="attention_back",
    )(
        low,
        high,
        rot,
        rot,
        rot,
        grad,
        out,
        lse,
        seg_row,
        seg_col,
        pre,
        pre,
        gain_q,
        gain_k,
        cosine,
        sine,
        cosine,
        sine,
    )


def expert_kernel(base, count, carried, mine_ref, x_ref, *refs):
    near = 1 if base == 0 else 0
    c_refs, refs = refs[: near + 1], refs[near + 1 :]
    wg_ref, wu_ref, wd_ref = refs[:3]
    refs = refs[3 + carried :]
    back_ref, out_ref, xs_ref, c_ref, hid_ref, gp_ref, up_ref = refs[:7]
    out_acc, back_acc, gate_scr, dot_scr = refs[7:]
    step = pl.program_id(1)
    per_plane, capacity, width = c_ref.shape
    rows = per_plane * capacity
    extra = x_ref.shape[2] - width
    lane = lax.broadcasted_iota(jnp.int32, (rows, extra), 1)
    high, low = lane == mine_ref[0], lane == mine_ref[0] + count

    @pl.when(step == 0)
    def _():
        xs_ref[...] = x_ref[:, :, :width]
        if near:

            @pl.when(pl.program_id(0) == 0)
            def _():
                c_ref[...] = c_refs[0][...]

            @pl.when(pl.program_id(0) > 0)
            def _():
                c_ref[...] = c_refs[1][...]

        else:
            c_ref[...] = c_refs[0][...]
        gates = x_ref[:, :, width:].reshape(rows, extra).astype(f32)
        gate_scr[...] = jnp.sum(jnp.where(high | low, gates, 0.0), axis=-1, keepdims=True)
        out_acc[...] = jnp.zeros_like(out_acc)
        back_acc[...] = jnp.zeros_like(back_acc)
        dot_scr[...] = jnp.zeros_like(dot_scr)

    x = x_ref[:, :, :width].reshape(rows, width)
    c = c_ref[...].reshape(rows, width)
    gate = gate_scr[...]
    wg, wu, wd = wg_ref[...], wu_ref[...], wd_ref[...]
    gate_pre, up_pre = dot_nn(x, wg), dot_nn(x, wu)
    sig = jax.nn.sigmoid(gate_pre)
    hidden = (gate_pre * sig * up_pre).astype(bf16)
    out_acc[...] += dot_nn(hidden, wd)
    plain = dot_nt(c, wd)
    wide = hidden.astype(f32)
    dot_scr[...] += jnp.sum(wide * plain, axis=-1, keepdims=True)
    hid_ref[...] = (wide * gate).astype(bf16).reshape(hid_ref.shape)
    hidden_grad = plain * gate
    gate_grad = (hidden_grad * up_pre * sig * (1.0 + gate_pre * (1.0 - sig))).astype(bf16)
    up_grad = (hidden_grad * gate_pre * sig).astype(bf16)
    gp_ref[...] = gate_grad.reshape(gp_ref.shape)
    up_ref[...] = up_grad.reshape(up_ref.shape)
    back_acc[...] += dot_nt(gate_grad, wg) + dot_nt(up_grad, wu)

    @pl.when(step == pl.num_programs(1) - 1)
    def _():
        dots = dot_scr[...]
        coarse = dots.astype(bf16).astype(f32)
        lanes = jnp.where(high, coarse, jnp.where(low, dots - coarse, 0.0)).astype(bf16)
        back_ref[:, :, :width] = back_acc[...].astype(bf16).reshape(c_ref.shape)
        back_ref[:, :, width:] = lanes.reshape(per_plane, capacity, extra)
        out_ref[...] = (out_acc[...] * gate).astype(bf16).reshape(out_ref.shape)


def experts(mine, x, near, far, wg, wu, wd, base, planes, count, kept):
    per_plane, blocks, capacity, wide = x.shape
    width = near.shape[3]
    halves, _, hidden = wg.shape
    rows = per_plane * capacity
    saved = jax.ShapeDtypeStruct((per_plane, planes, capacity, width), bf16)
    thin = jax.ShapeDtypeStruct((per_plane, planes, capacity, halves * hidden), bf16)
    moved = pl.BlockSpec((per_plane, None, capacity, wide), lambda i, f, s: (0, i, 0, 0))
    saved_spec = pl.BlockSpec((per_plane, None, capacity, width), lambda i, f, s: (0, base + i, 0, 0))
    thin_spec = pl.BlockSpec((per_plane, None, capacity, hidden), lambda i, f, s: (0, base + i, 0, f))
    carried = 0 if kept is None else len(kept)
    cots = (near, far) if base == 0 else (far,)
    cot_specs = [
        pl.BlockSpec(
            (per_plane, None, capacity, width), lambda i, f, s: (0, jnp.maximum(base + i - 1, 0), 0, 0)
        )
    ]
    if base == 0:
        cot_specs = [pl.BlockSpec((per_plane, None, capacity, width), lambda i, f, s: (0, 0, 0, 0))] + cot_specs
    result = pl.pallas_call(
        functools.partial(expert_kernel, base, count, carried),
        out_shape=(jax.ShapeDtypeStruct(x.shape, bf16), saved, saved, saved, thin, thin, thin),
        grid_spec=pltpu.PrefetchScalarGridSpec(
            num_scalar_prefetch=1,
            grid=(blocks, halves),
            in_specs=[
                moved,
                *cot_specs,
                pl.BlockSpec((None, width, hidden), lambda i, f, s: (f, 0, 0)),
                pl.BlockSpec((None, width, hidden), lambda i, f, s: (f, 0, 0)),
                pl.BlockSpec((None, hidden, width), lambda i, f, s: (f, 0, 0)),
            ]
            + [pl.BlockSpec(memory_space=pl.ANY)] * carried,
            out_specs=(moved, saved_spec, saved_spec, saved_spec, thin_spec, thin_spec, thin_spec),
            scratch_shapes=[
                pltpu.VMEM((rows, width), f32),
                pltpu.VMEM((rows, width), f32),
                pltpu.VMEM((rows, 1), f32),
                pltpu.VMEM((rows, 1), f32),
            ],
        ),
        input_output_aliases={5 + len(cots) + i: 1 + i for i in range(carried)},
        compiler_params=params(2, 60),
        cost_estimate=estimate(
            flops=12 * blocks * rows * width * hidden * halves,
            bytes_accessed=10 * blocks * rows * width + 6 * blocks * width * hidden * halves,
            transcendentals=blocks * rows * hidden * halves,
        ),
        name="experts",
    )(mine, x, *cots, wg, wu, wd, *(kept or ()))
    return result[0], result[1:]


def gram_kernel(plus, left_ref, right_ref, *refs):
    total = dot_tn(left_ref[...], right_ref[...])
    if plus:
        total = total + refs[0][...]
    refs[-1][...] = total.astype(refs[-1].dtype)


def gram(left, right, left_cols, right_cols, dtype, plus=None):
    rows = left.shape[0]
    left_at, left_count = left_cols
    right_at, right_count = right_cols
    tall = min(left_count, 256)
    wide = min(right_count, 1024)
    out_spec = pl.BlockSpec((tall, wide), lambda j, i: (i, j))
    return pl.pallas_call(
        functools.partial(gram_kernel, plus is not None),
        out_shape=jax.ShapeDtypeStruct((left_count, right_count), dtype),
        grid=(right_count // wide, left_count // tall),
        in_specs=[
            pl.BlockSpec((rows, tall), lambda j, i: (0, left_at // tall + i)),
            pl.BlockSpec((rows, wide), lambda j, i: (0, right_at // wide + j)),
        ]
        + [out_spec] * (plus is not None),
        out_specs=out_spec,
        compiler_params=params(2, 48),
        cost_estimate=estimate(
            flops=2 * rows * left_count * right_count,
            bytes_accessed=2 * rows * (left_count + right_count) + 4 * left_count * right_count,
            transcendentals=0,
        ),
        name="gram",
    )(left, right, *(() if plus is None else (plus,)))


def project_kernel(plus, core_ref, rows_ref, weights_ref, *refs):
    total = dot_nt(rows_ref[...], weights_ref[...])
    if plus:
        total = total + refs[0][...].astype(f32)
    refs[-1][...] = total.astype(bf16)


def project_back(core, rows, weights, tok_rows, plus=None):
    count, depth = rows.shape
    width = weights.shape[0]
    chips = count // tok_rows // 2
    out_spec = pl.BlockSpec((tok_rows, width), lambda i, s: (i, 0))
    return pl.pallas_call(
        functools.partial(project_kernel, plus is not None),
        out_shape=jax.ShapeDtypeStruct((chips * tok_rows, width), bf16),
        grid_spec=pltpu.PrefetchScalarGridSpec(
            num_scalar_prefetch=1,
            grid=(chips,),
            in_specs=[
                pl.BlockSpec((tok_rows, depth), lambda i, s: (2 * i + s[0], 0)),
                pl.BlockSpec((width, depth), lambda i, s: (0, 0)),
            ]
            + [out_spec] * (plus is not None),
            out_specs=out_spec,
        ),
        compiler_params=params(1, 40),
        cost_estimate=estimate(
            flops=count * depth * width,
            bytes_accessed=2 * width * depth + count * depth + count * width,
            transcendentals=0,
        ),
        name="project_back",
    )(core, rows, weights, *(() if plus is None else (plus,)))


def after(value, *others):
    return lax.optimization_barrier((value,) + others)[0]


def body(
    hidden_in,
    out_cotangent,
    segment_number,
    expert_routes,
    pair_order,
    norm_gain,
    query_weight,
    key_weight,
    value_weight,
    output_weight,
    query_gain,
    key_gain,
    ffn_norm_gain,
    router_weight,
    expert_gate,
    expert_up,
    expert_down,
):
    tok_rows, width = hidden_in.shape
    devices = lax.axis_size(AXIS)
    members = max(1, SEQ_MIN // tok_rows)
    planes = devices // members
    per_plane = members // 2
    expert_count = devices // 2
    capacity = tok_rows * TOPK // expert_count
    heads = width // HD // members
    head_width = heads * HD
    own_rows = norm_gain.shape[0]
    seq = members * tok_rows
    me = lax.axis_index(AXIS)
    plane, member = me // members, me % members
    mine = (me // 2).astype(jnp.int32).reshape(1)
    first = (plane * per_plane).astype(jnp.int32)
    places = (plane ^ jnp.arange(planes, dtype=jnp.int32)).astype(jnp.int32)
    counted = jnp.concatenate([first[None], jnp.arange(planes, dtype=jnp.int32)])
    halfway = -(-planes // 2)
    chunks = [part for part in (range(halfway), range(halfway, planes)) if len(part)]

    def placed(part):
        return jnp.concatenate([first[None], places[part.start : part.stop]])

    plane_groups = [[g * members + j for j in range(members)] for g in range(planes)]
    stack_groups = [[g * members + j for g in range(planes)] for j in range(members)]
    core_groups = [
        [g * members + 2 * c + h for c in range(per_plane)] for g in range(planes) for h in (0, 1)
    ]

    def exchange(value, groups=None):
        return lax.all_to_all(
            value, AXIS, split_axis=0, concat_axis=0, tiled=True, axis_index_groups=groups
        )

    def gather(value, groups=None):
        return lax.all_gather(value, AXIS, axis=0, tiled=True, axis_index_groups=groups)

    def flip(value, bits):
        if bits == 0:
            return value
        return lax.ppermute(value, AXIS, [(i, i ^ bits) for i in range(devices)])

    def to_core(value):
        return flip(value, 1)

    def to_plane(value, d):
        return flip(value, members * d)

    def over_stack(value):
        return lax.psum_scatter(
            value.reshape(planes * tok_rows, -1),
            AXIS,
            scatter_dimension=0,
            tiled=True,
            axis_index_groups=stack_groups,
        )

    wire, core_op = [], []

    def on_wire(value, groups):
        came = exchange(after(value, *wire[-1:]), groups)
        wire.append(came)
        return came

    def to_chips(value):
        return on_wire(value, core_groups)

    def in_turn(value):
        return after(value, *core_op[-1:])

    def ran(value):
        core_op.append(value)
        return value

    pieces = (
        router_weight.reshape(-1),
        norm_gain,
        ffn_norm_gain,
        query_gain,
        key_gain,
        segment_number.astype(bf16),
    )
    packed = jnp.concatenate(pieces)
    length = packed.shape[0]
    padded = -(-length // 128) * 128
    packed = jnp.pad(packed, (0, padded - length))
    packed = on_wire(jnp.broadcast_to(packed[None], (devices, padded)), None)
    small = []
    at = 0
    for piece in pieces:
        small.append(packed[:, at : at + piece.shape[0]])
        at += piece.shape[0]
    router_full = small[0].reshape(width, expert_count)
    gain_one = small[1].reshape(1, width).astype(f32)
    gain_two = small[2].reshape(1, width).astype(f32)
    gain_q = small[3].reshape(1, HD).astype(f32)
    gain_k = small[4].reshape(1, HD).astype(f32)
    segments = lax.dynamic_slice_in_dim(small[5], plane * members, members, 0).astype(f32)
    seg_row, seg_col = segments.reshape(1, seq), segments.reshape(seq, 1)
    seg_blocks = segments.reshape(seq // ROWS, ROWS)
    seg_first, seg_last = seg_blocks[:, 0], seg_blocks[:, -1]
    low = jnp.sum((seg_last[None, :] < seg_first[:, None]).astype(jnp.int32), axis=1)
    high = jnp.sum((seg_first[None, :] <= seg_last[:, None]).astype(jnp.int32), axis=1)

    columns = jnp.concatenate(
        [w.reshape(own_rows, members, head_width) for w in (query_weight, key_weight, value_weight)],
        axis=2,
    )
    slots = block_slots(expert_routes, pair_order, expert_count)
    columns = on_wire(
        after(columns, slots).transpose(1, 0, 2).reshape(members * own_rows, 3 * head_width), plane_groups
    )
    slots = [to_plane(slots, d) for d in range(planes)]
    weights = [to_plane(after(columns, *slots), d) for d in range(planes)]
    rows_all = gather(hidden_in, plane_groups)
    output_full = gather(after(output_weight, columns), stack_groups)

    cot_own = dispatch(counted, slots[0][None], out_cotangent[None], per_plane, capacity)
    cot_parts = [to_chips(cot_own)]
    output_full = gather(after(output_full, cot_own, *weights), plane_groups)
    slots = jnp.stack(slots)
    cot_rows = {0: out_cotangent}
    top = planes // 2
    early, late = [], []
    if planes > 1:
        cot_rows[top] = to_plane(after(out_cotangent, *weights), top)
        early.append(cot_rows[top])
    for d in range(1, planes):
        if d != top:
            lowest = d & -d
            start = after(out_cotangent, *early) if d == lowest else cot_rows[d ^ lowest]
            cot_rows[d] = to_plane(start, lowest)
            late.append(cot_rows[d])

    halves = lambda w: jnp.concatenate([w, to_core(w)], axis=0)
    wg, wu, wd = halves(expert_gate), halves(expert_up), halves(expert_down)

    cosine, sine = rope_tables(seq)
    act_one, pre, rot, ordered = qkv_project(
        places, rows_all, gain_one, weights, gain_q, gain_k, cosine, sine, heads
    )
    out_wide, out_heads, lse = attention(rot, seg_col, seg_row, low, high, heads)
    out_low = on_wire(after(out_heads, *early), plane_groups)
    out_low = out_low.reshape(members, tok_rows, head_width).transpose(1, 0, 2)
    out_low = out_low.reshape(tok_rows, planes, members, own_rows).transpose(0, 2, 1, 3)
    out_low = after(out_low.reshape(tok_rows, width), wg, wu, wd)
    tokens = hidden_in.astype(f32)
    cotangent = out_cotangent.astype(f32)
    middle = tokens + dot_nn(out_low, output_full)
    inverse_two = lax.rsqrt(jnp.mean(middle * middle, axis=-1, keepdims=True) + norm_eps)
    act_two = (middle * inverse_two * gain_two).astype(bf16)

    logits = dot_nn(act_two, router_full)
    expert_ids = jnp.arange(expert_count, dtype=jnp.int32)
    routed = jnp.any(expert_routes[:, :, None] == expert_ids[None, None, :], axis=1)
    logits = jnp.where(routed, logits, masked_score)
    gates = jnp.where(routed, jnp.exp(logits - jnp.max(logits, axis=1, keepdims=True)), 0.0)
    gates = gates / jnp.sum(gates, axis=1, keepdims=True)
    coarse = lax.reduce_precision(gates, 8, 7)
    extra = -(-2 * expert_count // 128) * 128
    act_wide = jnp.concatenate(
        [
            act_two,
            coarse.astype(bf16),
            (gates - coarse).astype(bf16),
            jnp.zeros((tok_rows, extra - 2 * expert_count), bf16),
        ],
        axis=1,
    )

    act_wide = after(act_wide, *late)
    act_all = gather(act_wide, stack_groups).reshape(planes, tok_rows, -1)
    if planes > 1:
        far = jnp.stack([after(cot_rows[d], act_wide) for d in range(1, planes)])
        sent = dispatch(counted[:planes], slots[1:], far, per_plane, capacity)
        cot_parts.append(to_chips(ran(sent)))

    act = []
    for part in chunks:
        own_slots = slots[part.start : part.stop]
        sent = dispatch(placed(part), own_slots, in_turn(act_all), per_plane, capacity)
        act.append(to_chips(ran(sent)))
    kept, back = None, []
    for part, rows in zip(chunks, act):
        sent, kept = experts(
            mine,
            in_turn(rows),
            cot_parts[0],
            cot_parts[-1],
            wg,
            wu,
            wd,
            part.start,
            planes,
            expert_count,
            kept,
        )
        back.append(to_chips(ran(sent)))
    out_all, x_all, c_all, hid_all, gp_all, up_all = kept

    hidden = expert_gate.shape[2]
    flat = lambda value: value.reshape(-1, value.shape[3])
    sides = (
        (flat(x_all), flat(gp_all), 1),
        (flat(x_all), flat(up_all), 1),
        (flat(hid_all), flat(c_all), 0),
    )

    def half(side, which, plus=None):
        left, right, split = side
        cut, whole = (which * hidden, hidden), (0, width)
        cols = (whole, cut) if split else (cut, whole)
        return gram(left, right, *cols, f32, plus)

    theirs = [half(side, 1) for side in sides]
    core_op.extend(theirs)
    theirs = [to_core(grad) for grad in theirs]
    returned = None
    for part, rows in zip(chunks, back):
        own_slots = slots[part.start : part.stop]
        rows = after(rows, *core_op[-3:])
        returned = ran(combine(placed(part), own_slots, rows, planes, returned))
    back_sum = over_stack(returned)
    outs = to_chips(out_all)
    grad_gate, grad_up, grad_down = (
        half(side, 0, other) for side, other in zip(sides, theirs)
    )

    back_sum = after(back_sum, grad_gate, grad_up, grad_down).astype(f32)
    expert_in_grad = back_sum[:, :width]
    gate_grad = (
        back_sum[:, width : width + expert_count]
        + back_sum[:, width + expert_count : width + 2 * expert_count]
    )
    select_grad = gates * (gate_grad - jnp.sum(gates * gate_grad, axis=1, keepdims=True))
    logit_grad = select_grad.astype(bf16)
    grad_router = dot_tn(act_two, logit_grad)
    act_two_grad = expert_in_grad + dot_nt(logit_grad, router_full)
    weighted = act_two_grad * gain_two
    grad_gain_two = jnp.sum(act_two_grad * middle * inverse_two, axis=0)
    middle_grad = (
        cotangent
        + inverse_two * weighted
        - middle * inverse_two**3 * jnp.mean(weighted * middle, axis=-1, keepdims=True)
    )
    middle_low = middle_grad.astype(bf16)

    out_grad = dot_nt(middle_low, output_full).astype(bf16)
    out_grad = out_grad.reshape(tok_rows, members, planes, own_rows).transpose(0, 2, 1, 3)
    out_grad = out_grad.reshape(tok_rows, members, head_width).transpose(1, 0, 2)
    out_grad = out_grad.reshape(seq, head_width)
    outs = after(outs, out_grad)
    out_grad = on_wire(out_grad, plane_groups)
    mixed = combine(placed(range(planes)), slots, outs, planes)
    mixture = over_stack(mixed)
    layer_out = (middle + mixture.astype(f32)).astype(bf16)
    dq, dk, dv, grad_gains = attention_back(
        rot,
        after(out_grad, mixed),
        out_wide,
        lse,
        seg_col,
        seg_row,
        low,
        high,
        pre,
        gain_q,
        gain_k,
        cosine,
        sine,
        heads,
    )
    dqkv = jnp.concatenate([dq, dk, dv], axis=1)
    middle_all = gather(after(middle_low, dq), plane_groups)

    sums = (
        grad_router.reshape(devices, -1),
        grad_gain_two.reshape(devices, -1),
        grad_gains[0].reshape(devices, -1),
        grad_gains[1].reshape(devices, -1),
    )
    packed = jnp.concatenate(sums, axis=1)
    length = packed.shape[1]
    padded = -(-length // 128) * 128
    packed = jnp.pad(packed, ((0, 0), (0, padded - length)))

    core = (me % 2).astype(jnp.int32).reshape(1)
    part = gram(act_one, dqkv, (0, width), (0, 3 * head_width), bf16)
    part = part.reshape(planes, members * own_rows, 3 * head_width)
    shares = [lax.dynamic_index_in_dim(part, places[d], 0, False) for d in range(planes)]
    given = to_core(project_back(1 - core, after(dqkv, *shares), ordered, tok_rows))
    taken = sum(to_plane(share, d).astype(f32) for d, share in enumerate(shares)).astype(bf16)
    act_one_grad = project_back(core, after(dqkv, mixture), ordered, tok_rows, given)
    act_one_grad = exchange(act_one_grad, core_groups)

    output_part = gram(out_heads, middle_all, (0, head_width), (0, width), bf16)
    output_part = output_part.reshape(planes, head_width // planes, width)
    grad_output = 0.0
    for d in range(planes):
        to_owner = [
            (g * members + j, j * planes + (g ^ d)) for g in range(planes) for j in range(members)
        ]
        rows = lax.dynamic_index_in_dim(output_part, places[d], 0, False)
        grad_output = grad_output + lax.ppermute(rows, AXIS, to_owner).astype(f32)
    packed, act_one_grad = lax.optimization_barrier((packed, act_one_grad))
    packed = exchange(packed)
    taken, packed, grad_output = lax.optimization_barrier((taken, packed, grad_output))
    part = exchange(taken, plane_groups).reshape(members, own_rows, 3, head_width)
    part = part.transpose(2, 1, 0, 3).reshape(3, own_rows, width).astype(f32)
    grad_query, grad_key, grad_value = part[0], part[1], part[2]
    act_one_grad = act_one_grad.reshape(per_plane, tok_rows, width)
    act_one_grad = jnp.sum(act_one_grad.astype(f32), axis=0)

    inverse_one = lax.rsqrt(jnp.mean(tokens * tokens, axis=-1, keepdims=True) + norm_eps)
    weighted = act_one_grad * gain_one
    grad_hidden = (
        middle_grad
        + inverse_one * weighted
        - tokens * inverse_one**3 * jnp.mean(weighted * tokens, axis=-1, keepdims=True)
    )
    grad_gain_one = (
        jnp.sum(
            grad_query * query_weight.astype(f32)
            + grad_key * key_weight.astype(f32)
            + grad_value * value_weight.astype(f32),
            axis=1,
        )
        / norm_gain.astype(f32)
    )

    summed = jnp.sum(packed, axis=0)
    at, tiny = 0, []
    for piece in sums:
        tiny.append(summed[at : at + piece.shape[1]])
        at += piece.shape[1]

    return (
        layer_out,
        grad_hidden,
        grad_gain_one,
        grad_query,
        grad_key,
        grad_value,
        grad_output,
        tiny[2],
        tiny[3],
        tiny[1],
        tiny[0].reshape(own_rows, expert_count),
        grad_gate[None],
        grad_up[None],
        grad_down[None],
    )


def solution(mesh):
    row, mat, cube = P(AXIS), P(AXIS, None), P(AXIS, None, None)
    return jax.shard_map(
        body,
        mesh=mesh,
        in_specs=(mat, mat, row, mat, mat, row, mat, mat, mat, mat, row, row, row, mat)
        + (cube,) * 3,
        out_specs=(mat, mat, row, mat, mat, mat, mat, row, row, row, mat) + (cube,) * 3,
        check_vma=False,
    )
```

```python
import functools
import math

import jax
import jax.numpy as jnp
from jax import lax
from jax.experimental import pallas as pl
from jax.experimental.pallas import tpu as pltpu
from jax.sharding import PartitionSpec as P

HD = 128
TOPK = 8
SEQ_MIN = 2048
ROWS = 256
SHARE = 32

norm_eps = 1e-05
head_eps = 1e-06
rope_base = 10000.0
masked_score = -1e30
absent_slot = 4096.0

AXIS = "fsdp"
f32 = jnp.float32
bf16 = jnp.bfloat16
MIB = 1 << 20


def dot_nt(left, right):
    return lax.dot_general(left, right, (((1,), (1,)), ((), ())), preferred_element_type=f32)


def dot_tn(left, right):
    return lax.dot_general(left, right, (((0,), (0,)), ((), ())), preferred_element_type=f32)


def dot_nn(left, right):
    return lax.dot_general(left, right, (((1,), (0,)), ((), ())), preferred_element_type=f32)


def params(steps, mib):
    return pltpu.CompilerParams(
        dimension_semantics=("arbitrary",) * steps, vmem_limit_bytes=mib * MIB
    )


def estimate(flops, bytes_accessed, transcendentals):
    return pl.CostEstimate(
        flops=flops // SHARE, bytes_accessed=bytes_accessed // SHARE, transcendentals=transcendentals // SHARE
    )


def rope_tables(count):
    half_width = HD // 2
    frequency = jnp.exp(-math.log(rope_base) * 2.0 * jnp.arange(half_width, dtype=f32) / HD)
    angles = jnp.arange(count, dtype=f32)[:, None] * frequency[None, :]
    cosine, sine = jnp.cos(angles), jnp.sin(angles)
    return jnp.concatenate([cosine, cosine], axis=-1), jnp.concatenate([-sine, sine], axis=-1)


def slots_kernel(expert_count, routes_ref, order_ref, slots_ref):
    tok_rows = routes_ref.shape[0]
    pair_count = order_ref.shape[1]
    order = order_ref[...]
    shift = TOPK.bit_length() - 1
    token_of = lax.shift_right_logical(order, jnp.full_like(order, shift))
    route_of = order & (TOPK - 1)
    token_iota = lax.broadcasted_iota(jnp.int32, (tok_rows, pair_count), 0)
    token_hot = jnp.where(token_iota == token_of, 1.0, 0.0).astype(bf16)
    place = lax.broadcasted_iota(jnp.int32, (TOPK, pair_count), 1)
    chosen = lax.broadcasted_iota(jnp.int32, (TOPK, pair_count), 0) == route_of
    high = lax.shift_right_logical(place, jnp.full_like(place, 8)).astype(f32)
    low = (place & 255).astype(f32)
    digits = jnp.concatenate([jnp.where(chosen, high, 0.0), jnp.where(chosen, low, 0.0)], axis=0)
    found = dot_nt(token_hot, digits.astype(bf16))
    rank = found[:, :TOPK] * 256.0 + found[:, TOPK:]
    routes = routes_ref[...]
    lanes = -(-expert_count // 128) * 128
    expert_iota = lax.broadcasted_iota(jnp.int32, (tok_rows, lanes), 1)
    never = 1e9
    by_expert = jnp.full((tok_rows, lanes), never, f32)
    for k in range(TOPK):
        by_expert = jnp.where(expert_iota == routes[:, k : k + 1], rank[:, k : k + 1], by_expert)
    turned = by_expert.T
    for e in range(expert_count):
        mine = turned[e : e + 1, :]
        earlier = jnp.where(by_expert[:, e : e + 1] < mine, 1.0, 0.0)
        count = jnp.sum(earlier, axis=0, keepdims=True)
        slots_ref[e : e + 1, :] = jnp.where(mine < never, count, absent_slot)


def block_slots(routes, order, expert_count):
    tok_rows = routes.shape[0]
    return pl.pallas_call(
        functools.partial(slots_kernel, expert_count),
        out_shape=jax.ShapeDtypeStruct((expert_count, tok_rows), f32),
        compiler_params=pltpu.CompilerParams(vmem_limit_bytes=32 * MIB),
        name="block_slots",
    )(routes, order)


def slot_hot(slots_ref, expert, capacity):
    slot_row = slots_ref[pl.ds(expert, 1), :]
    slot_iota = lax.broadcasted_iota(jnp.int32, (capacity, slot_row.shape[1]), 0).astype(f32)
    return jnp.where(slot_iota == slot_row, 1.0, 0.0).astype(bf16)


def plane_hot(slots_ref, first, shape):
    return jnp.concatenate([slot_hot(slots_ref, first + r, shape[1]) for r in range(shape[0])])


def dispatch_kernel(at_ref, slots_ref, rows_ref, out_ref):
    hot = plane_hot(slots_ref, at_ref[0], out_ref.shape)
    out_ref[...] = dot_nn(hot, rows_ref[...]).astype(bf16).reshape(out_ref.shape)


def dispatch(at, slots, rows, per_plane, capacity):
    blocks, experts, tok_rows = slots.shape
    width = rows.shape[2]
    slot_rows = per_plane * capacity
    return pl.pallas_call(
        dispatch_kernel,
        out_shape=jax.ShapeDtypeStruct((per_plane, blocks, capacity, width), bf16),
        grid_spec=pltpu.PrefetchScalarGridSpec(
            num_scalar_prefetch=1,
            grid=(blocks,),
            in_specs=[
                pl.BlockSpec((None, experts, tok_rows), lambda i, s: (i, 0, 0)),
                pl.BlockSpec((None, tok_rows, width), lambda i, s: (s[1 + i], 0, 0)),
            ],
            out_specs=pl.BlockSpec((per_plane, None, capacity, width), lambda i, s: (0, i, 0, 0)),
        ),
        compiler_params=params(1, 40),
        cost_estimate=estimate(
            flops=2 * blocks * slot_rows * tok_rows * width,
            bytes_accessed=2 * blocks * (slot_rows + tok_rows) * width,
            transcendentals=0,
        ),
        name="dispatch",
    )(at, slots, rows)


def combine_kernel(first_ref, slots_ref, rows_ref, out_ref):
    hot = plane_hot(slots_ref, first_ref[0], rows_ref.shape)
    rows = rows_ref[...].reshape(hot.shape[0], rows_ref.shape[2])
    out_ref[...] = dot_tn(hot, rows).astype(bf16)


def combine(first, slots, rows, block):
    experts, tok_rows = slots.shape
    per_plane, _, capacity, width = rows.shape
    slot_rows = per_plane * capacity
    return pl.pallas_call(
        combine_kernel,
        out_shape=jax.ShapeDtypeStruct((tok_rows, width), bf16),
        grid_spec=pltpu.PrefetchScalarGridSpec(
            num_scalar_prefetch=1,
            grid=(1,),
            in_specs=[
                pl.BlockSpec((experts, tok_rows), lambda i, s: (0, 0)),
                pl.BlockSpec((per_plane, None, capacity, width), lambda i, s: (0, block, 0, 0)),
            ],
            out_specs=pl.BlockSpec((tok_rows, width), lambda i, s: (0, 0)),
        ),
        compiler_params=params(1, 40),
        cost_estimate=estimate(
            flops=2 * slot_rows * tok_rows * width,
            bytes_accessed=2 * (slot_rows + tok_rows) * width,
            transcendentals=0,
        ),
        name="combine",
    )(first, slots, rows)


def qkv_kernel(heads, planes, at_ref, x_ref, gain_ref, *refs):
    w_refs = refs[:planes]
    gq_ref, gk_ref, cos_ref, sin_ref, act_ref, pre_ref, rot_ref, all_ref = refs[planes:]
    depth = w_refs[0].shape[0]

    @pl.when(pl.program_id(0) == 0)
    def _():
        for d in range(planes):
            place = pl.ds(pl.multiple_of(at_ref[d] * depth, depth), depth)
            all_ref[place, :] = w_refs[d][...]

    x = x_ref[...].astype(f32)
    inverse = lax.rsqrt(jnp.mean(x * x, axis=-1, keepdims=True) + norm_eps)
    act = (x * inverse * gain_ref[...]).astype(bf16)
    act_ref[...] = act
    y = None
    for d in range(planes):
        columns = pl.ds(pl.multiple_of(at_ref[d] * depth, depth), depth)
        term = dot_nn(act_ref[:, columns], w_refs[d][...])
        y = term if y is None else y + term
    cosine, sine = cos_ref[...], sin_ref[...]
    for part, gain in enumerate((gq_ref[...], gk_ref[...])):
        for h in range(heads):
            at = (part * heads + h) * HD
            u = y[:, at : at + HD]
            pre_ref[:, at : at + HD] = u
            n = u * lax.rsqrt(jnp.mean(u * u, axis=-1, keepdims=True) + head_eps) * gain
            rot_ref[:, at : at + HD] = (n * cosine + pltpu.roll(n, HD // 2, 1) * sine).astype(bf16)
    at = 2 * heads * HD
    rot_ref[:, at:] = y[:, at:].astype(bf16)


def qkv_project(places, rows, gain, weights, gain_q, gain_k, cosine, sine, heads):
    count, width = rows.shape
    planes = len(weights)
    depth, out_width = weights[0].shape
    pre_width = 2 * heads * HD
    whole = lambda i, s: (0, 0)
    block = lambda i, s: (i, 0)
    return pl.pallas_call(
        functools.partial(qkv_kernel, heads, planes),
        out_shape=(
            jax.ShapeDtypeStruct((count, width), bf16),
            jax.ShapeDtypeStruct((count, pre_width), f32),
            jax.ShapeDtypeStruct((count, out_width), bf16),
            jax.ShapeDtypeStruct((width, out_width), bf16),
        ),
        grid_spec=pltpu.PrefetchScalarGridSpec(
            num_scalar_prefetch=1,
            grid=(count // ROWS,),
            in_specs=[
                pl.BlockSpec((ROWS, width), block),
                pl.BlockSpec((1, width), whole),
            ]
            + [pl.BlockSpec((depth, out_width), whole)] * planes
            + [
                pl.BlockSpec((1, HD), whole),
                pl.BlockSpec((1, HD), whole),
                pl.BlockSpec((ROWS, HD), block),
                pl.BlockSpec((ROWS, HD), block),
            ],
            out_specs=(
                pl.BlockSpec((ROWS, width), block),
                pl.BlockSpec((ROWS, pre_width), block),
                pl.BlockSpec((ROWS, out_width), block),
                pl.BlockSpec((width, out_width), whole),
            ),
        ),
        compiler_params=params(1, 56),
        cost_estimate=estimate(
            flops=2 * count * width * out_width,
            bytes_accessed=4 * count * width + 2 * width * out_width + 6 * count * out_width,
            transcendentals=0,
        ),
        name="qkv_project",
    )(places, rows, gain, *weights, gain_q, gain_k, cosine, sine)


def attn_kernel(
    scale, low_ref, high_ref, q_ref, k_ref, v_ref, sq_ref, sk_ref, o_ref, ol_ref, lse_ref, s_scr
):
    block = pl.program_id(1)
    low, high = low_ref[block], high_ref[block]
    q = q_ref[...]
    seg_q = sq_ref[...]
    half = ROWS // 2

    def scores(kb, top):
        at = pl.ds(pl.multiple_of(kb * ROWS, ROWS), ROWS)
        s = dot_nt(q, k_ref[at, :]) * scale
        s = jnp.where(seg_q == sk_ref[:, at], s, masked_score)
        s_scr[:, at] = s
        return jnp.maximum(top, jnp.maximum(s[:, :half], s[:, half:]))

    top = lax.fori_loop(low, high, scores, jnp.full((ROWS, half), masked_score, f32))
    top = jnp.max(top, axis=-1, keepdims=True)

    def weigh(kb, carry):
        total, acc = carry
        at = pl.ds(pl.multiple_of(kb * ROWS, ROWS), ROWS)
        p = jnp.exp(s_scr[:, at] - top)
        acc = acc + dot_nn(p.astype(bf16), v_ref[at, :])
        return total + (p[:, :half] + p[:, half:]), acc

    total, acc = lax.fori_loop(
        low, high, weigh, (jnp.zeros((ROWS, half), f32), jnp.zeros((ROWS, HD), f32))
    )
    total = jnp.sum(total, axis=-1, keepdims=True)
    out = acc / total
    o_ref[...] = out
    ol_ref[...] = out.astype(bf16)
    lse = jnp.broadcast_to(top + jnp.log(total), (ROWS, HD)).T
    lse_ref[0] = lse[0:1, :]


def attention(rot, seg_col, seg_row, low, high, heads):
    count = rot.shape[0]
    blocks = count // ROWS
    scale = HD ** (-0.5)
    return pl.pallas_call(
        functools.partial(attn_kernel, scale),
        out_shape=(
            jax.ShapeDtypeStruct((count, heads * HD), f32),
            jax.ShapeDtypeStruct((count, heads * HD), bf16),
            jax.ShapeDtypeStruct((heads * blocks, 1, ROWS), f32),
        ),
        grid_spec=pltpu.PrefetchScalarGridSpec(
            num_scalar_prefetch=2,
            grid=(heads, blocks),
            in_specs=[
                pl.BlockSpec((ROWS, HD), lambda h, i, *s: (i, h)),
                pl.BlockSpec((count, HD), lambda h, i, *s: (0, heads + h)),
                pl.BlockSpec((count, HD), lambda h, i, *s: (0, 2 * heads + h)),
                pl.BlockSpec((ROWS, 1), lambda h, i, *s: (i, 0)),
                pl.BlockSpec((1, count), lambda h, i, *s: (0, 0)),
            ],
            out_specs=(
                pl.BlockSpec((ROWS, HD), lambda h, i, *s: (i, h)),
                pl.BlockSpec((ROWS, HD), lambda h, i, *s: (i, h)),
                pl.BlockSpec((1, 1, ROWS), lambda h, i, *s: (h * blocks + i, 0, 0)),
            ),
            scratch_shapes=[pltpu.VMEM((ROWS, count), f32)],
        ),
        compiler_params=params(2, 32),
        cost_estimate=estimate(
            flops=2 * heads * count * count * HD,
            bytes_accessed=12 * heads * count * HD,
            transcendentals=heads * count * count // 2,
        ),
        name="attention",
    )(low, high, rot, rot, rot, seg_col, seg_row)


def head_back(grad, pre, gain, cosine, sine):
    n = grad * cosine - pltpu.roll(grad, HD // 2, 1) * sine
    inverse = lax.rsqrt(jnp.mean(pre * pre, axis=-1, keepdims=True) + head_eps)
    w = n * gain
    back = inverse * w - pre * inverse**3 * jnp.mean(w * pre, axis=-1, keepdims=True)
    return back, jnp.sum(n * pre * inverse, axis=0, keepdims=True)


def attn_back_kernel(
    scale,
    low_ref,
    high_ref,
    q_ref,
    k_ref,
    v_ref,
    do_ref,
    o_ref,
    lse_ref,
    sq_ref,
    sk_ref,
    qpre_ref,
    kpre_ref,
    gq_ref,
    gk_ref,
    cosq_ref,
    sinq_ref,
    cosk_ref,
    sink_ref,
    dq_ref,
    dk_ref,
    dv_ref,
    gain_ref,
    dk_scr,
    dv_scr,
):
    head, block = pl.program_id(0), pl.program_id(1)
    low, high = low_ref[block], high_ref[block]

    @pl.when(block == 0)
    def _():
        dk_scr[...] = jnp.zeros_like(dk_scr)
        dv_scr[...] = jnp.zeros_like(dv_scr)

    @pl.when((block == 0) & (head == 0))
    def _():
        gain_ref[...] = jnp.zeros_like(gain_ref)

    q, do = q_ref[...], do_ref[...]
    row_dot = jnp.sum((do.astype(f32) * o_ref[...]).T, axis=0, keepdims=True)
    lse = lse_ref[0]
    seg_q = sq_ref[...]

    def tile(kb, dq):
        at = pl.ds(pl.multiple_of(kb * ROWS, ROWS), ROWS)
        k, v = k_ref[at, :], v_ref[at, :]
        s = dot_nt(k, q) * scale
        p = jnp.where(sk_ref[at, :] == seg_q, jnp.exp(s - lse), 0.0)
        dp = dot_nt(v, do)
        ds = (p * (dp - row_dot)).astype(bf16)
        dv_scr[at, :] += dot_nn(p.astype(bf16), do)
        dk_scr[at, :] += dot_nn(ds, q)
        return dq + dot_tn(ds, k)

    dq = lax.fori_loop(low, high, tile, jnp.zeros((ROWS, HD), f32))
    back, gain_q = head_back(dq * scale, qpre_ref[...], gq_ref[...], cosq_ref[...], sinq_ref[...])
    dq_ref[...] = back.astype(bf16)
    gain_ref[0:1, :] += gain_q

    @pl.when(block == pl.num_programs(1) - 1)
    def _():
        @pl.loop(0, dk_scr.shape[0] // ROWS)
        def _(i):
            at = pl.ds(pl.multiple_of(i * ROWS, ROWS), ROWS)
            back, gain_k = head_back(
                dk_scr[at, :] * scale, kpre_ref[at, :], gk_ref[...], cosk_ref[at, :], sink_ref[at, :]
            )
            dk_ref[at, :] = back.astype(bf16)
            dv_ref[at, :] = dv_scr[at, :].astype(bf16)
            gain_ref[1:2, :] += gain_k


def attention_back(
    rot, grad, out, lse, seg_col, seg_row, low, high, pre, gain_q, gain_k, cosine, sine, heads
):
    count = rot.shape[0]
    blocks = count // ROWS
    scale = HD ** (-0.5)
    mine = lambda h, i, *s: (i, h)
    whole = lambda h, i, *s: (0, 0)
    return pl.pallas_call(
        functools.partial(attn_back_kernel, scale),
        out_shape=(
            jax.ShapeDtypeStruct((count, heads * HD), bf16),
            jax.ShapeDtypeStruct((count, heads * HD), bf16),
            jax.ShapeDtypeStruct((count, heads * HD), bf16),
            jax.ShapeDtypeStruct((8, HD), f32),
        ),
        grid_spec=pltpu.PrefetchScalarGridSpec(
            num_scalar_prefetch=2,
            grid=(heads, blocks),
            in_specs=[
                pl.BlockSpec((ROWS, HD), mine),
                pl.BlockSpec((count, HD), lambda h, i, *s: (0, heads + h)),
                pl.BlockSpec((count, HD), lambda h, i, *s: (0, 2 * heads + h)),
                pl.BlockSpec((ROWS, HD), mine),
                pl.BlockSpec((ROWS, HD), mine),
                pl.BlockSpec((1, 1, ROWS), lambda h, i, *s: (h * blocks + i, 0, 0)),
                pl.BlockSpec((1, ROWS), lambda h, i, *s: (0, i)),
                pl.BlockSpec((count, 1), whole),
                pl.BlockSpec((ROWS, HD), mine),
                pl.BlockSpec((count, HD), lambda h, i, *s: (0, heads + h)),
                pl.BlockSpec((1, HD), whole),
                pl.BlockSpec((1, HD), whole),
                pl.BlockSpec((ROWS, HD), lambda h, i, *s: (i, 0)),
                pl.BlockSpec((ROWS, HD), lambda h, i, *s: (i, 0)),
                pl.BlockSpec((count, HD), whole),
                pl.BlockSpec((count, HD), whole),
            ],
            out_specs=(
                pl.BlockSpec((ROWS, HD), mine),
                pl.BlockSpec((count, HD), lambda h, i, *s: (0, h)),
                pl.BlockSpec((count, HD), lambda h, i, *s: (0, h)),
                pl.BlockSpec((8, HD), whole),
            ),
            scratch_shapes=[pltpu.VMEM((count, HD), f32), pltpu.VMEM((count, HD), f32)],
        ),
        compiler_params=params(2, 48),
        cost_estimate=estimate(
            flops=5 * heads * count * count * HD,
            bytes_accessed=30 * heads * count * HD,
            transcendentals=heads * count * count // 2,
        ),
        name="attention_back",
    )(
        low,
        high,
        rot,
        rot,
        rot,
        grad,
        out,
        lse,
        seg_row,
        seg_col,
        pre,
        pre,
        gain_q,
        gain_k,
        cosine,
        sine,
        cosine,
        sine,
    )


def expert_kernel(base, count, carried, mine_ref, x_ref, *refs):
    near = 1 if base == 0 else 0
    c_refs, refs = refs[: near + 1], refs[near + 1 :]
    wg_ref, wu_ref, wd_ref = refs[:3]
    refs = refs[3 + carried :]
    back_ref, out_ref, xs_ref, c_ref, hid_ref, gp_ref, up_ref = refs[:7]
    out_acc, back_acc, gate_scr, dot_scr = refs[7:]
    step = pl.program_id(1)
    per_plane, capacity, width = c_ref.shape
    rows = per_plane * capacity
    extra = x_ref.shape[2] - width
    lane = lax.broadcasted_iota(jnp.int32, (rows, extra), 1)
    high, low = lane == mine_ref[0], lane == mine_ref[0] + count

    @pl.when(step == 0)
    def _():
        xs_ref[...] = x_ref[:, :, :width]
        if near:

            @pl.when(pl.program_id(0) == 0)
            def _():
                c_ref[...] = c_refs[0][...]

            @pl.when(pl.program_id(0) > 0)
            def _():
                c_ref[...] = c_refs[1][...]

        else:
            c_ref[...] = c_refs[0][...]
        gates = x_ref[:, :, width:].reshape(rows, extra).astype(f32)
        gate_scr[...] = jnp.sum(jnp.where(high | low, gates, 0.0), axis=-1, keepdims=True)
        out_acc[...] = jnp.zeros_like(out_acc)
        back_acc[...] = jnp.zeros_like(back_acc)
        dot_scr[...] = jnp.zeros_like(dot_scr)

    x = x_ref[:, :, :width].reshape(rows, width)
    c = c_ref[...].reshape(rows, width)
    gate = gate_scr[...]
    wg, wu, wd = wg_ref[...], wu_ref[...], wd_ref[...]
    gate_pre, up_pre = dot_nn(x, wg), dot_nn(x, wu)
    sig = jax.nn.sigmoid(gate_pre)
    hidden = (gate_pre * sig * up_pre).astype(bf16)
    out_acc[...] += dot_nn(hidden, wd)
    plain = dot_nt(c, wd)
    wide = hidden.astype(f32)
    dot_scr[...] += jnp.sum(wide * plain, axis=-1, keepdims=True)
    hid_ref[...] = (wide * gate).astype(bf16).reshape(hid_ref.shape)
    hidden_grad = plain * gate
    gate_grad = (hidden_grad * up_pre * sig * (1.0 + gate_pre * (1.0 - sig))).astype(bf16)
    up_grad = (hidden_grad * gate_pre * sig).astype(bf16)
    gp_ref[...] = gate_grad.reshape(gp_ref.shape)
    up_ref[...] = up_grad.reshape(up_ref.shape)
    back_acc[...] += dot_nt(gate_grad, wg) + dot_nt(up_grad, wu)

    @pl.when(step == pl.num_programs(1) - 1)
    def _():
        dots = dot_scr[...]
        coarse = dots.astype(bf16).astype(f32)
        lanes = jnp.where(high, coarse, jnp.where(low, dots - coarse, 0.0)).astype(bf16)
        back_ref[:, :, :width] = back_acc[...].astype(bf16).reshape(c_ref.shape)
        back_ref[:, :, width:] = lanes.reshape(per_plane, capacity, extra)
        out_ref[...] = (out_acc[...] * gate).astype(bf16).reshape(out_ref.shape)


def experts(mine, x, near, far, wg, wu, wd, base, planes, count, kept):
    per_plane, blocks, capacity, wide = x.shape
    width = near.shape[3]
    halves, _, hidden = wg.shape
    rows = per_plane * capacity
    saved = jax.ShapeDtypeStruct((per_plane, planes, capacity, width), bf16)
    thin = jax.ShapeDtypeStruct((per_plane, planes, capacity, halves * hidden), bf16)
    moved = pl.BlockSpec((per_plane, None, capacity, wide), lambda i, f, s: (0, i, 0, 0))
    saved_spec = pl.BlockSpec((per_plane, None, capacity, width), lambda i, f, s: (0, base + i, 0, 0))
    thin_spec = pl.BlockSpec((per_plane, None, capacity, hidden), lambda i, f, s: (0, base + i, 0, f))
    carried = 0 if kept is None else len(kept)
    cots = (near, far) if base == 0 else (far,)
    cot_specs = [
        pl.BlockSpec(
            (per_plane, None, capacity, width), lambda i, f, s: (0, jnp.maximum(base + i - 1, 0), 0, 0)
        )
    ]
    if base == 0:
        cot_specs = [pl.BlockSpec((per_plane, None, capacity, width), lambda i, f, s: (0, 0, 0, 0))] + cot_specs
    result = pl.pallas_call(
        functools.partial(expert_kernel, base, count, carried),
        out_shape=(
            jax.ShapeDtypeStruct(x.shape, bf16),
            jax.ShapeDtypeStruct((per_plane, blocks, capacity, width), bf16),
            saved,
            saved,
            thin,
            thin,
            thin,
        ),
        grid_spec=pltpu.PrefetchScalarGridSpec(
            num_scalar_prefetch=1,
            grid=(blocks, halves),
            in_specs=[
                moved,
                *cot_specs,
                pl.BlockSpec((None, width, hidden), lambda i, f, s: (f, 0, 0)),
                pl.BlockSpec((None, width, hidden), lambda i, f, s: (f, 0, 0)),
                pl.BlockSpec((None, hidden, width), lambda i, f, s: (f, 0, 0)),
            ]
            + [pl.BlockSpec(memory_space=pl.ANY)] * carried,
            out_specs=(
                moved,
                pl.BlockSpec((per_plane, None, capacity, width), lambda i, f, s: (0, i, 0, 0)),
                saved_spec,
                saved_spec,
                thin_spec,
                thin_spec,
                thin_spec,
            ),
            scratch_shapes=[
                pltpu.VMEM((rows, width), f32),
                pltpu.VMEM((rows, width), f32),
                pltpu.VMEM((rows, 1), f32),
                pltpu.VMEM((rows, 1), f32),
            ],
        ),
        input_output_aliases={5 + len(cots) + i: 2 + i for i in range(carried)},
        compiler_params=params(2, 60),
        cost_estimate=estimate(
            flops=12 * blocks * rows * width * hidden * halves,
            bytes_accessed=10 * blocks * rows * width + 6 * blocks * width * hidden * halves,
            transcendentals=blocks * rows * hidden * halves,
        ),
        name="experts",
    )(mine, x, *cots, wg, wu, wd, *(kept or ()))
    return result[0], result[1], result[2:]


def gram_kernel(plus, left_ref, right_ref, *refs):
    total = dot_tn(left_ref[...], right_ref[...])
    if plus:
        total = total + refs[0][...]
    refs[-1][...] = total.astype(refs[-1].dtype)


def gram(left, right, left_cols, right_cols, dtype, plus=None):
    rows = left.shape[0]
    left_at, left_count = left_cols
    right_at, right_count = right_cols
    tall = min(left_count, 256)
    wide = min(right_count, 1024)
    out_spec = pl.BlockSpec((tall, wide), lambda j, i: (i, j))
    return pl.pallas_call(
        functools.partial(gram_kernel, plus is not None),
        out_shape=jax.ShapeDtypeStruct((left_count, right_count), dtype),
        grid=(right_count // wide, left_count // tall),
        in_specs=[
            pl.BlockSpec((rows, tall), lambda j, i: (0, left_at // tall + i)),
            pl.BlockSpec((rows, wide), lambda j, i: (0, right_at // wide + j)),
        ]
        + [out_spec] * (plus is not None),
        out_specs=out_spec,
        compiler_params=params(2, 48),
        cost_estimate=estimate(
            flops=2 * rows * left_count * right_count,
            bytes_accessed=2 * rows * (left_count + right_count) + 4 * left_count * right_count,
            transcendentals=0,
        ),
        name="gram",
    )(left, right, *(() if plus is None else (plus,)))


def project_kernel(plus, core_ref, rows_ref, weights_ref, *refs):
    total = dot_nt(rows_ref[...], weights_ref[...])
    if plus:
        total = total + refs[0][...].astype(f32)
    refs[-1][...] = total.astype(bf16)


def project_back(core, rows, weights, tok_rows, plus=None):
    count, depth = rows.shape
    width = weights.shape[0]
    chips = count // tok_rows // 2
    out_spec = pl.BlockSpec((tok_rows, width), lambda i, s: (i, 0))
    return pl.pallas_call(
        functools.partial(project_kernel, plus is not None),
        out_shape=jax.ShapeDtypeStruct((chips * tok_rows, width), bf16),
        grid_spec=pltpu.PrefetchScalarGridSpec(
            num_scalar_prefetch=1,
            grid=(chips,),
            in_specs=[
                pl.BlockSpec((tok_rows, depth), lambda i, s: (2 * i + s[0], 0)),
                pl.BlockSpec((width, depth), lambda i, s: (0, 0)),
            ]
            + [out_spec] * (plus is not None),
            out_specs=out_spec,
        ),
        compiler_params=params(1, 40),
        cost_estimate=estimate(
            flops=count * depth * width,
            bytes_accessed=2 * width * depth + count * depth + count * width,
            transcendentals=0,
        ),
        name="project_back",
    )(core, rows, weights, *(() if plus is None else (plus,)))


def after(value, *others):
    return lax.optimization_barrier((value,) + others)[0]


def body(
    hidden_in,
    out_cotangent,
    segment_number,
    expert_routes,
    pair_order,
    norm_gain,
    query_weight,
    key_weight,
    value_weight,
    output_weight,
    query_gain,
    key_gain,
    ffn_norm_gain,
    router_weight,
    expert_gate,
    expert_up,
    expert_down,
):
    tok_rows, width = hidden_in.shape
    devices = lax.axis_size(AXIS)
    members = max(1, SEQ_MIN // tok_rows)
    planes = devices // members
    per_plane = members // 2
    expert_count = devices // 2
    capacity = tok_rows * TOPK // expert_count
    heads = width // HD // members
    head_width = heads * HD
    own_rows = norm_gain.shape[0]
    seq = members * tok_rows
    me = lax.axis_index(AXIS)
    plane, member = me // members, me % members
    mine = (me // 2).astype(jnp.int32).reshape(1)
    first = (plane * per_plane).astype(jnp.int32)
    places = (plane ^ jnp.arange(planes, dtype=jnp.int32)).astype(jnp.int32)
    counted = jnp.concatenate([first[None], jnp.arange(planes, dtype=jnp.int32)])
    halfway = -(-planes // 2)
    chunks = [part for part in (range(halfway, planes), range(halfway)) if len(part)]

    def placed(part):
        return jnp.concatenate([first[None], places[part.start : part.stop]])

    plane_groups = [[g * members + j for j in range(members)] for g in range(planes)]
    stack_groups = [[g * members + j for g in range(planes)] for j in range(members)]
    core_groups = [
        [g * members + 2 * c + h for c in range(per_plane)] for g in range(planes) for h in (0, 1)
    ]

    def exchange(value, groups=None):
        return lax.all_to_all(
            value, AXIS, split_axis=0, concat_axis=0, tiled=True, axis_index_groups=groups
        )

    def gather(value, groups=None):
        return lax.all_gather(value, AXIS, axis=0, tiled=True, axis_index_groups=groups)

    def flip(value, bits):
        if bits == 0:
            return value
        return lax.ppermute(value, AXIS, [(i, i ^ bits) for i in range(devices)])

    def to_core(value):
        return flip(value, 1)

    def to_plane(value, d):
        return flip(value, members * d)

    wire, core_op = [], []

    def on_wire(value, groups):
        came = exchange(after(value, *wire[-1:]), groups)
        wire.append(came)
        return came

    def to_chips(value):
        return on_wire(value, core_groups)

    def in_turn(value):
        return after(value, *core_op[-1:])

    def ran(value):
        core_op.append(value)
        return value

    pieces = (
        router_weight.reshape(-1),
        norm_gain,
        ffn_norm_gain,
        query_gain,
        key_gain,
        segment_number.astype(bf16),
    )
    packed = jnp.concatenate(pieces)
    length = packed.shape[0]
    padded = -(-length // 128) * 128
    packed = jnp.pad(packed, (0, padded - length))
    packed = on_wire(jnp.broadcast_to(packed[None], (devices, padded)), None)
    small = []
    at = 0
    for piece in pieces:
        small.append(packed[:, at : at + piece.shape[0]])
        at += piece.shape[0]
    router_full = small[0].reshape(width, expert_count)
    gain_one = small[1].reshape(1, width).astype(f32)
    gain_two = small[2].reshape(1, width).astype(f32)
    gain_q = small[3].reshape(1, HD).astype(f32)
    gain_k = small[4].reshape(1, HD).astype(f32)
    segments = lax.dynamic_slice_in_dim(small[5], plane * members, members, 0).astype(f32)
    seg_row, seg_col = segments.reshape(1, seq), segments.reshape(seq, 1)
    seg_blocks = segments.reshape(seq // ROWS, ROWS)
    seg_first, seg_last = seg_blocks[:, 0], seg_blocks[:, -1]
    low = jnp.sum((seg_last[None, :] < seg_first[:, None]).astype(jnp.int32), axis=1)
    high = jnp.sum((seg_first[None, :] <= seg_last[:, None]).astype(jnp.int32), axis=1)

    columns = jnp.concatenate(
        [w.reshape(own_rows, members, head_width) for w in (query_weight, key_weight, value_weight)],
        axis=2,
    )
    slots = block_slots(expert_routes, pair_order, expert_count)
    columns = on_wire(
        after(columns, slots).transpose(1, 0, 2).reshape(members * own_rows, 3 * head_width), plane_groups
    )
    slots = [to_plane(slots, d) for d in range(planes)]
    stacked = [to_plane(after(output_weight, slots[0]), d) for d in range(planes)]
    weights = [to_plane(after(columns, *slots, *stacked), d) for d in range(planes)]
    output_rows = jnp.zeros((planes * own_rows, width), bf16)
    for d, rows in enumerate(stacked):
        output_rows = lax.dynamic_update_slice_in_dim(output_rows, rows, places[d] * own_rows, 0)
    rows_all = gather(hidden_in, plane_groups)

    cot_own = dispatch(counted, slots[0][None], out_cotangent[None], per_plane, capacity)
    cot_parts = [to_chips(cot_own)]
    output_full = gather(after(output_rows, columns), plane_groups)
    slots = jnp.stack(slots)
    cot_rows = {0: out_cotangent}
    top = planes // 2
    early, late = [], []
    if planes > 1:
        cot_rows[top] = to_plane(after(out_cotangent, *weights), top)
        early.append(cot_rows[top])
    for d in range(1, planes):
        if d != top:
            lowest = d & -d
            start = after(out_cotangent, *early) if d == lowest else cot_rows[d ^ lowest]
            cot_rows[d] = to_plane(start, lowest)
            late.append(cot_rows[d])

    halves = lambda w: jnp.concatenate([w, to_core(w)], axis=0)
    wg, wu, wd = halves(expert_gate), halves(expert_up), halves(expert_down)

    cosine, sine = rope_tables(seq)
    act_one, pre, rot, ordered = qkv_project(
        places, rows_all, gain_one, weights, gain_q, gain_k, cosine, sine, heads
    )
    out_wide, out_heads, lse = attention(rot, seg_col, seg_row, low, high, heads)
    out_low = on_wire(after(out_heads, *early), plane_groups)
    out_low = out_low.reshape(members, tok_rows, head_width).transpose(1, 0, 2)
    out_low = out_low.reshape(tok_rows, planes, members, own_rows).transpose(0, 2, 1, 3)
    out_low = after(out_low.reshape(tok_rows, width), wg, wu, wd)
    tokens = hidden_in.astype(f32)
    cotangent = out_cotangent.astype(f32)
    middle = tokens + dot_nn(out_low, output_full)
    inverse_two = lax.rsqrt(jnp.mean(middle * middle, axis=-1, keepdims=True) + norm_eps)
    act_two = (middle * inverse_two * gain_two).astype(bf16)

    logits = dot_nn(act_two, router_full)
    expert_ids = jnp.arange(expert_count, dtype=jnp.int32)
    routed = jnp.any(expert_routes[:, :, None] == expert_ids[None, None, :], axis=1)
    logits = jnp.where(routed, logits, masked_score)
    gates = jnp.where(routed, jnp.exp(logits - jnp.max(logits, axis=1, keepdims=True)), 0.0)
    gates = gates / jnp.sum(gates, axis=1, keepdims=True)
    coarse = lax.reduce_precision(gates, 8, 7)
    extra = -(-2 * expert_count // 128) * 128
    act_wide = jnp.concatenate(
        [
            act_two,
            coarse.astype(bf16),
            (gates - coarse).astype(bf16),
            jnp.zeros((tok_rows, extra - 2 * expert_count), bf16),
        ],
        axis=1,
    )

    act_wide = after(act_wide, *late)
    act_all = gather(act_wide, stack_groups).reshape(planes, tok_rows, -1)
    if planes > 1:
        far = jnp.stack([after(cot_rows[d], act_wide) for d in range(1, planes)])
        sent = dispatch(counted[:planes], slots[1:], far, per_plane, capacity)
        cot_parts.append(to_chips(ran(sent)))

    act = []
    for part in chunks:
        own_slots = slots[part.start : part.stop]
        sent = dispatch(placed(part), own_slots, in_turn(act_all), per_plane, capacity)
        act.append(to_chips(ran(sent)))
    kept, back, outs = None, [], []
    for part, rows in zip(chunks, act):
        sent, out, kept = experts(
            mine,
            in_turn(rows),
            cot_parts[0],
            cot_parts[-1],
            wg,
            wu,
            wd,
            part.start,
            planes,
            expert_count,
            kept,
        )
        back.append(to_chips(ran(sent)))
        outs.append(out)
    x_all, c_all, hid_all, gp_all, up_all = kept

    hidden = expert_gate.shape[2]
    flat = lambda value: value.reshape(-1, value.shape[3])
    sides = (
        (flat(x_all), flat(gp_all), 1),
        (flat(x_all), flat(up_all), 1),
        (flat(hid_all), flat(c_all), 0),
    )

    def half(side, which, plus=None):
        left, right, split = side
        cut, whole = (which * hidden, hidden), (0, width)
        cols = (whole, cut) if split else (cut, whole)
        return gram(in_turn(left), right, *cols, f32, plus)

    def home(part, rows, *others):
        came = []
        for i, d in enumerate(part):
            summed = combine(first[None], slots[d], after(rows, *core_op[-1:], *others), i)
            came.append(to_plane(ran(summed), d))
        return came

    came = home(chunks[0], back[0])
    theirs = [to_core(ran(half(side, 1))) for side in sides]
    if len(chunks) > 1:
        came += home(chunks[1], back[1])
    outs[0] = to_chips(outs[0])
    back_sum = sum(rows.astype(f32) for rows in came)

    expert_in_grad = back_sum[:, :width]
    gate_grad = (
        back_sum[:, width : width + expert_count]
        + back_sum[:, width + expert_count : width + 2 * expert_count]
    )
    select_grad = gates * (gate_grad - jnp.sum(gates * gate_grad, axis=1, keepdims=True))
    logit_grad = select_grad.astype(bf16)
    grad_router = dot_tn(act_two, logit_grad)
    act_two_grad = expert_in_grad + dot_nt(logit_grad, router_full)
    weighted = act_two_grad * gain_two
    grad_gain_two = jnp.sum(act_two_grad * middle * inverse_two, axis=0)
    middle_grad = (
        cotangent
        + inverse_two * weighted
        - middle * inverse_two**3 * jnp.mean(weighted * middle, axis=-1, keepdims=True)
    )
    middle_low = middle_grad.astype(bf16)

    out_grad = dot_nt(middle_low, output_full).astype(bf16)
    out_grad = out_grad.reshape(tok_rows, members, planes, own_rows).transpose(0, 2, 1, 3)
    out_grad = out_grad.reshape(tok_rows, members, head_width).transpose(1, 0, 2)
    out_grad = out_grad.reshape(seq, head_width)
    ran(out_grad)
    out_grad = on_wire(out_grad, plane_groups)
    mixture = home(chunks[0], outs[0])
    dq, dk, dv, grad_gains = attention_back(
        rot,
        in_turn(out_grad),
        out_wide,
        lse,
        seg_col,
        seg_row,
        low,
        high,
        pre,
        gain_q,
        gain_k,
        cosine,
        sine,
        heads,
    )
    ran(dq)
    if len(chunks) > 1:
        mixture += home(chunks[1], to_chips(outs[1]))
        done = (*core_op[-2:], mixture[0])
        dq, dk, dv, grad_gains = (after(grad, *done) for grad in (dq, dk, dv, grad_gains))
    dqkv = jnp.concatenate([dq, dk, dv], axis=1)
    middle_all = gather(after(middle_low, dq), plane_groups)

    sums = (
        grad_router.reshape(devices, -1),
        grad_gain_two.reshape(devices, -1),
        grad_gains[0].reshape(devices, -1),
        grad_gains[1].reshape(devices, -1),
    )
    packed = jnp.concatenate(sums, axis=1)
    length = packed.shape[1]
    padded = -(-length // 128) * 128
    packed = jnp.pad(packed, ((0, 0), (0, padded - length)))

    core = (me % 2).astype(jnp.int32).reshape(1)
    part = gram(in_turn(act_one), dqkv, (0, width), (0, 3 * head_width), bf16)
    part = part.reshape(planes, members * own_rows, 3 * head_width)
    shares = [lax.dynamic_index_in_dim(part, places[d], 0, False) for d in range(planes)]
    given = to_core(project_back(1 - core, after(dqkv, *shares), ordered, tok_rows))
    shares = [to_plane(share, d) for d, share in enumerate(shares)]
    act_one_grad = project_back(core, dqkv, ordered, tok_rows, given)
    shares = [after(share, act_one_grad) for share in shares]
    taken = sum(share.astype(f32) for share in shares).astype(bf16)
    grad_gate, grad_up, grad_down = (
        half(side, 0, other)
        for side, other in zip(sides, (after(other, act_one_grad) for other in theirs))
    )
    act_one_grad = on_wire(act_one_grad, core_groups)

    output_part = gram(out_heads, middle_all, (0, head_width), (0, width), bf16)
    output_part = output_part.reshape(planes, head_width // planes, width)
    grad_output = 0.0
    for d in range(planes):
        to_owner = [
            (g * members + j, j * planes + (g ^ d)) for g in range(planes) for j in range(members)
        ]
        rows = lax.dynamic_index_in_dim(output_part, places[d], 0, False)
        grad_output = grad_output + lax.ppermute(rows, AXIS, to_owner).astype(f32)
    packed, act_one_grad, grad_gate, grad_up, grad_down, *mixture = lax.optimization_barrier(
        (packed, act_one_grad, grad_gate, grad_up, grad_down, *mixture)
    )
    layer_out = (middle + sum(rows.astype(f32) for rows in mixture)).astype(bf16)
    packed = exchange(packed)
    taken, packed, grad_output = lax.optimization_barrier((taken, packed, grad_output))
    part = exchange(taken, plane_groups).reshape(members, own_rows, 3, head_width)
    part = part.transpose(2, 1, 0, 3).reshape(3, own_rows, width).astype(f32)
    grad_query, grad_key, grad_value = part[0], part[1], part[2]
    act_one_grad = act_one_grad.reshape(per_plane, tok_rows, width)
    act_one_grad = jnp.sum(act_one_grad.astype(f32), axis=0)

    inverse_one = lax.rsqrt(jnp.mean(tokens * tokens, axis=-1, keepdims=True) + norm_eps)
    weighted = act_one_grad * gain_one
    grad_hidden = (
        middle_grad
        + inverse_one * weighted
        - tokens * inverse_one**3 * jnp.mean(weighted * tokens, axis=-1, keepdims=True)
    )
    grad_gain_one = (
        jnp.sum(
            grad_query * query_weight.astype(f32)
            + grad_key * key_weight.astype(f32)
            + grad_value * value_weight.astype(f32),
            axis=1,
        )
        / norm_gain.astype(f32)
    )

    summed = jnp.sum(packed, axis=0)
    at, tiny = 0, []
    for piece in sums:
        tiny.append(summed[at : at + piece.shape[1]])
        at += piece.shape[1]

    return (
        layer_out,
        grad_hidden,
        grad_gain_one,
        grad_query,
        grad_key,
        grad_value,
        grad_output,
        tiny[2],
        tiny[3],
        tiny[1],
        tiny[0].reshape(own_rows, expert_count),
        grad_gate[None],
        grad_up[None],
        grad_down[None],
    )


def solution(mesh):
    row, mat, cube = P(AXIS), P(AXIS, None), P(AXIS, None, None)
    return jax.shard_map(
        body,
        mesh=mesh,
        in_specs=(mat, mat, row, mat, mat, row, mat, mat, mat, mat, row, row, row, mat)
        + (cube,) * 3,
        out_specs=(mat, mat, row, mat, mat, mat, mat, row, row, row, mat) + (cube,) * 3,
        check_vma=False,
    )
```

```python
import functools
import math

import jax
import jax.numpy as jnp
from jax import lax
from jax.experimental import pallas as pl
from jax.experimental.pallas import tpu as pltpu
from jax.sharding import PartitionSpec as P

HD = 128
TOPK = 8
SEQ_MIN = 2048
ROWS = 256
SHARE = 32

norm_eps = 1e-05
head_eps = 1e-06
rope_base = 10000.0
masked_score = -1e30
absent_slot = 4096.0

AXIS = "fsdp"
f32 = jnp.float32
bf16 = jnp.bfloat16
MIB = 1 << 20


def dot_nt(left, right):
    return lax.dot_general(left, right, (((1,), (1,)), ((), ())), preferred_element_type=f32)


def dot_tn(left, right):
    return lax.dot_general(left, right, (((0,), (0,)), ((), ())), preferred_element_type=f32)


def dot_nn(left, right):
    return lax.dot_general(left, right, (((1,), (0,)), ((), ())), preferred_element_type=f32)


def params(steps, mib):
    return pltpu.CompilerParams(
        dimension_semantics=("arbitrary",) * steps, vmem_limit_bytes=mib * MIB
    )


def estimate(flops, bytes_accessed, transcendentals):
    return pl.CostEstimate(
        flops=flops // SHARE, bytes_accessed=bytes_accessed // SHARE, transcendentals=transcendentals // SHARE
    )


def rope_tables(count):
    half_width = HD // 2
    frequency = jnp.exp(-math.log(rope_base) * 2.0 * jnp.arange(half_width, dtype=f32) / HD)
    angles = jnp.arange(count, dtype=f32)[:, None] * frequency[None, :]
    cosine, sine = jnp.cos(angles), jnp.sin(angles)
    return jnp.concatenate([cosine, cosine], axis=-1), jnp.concatenate([-sine, sine], axis=-1)


def slots_kernel(expert_count, routes_ref, order_ref, slots_ref):
    tok_rows = routes_ref.shape[0]
    pair_count = order_ref.shape[1]
    order = order_ref[...]
    shift = TOPK.bit_length() - 1
    token_of = lax.shift_right_logical(order, jnp.full_like(order, shift))
    route_of = order & (TOPK - 1)
    token_iota = lax.broadcasted_iota(jnp.int32, (tok_rows, pair_count), 0)
    token_hot = jnp.where(token_iota == token_of, 1.0, 0.0).astype(bf16)
    place = lax.broadcasted_iota(jnp.int32, (TOPK, pair_count), 1)
    chosen = lax.broadcasted_iota(jnp.int32, (TOPK, pair_count), 0) == route_of
    high = lax.shift_right_logical(place, jnp.full_like(place, 8)).astype(f32)
    low = (place & 255).astype(f32)
    digits = jnp.concatenate([jnp.where(chosen, high, 0.0), jnp.where(chosen, low, 0.0)], axis=0)
    found = dot_nt(token_hot, digits.astype(bf16))
    rank = found[:, :TOPK] * 256.0 + found[:, TOPK:]
    routes = routes_ref[...]
    lanes = -(-expert_count // 128) * 128
    expert_iota = lax.broadcasted_iota(jnp.int32, (tok_rows, lanes), 1)
    never = 1e9
    by_expert = jnp.full((tok_rows, lanes), never, f32)
    for k in range(TOPK):
        by_expert = jnp.where(expert_iota == routes[:, k : k + 1], rank[:, k : k + 1], by_expert)
    turned = by_expert.T
    for e in range(expert_count):
        mine = turned[e : e + 1, :]
        earlier = jnp.where(by_expert[:, e : e + 1] < mine, 1.0, 0.0)
        count = jnp.sum(earlier, axis=0, keepdims=True)
        slots_ref[e : e + 1, :] = jnp.where(mine < never, count, absent_slot)


def block_slots(routes, order, expert_count):
    tok_rows = routes.shape[0]
    return pl.pallas_call(
        functools.partial(slots_kernel, expert_count),
        out_shape=jax.ShapeDtypeStruct((expert_count, tok_rows), f32),
        compiler_params=pltpu.CompilerParams(vmem_limit_bytes=32 * MIB),
        name="block_slots",
    )(routes, order)


def slot_hot(slots_ref, expert, capacity):
    slot_row = slots_ref[pl.ds(expert, 1), :]
    slot_iota = lax.broadcasted_iota(jnp.int32, (capacity, slot_row.shape[1]), 0).astype(f32)
    return jnp.where(slot_iota == slot_row, 1.0, 0.0).astype(bf16)


def plane_hot(slots_ref, first, shape):
    return jnp.concatenate([slot_hot(slots_ref, first + r, shape[1]) for r in range(shape[0])])


def dispatch_kernel(at_ref, slots_ref, rows_ref, out_ref):
    hot = plane_hot(slots_ref, at_ref[0], out_ref.shape)
    out_ref[...] = dot_nn(hot, rows_ref[...]).astype(bf16).reshape(out_ref.shape)


def dispatch(at, slots, rows, per_plane, capacity):
    blocks, experts, tok_rows = slots.shape
    width = rows.shape[2]
    slot_rows = per_plane * capacity
    return pl.pallas_call(
        dispatch_kernel,
        out_shape=jax.ShapeDtypeStruct((per_plane, blocks, capacity, width), bf16),
        grid_spec=pltpu.PrefetchScalarGridSpec(
            num_scalar_prefetch=1,
            grid=(blocks,),
            in_specs=[
                pl.BlockSpec((None, experts, tok_rows), lambda i, s: (i, 0, 0)),
                pl.BlockSpec((None, tok_rows, width), lambda i, s: (s[1 + i], 0, 0)),
            ],
            out_specs=pl.BlockSpec((per_plane, None, capacity, width), lambda i, s: (0, i, 0, 0)),
        ),
        compiler_params=params(1, 40),
        cost_estimate=estimate(
            flops=2 * blocks * slot_rows * tok_rows * width,
            bytes_accessed=2 * blocks * (slot_rows + tok_rows) * width,
            transcendentals=0,
        ),
        name="dispatch",
    )(at, slots, rows)


def combine_kernel(first_ref, slots_ref, rows_ref, out_ref):
    hot = plane_hot(slots_ref, first_ref[0], rows_ref.shape)
    rows = rows_ref[...].reshape(hot.shape[0], rows_ref.shape[2])
    out_ref[...] = dot_tn(hot, rows).astype(bf16)


def combine(first, slots, rows, block):
    experts, tok_rows = slots.shape
    per_plane, _, capacity, width = rows.shape
    slot_rows = per_plane * capacity
    return pl.pallas_call(
        combine_kernel,
        out_shape=jax.ShapeDtypeStruct((tok_rows, width), bf16),
        grid_spec=pltpu.PrefetchScalarGridSpec(
            num_scalar_prefetch=1,
            grid=(1,),
            in_specs=[
                pl.BlockSpec((experts, tok_rows), lambda i, s: (0, 0)),
                pl.BlockSpec((per_plane, None, capacity, width), lambda i, s: (0, block, 0, 0)),
            ],
            out_specs=pl.BlockSpec((tok_rows, width), lambda i, s: (0, 0)),
        ),
        compiler_params=params(1, 40),
        cost_estimate=estimate(
            flops=2 * slot_rows * tok_rows * width,
            bytes_accessed=2 * (slot_rows + tok_rows) * width,
            transcendentals=0,
        ),
        name="combine",
    )(first, slots, rows)


def qkv_kernel(heads, planes, at_ref, x_ref, gain_ref, *refs):
    w_refs = refs[:planes]
    gq_ref, gk_ref, cos_ref, sin_ref, act_ref, pre_ref, rot_ref, all_ref = refs[planes:]
    depth = w_refs[0].shape[0]

    @pl.when(pl.program_id(0) == 0)
    def _():
        for d in range(planes):
            place = pl.ds(pl.multiple_of(at_ref[d] * depth, depth), depth)
            all_ref[place, :] = w_refs[d][...]

    x = x_ref[...].astype(f32)
    inverse = lax.rsqrt(jnp.mean(x * x, axis=-1, keepdims=True) + norm_eps)
    act = (x * inverse * gain_ref[...]).astype(bf16)
    act_ref[...] = act
    y = None
    for d in range(planes):
        columns = pl.ds(pl.multiple_of(at_ref[d] * depth, depth), depth)
        term = dot_nn(act_ref[:, columns], w_refs[d][...])
        y = term if y is None else y + term
    cosine, sine = cos_ref[...], sin_ref[...]
    for part, gain in enumerate((gq_ref[...], gk_ref[...])):
        for h in range(heads):
            at = (part * heads + h) * HD
            u = y[:, at : at + HD]
            pre_ref[:, at : at + HD] = u
            n = u * lax.rsqrt(jnp.mean(u * u, axis=-1, keepdims=True) + head_eps) * gain
            rot_ref[:, at : at + HD] = (n * cosine + pltpu.roll(n, HD // 2, 1) * sine).astype(bf16)
    at = 2 * heads * HD
    rot_ref[:, at:] = y[:, at:].astype(bf16)


def qkv_project(places, rows, gain, weights, gain_q, gain_k, cosine, sine, heads):
    count, width = rows.shape
    planes = len(weights)
    depth, out_width = weights[0].shape
    pre_width = 2 * heads * HD
    whole = lambda i, s: (0, 0)
    block = lambda i, s: (i, 0)
    return pl.pallas_call(
        functools.partial(qkv_kernel, heads, planes),
        out_shape=(
            jax.ShapeDtypeStruct((count, width), bf16),
            jax.ShapeDtypeStruct((count, pre_width), f32),
            jax.ShapeDtypeStruct((count, out_width), bf16),
            jax.ShapeDtypeStruct((width, out_width), bf16),
        ),
        grid_spec=pltpu.PrefetchScalarGridSpec(
            num_scalar_prefetch=1,
            grid=(count // ROWS,),
            in_specs=[
                pl.BlockSpec((ROWS, width), block),
                pl.BlockSpec((1, width), whole),
            ]
            + [pl.BlockSpec((depth, out_width), whole)] * planes
            + [
                pl.BlockSpec((1, HD), whole),
                pl.BlockSpec((1, HD), whole),
                pl.BlockSpec((ROWS, HD), block),
                pl.BlockSpec((ROWS, HD), block),
            ],
            out_specs=(
                pl.BlockSpec((ROWS, width), block),
                pl.BlockSpec((ROWS, pre_width), block),
                pl.BlockSpec((ROWS, out_width), block),
                pl.BlockSpec((width, out_width), whole),
            ),
        ),
        compiler_params=params(1, 56),
        cost_estimate=estimate(
            flops=2 * count * width * out_width,
            bytes_accessed=4 * count * width + 2 * width * out_width + 6 * count * out_width,
            transcendentals=0,
        ),
        name="qkv_project",
    )(places, rows, gain, *weights, gain_q, gain_k, cosine, sine)


def attn_kernel(
    scale, low_ref, high_ref, q_ref, k_ref, v_ref, sq_ref, sk_ref, o_ref, ol_ref, lse_ref, s_scr
):
    block = pl.program_id(1)
    low, high = low_ref[block], high_ref[block]
    q = q_ref[...]
    seg_q = sq_ref[...]
    half = ROWS // 2

    def scores(kb, top):
        at = pl.ds(pl.multiple_of(kb * ROWS, ROWS), ROWS)
        s = dot_nt(q, k_ref[at, :]) * scale
        s = jnp.where(seg_q == sk_ref[:, at], s, masked_score)
        s_scr[:, at] = s
        return jnp.maximum(top, jnp.maximum(s[:, :half], s[:, half:]))

    top = lax.fori_loop(low, high, scores, jnp.full((ROWS, half), masked_score, f32))
    top = jnp.max(top, axis=-1, keepdims=True)

    def weigh(kb, carry):
        total, acc = carry
        at = pl.ds(pl.multiple_of(kb * ROWS, ROWS), ROWS)
        p = jnp.exp(s_scr[:, at] - top)
        acc = acc + dot_nn(p.astype(bf16), v_ref[at, :])
        return total + (p[:, :half] + p[:, half:]), acc

    total, acc = lax.fori_loop(
        low, high, weigh, (jnp.zeros((ROWS, half), f32), jnp.zeros((ROWS, HD), f32))
    )
    total = jnp.sum(total, axis=-1, keepdims=True)
    out = acc / total
    o_ref[...] = out
    ol_ref[...] = out.astype(bf16)
    lse = jnp.broadcast_to(top + jnp.log(total), (ROWS, HD)).T
    lse_ref[0] = lse[0:1, :]


def attention(rot, seg_col, seg_row, low, high, heads):
    count = rot.shape[0]
    blocks = count // ROWS
    scale = HD ** (-0.5)
    return pl.pallas_call(
        functools.partial(attn_kernel, scale),
        out_shape=(
            jax.ShapeDtypeStruct((count, heads * HD), f32),
            jax.ShapeDtypeStruct((count, heads * HD), bf16),
            jax.ShapeDtypeStruct((heads * blocks, 1, ROWS), f32),
        ),
        grid_spec=pltpu.PrefetchScalarGridSpec(
            num_scalar_prefetch=2,
            grid=(heads, blocks),
            in_specs=[
                pl.BlockSpec((ROWS, HD), lambda h, i, *s: (i, h)),
                pl.BlockSpec((count, HD), lambda h, i, *s: (0, heads + h)),
                pl.BlockSpec((count, HD), lambda h, i, *s: (0, 2 * heads + h)),
                pl.BlockSpec((ROWS, 1), lambda h, i, *s: (i, 0)),
                pl.BlockSpec((1, count), lambda h, i, *s: (0, 0)),
            ],
            out_specs=(
                pl.BlockSpec((ROWS, HD), lambda h, i, *s: (i, h)),
                pl.BlockSpec((ROWS, HD), lambda h, i, *s: (i, h)),
                pl.BlockSpec((1, 1, ROWS), lambda h, i, *s: (h * blocks + i, 0, 0)),
            ),
            scratch_shapes=[pltpu.VMEM((ROWS, count), f32)],
        ),
        compiler_params=params(2, 32),
        cost_estimate=estimate(
            flops=2 * heads * count * count * HD,
            bytes_accessed=12 * heads * count * HD,
            transcendentals=heads * count * count // 2,
        ),
        name="attention",
    )(low, high, rot, rot, rot, seg_col, seg_row)


def head_back(grad, pre, gain, cosine, sine):
    n = grad * cosine - pltpu.roll(grad, HD // 2, 1) * sine
    inverse = lax.rsqrt(jnp.mean(pre * pre, axis=-1, keepdims=True) + head_eps)
    w = n * gain
    back = inverse * w - pre * inverse**3 * jnp.mean(w * pre, axis=-1, keepdims=True)
    return back, jnp.sum(n * pre * inverse, axis=0, keepdims=True)


def attn_back_kernel(
    scale,
    low_ref,
    high_ref,
    q_ref,
    k_ref,
    v_ref,
    do_ref,
    o_ref,
    lse_ref,
    sq_ref,
    sk_ref,
    qpre_ref,
    kpre_ref,
    gq_ref,
    gk_ref,
    cosq_ref,
    sinq_ref,
    cosk_ref,
    sink_ref,
    grad_ref,
    gain_ref,
    dk_scr,
    dv_scr,
):
    head, block = pl.program_id(0), pl.program_id(1)
    heads = pl.num_programs(0)

    def columns(part):
        return pl.ds(pl.multiple_of((part * heads + head) * HD, HD), HD)

    low, high = low_ref[block], high_ref[block]

    @pl.when(block == 0)
    def _():
        dk_scr[...] = jnp.zeros_like(dk_scr)
        dv_scr[...] = jnp.zeros_like(dv_scr)

    @pl.when((block == 0) & (head == 0))
    def _():
        gain_ref[...] = jnp.zeros_like(gain_ref)

    q, do = q_ref[...], do_ref[...]
    row_dot = jnp.sum((do.astype(f32) * o_ref[...]).T, axis=0, keepdims=True)
    lse = lse_ref[0]
    seg_q = sq_ref[...]

    def tile(kb, dq):
        at = pl.ds(pl.multiple_of(kb * ROWS, ROWS), ROWS)
        k, v = k_ref[at, :], v_ref[at, :]
        s = dot_nt(k, q) * scale
        p = jnp.where(sk_ref[at, :] == seg_q, jnp.exp(s - lse), 0.0)
        dp = dot_nt(v, do)
        ds = (p * (dp - row_dot)).astype(bf16)
        dv_scr[at, :] += dot_nn(p.astype(bf16), do)
        dk_scr[at, :] += dot_nn(ds, q)
        return dq + dot_tn(ds, k)

    dq = lax.fori_loop(low, high, tile, jnp.zeros((ROWS, HD), f32))
    back, gain_q = head_back(dq * scale, qpre_ref[...], gq_ref[...], cosq_ref[...], sinq_ref[...])
    grad_ref[pl.ds(pl.multiple_of(block * ROWS, ROWS), ROWS), columns(0)] = back.astype(bf16)
    gain_ref[0:1, :] += gain_q

    @pl.when(block == pl.num_programs(1) - 1)
    def _():
        @pl.loop(0, dk_scr.shape[0] // ROWS)
        def _(i):
            at = pl.ds(pl.multiple_of(i * ROWS, ROWS), ROWS)
            back, gain_k = head_back(
                dk_scr[at, :] * scale, kpre_ref[at, :], gk_ref[...], cosk_ref[at, :], sink_ref[at, :]
            )
            grad_ref[at, columns(1)] = back.astype(bf16)
            grad_ref[at, columns(2)] = dv_scr[at, :].astype(bf16)
            gain_ref[1:2, :] += gain_k


def attention_back(
    rot, grad, out, lse, seg_col, seg_row, low, high, pre, gain_q, gain_k, cosine, sine, heads
):
    count = rot.shape[0]
    blocks = count // ROWS
    scale = HD ** (-0.5)
    mine = lambda h, i, *s: (i, h)
    whole = lambda h, i, *s: (0, 0)
    return pl.pallas_call(
        functools.partial(attn_back_kernel, scale),
        out_shape=(
            jax.ShapeDtypeStruct((count, 3 * heads * HD), bf16),
            jax.ShapeDtypeStruct((8, HD), f32),
        ),
        grid_spec=pltpu.PrefetchScalarGridSpec(
            num_scalar_prefetch=2,
            grid=(heads, blocks),
            in_specs=[
                pl.BlockSpec((ROWS, HD), mine),
                pl.BlockSpec((count, HD), lambda h, i, *s: (0, heads + h)),
                pl.BlockSpec((count, HD), lambda h, i, *s: (0, 2 * heads + h)),
                pl.BlockSpec((ROWS, HD), mine),
                pl.BlockSpec((ROWS, HD), mine),
                pl.BlockSpec((1, 1, ROWS), lambda h, i, *s: (h * blocks + i, 0, 0)),
                pl.BlockSpec((1, ROWS), lambda h, i, *s: (0, i)),
                pl.BlockSpec((count, 1), whole),
                pl.BlockSpec((ROWS, HD), mine),
                pl.BlockSpec((count, HD), lambda h, i, *s: (0, heads + h)),
                pl.BlockSpec((1, HD), whole),
                pl.BlockSpec((1, HD), whole),
                pl.BlockSpec((ROWS, HD), lambda h, i, *s: (i, 0)),
                pl.BlockSpec((ROWS, HD), lambda h, i, *s: (i, 0)),
                pl.BlockSpec((count, HD), whole),
                pl.BlockSpec((count, HD), whole),
            ],
            out_specs=(
                pl.BlockSpec((count, 3 * heads * HD), whole),
                pl.BlockSpec((8, HD), whole),
            ),
            scratch_shapes=[pltpu.VMEM((count, HD), f32), pltpu.VMEM((count, HD), f32)],
        ),
        compiler_params=params(2, 48),
        cost_estimate=estimate(
            flops=5 * heads * count * count * HD,
            bytes_accessed=30 * heads * count * HD,
            transcendentals=heads * count * count // 2,
        ),
        name="attention_back",
    )(
        low,
        high,
        rot,
        rot,
        rot,
        grad,
        out,
        lse,
        seg_row,
        seg_col,
        pre,
        pre,
        gain_q,
        gain_k,
        cosine,
        sine,
        cosine,
        sine,
    )


def expert_kernel(base, count, carried, mine_ref, x_ref, *refs):
    near = 1 if base == 0 else 0
    c_refs, refs = refs[: near + 1], refs[near + 1 :]
    wg_ref, wu_ref, wd_ref = refs[:3]
    refs = refs[3 + carried :]
    back_ref, out_ref, xs_ref, c_ref, hid_ref, gp_ref, up_ref = refs[:7]
    out_acc, back_acc, gate_scr, dot_scr = refs[7:]
    step = pl.program_id(1)
    per_plane, capacity, width = c_ref.shape
    rows = per_plane * capacity
    extra = x_ref.shape[2] - width
    lane = lax.broadcasted_iota(jnp.int32, (rows, extra), 1)
    high, low = lane == mine_ref[0], lane == mine_ref[0] + count

    @pl.when(step == 0)
    def _():
        xs_ref[...] = x_ref[:, :, :width]
        if near:

            @pl.when(pl.program_id(0) == 0)
            def _():
                c_ref[...] = c_refs[0][...]

            @pl.when(pl.program_id(0) > 0)
            def _():
                c_ref[...] = c_refs[1][...]

        else:
            c_ref[...] = c_refs[0][...]
        gates = x_ref[:, :, width:].reshape(rows, extra).astype(f32)
        gate_scr[...] = jnp.sum(jnp.where(high | low, gates, 0.0), axis=-1, keepdims=True)
        out_acc[...] = jnp.zeros_like(out_acc)
        back_acc[...] = jnp.zeros_like(back_acc)
        dot_scr[...] = jnp.zeros_like(dot_scr)

    x = x_ref[:, :, :width].reshape(rows, width)
    c = c_ref[...].reshape(rows, width)
    gate = gate_scr[...]
    wg, wu, wd = wg_ref[...], wu_ref[...], wd_ref[...]
    gate_pre, up_pre = dot_nn(x, wg), dot_nn(x, wu)
    sig = jax.nn.sigmoid(gate_pre)
    hidden = (gate_pre * sig * up_pre).astype(bf16)
    out_acc[...] += dot_nn(hidden, wd)
    plain = dot_nt(c, wd)
    wide = hidden.astype(f32)
    dot_scr[...] += jnp.sum(wide * plain, axis=-1, keepdims=True)
    hid_ref[...] = (wide * gate).astype(bf16).reshape(hid_ref.shape)
    hidden_grad = plain * gate
    gate_grad = (hidden_grad * up_pre * sig * (1.0 + gate_pre * (1.0 - sig))).astype(bf16)
    up_grad = (hidden_grad * gate_pre * sig).astype(bf16)
    gp_ref[...] = gate_grad.reshape(gp_ref.shape)
    up_ref[...] = up_grad.reshape(up_ref.shape)
    back_acc[...] += dot_nt(gate_grad, wg) + dot_nt(up_grad, wu)

    @pl.when(step == pl.num_programs(1) - 1)
    def _():
        dots = dot_scr[...]
        coarse = dots.astype(bf16).astype(f32)
        lanes = jnp.where(high, coarse, jnp.where(low, dots - coarse, 0.0)).astype(bf16)
        back_ref[:, :, :width] = back_acc[...].astype(bf16).reshape(c_ref.shape)
        back_ref[:, :, width:] = lanes.reshape(per_plane, capacity, extra)
        out_ref[...] = (out_acc[...] * gate).astype(bf16).reshape(out_ref.shape)


def experts(mine, x, near, far, wg, wu, wd, base, planes, count, kept):
    per_plane, blocks, capacity, wide = x.shape
    width = near.shape[3]
    halves, _, hidden = wg.shape
    rows = per_plane * capacity
    saved = jax.ShapeDtypeStruct((per_plane, planes, capacity, width), bf16)
    thin = jax.ShapeDtypeStruct((per_plane, planes, capacity, halves * hidden), bf16)
    moved = pl.BlockSpec((per_plane, None, capacity, wide), lambda i, f, s: (0, i, 0, 0))
    saved_spec = pl.BlockSpec((per_plane, None, capacity, width), lambda i, f, s: (0, base + i, 0, 0))
    thin_spec = pl.BlockSpec((per_plane, None, capacity, hidden), lambda i, f, s: (0, base + i, 0, f))
    carried = 0 if kept is None else len(kept)
    cots = (near, far) if base == 0 else (far,)
    cot_specs = [
        pl.BlockSpec(
            (per_plane, None, capacity, width), lambda i, f, s: (0, jnp.maximum(base + i - 1, 0), 0, 0)
        )
    ]
    if base == 0:
        cot_specs = [pl.BlockSpec((per_plane, None, capacity, width), lambda i, f, s: (0, 0, 0, 0))] + cot_specs
    result = pl.pallas_call(
        functools.partial(expert_kernel, base, count, carried),
        out_shape=(
            jax.ShapeDtypeStruct(x.shape, bf16),
            jax.ShapeDtypeStruct((per_plane, blocks, capacity, width), bf16),
            saved,
            saved,
            thin,
            thin,
            thin,
        ),
        grid_spec=pltpu.PrefetchScalarGridSpec(
            num_scalar_prefetch=1,
            grid=(blocks, halves),
            in_specs=[
                moved,
                *cot_specs,
                pl.BlockSpec((None, width, hidden), lambda i, f, s: (f, 0, 0)),
                pl.BlockSpec((None, width, hidden), lambda i, f, s: (f, 0, 0)),
                pl.BlockSpec((None, hidden, width), lambda i, f, s: (f, 0, 0)),
            ]
            + [pl.BlockSpec(memory_space=pl.ANY)] * carried,
            out_specs=(
                moved,
                pl.BlockSpec((per_plane, None, capacity, width), lambda i, f, s: (0, i, 0, 0)),
                saved_spec,
                saved_spec,
                thin_spec,
                thin_spec,
                thin_spec,
            ),
            scratch_shapes=[
                pltpu.VMEM((rows, width), f32),
                pltpu.VMEM((rows, width), f32),
                pltpu.VMEM((rows, 1), f32),
                pltpu.VMEM((rows, 1), f32),
            ],
        ),
        input_output_aliases={5 + len(cots) + i: 2 + i for i in range(carried)},
        compiler_params=params(2, 60),
        cost_estimate=estimate(
            flops=12 * blocks * rows * width * hidden * halves,
            bytes_accessed=10 * blocks * rows * width + 6 * blocks * width * hidden * halves,
            transcendentals=blocks * rows * hidden * halves,
        ),
        name="experts",
    )(mine, x, *cots, wg, wu, wd, *(kept or ()))
    return result[0], result[1], result[2:]


def gram_kernel(plus, left_ref, right_ref, *refs):
    total = dot_tn(left_ref[...], right_ref[...])
    if plus:
        total = total + refs[0][...]
    refs[-1][...] = total.astype(refs[-1].dtype)


def gram(left, right, left_cols, right_cols, dtype, plus=None):
    rows = left.shape[0]
    left_at, left_count = left_cols
    right_at, right_count = right_cols
    tall = min(left_count, 256)
    wide = min(right_count, 1024)
    out_spec = pl.BlockSpec((tall, wide), lambda j, i: (i, j))
    return pl.pallas_call(
        functools.partial(gram_kernel, plus is not None),
        out_shape=jax.ShapeDtypeStruct((left_count, right_count), dtype),
        grid=(right_count // wide, left_count // tall),
        in_specs=[
            pl.BlockSpec((rows, tall), lambda j, i: (0, left_at // tall + i)),
            pl.BlockSpec((rows, wide), lambda j, i: (0, right_at // wide + j)),
        ]
        + [out_spec] * (plus is not None),
        out_specs=out_spec,
        compiler_params=params(2, 48),
        cost_estimate=estimate(
            flops=2 * rows * left_count * right_count,
            bytes_accessed=2 * rows * (left_count + right_count) + 4 * left_count * right_count,
            transcendentals=0,
        ),
        name="gram",
    )(left, right, *(() if plus is None else (plus,)))


def project_kernel(plus, core_ref, rows_ref, weights_ref, *refs):
    total = dot_nt(rows_ref[...], weights_ref[...])
    if plus:
        total = total + refs[0][...].astype(f32)
    refs[-1][...] = total.astype(bf16)


def project_back(core, rows, weights, tok_rows, plus=None):
    count, depth = rows.shape
    width = weights.shape[0]
    chips = count // tok_rows // 2
    out_spec = pl.BlockSpec((tok_rows, width), lambda i, s: (i, 0))
    return pl.pallas_call(
        functools.partial(project_kernel, plus is not None),
        out_shape=jax.ShapeDtypeStruct((chips * tok_rows, width), bf16),
        grid_spec=pltpu.PrefetchScalarGridSpec(
            num_scalar_prefetch=1,
            grid=(chips,),
            in_specs=[
                pl.BlockSpec((tok_rows, depth), lambda i, s: (2 * i + s[0], 0)),
                pl.BlockSpec((width, depth), lambda i, s: (0, 0)),
            ]
            + [out_spec] * (plus is not None),
            out_specs=out_spec,
        ),
        compiler_params=params(1, 40),
        cost_estimate=estimate(
            flops=count * depth * width,
            bytes_accessed=2 * width * depth + count * depth + count * width,
            transcendentals=0,
        ),
        name="project_back",
    )(core, rows, weights, *(() if plus is None else (plus,)))


def after(value, *others):
    return lax.optimization_barrier((value,) + others)[0]


def body(
    hidden_in,
    out_cotangent,
    segment_number,
    expert_routes,
    pair_order,
    norm_gain,
    query_weight,
    key_weight,
    value_weight,
    output_weight,
    query_gain,
    key_gain,
    ffn_norm_gain,
    router_weight,
    expert_gate,
    expert_up,
    expert_down,
):
    tok_rows, width = hidden_in.shape
    devices = lax.axis_size(AXIS)
    members = max(1, SEQ_MIN // tok_rows)
    planes = devices // members
    per_plane = members // 2
    expert_count = devices // 2
    capacity = tok_rows * TOPK // expert_count
    heads = width // HD // members
    head_width = heads * HD
    own_rows = norm_gain.shape[0]
    seq = members * tok_rows
    me = lax.axis_index(AXIS)
    plane, member = me // members, me % members
    mine = (me // 2).astype(jnp.int32).reshape(1)
    first = (plane * per_plane).astype(jnp.int32)
    places = (plane ^ jnp.arange(planes, dtype=jnp.int32)).astype(jnp.int32)
    counted = jnp.concatenate([first[None], jnp.arange(planes, dtype=jnp.int32)])
    halfway = -(-planes // 2)
    chunks = [part for part in (range(halfway, planes), range(halfway)) if len(part)]

    def placed(part):
        return jnp.concatenate([first[None], places[part.start : part.stop]])

    plane_groups = [[g * members + j for j in range(members)] for g in range(planes)]
    stack_groups = [[g * members + j for g in range(planes)] for j in range(members)]
    core_groups = [
        [g * members + 2 * c + h for c in range(per_plane)] for g in range(planes) for h in (0, 1)
    ]

    def exchange(value, groups=None):
        return lax.all_to_all(
            value, AXIS, split_axis=0, concat_axis=0, tiled=True, axis_index_groups=groups
        )

    def gather(value, groups=None):
        return lax.all_gather(value, AXIS, axis=0, tiled=True, axis_index_groups=groups)

    def flip(value, bits):
        if bits == 0:
            return value
        return lax.ppermute(value, AXIS, [(i, i ^ bits) for i in range(devices)])

    def to_core(value):
        return flip(value, 1)

    def to_plane(value, d):
        return flip(value, members * d)

    wire, core_op = [], []

    def on_wire(value, groups):
        came = exchange(after(value, *wire[-1:]), groups)
        wire.append(came)
        return came

    def to_chips(value):
        return on_wire(value, core_groups)

    def in_turn(value):
        return after(value, *core_op[-1:])

    def ran(value):
        core_op.append(value)
        return value

    pieces = (
        router_weight.reshape(-1),
        norm_gain,
        ffn_norm_gain,
        query_gain,
        key_gain,
        segment_number.astype(bf16),
    )
    packed = jnp.concatenate(pieces)
    length = packed.shape[0]
    padded = -(-length // 128) * 128
    packed = jnp.pad(packed, (0, padded - length))
    packed = on_wire(jnp.broadcast_to(packed[None], (devices, padded)), None)
    small = []
    at = 0
    for piece in pieces:
        small.append(packed[:, at : at + piece.shape[0]])
        at += piece.shape[0]
    router_full = small[0].reshape(width, expert_count)
    gain_one = small[1].reshape(1, width).astype(f32)
    gain_two = small[2].reshape(1, width).astype(f32)
    gain_q = small[3].reshape(1, HD).astype(f32)
    gain_k = small[4].reshape(1, HD).astype(f32)
    segments = lax.dynamic_slice_in_dim(small[5], plane * members, members, 0).astype(f32)
    seg_row, seg_col = segments.reshape(1, seq), segments.reshape(seq, 1)
    seg_blocks = segments.reshape(seq // ROWS, ROWS)
    seg_first, seg_last = seg_blocks[:, 0], seg_blocks[:, -1]
    low = jnp.sum((seg_last[None, :] < seg_first[:, None]).astype(jnp.int32), axis=1)
    high = jnp.sum((seg_first[None, :] <= seg_last[:, None]).astype(jnp.int32), axis=1)

    columns = jnp.concatenate(
        [w.reshape(own_rows, members, head_width) for w in (query_weight, key_weight, value_weight)],
        axis=2,
    )
    slots = block_slots(expert_routes, pair_order, expert_count)
    columns = on_wire(
        after(columns, slots).transpose(1, 0, 2).reshape(members * own_rows, 3 * head_width), plane_groups
    )
    slots = [to_plane(slots, d) for d in range(planes)]
    stacked = [to_plane(after(output_weight, slots[0]), d) for d in range(planes)]
    weights = [to_plane(after(columns, *slots, *stacked), d) for d in range(planes)]
    output_rows = jnp.zeros((planes * own_rows, width), bf16)
    for d, rows in enumerate(stacked):
        output_rows = lax.dynamic_update_slice_in_dim(output_rows, rows, places[d] * own_rows, 0)
    rows_all = gather(hidden_in, plane_groups)

    cot_own = dispatch(counted, slots[0][None], out_cotangent[None], per_plane, capacity)
    cot_parts = [to_chips(cot_own)]
    output_full = gather(after(output_rows, columns), plane_groups)
    slots = jnp.stack(slots)
    cot_rows = {0: out_cotangent}
    top = planes // 2
    early, late = [], []
    if planes > 1:
        cot_rows[top] = to_plane(after(out_cotangent, *weights), top)
        early.append(cot_rows[top])
    for d in range(1, planes):
        if d != top:
            lowest = d & -d
            start = after(out_cotangent, *early) if d == lowest else cot_rows[d ^ lowest]
            cot_rows[d] = to_plane(start, lowest)
            late.append(cot_rows[d])

    halves = lambda w: jnp.concatenate([w, to_core(w)], axis=0)
    wg, wu, wd = halves(expert_gate), halves(expert_up), halves(expert_down)

    cosine, sine = rope_tables(seq)
    act_one, pre, rot, ordered = qkv_project(
        places, after(rows_all, wg, wu, wd), gain_one, weights, gain_q, gain_k, cosine, sine, heads
    )
    out_wide, out_heads, lse = attention(rot, seg_col, seg_row, low, high, heads)
    out_low = on_wire(after(out_heads, *early), plane_groups)
    out_low = out_low.reshape(members, tok_rows, head_width).transpose(1, 0, 2)
    out_low = out_low.reshape(tok_rows, planes, members, own_rows).transpose(0, 2, 1, 3)
    out_low = out_low.reshape(tok_rows, width)
    tokens = hidden_in.astype(f32)
    cotangent = out_cotangent.astype(f32)
    middle = tokens + dot_nn(out_low, output_full)
    inverse_two = lax.rsqrt(jnp.mean(middle * middle, axis=-1, keepdims=True) + norm_eps)
    act_two = (middle * inverse_two * gain_two).astype(bf16)

    logits = dot_nn(act_two, router_full)
    expert_ids = jnp.arange(expert_count, dtype=jnp.int32)
    routed = jnp.any(expert_routes[:, :, None] == expert_ids[None, None, :], axis=1)
    logits = jnp.where(routed, logits, masked_score)
    gates = jnp.where(routed, jnp.exp(logits - jnp.max(logits, axis=1, keepdims=True)), 0.0)
    gates = gates / jnp.sum(gates, axis=1, keepdims=True)
    coarse = lax.reduce_precision(gates, 8, 7)
    extra = -(-2 * expert_count // 128) * 128
    act_wide = jnp.concatenate(
        [
            act_two,
            coarse.astype(bf16),
            (gates - coarse).astype(bf16),
            jnp.zeros((tok_rows, extra - 2 * expert_count), bf16),
        ],
        axis=1,
    )

    act_wide = after(act_wide, *late)
    act_all = gather(act_wide, stack_groups).reshape(planes, tok_rows, -1)
    if planes > 1:
        far = jnp.stack([after(cot_rows[d], act_wide) for d in range(1, planes)])
        sent = dispatch(counted[:planes], slots[1:], far, per_plane, capacity)
        cot_parts.append(to_chips(ran(sent)))

    act = []
    for part in chunks:
        own_slots = slots[part.start : part.stop]
        sent = dispatch(placed(part), own_slots, in_turn(act_all), per_plane, capacity)
        act.append(to_chips(ran(sent)))
    kept, back, outs = None, [], []
    for part, rows in zip(chunks, act):
        sent, out, kept = experts(
            mine,
            in_turn(rows),
            cot_parts[0],
            cot_parts[-1],
            wg,
            wu,
            wd,
            part.start,
            planes,
            expert_count,
            kept,
        )
        back.append(to_chips(ran(sent)))
        outs.append(out)
    x_all, c_all, hid_all, gp_all, up_all = kept

    hidden = expert_gate.shape[2]
    flat = lambda value: value.reshape(-1, value.shape[3])
    sides = (
        (flat(x_all), flat(gp_all), 1),
        (flat(x_all), flat(up_all), 1),
        (flat(hid_all), flat(c_all), 0),
    )

    def half(side, which, plus=None):
        left, right, split = side
        cut, whole = (which * hidden, hidden), (0, width)
        cols = (whole, cut) if split else (cut, whole)
        return ran(gram(in_turn(left), right, *cols, f32, plus))

    def home(part, rows, *others):
        came = []
        for i, d in enumerate(part):
            summed = combine(first[None], slots[d], after(rows, *core_op[-1:], *others), i)
            came.append(to_plane(ran(summed), d))
        return came

    came = home(chunks[0], back[0])
    theirs = [half(side, 1) for side in sides]
    if len(chunks) > 1:
        came += home(chunks[1], back[1])
    outs[0] = to_chips(outs[0])
    back_sum = sum(rows.astype(f32) for rows in came)

    expert_in_grad = back_sum[:, :width]
    gate_grad = (
        back_sum[:, width : width + expert_count]
        + back_sum[:, width + expert_count : width + 2 * expert_count]
    )
    select_grad = gates * (gate_grad - jnp.sum(gates * gate_grad, axis=1, keepdims=True))
    logit_grad = select_grad.astype(bf16)
    grad_router = dot_tn(act_two, logit_grad)
    act_two_grad = expert_in_grad + dot_nt(logit_grad, router_full)
    weighted = act_two_grad * gain_two
    grad_gain_two = jnp.sum(act_two_grad * middle * inverse_two, axis=0)
    middle_grad = (
        cotangent
        + inverse_two * weighted
        - middle * inverse_two**3 * jnp.mean(weighted * middle, axis=-1, keepdims=True)
    )
    middle_low = middle_grad.astype(bf16)

    out_grad = dot_nt(middle_low, output_full).astype(bf16)
    out_grad = out_grad.reshape(tok_rows, members, planes, own_rows).transpose(0, 2, 1, 3)
    out_grad = out_grad.reshape(tok_rows, members, head_width).transpose(1, 0, 2)
    out_grad = out_grad.reshape(seq, head_width)
    ran(out_grad)
    theirs = [to_core(after(grad, out_grad)) for grad in theirs]
    out_grad = on_wire(out_grad, plane_groups)
    mixture = home(chunks[0], outs[0])
    dqkv, grad_gains = attention_back(
        rot,
        in_turn(out_grad),
        out_wide,
        lse,
        seg_col,
        seg_row,
        low,
        high,
        pre,
        gain_q,
        gain_k,
        cosine,
        sine,
        heads,
    )
    ran(dqkv)
    if len(chunks) > 1:
        mixture += home(chunks[1], to_chips(outs[1]))
        done = (*core_op[-2:], mixture[0], *theirs)
        dqkv, grad_gains = after(dqkv, *done), after(grad_gains, *done)
    middle_all = gather(after(middle_low, dqkv), plane_groups)

    sums = (
        grad_router.reshape(devices, -1),
        grad_gain_two.reshape(devices, -1),
        grad_gains[0].reshape(devices, -1),
        grad_gains[1].reshape(devices, -1),
    )
    packed = jnp.concatenate(sums, axis=1)
    length = packed.shape[1]
    padded = -(-length // 128) * 128
    packed = jnp.pad(packed, ((0, 0), (0, padded - length)))

    core = (me % 2).astype(jnp.int32).reshape(1)
    given = project_back(1 - core, dqkv, ordered, tok_rows)
    part = gram(after(act_one, given), dqkv, (0, width), (0, 3 * head_width), bf16)
    part = part.reshape(planes, members * own_rows, 3 * head_width)
    shares = [lax.dynamic_index_in_dim(part, places[d], 0, False) for d in range(planes)]
    given = after(to_core(given), *shares)
    act_one_grad = project_back(core, dqkv, ordered, tok_rows, given)
    ran(act_one_grad)
    grad_gate, grad_up, grad_down = (
        half(side, 0, other) for side, other in zip(sides, theirs)
    )
    output_part = gram(out_heads, in_turn(middle_all), (0, head_width), (0, width), bf16)
    done = (*core_op[-4:], output_part)
    shares = [after(to_plane(share, d), *done) for d, share in enumerate(shares)]
    taken = sum(share.astype(f32) for share in shares).astype(bf16)
    act_one_grad = on_wire(act_one_grad, core_groups)

    output_part = output_part.reshape(planes, head_width // planes, width)
    grad_output = 0.0
    for d in range(planes):
        to_owner = [
            (g * members + j, j * planes + (g ^ d)) for g in range(planes) for j in range(members)
        ]
        rows = lax.dynamic_index_in_dim(output_part, places[d], 0, False)
        grad_output = grad_output + lax.ppermute(rows, AXIS, to_owner).astype(f32)
    packed, act_one_grad, mixture = lax.optimization_barrier((packed, act_one_grad, mixture))
    layer_out = (middle + sum(rows.astype(f32) for rows in mixture)).astype(bf16)
    packed = exchange(packed)
    taken, packed, grad_output = lax.optimization_barrier((taken, packed, grad_output))
    part = exchange(taken, plane_groups).reshape(members, own_rows, 3, head_width)
    part = part.transpose(2, 1, 0, 3).reshape(3, own_rows, width).astype(f32)
    grad_query, grad_key, grad_value = part[0], part[1], part[2]
    act_one_grad = act_one_grad.reshape(per_plane, tok_rows, width)
    act_one_grad = jnp.sum(act_one_grad.astype(f32), axis=0)

    inverse_one = lax.rsqrt(jnp.mean(tokens * tokens, axis=-1, keepdims=True) + norm_eps)
    weighted = act_one_grad * gain_one
    grad_hidden = (
        middle_grad
        + inverse_one * weighted
        - tokens * inverse_one**3 * jnp.mean(weighted * tokens, axis=-1, keepdims=True)
    )
    grad_gain_one = (
        jnp.sum(
            grad_query * query_weight.astype(f32)
            + grad_key * key_weight.astype(f32)
            + grad_value * value_weight.astype(f32),
            axis=1,
        )
        / norm_gain.astype(f32)
    )

    summed = jnp.sum(packed, axis=0)
    at, tiny = 0, []
    for piece in sums:
        tiny.append(summed[at : at + piece.shape[1]])
        at += piece.shape[1]

    return (
        layer_out,
        grad_hidden,
        grad_gain_one,
        grad_query,
        grad_key,
        grad_value,
        grad_output,
        tiny[2],
        tiny[3],
        tiny[1],
        tiny[0].reshape(own_rows, expert_count),
        grad_gate[None],
        grad_up[None],
        grad_down[None],
    )


def solution(mesh):
    row, mat, cube = P(AXIS), P(AXIS, None), P(AXIS, None, None)
    return jax.shard_map(
        body,
        mesh=mesh,
        in_specs=(mat, mat, row, mat, mat, row, mat, mat, mat, mat, row, row, row, mat)
        + (cube,) * 3,
        out_specs=(mat, mat, row, mat, mat, mat, mat, row, row, row, mat) + (cube,) * 3,
        check_vma=False,
    )
```

```python
import functools
import math

import jax
import jax.numpy as jnp
from jax import lax
from jax.experimental import pallas as pl
from jax.experimental.pallas import tpu as pltpu
from jax.sharding import PartitionSpec as P

HD = 128
TOPK = 8
SEQ_MIN = 2048
ROWS = 256
SHARE = 32

norm_eps = 1e-05
head_eps = 1e-06
rope_base = 10000.0
masked_score = -1e30
absent_slot = 4096.0

AXIS = "fsdp"
f32 = jnp.float32
bf16 = jnp.bfloat16
MIB = 1 << 20


def dot_nt(left, right):
    return lax.dot_general(left, right, (((1,), (1,)), ((), ())), preferred_element_type=f32)


def dot_tn(left, right):
    return lax.dot_general(left, right, (((0,), (0,)), ((), ())), preferred_element_type=f32)


def dot_nn(left, right):
    return lax.dot_general(left, right, (((1,), (0,)), ((), ())), preferred_element_type=f32)


def params(steps, mib):
    return pltpu.CompilerParams(
        dimension_semantics=("arbitrary",) * steps, vmem_limit_bytes=mib * MIB
    )


def estimate(flops, bytes_accessed, transcendentals):
    return pl.CostEstimate(
        flops=flops // SHARE, bytes_accessed=bytes_accessed // SHARE, transcendentals=transcendentals // SHARE
    )


def rope_tables(count):
    half_width = HD // 2
    frequency = jnp.exp(-math.log(rope_base) * 2.0 * jnp.arange(half_width, dtype=f32) / HD)
    angles = jnp.arange(count, dtype=f32)[:, None] * frequency[None, :]
    cosine, sine = jnp.cos(angles), jnp.sin(angles)
    return jnp.concatenate([cosine, cosine], axis=-1), jnp.concatenate([-sine, sine], axis=-1)


def slots_kernel(expert_count, routes_ref, order_ref, slots_ref):
    tok_rows = routes_ref.shape[0]
    pair_count = order_ref.shape[1]
    order = order_ref[...]
    shift = TOPK.bit_length() - 1
    token_of = lax.shift_right_logical(order, jnp.full_like(order, shift))
    route_of = order & (TOPK - 1)
    token_iota = lax.broadcasted_iota(jnp.int32, (tok_rows, pair_count), 0)
    token_hot = jnp.where(token_iota == token_of, 1.0, 0.0).astype(bf16)
    place = lax.broadcasted_iota(jnp.int32, (TOPK, pair_count), 1)
    chosen = lax.broadcasted_iota(jnp.int32, (TOPK, pair_count), 0) == route_of
    high = lax.shift_right_logical(place, jnp.full_like(place, 8)).astype(f32)
    low = (place & 255).astype(f32)
    digits = jnp.concatenate([jnp.where(chosen, high, 0.0), jnp.where(chosen, low, 0.0)], axis=0)
    found = dot_nt(token_hot, digits.astype(bf16))
    rank = found[:, :TOPK] * 256.0 + found[:, TOPK:]
    routes = routes_ref[...]
    lanes = -(-expert_count // 128) * 128
    expert_iota = lax.broadcasted_iota(jnp.int32, (tok_rows, lanes), 1)
    never = 1e9
    by_expert = jnp.full((tok_rows, lanes), never, f32)
    for k in range(TOPK):
        by_expert = jnp.where(expert_iota == routes[:, k : k + 1], rank[:, k : k + 1], by_expert)
    turned = by_expert.T
    for e in range(expert_count):
        mine = turned[e : e + 1, :]
        earlier = jnp.where(by_expert[:, e : e + 1] < mine, 1.0, 0.0)
        count = jnp.sum(earlier, axis=0, keepdims=True)
        slots_ref[e : e + 1, :] = jnp.where(mine < never, count, absent_slot)


def block_slots(routes, order, expert_count):
    tok_rows = routes.shape[0]
    return pl.pallas_call(
        functools.partial(slots_kernel, expert_count),
        out_shape=jax.ShapeDtypeStruct((expert_count, tok_rows), f32),
        compiler_params=pltpu.CompilerParams(vmem_limit_bytes=32 * MIB),
        name="block_slots",
    )(routes, order)


def slot_hot(slots_ref, expert, capacity):
    slot_row = slots_ref[pl.ds(expert, 1), :]
    slot_iota = lax.broadcasted_iota(jnp.int32, (capacity, slot_row.shape[1]), 0).astype(f32)
    return jnp.where(slot_iota == slot_row, 1.0, 0.0).astype(bf16)


def plane_hot(slots_ref, first, shape):
    return jnp.concatenate([slot_hot(slots_ref, first + r, shape[1]) for r in range(shape[0])])


def dispatch_kernel(at_ref, slots_ref, rows_ref, out_ref):
    hot = plane_hot(slots_ref, at_ref[0], out_ref.shape)
    out_ref[...] = dot_nn(hot, rows_ref[...]).astype(bf16).reshape(out_ref.shape)


def dispatch(at, slots, rows, per_plane, capacity):
    blocks, experts, tok_rows = slots.shape
    width = rows.shape[2]
    slot_rows = per_plane * capacity
    return pl.pallas_call(
        dispatch_kernel,
        out_shape=jax.ShapeDtypeStruct((per_plane, blocks, capacity, width), bf16),
        grid_spec=pltpu.PrefetchScalarGridSpec(
            num_scalar_prefetch=1,
            grid=(blocks,),
            in_specs=[
                pl.BlockSpec((None, experts, tok_rows), lambda i, s: (i, 0, 0)),
                pl.BlockSpec((None, tok_rows, width), lambda i, s: (s[1 + i], 0, 0)),
            ],
            out_specs=pl.BlockSpec((per_plane, None, capacity, width), lambda i, s: (0, i, 0, 0)),
        ),
        compiler_params=params(1, 40),
        cost_estimate=estimate(
            flops=2 * blocks * slot_rows * tok_rows * width,
            bytes_accessed=2 * blocks * (slot_rows + tok_rows) * width,
            transcendentals=0,
        ),
        name="dispatch",
    )(at, slots, rows)


def combine_kernel(first_ref, slots_ref, rows_ref, out_ref):
    hot = plane_hot(slots_ref, first_ref[0], rows_ref.shape)
    rows = rows_ref[...].reshape(hot.shape[0], rows_ref.shape[2])
    out_ref[...] = dot_tn(hot, rows).astype(bf16)


def combine(first, slots, rows, block):
    experts, tok_rows = slots.shape
    per_plane, _, capacity, width = rows.shape
    slot_rows = per_plane * capacity
    return pl.pallas_call(
        combine_kernel,
        out_shape=jax.ShapeDtypeStruct((tok_rows, width), bf16),
        grid_spec=pltpu.PrefetchScalarGridSpec(
            num_scalar_prefetch=1,
            grid=(1,),
            in_specs=[
                pl.BlockSpec((experts, tok_rows), lambda i, s: (0, 0)),
                pl.BlockSpec((per_plane, None, capacity, width), lambda i, s: (0, block, 0, 0)),
            ],
            out_specs=pl.BlockSpec((tok_rows, width), lambda i, s: (0, 0)),
        ),
        compiler_params=params(1, 40),
        cost_estimate=estimate(
            flops=2 * slot_rows * tok_rows * width,
            bytes_accessed=2 * (slot_rows + tok_rows) * width,
            transcendentals=0,
        ),
        name="combine",
    )(first, slots, rows)


def qkv_kernel(heads, planes, at_ref, x_ref, gain_ref, *refs):
    w_refs = refs[:planes]
    gq_ref, gk_ref, cos_ref, sin_ref, act_ref, pre_ref, rot_ref, all_ref = refs[planes:]
    depth = w_refs[0].shape[0]

    @pl.when(pl.program_id(0) == 0)
    def _():
        for d in range(planes):
            place = pl.ds(pl.multiple_of(at_ref[d] * depth, depth), depth)
            all_ref[place, :] = w_refs[d][...]

    x = x_ref[...].astype(f32)
    inverse = lax.rsqrt(jnp.mean(x * x, axis=-1, keepdims=True) + norm_eps)
    act = (x * inverse * gain_ref[...]).astype(bf16)
    act_ref[...] = act
    y = None
    for d in range(planes):
        columns = pl.ds(pl.multiple_of(at_ref[d] * depth, depth), depth)
        term = dot_nn(act_ref[:, columns], w_refs[d][...])
        y = term if y is None else y + term
    cosine, sine = cos_ref[...], sin_ref[...]
    for part, gain in enumerate((gq_ref[...], gk_ref[...])):
        for h in range(heads):
            at = (part * heads + h) * HD
            u = y[:, at : at + HD]
            pre_ref[:, at : at + HD] = u
            n = u * lax.rsqrt(jnp.mean(u * u, axis=-1, keepdims=True) + head_eps) * gain
            rot_ref[:, at : at + HD] = (n * cosine + pltpu.roll(n, HD // 2, 1) * sine).astype(bf16)
    at = 2 * heads * HD
    rot_ref[:, at:] = y[:, at:].astype(bf16)


def qkv_project(places, rows, gain, weights, gain_q, gain_k, cosine, sine, heads):
    count, width = rows.shape
    planes = len(weights)
    depth, out_width = weights[0].shape
    pre_width = 2 * heads * HD
    whole = lambda i, s: (0, 0)
    block = lambda i, s: (i, 0)
    return pl.pallas_call(
        functools.partial(qkv_kernel, heads, planes),
        out_shape=(
            jax.ShapeDtypeStruct((count, width), bf16),
            jax.ShapeDtypeStruct((count, pre_width), f32),
            jax.ShapeDtypeStruct((count, out_width), bf16),
            jax.ShapeDtypeStruct((width, out_width), bf16),
        ),
        grid_spec=pltpu.PrefetchScalarGridSpec(
            num_scalar_prefetch=1,
            grid=(count // ROWS,),
            in_specs=[
                pl.BlockSpec((ROWS, width), block),
                pl.BlockSpec((1, width), whole),
            ]
            + [pl.BlockSpec((depth, out_width), whole)] * planes
            + [
                pl.BlockSpec((1, HD), whole),
                pl.BlockSpec((1, HD), whole),
                pl.BlockSpec((ROWS, HD), block),
                pl.BlockSpec((ROWS, HD), block),
            ],
            out_specs=(
                pl.BlockSpec((ROWS, width), block),
                pl.BlockSpec((ROWS, pre_width), block),
                pl.BlockSpec((ROWS, out_width), block),
                pl.BlockSpec((width, out_width), whole),
            ),
        ),
        compiler_params=params(1, 56),
        cost_estimate=estimate(
            flops=2 * count * width * out_width,
            bytes_accessed=4 * count * width + 2 * width * out_width + 6 * count * out_width,
            transcendentals=0,
        ),
        name="qkv_project",
    )(places, rows, gain, *weights, gain_q, gain_k, cosine, sine)


def attn_kernel(
    scale, low_ref, high_ref, q_ref, k_ref, v_ref, sq_ref, sk_ref, o_ref, ol_ref, lse_ref, s_scr
):
    block = pl.program_id(1)
    low, high = low_ref[block], high_ref[block]
    q = q_ref[...]
    seg_q = sq_ref[...]
    half = ROWS // 2

    def scores(kb, top):
        at = pl.ds(pl.multiple_of(kb * ROWS, ROWS), ROWS)
        s = dot_nt(q, k_ref[at, :]) * scale
        s = jnp.where(seg_q == sk_ref[:, at], s, masked_score)
        s_scr[:, at] = s
        return jnp.maximum(top, jnp.maximum(s[:, :half], s[:, half:]))

    top = lax.fori_loop(low, high, scores, jnp.full((ROWS, half), masked_score, f32))
    top = jnp.max(top, axis=-1, keepdims=True)

    def weigh(kb, carry):
        total, acc = carry
        at = pl.ds(pl.multiple_of(kb * ROWS, ROWS), ROWS)
        p = jnp.exp(s_scr[:, at] - top)
        acc = acc + dot_nn(p.astype(bf16), v_ref[at, :])
        return total + (p[:, :half] + p[:, half:]), acc

    total, acc = lax.fori_loop(
        low, high, weigh, (jnp.zeros((ROWS, half), f32), jnp.zeros((ROWS, HD), f32))
    )
    total = jnp.sum(total, axis=-1, keepdims=True)
    out = acc / total
    o_ref[...] = out
    ol_ref[...] = out.astype(bf16)
    lse = jnp.broadcast_to(top + jnp.log(total), (ROWS, HD)).T
    lse_ref[0] = lse[0:1, :]


def attention(rot, seg_col, seg_row, low, high, heads):
    count = rot.shape[0]
    blocks = count // ROWS
    scale = HD ** (-0.5)
    return pl.pallas_call(
        functools.partial(attn_kernel, scale),
        out_shape=(
            jax.ShapeDtypeStruct((count, heads * HD), f32),
            jax.ShapeDtypeStruct((count, heads * HD), bf16),
            jax.ShapeDtypeStruct((heads * blocks, 1, ROWS), f32),
        ),
        grid_spec=pltpu.PrefetchScalarGridSpec(
            num_scalar_prefetch=2,
            grid=(heads, blocks),
            in_specs=[
                pl.BlockSpec((ROWS, HD), lambda h, i, *s: (i, h)),
                pl.BlockSpec((count, HD), lambda h, i, *s: (0, heads + h)),
                pl.BlockSpec((count, HD), lambda h, i, *s: (0, 2 * heads + h)),
                pl.BlockSpec((ROWS, 1), lambda h, i, *s: (i, 0)),
                pl.BlockSpec((1, count), lambda h, i, *s: (0, 0)),
            ],
            out_specs=(
                pl.BlockSpec((ROWS, HD), lambda h, i, *s: (i, h)),
                pl.BlockSpec((ROWS, HD), lambda h, i, *s: (i, h)),
                pl.BlockSpec((1, 1, ROWS), lambda h, i, *s: (h * blocks + i, 0, 0)),
            ),
            scratch_shapes=[pltpu.VMEM((ROWS, count), f32)],
        ),
        compiler_params=params(2, 32),
        cost_estimate=estimate(
            flops=2 * heads * count * count * HD,
            bytes_accessed=12 * heads * count * HD,
            transcendentals=heads * count * count // 2,
        ),
        name="attention",
    )(low, high, rot, rot, rot, seg_col, seg_row)


def head_back(grad, pre, gain, cosine, sine):
    n = grad * cosine - pltpu.roll(grad, HD // 2, 1) * sine
    inverse = lax.rsqrt(jnp.mean(pre * pre, axis=-1, keepdims=True) + head_eps)
    w = n * gain
    back = inverse * w - pre * inverse**3 * jnp.mean(w * pre, axis=-1, keepdims=True)
    return back, jnp.sum(n * pre * inverse, axis=0, keepdims=True)


def attn_back_kernel(
    scale,
    low_ref,
    high_ref,
    q_ref,
    k_ref,
    v_ref,
    do_ref,
    o_ref,
    lse_ref,
    sq_ref,
    sk_ref,
    qpre_ref,
    kpre_ref,
    gq_ref,
    gk_ref,
    cosq_ref,
    sinq_ref,
    cosk_ref,
    sink_ref,
    grad_ref,
    gain_ref,
    dk_scr,
    dv_scr,
):
    head, block = pl.program_id(0), pl.program_id(1)
    heads = pl.num_programs(0)

    def columns(part):
        return pl.ds(pl.multiple_of((part * heads + head) * HD, HD), HD)

    low, high = low_ref[block], high_ref[block]

    @pl.when(block == 0)
    def _():
        dk_scr[...] = jnp.zeros_like(dk_scr)
        dv_scr[...] = jnp.zeros_like(dv_scr)

    @pl.when((block == 0) & (head == 0))
    def _():
        gain_ref[...] = jnp.zeros_like(gain_ref)

    q, do = q_ref[...], do_ref[...]
    row_dot = jnp.sum((do.astype(f32) * o_ref[...]).T, axis=0, keepdims=True)
    lse = lse_ref[0]
    seg_q = sq_ref[...]

    def tile(kb, dq):
        at = pl.ds(pl.multiple_of(kb * ROWS, ROWS), ROWS)
        k, v = k_ref[at, :], v_ref[at, :]
        s = dot_nt(k, q) * scale
        p = jnp.where(sk_ref[at, :] == seg_q, jnp.exp(s - lse), 0.0)
        dp = dot_nt(v, do)
        ds = (p * (dp - row_dot)).astype(bf16)
        dv_scr[at, :] += dot_nn(p.astype(bf16), do)
        dk_scr[at, :] += dot_nn(ds, q)
        return dq + dot_tn(ds, k)

    dq = lax.fori_loop(low, high, tile, jnp.zeros((ROWS, HD), f32))
    back, gain_q = head_back(dq * scale, qpre_ref[...], gq_ref[...], cosq_ref[...], sinq_ref[...])
    grad_ref[pl.ds(pl.multiple_of(block * ROWS, ROWS), ROWS), columns(0)] = back.astype(bf16)
    gain_ref[0:1, :] += gain_q

    @pl.when(block == pl.num_programs(1) - 1)
    def _():
        @pl.loop(0, dk_scr.shape[0] // ROWS)
        def _(i):
            at = pl.ds(pl.multiple_of(i * ROWS, ROWS), ROWS)
            back, gain_k = head_back(
                dk_scr[at, :] * scale, kpre_ref[at, :], gk_ref[...], cosk_ref[at, :], sink_ref[at, :]
            )
            grad_ref[at, columns(1)] = back.astype(bf16)
            grad_ref[at, columns(2)] = dv_scr[at, :].astype(bf16)
            gain_ref[1:2, :] += gain_k


def attention_back(
    rot, grad, out, lse, seg_col, seg_row, low, high, pre, gain_q, gain_k, cosine, sine, heads
):
    count = rot.shape[0]
    blocks = count // ROWS
    scale = HD ** (-0.5)
    mine = lambda h, i, *s: (i, h)
    whole = lambda h, i, *s: (0, 0)
    return pl.pallas_call(
        functools.partial(attn_back_kernel, scale),
        out_shape=(
            jax.ShapeDtypeStruct((count, 3 * heads * HD), bf16),
            jax.ShapeDtypeStruct((8, HD), f32),
        ),
        grid_spec=pltpu.PrefetchScalarGridSpec(
            num_scalar_prefetch=2,
            grid=(heads, blocks),
            in_specs=[
                pl.BlockSpec((ROWS, HD), mine),
                pl.BlockSpec((count, HD), lambda h, i, *s: (0, heads + h)),
                pl.BlockSpec((count, HD), lambda h, i, *s: (0, 2 * heads + h)),
                pl.BlockSpec((ROWS, HD), mine),
                pl.BlockSpec((ROWS, HD), mine),
                pl.BlockSpec((1, 1, ROWS), lambda h, i, *s: (h * blocks + i, 0, 0)),
                pl.BlockSpec((1, ROWS), lambda h, i, *s: (0, i)),
                pl.BlockSpec((count, 1), whole),
                pl.BlockSpec((ROWS, HD), mine),
                pl.BlockSpec((count, HD), lambda h, i, *s: (0, heads + h)),
                pl.BlockSpec((1, HD), whole),
                pl.BlockSpec((1, HD), whole),
                pl.BlockSpec((ROWS, HD), lambda h, i, *s: (i, 0)),
                pl.BlockSpec((ROWS, HD), lambda h, i, *s: (i, 0)),
                pl.BlockSpec((count, HD), whole),
                pl.BlockSpec((count, HD), whole),
            ],
            out_specs=(
                pl.BlockSpec((count, 3 * heads * HD), whole),
                pl.BlockSpec((8, HD), whole),
            ),
            scratch_shapes=[pltpu.VMEM((count, HD), f32), pltpu.VMEM((count, HD), f32)],
        ),
        compiler_params=params(2, 48),
        cost_estimate=estimate(
            flops=5 * heads * count * count * HD,
            bytes_accessed=30 * heads * count * HD,
            transcendentals=heads * count * count // 2,
        ),
        name="attention_back",
    )(
        low,
        high,
        rot,
        rot,
        rot,
        grad,
        out,
        lse,
        seg_row,
        seg_col,
        pre,
        pre,
        gain_q,
        gain_k,
        cosine,
        sine,
        cosine,
        sine,
    )


def expert_kernel(count, carried, mine_ref, x_ref, near_ref, far_ref, *refs):
    wg_ref, wu_ref, wd_ref = refs[:3]
    refs = refs[3 + carried :]
    back_ref, out_ref, xs_ref, c_ref, hid_ref, gp_ref, up_ref = refs[:7]
    out_acc, back_acc, gate_scr, dot_scr = refs[7:]
    step = pl.program_id(1)
    per_plane, capacity, width = c_ref.shape
    rows = per_plane * capacity
    extra = x_ref.shape[2] - width
    lane = lax.broadcasted_iota(jnp.int32, (rows, extra), 1)
    high, low = lane == mine_ref[0], lane == mine_ref[0] + count

    @pl.when(step == 0)
    def _():
        xs_ref[...] = x_ref[:, :, :width]

        @pl.when(pl.program_id(0) == 0)
        def _():
            c_ref[...] = near_ref[...]

        @pl.when(pl.program_id(0) > 0)
        def _():
            c_ref[...] = far_ref[...]
        gates = x_ref[:, :, width:].reshape(rows, extra).astype(f32)
        gate_scr[...] = jnp.sum(jnp.where(high | low, gates, 0.0), axis=-1, keepdims=True)
        out_acc[...] = jnp.zeros_like(out_acc)
        back_acc[...] = jnp.zeros_like(back_acc)
        dot_scr[...] = jnp.zeros_like(dot_scr)

    x = x_ref[:, :, :width].reshape(rows, width)
    c = c_ref[...].reshape(rows, width)
    gate = gate_scr[...]
    wg, wu, wd = wg_ref[...], wu_ref[...], wd_ref[...]
    gate_pre, up_pre = dot_nn(x, wg), dot_nn(x, wu)
    sig = jax.nn.sigmoid(gate_pre)
    hidden = (gate_pre * sig * up_pre).astype(bf16)
    out_acc[...] += dot_nn(hidden, wd)
    plain = dot_nt(c, wd)
    wide = hidden.astype(f32)
    dot_scr[...] += jnp.sum(wide * plain, axis=-1, keepdims=True)
    hid_ref[...] = (wide * gate).astype(bf16).reshape(hid_ref.shape)
    hidden_grad = plain * gate
    gate_grad = (hidden_grad * up_pre * sig * (1.0 + gate_pre * (1.0 - sig))).astype(bf16)
    up_grad = (hidden_grad * gate_pre * sig).astype(bf16)
    gp_ref[...] = gate_grad.reshape(gp_ref.shape)
    up_ref[...] = up_grad.reshape(up_ref.shape)
    back_acc[...] += dot_nt(gate_grad, wg) + dot_nt(up_grad, wu)

    @pl.when(step == pl.num_programs(1) - 1)
    def _():
        dots = dot_scr[...]
        coarse = dots.astype(bf16).astype(f32)
        lanes = jnp.where(high, coarse, jnp.where(low, dots - coarse, 0.0)).astype(bf16)
        back_ref[:, :, :width] = back_acc[...].astype(bf16).reshape(c_ref.shape)
        back_ref[:, :, width:] = lanes.reshape(per_plane, capacity, extra)
        out_ref[...] = (out_acc[...] * gate).astype(bf16).reshape(out_ref.shape)


def experts(mine, x, near, far, wg, wu, wd, base, planes, count, kept):
    per_plane, blocks, capacity, wide = x.shape
    width = near.shape[3]
    halves, _, hidden = wg.shape
    rows = per_plane * capacity
    saved = jax.ShapeDtypeStruct((per_plane, planes, capacity, width), bf16)
    thin = jax.ShapeDtypeStruct((per_plane, planes, capacity, halves * hidden), bf16)
    moved = pl.BlockSpec((per_plane, None, capacity, wide), lambda i, f, s: (0, i, 0, 0))
    saved_spec = pl.BlockSpec((per_plane, None, capacity, width), lambda i, f, s: (0, base + i, 0, 0))
    thin_spec = pl.BlockSpec((per_plane, None, capacity, hidden), lambda i, f, s: (0, base + i, 0, f))
    carried = 0 if kept is None else len(kept)
    skip = base - 1 if base else 0
    cot_specs = [
        pl.BlockSpec((per_plane, None, capacity, width), lambda i, f, s: (0, 0, 0, 0)),
        pl.BlockSpec(
            (per_plane, None, capacity, width),
            lambda i, f, s: (0, jnp.maximum(skip + i - 1, 0), 0, 0),
        ),
    ]
    result = pl.pallas_call(
        functools.partial(expert_kernel, count, carried),
        out_shape=(
            jax.ShapeDtypeStruct(x.shape, bf16),
            jax.ShapeDtypeStruct((per_plane, blocks, capacity, width), bf16),
            saved,
            saved,
            thin,
            thin,
            thin,
        ),
        grid_spec=pltpu.PrefetchScalarGridSpec(
            num_scalar_prefetch=1,
            grid=(blocks, halves),
            in_specs=[
                moved,
                *cot_specs,
                pl.BlockSpec((None, width, hidden), lambda i, f, s: (f, 0, 0)),
                pl.BlockSpec((None, width, hidden), lambda i, f, s: (f, 0, 0)),
                pl.BlockSpec((None, hidden, width), lambda i, f, s: (f, 0, 0)),
            ]
            + [pl.BlockSpec(memory_space=pl.ANY)] * carried,
            out_specs=(
                moved,
                pl.BlockSpec((per_plane, None, capacity, width), lambda i, f, s: (0, i, 0, 0)),
                saved_spec,
                saved_spec,
                thin_spec,
                thin_spec,
                thin_spec,
            ),
            scratch_shapes=[
                pltpu.VMEM((rows, width), f32),
                pltpu.VMEM((rows, width), f32),
                pltpu.VMEM((rows, 1), f32),
                pltpu.VMEM((rows, 1), f32),
            ],
        ),
        input_output_aliases={7 + i: 2 + i for i in range(carried)},
        compiler_params=params(2, 60),
        cost_estimate=estimate(
            flops=12 * blocks * rows * width * hidden * halves,
            bytes_accessed=10 * blocks * rows * width + 6 * blocks * width * hidden * halves,
            transcendentals=blocks * rows * hidden * halves,
        ),
        name="experts",
    )(mine, x, near, far, wg, wu, wd, *(kept or ()))
    return result[0], result[1], result[2:]


def gram_kernel(plus, left_ref, right_ref, *refs):
    total = dot_tn(left_ref[...], right_ref[...])
    if plus:
        total = total + refs[0][...]
    refs[-1][...] = total.astype(refs[-1].dtype)


def gram(left, right, left_cols, right_cols, dtype, plus=None):
    rows = left.shape[0]
    left_at, left_count = left_cols
    right_at, right_count = right_cols
    tall = min(left_count, 256)
    wide = min(right_count, 1024)
    out_spec = pl.BlockSpec((tall, wide), lambda j, i: (i, j))
    return pl.pallas_call(
        functools.partial(gram_kernel, plus is not None),
        out_shape=jax.ShapeDtypeStruct((left_count, right_count), dtype),
        grid=(right_count // wide, left_count // tall),
        in_specs=[
            pl.BlockSpec((rows, tall), lambda j, i: (0, left_at // tall + i)),
            pl.BlockSpec((rows, wide), lambda j, i: (0, right_at // wide + j)),
        ]
        + [out_spec] * (plus is not None),
        out_specs=out_spec,
        compiler_params=params(2, 48),
        cost_estimate=estimate(
            flops=2 * rows * left_count * right_count,
            bytes_accessed=2 * rows * (left_count + right_count) + 4 * left_count * right_count,
            transcendentals=0,
        ),
        name="gram",
    )(left, right, *(() if plus is None else (plus,)))


def project_kernel(plus, core_ref, rows_ref, weights_ref, *refs):
    total = dot_nt(rows_ref[...], weights_ref[...])
    if plus:
        total = total + refs[0][...].astype(f32)
    refs[-1][...] = total.astype(bf16)


def project_back(core, rows, weights, tok_rows, plus=None):
    count, depth = rows.shape
    width = weights.shape[0]
    chips = count // tok_rows // 2
    out_spec = pl.BlockSpec((tok_rows, width), lambda i, s: (i, 0))
    return pl.pallas_call(
        functools.partial(project_kernel, plus is not None),
        out_shape=jax.ShapeDtypeStruct((chips * tok_rows, width), bf16),
        grid_spec=pltpu.PrefetchScalarGridSpec(
            num_scalar_prefetch=1,
            grid=(chips,),
            in_specs=[
                pl.BlockSpec((tok_rows, depth), lambda i, s: (2 * i + s[0], 0)),
                pl.BlockSpec((width, depth), lambda i, s: (0, 0)),
            ]
            + [out_spec] * (plus is not None),
            out_specs=out_spec,
        ),
        compiler_params=params(1, 40),
        cost_estimate=estimate(
            flops=count * depth * width,
            bytes_accessed=2 * width * depth + count * depth + count * width,
            transcendentals=0,
        ),
        name="project_back",
    )(core, rows, weights, *(() if plus is None else (plus,)))


def after(value, *others):
    return lax.optimization_barrier((value,) + others)[0]


def body(
    hidden_in,
    out_cotangent,
    segment_number,
    expert_routes,
    pair_order,
    norm_gain,
    query_weight,
    key_weight,
    value_weight,
    output_weight,
    query_gain,
    key_gain,
    ffn_norm_gain,
    router_weight,
    expert_gate,
    expert_up,
    expert_down,
):
    tok_rows, width = hidden_in.shape
    devices = lax.axis_size(AXIS)
    members = max(1, SEQ_MIN // tok_rows)
    planes = devices // members
    per_plane = members // 2
    expert_count = devices // 2
    capacity = tok_rows * TOPK // expert_count
    heads = width // HD // members
    head_width = heads * HD
    own_rows = norm_gain.shape[0]
    seq = members * tok_rows
    me = lax.axis_index(AXIS)
    plane, member = me // members, me % members
    mine = (me // 2).astype(jnp.int32).reshape(1)
    first = (plane * per_plane).astype(jnp.int32)
    places = (plane ^ jnp.arange(planes, dtype=jnp.int32)).astype(jnp.int32)
    counted = jnp.concatenate([first[None], jnp.arange(planes, dtype=jnp.int32)])
    halfway = -(-planes // 2)
    chunks = [part for part in (range(halfway, planes), range(halfway)) if len(part)]

    def placed(part):
        return jnp.concatenate([first[None], places[part.start : part.stop]])

    plane_groups = [[g * members + j for j in range(members)] for g in range(planes)]
    stack_groups = [[g * members + j for g in range(planes)] for j in range(members)]
    core_groups = [
        [g * members + 2 * c + h for c in range(per_plane)] for g in range(planes) for h in (0, 1)
    ]

    def exchange(value, groups=None):
        return lax.all_to_all(
            value, AXIS, split_axis=0, concat_axis=0, tiled=True, axis_index_groups=groups
        )

    def gather(value, groups=None):
        return lax.all_gather(value, AXIS, axis=0, tiled=True, axis_index_groups=groups)

    def flip(value, bits):
        if bits == 0:
            return value
        return lax.ppermute(value, AXIS, [(i, i ^ bits) for i in range(devices)])

    def to_core(value):
        return flip(value, 1)

    def to_plane(value, d):
        return flip(value, members * d)

    wire, core_op = [], []

    def on_wire(value, groups):
        came = exchange(after(value, *wire[-1:]), groups)
        wire.append(came)
        return came

    def to_chips(value):
        return on_wire(value, core_groups)

    def in_turn(value):
        return after(value, *core_op[-1:])

    def ran(value):
        core_op.append(value)
        return value

    pieces = (
        router_weight.reshape(-1),
        norm_gain,
        ffn_norm_gain,
        query_gain,
        key_gain,
        segment_number.astype(bf16),
    )
    packed = jnp.concatenate(pieces)
    length = packed.shape[0]
    padded = -(-length // 128) * 128
    packed = jnp.pad(packed, (0, padded - length))
    packed = on_wire(jnp.broadcast_to(packed[None], (devices, padded)), None)
    small = []
    at = 0
    for piece in pieces:
        small.append(packed[:, at : at + piece.shape[0]])
        at += piece.shape[0]
    router_full = small[0].reshape(width, expert_count)
    gain_one = small[1].reshape(1, width).astype(f32)
    gain_two = small[2].reshape(1, width).astype(f32)
    gain_q = small[3].reshape(1, HD).astype(f32)
    gain_k = small[4].reshape(1, HD).astype(f32)
    segments = lax.dynamic_slice_in_dim(small[5], plane * members, members, 0).astype(f32)
    seg_row, seg_col = segments.reshape(1, seq), segments.reshape(seq, 1)
    seg_blocks = segments.reshape(seq // ROWS, ROWS)
    seg_first, seg_last = seg_blocks[:, 0], seg_blocks[:, -1]
    low = jnp.sum((seg_last[None, :] < seg_first[:, None]).astype(jnp.int32), axis=1)
    high = jnp.sum((seg_first[None, :] <= seg_last[:, None]).astype(jnp.int32), axis=1)

    columns = jnp.concatenate(
        [w.reshape(own_rows, members, head_width) for w in (query_weight, key_weight, value_weight)],
        axis=2,
    )
    slots = block_slots(expert_routes, pair_order, expert_count)
    columns = on_wire(
        after(columns, slots).transpose(1, 0, 2).reshape(members * own_rows, 3 * head_width), plane_groups
    )
    slots = [to_plane(slots, d) for d in range(planes)]
    stacked = [to_plane(after(output_weight, packed), d) for d in range(planes)]
    weights = [to_plane(after(columns, *slots, *stacked), d) for d in range(planes)]
    output_rows = jnp.zeros((planes * own_rows, width), bf16)
    for d, rows in enumerate(stacked):
        output_rows = lax.dynamic_update_slice_in_dim(output_rows, rows, places[d] * own_rows, 0)
    rows_all = gather(hidden_in, plane_groups)

    cot_own = dispatch(counted, slots[0][None], out_cotangent[None], per_plane, capacity)
    cot_first = [to_chips(cot_own)]
    output_full = gather(after(output_rows, columns), plane_groups)
    slots = jnp.stack(slots)
    cot_rows = {0: out_cotangent}
    top = planes // 2
    early, late = [], []
    if planes > 1:
        cot_rows[top] = to_plane(after(out_cotangent, *weights), top)
        early.append(cot_rows[top])
    for d in range(1, planes):
        if d != top:
            lowest = d & -d
            start = after(out_cotangent, *early) if d == lowest else cot_rows[d ^ lowest]
            cot_rows[d] = to_plane(start, lowest)
            late.append(cot_rows[d])

    halves = lambda w: jnp.concatenate([w, to_core(w)], axis=0)
    wg, wu, wd = halves(expert_gate), halves(expert_up), halves(expert_down)

    cosine, sine = rope_tables(seq)
    act_one, pre, rot, ordered = qkv_project(
        places, rows_all, gain_one, weights, gain_q, gain_k, cosine, sine, heads
    )
    out_wide, out_heads, lse = attention(rot, seg_col, seg_row, low, high, heads)
    out_low = on_wire(after(out_heads, *early), plane_groups)
    if planes > 1:
        rows = after(cot_rows[top], out_heads)
        sent = dispatch(counted, slots[top : top + 1], rows[None], per_plane, capacity)
        cot_first.append(to_chips(sent))
    out_low = out_low.reshape(members, tok_rows, head_width).transpose(1, 0, 2)
    out_low = out_low.reshape(tok_rows, planes, members, own_rows).transpose(0, 2, 1, 3)
    out_low = after(out_low.reshape(tok_rows, width), wg, wu, wd)
    tokens = hidden_in.astype(f32)
    cotangent = out_cotangent.astype(f32)
    middle = tokens + dot_nn(out_low, output_full)
    inverse_two = lax.rsqrt(jnp.mean(middle * middle, axis=-1, keepdims=True) + norm_eps)
    act_two = (middle * inverse_two * gain_two).astype(bf16)

    logits = dot_nn(act_two, router_full)
    expert_ids = jnp.arange(expert_count, dtype=jnp.int32)
    routed = jnp.any(expert_routes[:, :, None] == expert_ids[None, None, :], axis=1)
    logits = jnp.where(routed, logits, masked_score)
    gates = jnp.where(routed, jnp.exp(logits - jnp.max(logits, axis=1, keepdims=True)), 0.0)
    gates = gates / jnp.sum(gates, axis=1, keepdims=True)
    coarse = lax.reduce_precision(gates, 8, 7)
    extra = -(-2 * expert_count // 128) * 128
    act_wide = jnp.concatenate(
        [
            act_two,
            coarse.astype(bf16),
            (gates - coarse).astype(bf16),
            jnp.zeros((tok_rows, extra - 2 * expert_count), bf16),
        ],
        axis=1,
    )

    act_wide = after(act_wide, *late, *cot_first)
    act_all = gather(act_wide, stack_groups).reshape(planes, tok_rows, -1)
    others = [d for d in range(1, planes) if d != top]
    cot_far = cot_first[0]
    if others:
        far = jnp.stack([after(cot_rows[d], act_wide) for d in others])
        far_slots = jnp.stack([slots[d] for d in others])
        cot_far = to_chips(
            ran(dispatch(counted[: len(others) + 1], far_slots, far, per_plane, capacity))
        )

    act = []
    for part in chunks:
        own_slots = slots[part.start : part.stop]
        sent = dispatch(placed(part), own_slots, in_turn(act_all), per_plane, capacity)
        act.append(to_chips(ran(sent)))
    kept, back, outs = None, [], []
    for part, rows in zip(chunks, act):
        sent, out, kept = experts(
            mine,
            in_turn(rows),
            cot_first[0 if part.start == 0 else 1],
            cot_far,
            wg,
            wu,
            wd,
            part.start,
            planes,
            expert_count,
            kept,
        )
        back.append(to_chips(ran(sent)))
        outs.append(out)
    x_all, c_all, hid_all, gp_all, up_all = kept

    hidden = expert_gate.shape[2]
    flat = lambda value: value.reshape(-1, value.shape[3])
    sides = (
        (flat(x_all), flat(gp_all), 1),
        (flat(x_all), flat(up_all), 1),
        (flat(hid_all), flat(c_all), 0),
    )

    def half(side, which, plus=None):
        left, right, split = side
        cut, whole = (which * hidden, hidden), (0, width)
        cols = (whole, cut) if split else (cut, whole)
        return ran(gram(in_turn(left), right, *cols, f32, plus))

    def home(part, rows, *others):
        came = []
        for i, d in enumerate(part):
            summed = combine(first[None], slots[d], after(rows, *core_op[-1:], *others), i)
            came.append(to_plane(ran(summed), d))
        return came

    came = home(chunks[0], back[0])
    theirs = [half(side, 1) for side in sides]
    if len(chunks) > 1:
        came += home(chunks[1], back[1])
    outs[0] = to_chips(outs[0])
    back_sum = sum(rows.astype(f32) for rows in came)

    expert_in_grad = back_sum[:, :width]
    gate_grad = (
        back_sum[:, width : width + expert_count]
        + back_sum[:, width + expert_count : width + 2 * expert_count]
    )
    select_grad = gates * (gate_grad - jnp.sum(gates * gate_grad, axis=1, keepdims=True))
    logit_grad = select_grad.astype(bf16)
    grad_router = dot_tn(act_two, logit_grad)
    act_two_grad = expert_in_grad + dot_nt(logit_grad, router_full)
    weighted = act_two_grad * gain_two
    grad_gain_two = jnp.sum(act_two_grad * middle * inverse_two, axis=0)
    middle_grad = (
        cotangent
        + inverse_two * weighted
        - middle * inverse_two**3 * jnp.mean(weighted * middle, axis=-1, keepdims=True)
    )
    middle_low = middle_grad.astype(bf16)

    out_grad = dot_nt(middle_low, output_full).astype(bf16)
    out_grad = out_grad.reshape(tok_rows, members, planes, own_rows).transpose(0, 2, 1, 3)
    out_grad = out_grad.reshape(tok_rows, members, head_width).transpose(1, 0, 2)
    out_grad = out_grad.reshape(seq, head_width)
    ran(out_grad)
    theirs = [to_core(after(grad, out_grad)) for grad in theirs]
    out_grad = on_wire(out_grad, plane_groups)
    mixture = home(chunks[0], outs[0])
    dqkv, grad_gains = attention_back(
        rot,
        in_turn(out_grad),
        out_wide,
        lse,
        seg_col,
        seg_row,
        low,
        high,
        pre,
        gain_q,
        gain_k,
        cosine,
        sine,
        heads,
    )
    ran(dqkv)
    if len(chunks) > 1:
        mixture += home(chunks[1], to_chips(outs[1]))
        done = (*core_op[-2:], mixture[0], *theirs)
        dqkv, grad_gains = after(dqkv, *done), after(grad_gains, *done)
    middle_all = gather(after(middle_low, dqkv), plane_groups)

    sums = (
        grad_router.reshape(devices, -1),
        grad_gain_two.reshape(devices, -1),
        grad_gains[0].reshape(devices, -1),
        grad_gains[1].reshape(devices, -1),
    )
    packed = jnp.concatenate(sums, axis=1)
    length = packed.shape[1]
    padded = -(-length // 128) * 128
    packed = jnp.pad(packed, ((0, 0), (0, padded - length)))

    core = (me % 2).astype(jnp.int32).reshape(1)
    given = project_back(1 - core, dqkv, ordered, tok_rows)
    part = gram(after(act_one, given), dqkv, (0, width), (0, 3 * head_width), bf16)
    part = part.reshape(planes, members * own_rows, 3 * head_width)
    shares = [lax.dynamic_index_in_dim(part, places[d], 0, False) for d in range(planes)]
    given = after(to_core(given), *shares, *mixture[1 : len(chunks[0])])
    act_one_grad = project_back(core, dqkv, ordered, tok_rows, given)
    ran(act_one_grad)
    grad_gate, grad_up, grad_down = (
        half(side, 0, other) for side, other in zip(sides, theirs)
    )
    output_part = gram(out_heads, in_turn(middle_all), (0, head_width), (0, width), bf16)
    done = (*core_op[-4:], output_part)
    shares = [after(to_plane(share, d), *done) for d, share in enumerate(shares)]
    taken = sum(share.astype(f32) for share in shares).astype(bf16)
    act_one_grad = on_wire(act_one_grad, core_groups)

    output_part = output_part.reshape(planes, head_width // planes, width)
    grad_output = 0.0
    for d in range(planes):
        to_owner = [
            (g * members + j, j * planes + (g ^ d)) for g in range(planes) for j in range(members)
        ]
        rows = lax.dynamic_index_in_dim(output_part, places[d], 0, False)
        grad_output = grad_output + lax.ppermute(rows, AXIS, to_owner).astype(f32)
    packed, act_one_grad, mixture = lax.optimization_barrier((packed, act_one_grad, mixture))
    layer_out = (middle + sum(rows.astype(f32) for rows in mixture)).astype(bf16)
    packed = exchange(packed)
    taken, packed, grad_output = lax.optimization_barrier((taken, packed, grad_output))
    part = exchange(taken, plane_groups).reshape(members, own_rows, 3, head_width)
    part = part.transpose(2, 1, 0, 3).reshape(3, own_rows, width).astype(f32)
    grad_query, grad_key, grad_value = part[0], part[1], part[2]
    act_one_grad = act_one_grad.reshape(per_plane, tok_rows, width)
    act_one_grad = jnp.sum(act_one_grad.astype(f32), axis=0)

    inverse_one = lax.rsqrt(jnp.mean(tokens * tokens, axis=-1, keepdims=True) + norm_eps)
    weighted = act_one_grad * gain_one
    grad_hidden = (
        middle_grad
        + inverse_one * weighted
        - tokens * inverse_one**3 * jnp.mean(weighted * tokens, axis=-1, keepdims=True)
    )
    grad_gain_one = (
        jnp.sum(
            grad_query * query_weight.astype(f32)
            + grad_key * key_weight.astype(f32)
            + grad_value * value_weight.astype(f32),
            axis=1,
        )
        / norm_gain.astype(f32)
    )

    summed = jnp.sum(packed, axis=0)
    at, tiny = 0, []
    for piece in sums:
        tiny.append(summed[at : at + piece.shape[1]])
        at += piece.shape[1]

    return (
        layer_out,
        grad_hidden,
        grad_gain_one,
        grad_query,
        grad_key,
        grad_value,
        grad_output,
        tiny[2],
        tiny[3],
        tiny[1],
        tiny[0].reshape(own_rows, expert_count),
        grad_gate[None],
        grad_up[None],
        grad_down[None],
    )


def solution(mesh):
    row, mat, cube = P(AXIS), P(AXIS, None), P(AXIS, None, None)
    return jax.shard_map(
        body,
        mesh=mesh,
        in_specs=(mat, mat, row, mat, mat, row, mat, mat, mat, mat, row, row, row, mat)
        + (cube,) * 3,
        out_specs=(mat, mat, row, mat, mat, mat, mat, row, row, row, mat) + (cube,) * 3,
        check_vma=False,
    )
```

```python
import functools
import math

import jax
import jax.numpy as jnp
from jax import lax
from jax.experimental import pallas as pl
from jax.experimental.pallas import tpu as pltpu
from jax.sharding import PartitionSpec as P

HD = 128
TOPK = 8
SEQ_MIN = 2048
ROWS = 256
SHARE = 32

norm_eps = 1e-05
head_eps = 1e-06
rope_base = 10000.0
masked_score = -1e30
absent_slot = 4096.0

AXIS = "fsdp"
f32 = jnp.float32
bf16 = jnp.bfloat16
MIB = 1 << 20


def dot_nt(left, right):
    return lax.dot_general(left, right, (((1,), (1,)), ((), ())), preferred_element_type=f32)


def dot_tn(left, right):
    return lax.dot_general(left, right, (((0,), (0,)), ((), ())), preferred_element_type=f32)


def dot_nn(left, right):
    return lax.dot_general(left, right, (((1,), (0,)), ((), ())), preferred_element_type=f32)


def params(steps, mib):
    return pltpu.CompilerParams(
        dimension_semantics=("arbitrary",) * steps, vmem_limit_bytes=mib * MIB
    )


def estimate(flops, bytes_accessed, transcendentals):
    return pl.CostEstimate(
        flops=flops // SHARE, bytes_accessed=bytes_accessed // SHARE, transcendentals=transcendentals // SHARE
    )


def rope_tables(count):
    half_width = HD // 2
    frequency = jnp.exp(-math.log(rope_base) * 2.0 * jnp.arange(half_width, dtype=f32) / HD)
    angles = jnp.arange(count, dtype=f32)[:, None] * frequency[None, :]
    cosine, sine = jnp.cos(angles), jnp.sin(angles)
    return jnp.concatenate([cosine, cosine], axis=-1), jnp.concatenate([-sine, sine], axis=-1)


def slots_kernel(expert_count, routes_ref, order_ref, slots_ref):
    tok_rows = routes_ref.shape[0]
    pair_count = order_ref.shape[1]
    order = order_ref[...]
    shift = TOPK.bit_length() - 1
    token_of = lax.shift_right_logical(order, jnp.full_like(order, shift))
    route_of = order & (TOPK - 1)
    token_iota = lax.broadcasted_iota(jnp.int32, (tok_rows, pair_count), 0)
    token_hot = jnp.where(token_iota == token_of, 1.0, 0.0).astype(bf16)
    place = lax.broadcasted_iota(jnp.int32, (TOPK, pair_count), 1)
    chosen = lax.broadcasted_iota(jnp.int32, (TOPK, pair_count), 0) == route_of
    high = lax.shift_right_logical(place, jnp.full_like(place, 8)).astype(f32)
    low = (place & 255).astype(f32)
    digits = jnp.concatenate([jnp.where(chosen, high, 0.0), jnp.where(chosen, low, 0.0)], axis=0)
    found = dot_nt(token_hot, digits.astype(bf16))
    rank = found[:, :TOPK] * 256.0 + found[:, TOPK:]
    routes = routes_ref[...]
    lanes = -(-expert_count // 128) * 128
    expert_iota = lax.broadcasted_iota(jnp.int32, (tok_rows, lanes), 1)
    never = 1e9
    by_expert = jnp.full((tok_rows, lanes), never, f32)
    for k in range(TOPK):
        by_expert = jnp.where(expert_iota == routes[:, k : k + 1], rank[:, k : k + 1], by_expert)
    turned = by_expert.T
    for e in range(expert_count):
        mine = turned[e : e + 1, :]
        earlier = jnp.where(by_expert[:, e : e + 1] < mine, 1.0, 0.0)
        count = jnp.sum(earlier, axis=0, keepdims=True)
        slots_ref[e : e + 1, :] = jnp.where(mine < never, count, absent_slot)


def block_slots(routes, order, expert_count):
    tok_rows = routes.shape[0]
    return pl.pallas_call(
        functools.partial(slots_kernel, expert_count),
        out_shape=jax.ShapeDtypeStruct((expert_count, tok_rows), f32),
        compiler_params=pltpu.CompilerParams(vmem_limit_bytes=32 * MIB),
        name="block_slots",
    )(routes, order)


def slot_hot(slots_ref, expert, capacity):
    slot_row = slots_ref[pl.ds(expert, 1), :]
    slot_iota = lax.broadcasted_iota(jnp.int32, (capacity, slot_row.shape[1]), 0).astype(f32)
    return jnp.where(slot_iota == slot_row, 1.0, 0.0).astype(bf16)


def plane_hot(slots_ref, first, shape):
    return jnp.concatenate([slot_hot(slots_ref, first + r, shape[1]) for r in range(shape[0])])


def dispatch_kernel(at_ref, slots_ref, rows_ref, out_ref):
    hot = plane_hot(slots_ref, at_ref[0], out_ref.shape)
    out_ref[...] = dot_nn(hot, rows_ref[...]).astype(bf16).reshape(out_ref.shape)


def dispatch(at, slots, rows, per_plane, capacity):
    blocks, experts, tok_rows = slots.shape
    width = rows.shape[2]
    slot_rows = per_plane * capacity
    return pl.pallas_call(
        dispatch_kernel,
        out_shape=jax.ShapeDtypeStruct((per_plane, blocks, capacity, width), bf16),
        grid_spec=pltpu.PrefetchScalarGridSpec(
            num_scalar_prefetch=1,
            grid=(blocks,),
            in_specs=[
                pl.BlockSpec((None, experts, tok_rows), lambda i, s: (i, 0, 0)),
                pl.BlockSpec((None, tok_rows, width), lambda i, s: (s[1 + i], 0, 0)),
            ],
            out_specs=pl.BlockSpec((per_plane, None, capacity, width), lambda i, s: (0, i, 0, 0)),
        ),
        compiler_params=params(1, 40),
        cost_estimate=estimate(
            flops=2 * blocks * slot_rows * tok_rows * width,
            bytes_accessed=2 * blocks * (slot_rows + tok_rows) * width,
            transcendentals=0,
        ),
        name="dispatch",
    )(at, slots, rows)


def combine_kernel(first_ref, slots_ref, rows_ref, out_ref):
    hot = plane_hot(slots_ref, first_ref[0], rows_ref.shape)
    rows = rows_ref[...].reshape(hot.shape[0], rows_ref.shape[2])
    out_ref[...] = dot_tn(hot, rows).astype(bf16)


def combine(first, slots, rows, block):
    experts, tok_rows = slots.shape
    per_plane, _, capacity, width = rows.shape
    slot_rows = per_plane * capacity
    return pl.pallas_call(
        combine_kernel,
        out_shape=jax.ShapeDtypeStruct((tok_rows, width), bf16),
        grid_spec=pltpu.PrefetchScalarGridSpec(
            num_scalar_prefetch=1,
            grid=(1,),
            in_specs=[
                pl.BlockSpec((experts, tok_rows), lambda i, s: (0, 0)),
                pl.BlockSpec((per_plane, None, capacity, width), lambda i, s: (0, block, 0, 0)),
            ],
            out_specs=pl.BlockSpec((tok_rows, width), lambda i, s: (0, 0)),
        ),
        compiler_params=params(1, 40),
        cost_estimate=estimate(
            flops=2 * slot_rows * tok_rows * width,
            bytes_accessed=2 * (slot_rows + tok_rows) * width,
            transcendentals=0,
        ),
        name="combine",
    )(first, slots, rows)


def qkv_kernel(heads, planes, at_ref, x_ref, gain_ref, *refs):
    w_refs = refs[:planes]
    gq_ref, gk_ref, cos_ref, sin_ref, act_ref, pre_ref, rot_ref, all_ref = refs[planes:]
    depth = w_refs[0].shape[0]

    @pl.when(pl.program_id(0) == 0)
    def _():
        for d in range(planes):
            place = pl.ds(pl.multiple_of(at_ref[d] * depth, depth), depth)
            all_ref[place, :] = w_refs[d][...]

    x = x_ref[...].astype(f32)
    inverse = lax.rsqrt(jnp.mean(x * x, axis=-1, keepdims=True) + norm_eps)
    act = (x * inverse * gain_ref[...]).astype(bf16)
    act_ref[...] = act
    y = None
    for d in range(planes):
        columns = pl.ds(pl.multiple_of(at_ref[d] * depth, depth), depth)
        term = dot_nn(act_ref[:, columns], w_refs[d][...])
        y = term if y is None else y + term
    cosine, sine = cos_ref[...], sin_ref[...]
    for part, gain in enumerate((gq_ref[...], gk_ref[...])):
        for h in range(heads):
            at = (part * heads + h) * HD
            u = y[:, at : at + HD]
            pre_ref[:, at : at + HD] = u
            n = u * lax.rsqrt(jnp.mean(u * u, axis=-1, keepdims=True) + head_eps) * gain
            rot_ref[:, at : at + HD] = (n * cosine + pltpu.roll(n, HD // 2, 1) * sine).astype(bf16)
    at = 2 * heads * HD
    rot_ref[:, at:] = y[:, at:].astype(bf16)


def qkv_project(places, rows, gain, weights, gain_q, gain_k, cosine, sine, heads):
    count, width = rows.shape
    planes = len(weights)
    depth, out_width = weights[0].shape
    pre_width = 2 * heads * HD
    whole = lambda i, s: (0, 0)
    block = lambda i, s: (i, 0)
    return pl.pallas_call(
        functools.partial(qkv_kernel, heads, planes),
        out_shape=(
            jax.ShapeDtypeStruct((count, width), bf16),
            jax.ShapeDtypeStruct((count, pre_width), f32),
            jax.ShapeDtypeStruct((count, out_width), bf16),
            jax.ShapeDtypeStruct((width, out_width), bf16),
        ),
        grid_spec=pltpu.PrefetchScalarGridSpec(
            num_scalar_prefetch=1,
            grid=(count // ROWS,),
            in_specs=[
                pl.BlockSpec((ROWS, width), block),
                pl.BlockSpec((1, width), whole),
            ]
            + [pl.BlockSpec((depth, out_width), whole)] * planes
            + [
                pl.BlockSpec((1, HD), whole),
                pl.BlockSpec((1, HD), whole),
                pl.BlockSpec((ROWS, HD), block),
                pl.BlockSpec((ROWS, HD), block),
            ],
            out_specs=(
                pl.BlockSpec((ROWS, width), block),
                pl.BlockSpec((ROWS, pre_width), block),
                pl.BlockSpec((ROWS, out_width), block),
                pl.BlockSpec((width, out_width), whole),
            ),
        ),
        compiler_params=params(1, 56),
        cost_estimate=estimate(
            flops=2 * count * width * out_width,
            bytes_accessed=4 * count * width + 2 * width * out_width + 6 * count * out_width,
            transcendentals=0,
        ),
        name="qkv_project",
    )(places, rows, gain, *weights, gain_q, gain_k, cosine, sine)


def attn_kernel(
    scale, low_ref, high_ref, q_ref, k_ref, v_ref, sq_ref, sk_ref, o_ref, ol_ref, lse_ref, s_scr
):
    block = pl.program_id(1)
    low, high = low_ref[block], high_ref[block]
    q = q_ref[...]
    seg_q = sq_ref[...]
    half = ROWS // 2

    def scores(kb, top):
        at = pl.ds(pl.multiple_of(kb * ROWS, ROWS), ROWS)
        s = dot_nt(q, k_ref[at, :]) * scale
        s = jnp.where(seg_q == sk_ref[:, at], s, masked_score)
        s_scr[:, at] = s
        return jnp.maximum(top, jnp.maximum(s[:, :half], s[:, half:]))

    top = lax.fori_loop(low, high, scores, jnp.full((ROWS, half), masked_score, f32))
    top = jnp.max(top, axis=-1, keepdims=True)

    def weigh(kb, carry):
        total, acc = carry
        at = pl.ds(pl.multiple_of(kb * ROWS, ROWS), ROWS)
        p = jnp.exp(s_scr[:, at] - top)
        acc = acc + dot_nn(p.astype(bf16), v_ref[at, :])
        return total + (p[:, :half] + p[:, half:]), acc

    total, acc = lax.fori_loop(
        low, high, weigh, (jnp.zeros((ROWS, half), f32), jnp.zeros((ROWS, HD), f32))
    )
    total = jnp.sum(total, axis=-1, keepdims=True)
    out = acc / total
    o_ref[...] = out
    ol_ref[...] = out.astype(bf16)
    lse = jnp.broadcast_to(top + jnp.log(total), (ROWS, HD)).T
    lse_ref[0] = lse[0:1, :]


def attention(rot, seg_col, seg_row, low, high, heads):
    count = rot.shape[0]
    blocks = count // ROWS
    scale = HD ** (-0.5)
    return pl.pallas_call(
        functools.partial(attn_kernel, scale),
        out_shape=(
            jax.ShapeDtypeStruct((count, heads * HD), f32),
            jax.ShapeDtypeStruct((count, heads * HD), bf16),
            jax.ShapeDtypeStruct((heads * blocks, 1, ROWS), f32),
        ),
        grid_spec=pltpu.PrefetchScalarGridSpec(
            num_scalar_prefetch=2,
            grid=(heads, blocks),
            in_specs=[
                pl.BlockSpec((ROWS, HD), lambda h, i, *s: (i, h)),
                pl.BlockSpec((count, HD), lambda h, i, *s: (0, heads + h)),
                pl.BlockSpec((count, HD), lambda h, i, *s: (0, 2 * heads + h)),
                pl.BlockSpec((ROWS, 1), lambda h, i, *s: (i, 0)),
                pl.BlockSpec((1, count), lambda h, i, *s: (0, 0)),
            ],
            out_specs=(
                pl.BlockSpec((ROWS, HD), lambda h, i, *s: (i, h)),
                pl.BlockSpec((ROWS, HD), lambda h, i, *s: (i, h)),
                pl.BlockSpec((1, 1, ROWS), lambda h, i, *s: (h * blocks + i, 0, 0)),
            ),
            scratch_shapes=[pltpu.VMEM((ROWS, count), f32)],
        ),
        compiler_params=params(2, 32),
        cost_estimate=estimate(
            flops=2 * heads * count * count * HD,
            bytes_accessed=12 * heads * count * HD,
            transcendentals=heads * count * count // 2,
        ),
        name="attention",
    )(low, high, rot, rot, rot, seg_col, seg_row)


def head_back(grad, pre, gain, cosine, sine):
    n = grad * cosine - pltpu.roll(grad, HD // 2, 1) * sine
    inverse = lax.rsqrt(jnp.mean(pre * pre, axis=-1, keepdims=True) + head_eps)
    w = n * gain
    back = inverse * w - pre * inverse**3 * jnp.mean(w * pre, axis=-1, keepdims=True)
    return back, jnp.sum(n * pre * inverse, axis=0, keepdims=True)


def attn_back_kernel(
    scale,
    low_ref,
    high_ref,
    q_ref,
    k_ref,
    v_ref,
    do_ref,
    o_ref,
    lse_ref,
    sq_ref,
    sk_ref,
    qpre_ref,
    kpre_ref,
    gq_ref,
    gk_ref,
    cosq_ref,
    sinq_ref,
    cosk_ref,
    sink_ref,
    grad_ref,
    gain_ref,
    dk_scr,
    dv_scr,
):
    head, block = pl.program_id(0), pl.program_id(1)
    heads = pl.num_programs(0)

    def columns(part):
        return pl.ds(pl.multiple_of((part * heads + head) * HD, HD), HD)

    low, high = low_ref[block], high_ref[block]

    @pl.when(block == 0)
    def _():
        dk_scr[...] = jnp.zeros_like(dk_scr)
        dv_scr[...] = jnp.zeros_like(dv_scr)

    @pl.when((block == 0) & (head == 0))
    def _():
        gain_ref[...] = jnp.zeros_like(gain_ref)

    q, do = q_ref[...], do_ref[...]
    row_dot = jnp.sum((do.astype(f32) * o_ref[...]).T, axis=0, keepdims=True)
    lse = lse_ref[0]
    seg_q = sq_ref[...]

    def tile(kb, dq):
        at = pl.ds(pl.multiple_of(kb * ROWS, ROWS), ROWS)
        k, v = k_ref[at, :], v_ref[at, :]
        s = dot_nt(k, q) * scale
        p = jnp.where(sk_ref[at, :] == seg_q, jnp.exp(s - lse), 0.0)
        dp = dot_nt(v, do)
        ds = (p * (dp - row_dot)).astype(bf16)
        dv_scr[at, :] += dot_nn(p.astype(bf16), do)
        dk_scr[at, :] += dot_nn(ds, q)
        return dq + dot_tn(ds, k)

    dq = lax.fori_loop(low, high, tile, jnp.zeros((ROWS, HD), f32))
    back, gain_q = head_back(dq * scale, qpre_ref[...], gq_ref[...], cosq_ref[...], sinq_ref[...])
    grad_ref[pl.ds(pl.multiple_of(block * ROWS, ROWS), ROWS), columns(0)] = back.astype(bf16)
    gain_ref[0:1, :] += gain_q

    @pl.when(block == pl.num_programs(1) - 1)
    def _():
        @pl.loop(0, dk_scr.shape[0] // ROWS)
        def _(i):
            at = pl.ds(pl.multiple_of(i * ROWS, ROWS), ROWS)
            back, gain_k = head_back(
                dk_scr[at, :] * scale, kpre_ref[at, :], gk_ref[...], cosk_ref[at, :], sink_ref[at, :]
            )
            grad_ref[at, columns(1)] = back.astype(bf16)
            grad_ref[at, columns(2)] = dv_scr[at, :].astype(bf16)
            gain_ref[1:2, :] += gain_k


def attention_back(
    rot, grad, out, lse, seg_col, seg_row, low, high, pre, gain_q, gain_k, cosine, sine, heads
):
    count = rot.shape[0]
    blocks = count // ROWS
    scale = HD ** (-0.5)
    mine = lambda h, i, *s: (i, h)
    whole = lambda h, i, *s: (0, 0)
    return pl.pallas_call(
        functools.partial(attn_back_kernel, scale),
        out_shape=(
            jax.ShapeDtypeStruct((count, 3 * heads * HD), bf16),
            jax.ShapeDtypeStruct((8, HD), f32),
        ),
        grid_spec=pltpu.PrefetchScalarGridSpec(
            num_scalar_prefetch=2,
            grid=(heads, blocks),
            in_specs=[
                pl.BlockSpec((ROWS, HD), mine),
                pl.BlockSpec((count, HD), lambda h, i, *s: (0, heads + h)),
                pl.BlockSpec((count, HD), lambda h, i, *s: (0, 2 * heads + h)),
                pl.BlockSpec((ROWS, HD), mine),
                pl.BlockSpec((ROWS, HD), mine),
                pl.BlockSpec((1, 1, ROWS), lambda h, i, *s: (h * blocks + i, 0, 0)),
                pl.BlockSpec((1, ROWS), lambda h, i, *s: (0, i)),
                pl.BlockSpec((count, 1), whole),
                pl.BlockSpec((ROWS, HD), mine),
                pl.BlockSpec((count, HD), lambda h, i, *s: (0, heads + h)),
                pl.BlockSpec((1, HD), whole),
                pl.BlockSpec((1, HD), whole),
                pl.BlockSpec((ROWS, HD), lambda h, i, *s: (i, 0)),
                pl.BlockSpec((ROWS, HD), lambda h, i, *s: (i, 0)),
                pl.BlockSpec((count, HD), whole),
                pl.BlockSpec((count, HD), whole),
            ],
            out_specs=(
                pl.BlockSpec((count, 3 * heads * HD), whole),
                pl.BlockSpec((8, HD), whole),
            ),
            scratch_shapes=[pltpu.VMEM((count, HD), f32), pltpu.VMEM((count, HD), f32)],
        ),
        compiler_params=params(2, 48),
        cost_estimate=estimate(
            flops=5 * heads * count * count * HD,
            bytes_accessed=30 * heads * count * HD,
            transcendentals=heads * count * count // 2,
        ),
        name="attention_back",
    )(
        low,
        high,
        rot,
        rot,
        rot,
        grad,
        out,
        lse,
        seg_row,
        seg_col,
        pre,
        pre,
        gain_q,
        gain_k,
        cosine,
        sine,
        cosine,
        sine,
    )


def expert_kernel(count, carried, mine_ref, x_ref, near_ref, far_ref, *refs):
    wg_ref, wu_ref, wd_ref = refs[:3]
    refs = refs[3 + carried :]
    back_ref, out_ref, xs_ref, c_ref, hid_ref, gp_ref, up_ref = refs[:7]
    out_acc, back_acc, gate_scr, dot_scr = refs[7:]
    step = pl.program_id(1)
    per_plane, capacity, width = c_ref.shape
    rows = per_plane * capacity
    extra = x_ref.shape[2] - width
    lane = lax.broadcasted_iota(jnp.int32, (rows, extra), 1)
    high, low = lane == mine_ref[0], lane == mine_ref[0] + count

    @pl.when(step == 0)
    def _():
        xs_ref[...] = x_ref[:, :, :width]

        @pl.when(pl.program_id(0) == 0)
        def _():
            c_ref[...] = near_ref[...]

        @pl.when(pl.program_id(0) > 0)
        def _():
            c_ref[...] = far_ref[...]
        gates = x_ref[:, :, width:].reshape(rows, extra).astype(f32)
        gate_scr[...] = jnp.sum(jnp.where(high | low, gates, 0.0), axis=-1, keepdims=True)
        out_acc[...] = jnp.zeros_like(out_acc)
        back_acc[...] = jnp.zeros_like(back_acc)
        dot_scr[...] = jnp.zeros_like(dot_scr)

    x = x_ref[:, :, :width].reshape(rows, width)
    c = c_ref[...].reshape(rows, width)
    gate = gate_scr[...]
    wg, wu, wd = wg_ref[...], wu_ref[...], wd_ref[...]
    gate_pre, up_pre = dot_nn(x, wg), dot_nn(x, wu)
    sig = jax.nn.sigmoid(gate_pre)
    hidden = (gate_pre * sig * up_pre).astype(bf16)
    out_acc[...] += dot_nn(hidden, wd)
    plain = dot_nt(c, wd)
    wide = hidden.astype(f32)
    dot_scr[...] += jnp.sum(wide * plain, axis=-1, keepdims=True)
    hid_ref[...] = (wide * gate).astype(bf16).reshape(hid_ref.shape)
    hidden_grad = plain * gate
    gate_grad = (hidden_grad * up_pre * sig * (1.0 + gate_pre * (1.0 - sig))).astype(bf16)
    up_grad = (hidden_grad * gate_pre * sig).astype(bf16)
    gp_ref[...] = gate_grad.reshape(gp_ref.shape)
    up_ref[...] = up_grad.reshape(up_ref.shape)
    back_acc[...] += dot_nt(gate_grad, wg) + dot_nt(up_grad, wu)

    @pl.when(step == pl.num_programs(1) - 1)
    def _():
        dots = dot_scr[...]
        coarse = dots.astype(bf16).astype(f32)
        lanes = jnp.where(high, coarse, jnp.where(low, dots - coarse, 0.0)).astype(bf16)
        back_ref[:, :, :width] = back_acc[...].astype(bf16).reshape(c_ref.shape)
        back_ref[:, :, width:] = lanes.reshape(per_plane, capacity, extra)
        out_ref[...] = (out_acc[...] * gate).astype(bf16).reshape(out_ref.shape)


def experts(mine, x, near, far, wg, wu, wd, base, planes, count, kept):
    per_plane, blocks, capacity, wide = x.shape
    width = near.shape[3]
    halves, _, hidden = wg.shape
    rows = per_plane * capacity
    saved = jax.ShapeDtypeStruct((per_plane, planes, capacity, width), bf16)
    thin = jax.ShapeDtypeStruct((per_plane, planes, capacity, halves * hidden), bf16)
    moved = pl.BlockSpec((per_plane, None, capacity, wide), lambda i, f, s: (0, i, 0, 0))
    saved_spec = pl.BlockSpec((per_plane, None, capacity, width), lambda i, f, s: (0, base + i, 0, 0))
    thin_spec = pl.BlockSpec((per_plane, None, capacity, hidden), lambda i, f, s: (0, base + i, 0, f))
    carried = 0 if kept is None else len(kept)
    skip = base - 1 if base else 0
    cot_specs = [
        pl.BlockSpec((per_plane, None, capacity, width), lambda i, f, s: (0, 0, 0, 0)),
        pl.BlockSpec(
            (per_plane, None, capacity, width),
            lambda i, f, s: (0, jnp.maximum(skip + i - 1, 0), 0, 0),
        ),
    ]
    result = pl.pallas_call(
        functools.partial(expert_kernel, count, carried),
        out_shape=(
            jax.ShapeDtypeStruct(x.shape, bf16),
            jax.ShapeDtypeStruct((per_plane, blocks, capacity, width), bf16),
            saved,
            saved,
            thin,
            thin,
            thin,
        ),
        grid_spec=pltpu.PrefetchScalarGridSpec(
            num_scalar_prefetch=1,
            grid=(blocks, halves),
            in_specs=[
                moved,
                *cot_specs,
                pl.BlockSpec((None, width, hidden), lambda i, f, s: (f, 0, 0)),
                pl.BlockSpec((None, width, hidden), lambda i, f, s: (f, 0, 0)),
                pl.BlockSpec((None, hidden, width), lambda i, f, s: (f, 0, 0)),
            ]
            + [pl.BlockSpec(memory_space=pl.ANY)] * carried,
            out_specs=(
                moved,
                pl.BlockSpec((per_plane, None, capacity, width), lambda i, f, s: (0, i, 0, 0)),
                saved_spec,
                saved_spec,
                thin_spec,
                thin_spec,
                thin_spec,
            ),
            scratch_shapes=[
                pltpu.VMEM((rows, width), f32),
                pltpu.VMEM((rows, width), f32),
                pltpu.VMEM((rows, 1), f32),
                pltpu.VMEM((rows, 1), f32),
            ],
        ),
        input_output_aliases={7 + i: 2 + i for i in range(carried)},
        compiler_params=params(2, 60),
        cost_estimate=estimate(
            flops=12 * blocks * rows * width * hidden * halves,
            bytes_accessed=10 * blocks * rows * width + 6 * blocks * width * hidden * halves,
            transcendentals=blocks * rows * hidden * halves,
        ),
        name="experts",
    )(mine, x, near, far, wg, wu, wd, *(kept or ()))
    return result[0], result[1], result[2:]


def gram_kernel(plus, left_ref, right_ref, *refs):
    total = dot_tn(left_ref[...], right_ref[...])
    if plus:
        total = total + refs[0][...]
    refs[-1][...] = total.astype(refs[-1].dtype)


def gram(left, right, left_cols, right_cols, dtype, plus=None):
    rows = left.shape[0]
    left_at, left_count = left_cols
    right_at, right_count = right_cols
    tall = min(left_count, 256)
    wide = min(right_count, 1024)
    out_spec = pl.BlockSpec((tall, wide), lambda j, i: (i, j))
    return pl.pallas_call(
        functools.partial(gram_kernel, plus is not None),
        out_shape=jax.ShapeDtypeStruct((left_count, right_count), dtype),
        grid=(right_count // wide, left_count // tall),
        in_specs=[
            pl.BlockSpec((rows, tall), lambda j, i: (0, left_at // tall + i)),
            pl.BlockSpec((rows, wide), lambda j, i: (0, right_at // wide + j)),
        ]
        + [out_spec] * (plus is not None),
        out_specs=out_spec,
        compiler_params=params(2, 48),
        cost_estimate=estimate(
            flops=2 * rows * left_count * right_count,
            bytes_accessed=2 * rows * (left_count + right_count) + 4 * left_count * right_count,
            transcendentals=0,
        ),
        name="gram",
    )(left, right, *(() if plus is None else (plus,)))


def project_kernel(plus, core_ref, rows_ref, weights_ref, *refs):
    total = dot_nt(rows_ref[...], weights_ref[...])
    if plus:
        total = total + refs[0][...].astype(f32)
    refs[-1][...] = total.astype(bf16)


def project_back(core, rows, weights, tok_rows, plus=None):
    count, depth = rows.shape
    width = weights.shape[0]
    chips = count // tok_rows // 2
    out_spec = pl.BlockSpec((tok_rows, width), lambda i, s: (i, 0))
    return pl.pallas_call(
        functools.partial(project_kernel, plus is not None),
        out_shape=jax.ShapeDtypeStruct((chips * tok_rows, width), bf16),
        grid_spec=pltpu.PrefetchScalarGridSpec(
            num_scalar_prefetch=1,
            grid=(chips,),
            in_specs=[
                pl.BlockSpec((tok_rows, depth), lambda i, s: (2 * i + s[0], 0)),
                pl.BlockSpec((width, depth), lambda i, s: (0, 0)),
            ]
            + [out_spec] * (plus is not None),
            out_specs=out_spec,
        ),
        compiler_params=params(1, 40),
        cost_estimate=estimate(
            flops=count * depth * width,
            bytes_accessed=2 * width * depth + count * depth + count * width,
            transcendentals=0,
        ),
        name="project_back",
    )(core, rows, weights, *(() if plus is None else (plus,)))


def after(value, *others):
    return lax.optimization_barrier((value,) + others)[0]


def body(
    hidden_in,
    out_cotangent,
    segment_number,
    expert_routes,
    pair_order,
    norm_gain,
    query_weight,
    key_weight,
    value_weight,
    output_weight,
    query_gain,
    key_gain,
    ffn_norm_gain,
    router_weight,
    expert_gate,
    expert_up,
    expert_down,
):
    tok_rows, width = hidden_in.shape
    devices = lax.axis_size(AXIS)
    members = max(1, SEQ_MIN // tok_rows)
    planes = devices // members
    per_plane = members // 2
    expert_count = devices // 2
    capacity = tok_rows * TOPK // expert_count
    heads = width // HD // members
    head_width = heads * HD
    own_rows = norm_gain.shape[0]
    seq = members * tok_rows
    me = lax.axis_index(AXIS)
    plane, member = me // members, me % members
    mine = (me // 2).astype(jnp.int32).reshape(1)
    first = (plane * per_plane).astype(jnp.int32)
    places = (plane ^ jnp.arange(planes, dtype=jnp.int32)).astype(jnp.int32)
    counted = jnp.concatenate([first[None], jnp.arange(planes, dtype=jnp.int32)])
    halfway = -(-planes // 2)
    chunks = [part for part in (range(halfway, planes), range(halfway)) if len(part)]

    def placed(part):
        return jnp.concatenate([first[None], places[part.start : part.stop]])

    plane_groups = [[g * members + j for j in range(members)] for g in range(planes)]
    stack_groups = [[g * members + j for g in range(planes)] for j in range(members)]
    core_groups = [
        [g * members + 2 * c + h for c in range(per_plane)] for g in range(planes) for h in (0, 1)
    ]

    def exchange(value, groups=None):
        return lax.all_to_all(
            value, AXIS, split_axis=0, concat_axis=0, tiled=True, axis_index_groups=groups
        )

    def gather(value, groups=None):
        return lax.all_gather(value, AXIS, axis=0, tiled=True, axis_index_groups=groups)

    def flip(value, bits):
        if bits == 0:
            return value
        return lax.ppermute(value, AXIS, [(i, i ^ bits) for i in range(devices)])

    def to_core(value):
        return flip(value, 1)

    def to_plane(value, d):
        return flip(value, members * d)

    wire, core_op = [], []

    def on_wire(value, groups):
        came = exchange(after(value, *wire[-1:]), groups)
        wire.append(came)
        return came

    def to_chips(value):
        return on_wire(value, core_groups)

    def in_turn(value):
        return after(value, *core_op[-1:])

    def ran(value):
        core_op.append(value)
        return value

    pieces = (
        router_weight.reshape(-1),
        norm_gain,
        ffn_norm_gain,
        query_gain,
        key_gain,
        segment_number.astype(bf16),
    )
    packed = jnp.concatenate(pieces)
    length = packed.shape[0]
    padded = -(-length // 128) * 128
    packed = jnp.pad(packed, (0, padded - length))
    packed = on_wire(jnp.broadcast_to(packed[None], (devices, padded)), None)
    small = []
    at = 0
    for piece in pieces:
        small.append(packed[:, at : at + piece.shape[0]])
        at += piece.shape[0]
    router_full = small[0].reshape(width, expert_count)
    gain_one = small[1].reshape(1, width).astype(f32)
    gain_two = small[2].reshape(1, width).astype(f32)
    gain_q = small[3].reshape(1, HD).astype(f32)
    gain_k = small[4].reshape(1, HD).astype(f32)
    segments = lax.dynamic_slice_in_dim(small[5], plane * members, members, 0).astype(f32)
    seg_row, seg_col = segments.reshape(1, seq), segments.reshape(seq, 1)
    seg_blocks = segments.reshape(seq // ROWS, ROWS)
    seg_first, seg_last = seg_blocks[:, 0], seg_blocks[:, -1]
    low = jnp.sum((seg_last[None, :] < seg_first[:, None]).astype(jnp.int32), axis=1)
    high = jnp.sum((seg_first[None, :] <= seg_last[:, None]).astype(jnp.int32), axis=1)

    columns = jnp.concatenate(
        [w.reshape(own_rows, members, head_width) for w in (query_weight, key_weight, value_weight)],
        axis=2,
    )
    slots = block_slots(expert_routes, pair_order, expert_count)
    columns = on_wire(
        after(columns, slots).transpose(1, 0, 2).reshape(members * own_rows, 3 * head_width), plane_groups
    )
    stacked = [to_plane(after(output_weight, packed), d) for d in range(planes)]
    weights = [to_plane(after(columns, *stacked), d) for d in range(planes)]
    slots = [to_plane(after(slots, *weights) if d else slots, d) for d in range(planes)]
    output_rows = jnp.zeros((planes * own_rows, width), bf16)
    for d, rows in enumerate(stacked):
        output_rows = lax.dynamic_update_slice_in_dim(output_rows, rows, places[d] * own_rows, 0)
    rows_all = gather(hidden_in, plane_groups)

    cot_own = dispatch(counted, slots[0][None], out_cotangent[None], per_plane, capacity)
    cot_first = [to_chips(cot_own)]
    output_full = gather(after(output_rows, columns), plane_groups)
    slot_list, slots = slots, jnp.stack(slots)
    cot_rows = {0: out_cotangent}
    top = planes // 2
    early, late = [], []
    if planes > 1:
        cot_rows[top] = to_plane(after(out_cotangent, *weights), top)
        early.append(cot_rows[top])
    for d in range(1, planes):
        if d != top:
            lowest = d & -d
            start = after(out_cotangent, *early) if d == lowest else cot_rows[d ^ lowest]
            cot_rows[d] = to_plane(start, lowest)
            late.append(cot_rows[d])

    halves = lambda w: jnp.concatenate([w, to_core(w)], axis=0)
    wg, wu, wd = halves(expert_gate), halves(expert_up), halves(expert_down)

    cosine, sine = rope_tables(seq)
    act_one, pre, rot, ordered = qkv_project(
        places, rows_all, gain_one, weights, gain_q, gain_k, cosine, sine, heads
    )
    out_wide, out_heads, lse = attention(rot, seg_col, seg_row, low, high, heads)
    out_low = on_wire(after(out_heads, *slot_list, *early), plane_groups)
    if planes > 1:
        rows = after(cot_rows[top], out_heads)
        sent = dispatch(counted, slots[top : top + 1], rows[None], per_plane, capacity)
        cot_first.append(to_chips(sent))
    out_low = out_low.reshape(members, tok_rows, head_width).transpose(1, 0, 2)
    out_low = out_low.reshape(tok_rows, planes, members, own_rows).transpose(0, 2, 1, 3)
    out_low = out_low.reshape(tok_rows, width)
    tokens = hidden_in.astype(f32)
    cotangent = out_cotangent.astype(f32)
    middle = tokens + dot_nn(out_low, output_full)
    inverse_two = lax.rsqrt(jnp.mean(middle * middle, axis=-1, keepdims=True) + norm_eps)
    act_two = (middle * inverse_two * gain_two).astype(bf16)

    logits = dot_nn(act_two, router_full)
    expert_ids = jnp.arange(expert_count, dtype=jnp.int32)
    routed = jnp.any(expert_routes[:, :, None] == expert_ids[None, None, :], axis=1)
    logits = jnp.where(routed, logits, masked_score)
    gates = jnp.where(routed, jnp.exp(logits - jnp.max(logits, axis=1, keepdims=True)), 0.0)
    gates = gates / jnp.sum(gates, axis=1, keepdims=True)
    coarse = lax.reduce_precision(gates, 8, 7)
    extra = -(-2 * expert_count // 128) * 128
    act_wide = jnp.concatenate(
        [
            act_two,
            coarse.astype(bf16),
            (gates - coarse).astype(bf16),
            jnp.zeros((tok_rows, extra - 2 * expert_count), bf16),
        ],
        axis=1,
    )

    act_wide = after(act_wide, *late, *cot_first)
    act_all = gather(act_wide, stack_groups).reshape(planes, tok_rows, -1)
    others = [d for d in range(1, planes) if d != top]
    cot_far = cot_first[0]
    if others:
        far = jnp.stack([after(cot_rows[d], act_wide) for d in others])
        far_slots = jnp.stack([slots[d] for d in others])
        cot_far = to_chips(
            ran(dispatch(counted[: len(others) + 1], far_slots, far, per_plane, capacity))
        )

    act = []
    for part in chunks:
        own_slots = slots[part.start : part.stop]
        rows = after(in_turn(act_all), wg, wu, wd)
        sent = dispatch(placed(part), own_slots, rows, per_plane, capacity)
        act.append(to_chips(ran(sent)))
    kept, back, outs = None, [], []
    for part, rows in zip(chunks, act):
        sent, out, kept = experts(
            mine,
            in_turn(rows),
            cot_first[0 if part.start == 0 else 1],
            cot_far,
            wg,
            wu,
            wd,
            part.start,
            planes,
            expert_count,
            kept,
        )
        back.append(to_chips(ran(sent)))
        outs.append(out)
    x_all, c_all, hid_all, gp_all, up_all = kept

    hidden = expert_gate.shape[2]
    flat = lambda value: value.reshape(-1, value.shape[3])
    sides = (
        (flat(x_all), flat(gp_all), 1),
        (flat(x_all), flat(up_all), 1),
        (flat(hid_all), flat(c_all), 0),
    )

    def half(side, which, plus=None):
        left, right, split = side
        cut, whole = (which * hidden, hidden), (0, width)
        cols = (whole, cut) if split else (cut, whole)
        return ran(gram(in_turn(left), right, *cols, f32, plus))

    passed = []

    def home(part, rows):
        sums = {}
        for d in sorted(part, key=lambda d: (-(d & 1), d)):
            sums[d] = ran(combine(first[None], slots[d], in_turn(rows), d - part.start))
        bit = 1
        while bit < len(part):
            for d in part:
                if d & bit and not d & (bit - 1):
                    came = to_plane(sums[d].astype(bf16), bit)
                    passed.append(came)
                    sums[d ^ bit] = sums[d ^ bit].astype(f32) + came.astype(f32)
            bit *= 2
        return sums[part.start]

    back_sum = home(chunks[0], back[0])
    theirs = [half(side, 1) for side in sides[:2]]
    if len(chunks) > 1:
        back_sum = ran(in_turn(back_sum.astype(bf16)))
        back_sum = to_plane(back_sum, top)
    theirs.append(half(sides[2], 1))
    if len(chunks) > 1:
        back_sum = back_sum.astype(f32) + home(chunks[1], back[1])
    outs[0] = to_chips(outs[0])

    expert_in_grad = back_sum[:, :width]
    gate_grad = (
        back_sum[:, width : width + expert_count]
        + back_sum[:, width + expert_count : width + 2 * expert_count]
    )
    select_grad = gates * (gate_grad - jnp.sum(gates * gate_grad, axis=1, keepdims=True))
    logit_grad = select_grad.astype(bf16)
    grad_router = dot_tn(act_two, logit_grad)
    act_two_grad = expert_in_grad + dot_nt(logit_grad, router_full)
    weighted = act_two_grad * gain_two
    grad_gain_two = jnp.sum(act_two_grad * middle * inverse_two, axis=0)
    middle_grad = (
        cotangent
        + inverse_two * weighted
        - middle * inverse_two**3 * jnp.mean(weighted * middle, axis=-1, keepdims=True)
    )
    middle_low = middle_grad.astype(bf16)

    out_grad = dot_nt(middle_low, output_full).astype(bf16)
    out_grad = out_grad.reshape(tok_rows, members, planes, own_rows).transpose(0, 2, 1, 3)
    out_grad = out_grad.reshape(tok_rows, members, head_width).transpose(1, 0, 2)
    out_grad = out_grad.reshape(seq, head_width)
    ran(out_grad)
    theirs = [to_core(after(grad, out_grad)) for grad in theirs]
    out_grad = on_wire(out_grad, plane_groups)
    mixture = home(chunks[0], outs[0]).astype(bf16)
    dqkv, grad_gains = attention_back(
        rot,
        in_turn(out_grad),
        out_wide,
        lse,
        seg_col,
        seg_row,
        low,
        high,
        pre,
        gain_q,
        gain_k,
        cosine,
        sine,
        heads,
    )
    ran(dqkv)
    if len(chunks) > 1:
        near_sum = home(chunks[1], to_chips(outs[1]))
        done = (*core_op[-2:], mixture, *theirs)
        dqkv, grad_gains = after(dqkv, *done), after(grad_gains, *done)
    middle_all = gather(after(middle_low, dqkv), plane_groups)

    sums = (
        grad_router.reshape(devices, -1),
        grad_gain_two.reshape(devices, -1),
        grad_gains[0].reshape(devices, -1),
        grad_gains[1].reshape(devices, -1),
    )
    packed = jnp.concatenate(sums, axis=1)
    length = packed.shape[1]
    padded = -(-length // 128) * 128
    packed = jnp.pad(packed, ((0, 0), (0, padded - length)))

    core = (me % 2).astype(jnp.int32).reshape(1)
    given = project_back(1 - core, dqkv, ordered, tok_rows)
    part = gram(after(act_one, given), dqkv, (0, width), (0, 3 * head_width), bf16)
    part = part.reshape(planes, members * own_rows, 3 * head_width)
    shares = [lax.dynamic_index_in_dim(part, places[d], 0, False) for d in range(planes)]
    mixture = to_plane(mixture, top) if len(chunks) > 1 else mixture
    given = after(to_core(given), *shares, mixture, *passed[-1:])
    act_one_grad = project_back(core, dqkv, ordered, tok_rows, given)
    ran(act_one_grad)
    grad_gate, grad_up, grad_down = (
        half(side, 0, other) for side, other in zip(sides, theirs)
    )
    output_part = gram(out_heads, in_turn(middle_all), (0, head_width), (0, width), bf16)
    done = (*core_op[-4:], output_part)
    shares = [after(to_plane(share, d), *done) for d, share in enumerate(shares)]
    taken = sum(share.astype(f32) for share in shares).astype(bf16)
    act_one_grad = on_wire(act_one_grad, core_groups)

    output_part = output_part.reshape(planes, head_width // planes, width)
    grad_output = 0.0
    for d in range(planes):
        to_owner = [
            (g * members + j, j * planes + (g ^ d)) for g in range(planes) for j in range(members)
        ]
        rows = lax.dynamic_index_in_dim(output_part, places[d], 0, False)
        grad_output = grad_output + lax.ppermute(rows, AXIS, to_owner).astype(f32)
    mixture = mixture.astype(f32)
    if len(chunks) > 1:
        mixture = mixture + near_sum
    packed, act_one_grad, mixture = lax.optimization_barrier((packed, act_one_grad, mixture))
    layer_out = (middle + mixture).astype(bf16)
    packed = exchange(packed)
    taken, packed = lax.optimization_barrier((taken, packed))
    part = exchange(taken, plane_groups).reshape(members, own_rows, 3, head_width)
    part = part.transpose(2, 1, 0, 3).reshape(3, own_rows, width).astype(f32)
    grad_query, grad_key, grad_value = part[0], part[1], part[2]
    act_one_grad = act_one_grad.reshape(per_plane, tok_rows, width)
    act_one_grad = jnp.sum(act_one_grad.astype(f32), axis=0)

    inverse_one = lax.rsqrt(jnp.mean(tokens * tokens, axis=-1, keepdims=True) + norm_eps)
    weighted = act_one_grad * gain_one
    grad_hidden = (
        middle_grad
        + inverse_one * weighted
        - tokens * inverse_one**3 * jnp.mean(weighted * tokens, axis=-1, keepdims=True)
    )
    grad_gain_one = (
        jnp.sum(
            grad_query * query_weight.astype(f32)
            + grad_key * key_weight.astype(f32)
            + grad_value * value_weight.astype(f32),
            axis=1,
        )
        / norm_gain.astype(f32)
    )

    summed = jnp.sum(packed, axis=0)
    at, tiny = 0, []
    for piece in sums:
        tiny.append(summed[at : at + piece.shape[1]])
        at += piece.shape[1]

    return (
        layer_out,
        grad_hidden,
        grad_gain_one,
        grad_query,
        grad_key,
        grad_value,
        grad_output,
        tiny[2],
        tiny[3],
        tiny[1],
        tiny[0].reshape(own_rows, expert_count),
        grad_gate[None],
        grad_up[None],
        grad_down[None],
    )


def solution(mesh):
    row, mat, cube = P(AXIS), P(AXIS, None), P(AXIS, None, None)
    return jax.shard_map(
        body,
        mesh=mesh,
        in_specs=(mat, mat, row, mat, mat, row, mat, mat, mat, mat, row, row, row, mat)
        + (cube,) * 3,
        out_specs=(mat, mat, row, mat, mat, mat, mat, row, row, row, mat) + (cube,) * 3,
        check_vma=False,
    )
```

```python
import functools
import math

import jax
import jax.numpy as jnp
from jax import lax
from jax.experimental import pallas as pl
from jax.experimental.pallas import tpu as pltpu
from jax.sharding import PartitionSpec as P

HD = 128
TOPK = 8
SEQ_MIN = 2048
ROWS = 256
SHARE = 32

norm_eps = 1e-05
head_eps = 1e-06
rope_base = 10000.0
masked_score = -1e30
absent_slot = 4096.0

AXIS = "fsdp"
f32 = jnp.float32
bf16 = jnp.bfloat16
MIB = 1 << 20


def dot_nt(left, right):
    return lax.dot_general(left, right, (((1,), (1,)), ((), ())), preferred_element_type=f32)


def dot_tn(left, right):
    return lax.dot_general(left, right, (((0,), (0,)), ((), ())), preferred_element_type=f32)


def dot_nn(left, right):
    return lax.dot_general(left, right, (((1,), (0,)), ((), ())), preferred_element_type=f32)


def params(steps, mib):
    return pltpu.CompilerParams(
        dimension_semantics=("arbitrary",) * steps, vmem_limit_bytes=mib * MIB
    )


def estimate(flops, bytes_accessed, transcendentals):
    return pl.CostEstimate(
        flops=flops // SHARE, bytes_accessed=bytes_accessed // SHARE, transcendentals=transcendentals // SHARE
    )


def rope_tables(count):
    half_width = HD // 2
    frequency = jnp.exp(-math.log(rope_base) * 2.0 * jnp.arange(half_width, dtype=f32) / HD)
    angles = jnp.arange(count, dtype=f32)[:, None] * frequency[None, :]
    cosine, sine = jnp.cos(angles), jnp.sin(angles)
    return jnp.concatenate([cosine, cosine], axis=-1), jnp.concatenate([-sine, sine], axis=-1)


def slots_kernel(expert_count, routes_ref, order_ref, slots_ref):
    tok_rows = routes_ref.shape[0]
    pair_count = order_ref.shape[1]
    order = order_ref[...]
    shift = TOPK.bit_length() - 1
    token_of = lax.shift_right_logical(order, jnp.full_like(order, shift))
    route_of = order & (TOPK - 1)
    token_iota = lax.broadcasted_iota(jnp.int32, (tok_rows, pair_count), 0)
    token_hot = jnp.where(token_iota == token_of, 1.0, 0.0).astype(bf16)
    place = lax.broadcasted_iota(jnp.int32, (TOPK, pair_count), 1)
    chosen = lax.broadcasted_iota(jnp.int32, (TOPK, pair_count), 0) == route_of
    high = lax.shift_right_logical(place, jnp.full_like(place, 8)).astype(f32)
    low = (place & 255).astype(f32)
    digits = jnp.concatenate([jnp.where(chosen, high, 0.0), jnp.where(chosen, low, 0.0)], axis=0)
    found = dot_nt(token_hot, digits.astype(bf16))
    rank = found[:, :TOPK] * 256.0 + found[:, TOPK:]
    routes = routes_ref[...]
    lanes = -(-expert_count // 128) * 128
    expert_iota = lax.broadcasted_iota(jnp.int32, (tok_rows, lanes), 1)
    never = 1e9
    by_expert = jnp.full((tok_rows, lanes), never, f32)
    for k in range(TOPK):
        by_expert = jnp.where(expert_iota == routes[:, k : k + 1], rank[:, k : k + 1], by_expert)
    turned = by_expert.T
    for e in range(expert_count):
        mine = turned[e : e + 1, :]
        earlier = jnp.where(by_expert[:, e : e + 1] < mine, 1.0, 0.0)
        count = jnp.sum(earlier, axis=0, keepdims=True)
        slots_ref[e : e + 1, :] = jnp.where(mine < never, count, absent_slot)


def block_slots(routes, order, expert_count):
    tok_rows = routes.shape[0]
    return pl.pallas_call(
        functools.partial(slots_kernel, expert_count),
        out_shape=jax.ShapeDtypeStruct((expert_count, tok_rows), f32),
        compiler_params=pltpu.CompilerParams(vmem_limit_bytes=32 * MIB),
        name="block_slots",
    )(routes, order)


def slot_hot(slots_ref, expert, capacity):
    slot_row = slots_ref[pl.ds(expert, 1), :]
    slot_iota = lax.broadcasted_iota(jnp.int32, (capacity, slot_row.shape[1]), 0).astype(f32)
    return jnp.where(slot_iota == slot_row, 1.0, 0.0).astype(bf16)


def plane_hot(slots_ref, first, shape):
    return jnp.concatenate([slot_hot(slots_ref, first + r, shape[1]) for r in range(shape[0])])


def dispatch_kernel(at_ref, slots_ref, rows_ref, out_ref):
    hot = plane_hot(slots_ref, at_ref[0], out_ref.shape)
    out_ref[...] = dot_nn(hot, rows_ref[...]).astype(bf16).reshape(out_ref.shape)


def dispatch(at, slots, rows, per_plane, capacity):
    blocks, experts, tok_rows = slots.shape
    width = rows.shape[2]
    slot_rows = per_plane * capacity
    return pl.pallas_call(
        dispatch_kernel,
        out_shape=jax.ShapeDtypeStruct((per_plane, blocks, capacity, width), bf16),
        grid_spec=pltpu.PrefetchScalarGridSpec(
            num_scalar_prefetch=1,
            grid=(blocks,),
            in_specs=[
                pl.BlockSpec((None, experts, tok_rows), lambda i, s: (i, 0, 0)),
                pl.BlockSpec((None, tok_rows, width), lambda i, s: (s[1 + i], 0, 0)),
            ],
            out_specs=pl.BlockSpec((per_plane, None, capacity, width), lambda i, s: (0, i, 0, 0)),
        ),
        compiler_params=params(1, 40),
        cost_estimate=estimate(
            flops=2 * blocks * slot_rows * tok_rows * width,
            bytes_accessed=2 * blocks * (slot_rows + tok_rows) * width,
            transcendentals=0,
        ),
        name="dispatch",
    )(at, slots, rows)


def combine_kernel(first_ref, slots_ref, rows_ref, out_ref):
    hot = plane_hot(slots_ref, first_ref[0], rows_ref.shape)
    rows = rows_ref[...].reshape(hot.shape[0], rows_ref.shape[2])
    out_ref[...] = dot_tn(hot, rows).astype(bf16)


def combine(first, slots, rows, block):
    experts, tok_rows = slots.shape
    per_plane, _, capacity, width = rows.shape
    slot_rows = per_plane * capacity
    return pl.pallas_call(
        combine_kernel,
        out_shape=jax.ShapeDtypeStruct((tok_rows, width), bf16),
        grid_spec=pltpu.PrefetchScalarGridSpec(
            num_scalar_prefetch=1,
            grid=(1,),
            in_specs=[
                pl.BlockSpec((experts, tok_rows), lambda i, s: (0, 0)),
                pl.BlockSpec((per_plane, None, capacity, width), lambda i, s: (0, block, 0, 0)),
            ],
            out_specs=pl.BlockSpec((tok_rows, width), lambda i, s: (0, 0)),
        ),
        compiler_params=params(1, 40),
        cost_estimate=estimate(
            flops=2 * slot_rows * tok_rows * width,
            bytes_accessed=2 * (slot_rows + tok_rows) * width,
            transcendentals=0,
        ),
        name="combine",
    )(first, slots, rows)


def qkv_kernel(heads, planes, at_ref, x_ref, gain_ref, *refs):
    w_refs = refs[:planes]
    gq_ref, gk_ref, cos_ref, sin_ref, act_ref, pre_ref, rot_ref, all_ref = refs[planes:]
    depth = w_refs[0].shape[0]

    @pl.when(pl.program_id(0) == 0)
    def _():
        for d in range(planes):
            place = pl.ds(pl.multiple_of(at_ref[d] * depth, depth), depth)
            all_ref[place, :] = w_refs[d][...]

    x = x_ref[...].astype(f32)
    inverse = lax.rsqrt(jnp.mean(x * x, axis=-1, keepdims=True) + norm_eps)
    act = (x * inverse * gain_ref[...]).astype(bf16)
    act_ref[...] = act
    y = None
    for d in range(planes):
        columns = pl.ds(pl.multiple_of(at_ref[d] * depth, depth), depth)
        term = dot_nn(act_ref[:, columns], w_refs[d][...])
        y = term if y is None else y + term
    cosine, sine = cos_ref[...], sin_ref[...]
    for part, gain in enumerate((gq_ref[...], gk_ref[...])):
        for h in range(heads):
            at = (part * heads + h) * HD
            u = y[:, at : at + HD]
            pre_ref[:, at : at + HD] = u
            n = u * lax.rsqrt(jnp.mean(u * u, axis=-1, keepdims=True) + head_eps) * gain
            rot_ref[:, at : at + HD] = (n * cosine + pltpu.roll(n, HD // 2, 1) * sine).astype(bf16)
    at = 2 * heads * HD
    rot_ref[:, at:] = y[:, at:].astype(bf16)


def qkv_project(places, rows, gain, weights, gain_q, gain_k, cosine, sine, heads):
    count, width = rows.shape
    planes = len(weights)
    depth, out_width = weights[0].shape
    pre_width = 2 * heads * HD
    whole = lambda i, s: (0, 0)
    block = lambda i, s: (i, 0)
    return pl.pallas_call(
        functools.partial(qkv_kernel, heads, planes),
        out_shape=(
            jax.ShapeDtypeStruct((count, width), bf16),
            jax.ShapeDtypeStruct((count, pre_width), f32),
            jax.ShapeDtypeStruct((count, out_width), bf16),
            jax.ShapeDtypeStruct((width, out_width), bf16),
        ),
        grid_spec=pltpu.PrefetchScalarGridSpec(
            num_scalar_prefetch=1,
            grid=(count // ROWS,),
            in_specs=[
                pl.BlockSpec((ROWS, width), block),
                pl.BlockSpec((1, width), whole),
            ]
            + [pl.BlockSpec((depth, out_width), whole)] * planes
            + [
                pl.BlockSpec((1, HD), whole),
                pl.BlockSpec((1, HD), whole),
                pl.BlockSpec((ROWS, HD), block),
                pl.BlockSpec((ROWS, HD), block),
            ],
            out_specs=(
                pl.BlockSpec((ROWS, width), block),
                pl.BlockSpec((ROWS, pre_width), block),
                pl.BlockSpec((ROWS, out_width), block),
                pl.BlockSpec((width, out_width), whole),
            ),
        ),
        compiler_params=params(1, 56),
        cost_estimate=estimate(
            flops=2 * count * width * out_width,
            bytes_accessed=4 * count * width + 2 * width * out_width + 6 * count * out_width,
            transcendentals=0,
        ),
        name="qkv_project",
    )(places, rows, gain, *weights, gain_q, gain_k, cosine, sine)


def attn_kernel(
    scale, low_ref, high_ref, q_ref, k_ref, v_ref, sq_ref, sk_ref, o_ref, ol_ref, lse_ref, s_scr
):
    block = pl.program_id(1)
    low, high = low_ref[block], high_ref[block]
    q = q_ref[...]
    seg_q = sq_ref[...]
    half = ROWS // 2

    def scores(kb, top):
        at = pl.ds(pl.multiple_of(kb * ROWS, ROWS), ROWS)
        s = dot_nt(q, k_ref[at, :]) * scale
        s = jnp.where(seg_q == sk_ref[:, at], s, masked_score)
        s_scr[:, at] = s
        return jnp.maximum(top, jnp.maximum(s[:, :half], s[:, half:]))

    top = lax.fori_loop(low, high, scores, jnp.full((ROWS, half), masked_score, f32))
    top = jnp.max(top, axis=-1, keepdims=True)

    def weigh(kb, carry):
        total, acc = carry
        at = pl.ds(pl.multiple_of(kb * ROWS, ROWS), ROWS)
        p = jnp.exp(s_scr[:, at] - top)
        acc = acc + dot_nn(p.astype(bf16), v_ref[at, :])
        return total + (p[:, :half] + p[:, half:]), acc

    total, acc = lax.fori_loop(
        low, high, weigh, (jnp.zeros((ROWS, half), f32), jnp.zeros((ROWS, HD), f32))
    )
    total = jnp.sum(total, axis=-1, keepdims=True)
    out = acc / total
    o_ref[...] = out
    ol_ref[...] = out.astype(bf16)
    lse = jnp.broadcast_to(top + jnp.log(total), (ROWS, HD)).T
    lse_ref[0] = lse[0:1, :]


def attention(rot, seg_col, seg_row, low, high, heads):
    count = rot.shape[0]
    blocks = count // ROWS
    scale = HD ** (-0.5)
    return pl.pallas_call(
        functools.partial(attn_kernel, scale),
        out_shape=(
            jax.ShapeDtypeStruct((count, heads * HD), f32),
            jax.ShapeDtypeStruct((count, heads * HD), bf16),
            jax.ShapeDtypeStruct((heads * blocks, 1, ROWS), f32),
        ),
        grid_spec=pltpu.PrefetchScalarGridSpec(
            num_scalar_prefetch=2,
            grid=(heads, blocks),
            in_specs=[
                pl.BlockSpec((ROWS, HD), lambda h, i, *s: (i, h)),
                pl.BlockSpec((count, HD), lambda h, i, *s: (0, heads + h)),
                pl.BlockSpec((count, HD), lambda h, i, *s: (0, 2 * heads + h)),
                pl.BlockSpec((ROWS, 1), lambda h, i, *s: (i, 0)),
                pl.BlockSpec((1, count), lambda h, i, *s: (0, 0)),
            ],
            out_specs=(
                pl.BlockSpec((ROWS, HD), lambda h, i, *s: (i, h)),
                pl.BlockSpec((ROWS, HD), lambda h, i, *s: (i, h)),
                pl.BlockSpec((1, 1, ROWS), lambda h, i, *s: (h * blocks + i, 0, 0)),
            ),
            scratch_shapes=[pltpu.VMEM((ROWS, count), f32)],
        ),
        compiler_params=params(2, 32),
        cost_estimate=estimate(
            flops=2 * heads * count * count * HD,
            bytes_accessed=12 * heads * count * HD,
            transcendentals=heads * count * count // 2,
        ),
        name="attention",
    )(low, high, rot, rot, rot, seg_col, seg_row)


def head_back(grad, pre, gain, cosine, sine):
    n = grad * cosine - pltpu.roll(grad, HD // 2, 1) * sine
    inverse = lax.rsqrt(jnp.mean(pre * pre, axis=-1, keepdims=True) + head_eps)
    w = n * gain
    back = inverse * w - pre * inverse**3 * jnp.mean(w * pre, axis=-1, keepdims=True)
    return back, jnp.sum(n * pre * inverse, axis=0, keepdims=True)


def attn_back_kernel(
    scale,
    low_ref,
    high_ref,
    q_ref,
    k_ref,
    v_ref,
    do_ref,
    o_ref,
    lse_ref,
    sq_ref,
    sk_ref,
    qpre_ref,
    kpre_ref,
    gq_ref,
    gk_ref,
    cosq_ref,
    sinq_ref,
    cosk_ref,
    sink_ref,
    grad_ref,
    gain_ref,
    dk_scr,
    dv_scr,
):
    head, block = pl.program_id(0), pl.program_id(1)
    heads = pl.num_programs(0)

    def columns(part):
        return pl.ds(pl.multiple_of((part * heads + head) * HD, HD), HD)

    low, high = low_ref[block], high_ref[block]

    @pl.when(block == 0)
    def _():
        dk_scr[...] = jnp.zeros_like(dk_scr)
        dv_scr[...] = jnp.zeros_like(dv_scr)

    @pl.when((block == 0) & (head == 0))
    def _():
        gain_ref[...] = jnp.zeros_like(gain_ref)

    q, do = q_ref[...], do_ref[...]
    row_dot = jnp.sum((do.astype(f32) * o_ref[...]).T, axis=0, keepdims=True)
    lse = lse_ref[0]
    seg_q = sq_ref[...]

    def tile(kb, dq):
        at = pl.ds(pl.multiple_of(kb * ROWS, ROWS), ROWS)
        k, v = k_ref[at, :], v_ref[at, :]
        s = dot_nt(k, q) * scale
        p = jnp.where(sk_ref[at, :] == seg_q, jnp.exp(s - lse), 0.0)
        dp = dot_nt(v, do)
        ds = (p * (dp - row_dot)).astype(bf16)
        dv_scr[at, :] += dot_nn(p.astype(bf16), do)
        dk_scr[at, :] += dot_nn(ds, q)
        return dq + dot_tn(ds, k)

    dq = lax.fori_loop(low, high, tile, jnp.zeros((ROWS, HD), f32))
    back, gain_q = head_back(dq * scale, qpre_ref[...], gq_ref[...], cosq_ref[...], sinq_ref[...])
    grad_ref[pl.ds(pl.multiple_of(block * ROWS, ROWS), ROWS), columns(0)] = back.astype(bf16)
    gain_ref[0:1, :] += gain_q

    @pl.when(block == pl.num_programs(1) - 1)
    def _():
        @pl.loop(0, dk_scr.shape[0] // ROWS)
        def _(i):
            at = pl.ds(pl.multiple_of(i * ROWS, ROWS), ROWS)
            back, gain_k = head_back(
                dk_scr[at, :] * scale, kpre_ref[at, :], gk_ref[...], cosk_ref[at, :], sink_ref[at, :]
            )
            grad_ref[at, columns(1)] = back.astype(bf16)
            grad_ref[at, columns(2)] = dv_scr[at, :].astype(bf16)
            gain_ref[1:2, :] += gain_k


def attention_back(
    rot, grad, out, lse, seg_col, seg_row, low, high, pre, gain_q, gain_k, cosine, sine, heads
):
    count = rot.shape[0]
    blocks = count // ROWS
    scale = HD ** (-0.5)
    mine = lambda h, i, *s: (i, h)
    whole = lambda h, i, *s: (0, 0)
    return pl.pallas_call(
        functools.partial(attn_back_kernel, scale),
        out_shape=(
            jax.ShapeDtypeStruct((count, 3 * heads * HD), bf16),
            jax.ShapeDtypeStruct((8, HD), f32),
        ),
        grid_spec=pltpu.PrefetchScalarGridSpec(
            num_scalar_prefetch=2,
            grid=(heads, blocks),
            in_specs=[
                pl.BlockSpec((ROWS, HD), mine),
                pl.BlockSpec((count, HD), lambda h, i, *s: (0, heads + h)),
                pl.BlockSpec((count, HD), lambda h, i, *s: (0, 2 * heads + h)),
                pl.BlockSpec((ROWS, HD), mine),
                pl.BlockSpec((ROWS, HD), mine),
                pl.BlockSpec((1, 1, ROWS), lambda h, i, *s: (h * blocks + i, 0, 0)),
                pl.BlockSpec((1, ROWS), lambda h, i, *s: (0, i)),
                pl.BlockSpec((count, 1), whole),
                pl.BlockSpec((ROWS, HD), mine),
                pl.BlockSpec((count, HD), lambda h, i, *s: (0, heads + h)),
                pl.BlockSpec((1, HD), whole),
                pl.BlockSpec((1, HD), whole),
                pl.BlockSpec((ROWS, HD), lambda h, i, *s: (i, 0)),
                pl.BlockSpec((ROWS, HD), lambda h, i, *s: (i, 0)),
                pl.BlockSpec((count, HD), whole),
                pl.BlockSpec((count, HD), whole),
            ],
            out_specs=(
                pl.BlockSpec((count, 3 * heads * HD), whole),
                pl.BlockSpec((8, HD), whole),
            ),
            scratch_shapes=[pltpu.VMEM((count, HD), f32), pltpu.VMEM((count, HD), f32)],
        ),
        compiler_params=params(2, 48),
        cost_estimate=estimate(
            flops=5 * heads * count * count * HD,
            bytes_accessed=30 * heads * count * HD,
            transcendentals=heads * count * count // 2,
        ),
        name="attention_back",
    )(
        low,
        high,
        rot,
        rot,
        rot,
        grad,
        out,
        lse,
        seg_row,
        seg_col,
        pre,
        pre,
        gain_q,
        gain_k,
        cosine,
        sine,
        cosine,
        sine,
    )


def expert_kernel(count, carried, mine_ref, x_ref, near_ref, far_ref, *refs):
    wg_ref, wu_ref, wd_ref = refs[:3]
    refs = refs[3 + carried :]
    back_ref, out_ref, xs_ref, c_ref, hid_ref, gp_ref, up_ref = refs[:7]
    out_acc, back_acc, gate_scr, dot_scr = refs[7:]
    step = pl.program_id(1)
    per_plane, capacity, width = c_ref.shape
    rows = per_plane * capacity
    extra = x_ref.shape[2] - width
    lane = lax.broadcasted_iota(jnp.int32, (rows, extra), 1)
    high, low = lane == mine_ref[0], lane == mine_ref[0] + count

    @pl.when(step == 0)
    def _():
        xs_ref[...] = x_ref[:, :, :width]

        @pl.when(pl.program_id(0) == 0)
        def _():
            c_ref[...] = near_ref[...]

        @pl.when(pl.program_id(0) > 0)
        def _():
            c_ref[...] = far_ref[...]
        gates = x_ref[:, :, width:].reshape(rows, extra).astype(f32)
        gate_scr[...] = jnp.sum(jnp.where(high | low, gates, 0.0), axis=-1, keepdims=True)
        out_acc[...] = jnp.zeros_like(out_acc)
        back_acc[...] = jnp.zeros_like(back_acc)
        dot_scr[...] = jnp.zeros_like(dot_scr)

    x = x_ref[:, :, :width].reshape(rows, width)
    c = c_ref[...].reshape(rows, width)
    gate = gate_scr[...]
    wg, wu, wd = wg_ref[...], wu_ref[...], wd_ref[...]
    gate_pre, up_pre = dot_nn(x, wg), dot_nn(x, wu)
    sig = jax.nn.sigmoid(gate_pre)
    hidden = (gate_pre * sig * up_pre).astype(bf16)
    out_acc[...] += dot_nn(hidden, wd)
    plain = dot_nt(c, wd)
    wide = hidden.astype(f32)
    dot_scr[...] += jnp.sum(wide * plain, axis=-1, keepdims=True)
    hid_ref[...] = (wide * gate).astype(bf16).reshape(hid_ref.shape)
    hidden_grad = plain * gate
    gate_grad = (hidden_grad * up_pre * sig * (1.0 + gate_pre * (1.0 - sig))).astype(bf16)
    up_grad = (hidden_grad * gate_pre * sig).astype(bf16)
    gp_ref[...] = gate_grad.reshape(gp_ref.shape)
    up_ref[...] = up_grad.reshape(up_ref.shape)
    back_acc[...] += dot_nt(gate_grad, wg) + dot_nt(up_grad, wu)

    @pl.when(step == pl.num_programs(1) - 1)
    def _():
        dots = dot_scr[...]
        coarse = dots.astype(bf16).astype(f32)
        lanes = jnp.where(high, coarse, jnp.where(low, dots - coarse, 0.0)).astype(bf16)
        back_ref[:, :, :width] = back_acc[...].astype(bf16).reshape(c_ref.shape)
        back_ref[:, :, width:] = lanes.reshape(per_plane, capacity, extra)
        out_ref[...] = (out_acc[...] * gate).astype(bf16).reshape(out_ref.shape)


def experts(mine, x, near, far, wg, wu, wd, base, planes, count, kept):
    per_plane, blocks, capacity, wide = x.shape
    width = near.shape[3]
    halves, _, hidden = wg.shape
    rows = per_plane * capacity
    saved = jax.ShapeDtypeStruct((per_plane, planes, capacity, width), bf16)
    thin = jax.ShapeDtypeStruct((per_plane, planes, capacity, halves * hidden), bf16)
    moved = pl.BlockSpec((per_plane, None, capacity, wide), lambda i, f, s: (0, i, 0, 0))
    saved_spec = pl.BlockSpec((per_plane, None, capacity, width), lambda i, f, s: (0, base + i, 0, 0))
    thin_spec = pl.BlockSpec((per_plane, None, capacity, hidden), lambda i, f, s: (0, base + i, 0, f))
    carried = 0 if kept is None else len(kept)
    skip = base - 1 if base else 0
    cot_specs = [
        pl.BlockSpec((per_plane, None, capacity, width), lambda i, f, s: (0, 0, 0, 0)),
        pl.BlockSpec(
            (per_plane, None, capacity, width),
            lambda i, f, s: (0, jnp.maximum(skip + i - 1, 0), 0, 0),
        ),
    ]
    result = pl.pallas_call(
        functools.partial(expert_kernel, count, carried),
        out_shape=(
            jax.ShapeDtypeStruct(x.shape, bf16),
            jax.ShapeDtypeStruct((per_plane, blocks, capacity, width), bf16),
            saved,
            saved,
            thin,
            thin,
            thin,
        ),
        grid_spec=pltpu.PrefetchScalarGridSpec(
            num_scalar_prefetch=1,
            grid=(blocks, halves),
            in_specs=[
                moved,
                *cot_specs,
                pl.BlockSpec((None, width, hidden), lambda i, f, s: (f, 0, 0)),
                pl.BlockSpec((None, width, hidden), lambda i, f, s: (f, 0, 0)),
                pl.BlockSpec((None, hidden, width), lambda i, f, s: (f, 0, 0)),
            ]
            + [pl.BlockSpec(memory_space=pl.ANY)] * carried,
            out_specs=(
                moved,
                pl.BlockSpec((per_plane, None, capacity, width), lambda i, f, s: (0, i, 0, 0)),
                saved_spec,
                saved_spec,
                thin_spec,
                thin_spec,
                thin_spec,
            ),
            scratch_shapes=[
                pltpu.VMEM((rows, width), f32),
                pltpu.VMEM((rows, width), f32),
                pltpu.VMEM((rows, 1), f32),
                pltpu.VMEM((rows, 1), f32),
            ],
        ),
        input_output_aliases={7 + i: 2 + i for i in range(carried)},
        compiler_params=params(2, 60),
        cost_estimate=estimate(
            flops=12 * blocks * rows * width * hidden * halves,
            bytes_accessed=10 * blocks * rows * width + 6 * blocks * width * hidden * halves,
            transcendentals=blocks * rows * hidden * halves,
        ),
        name="experts",
    )(mine, x, near, far, wg, wu, wd, *(kept or ()))
    return result[0], result[1], result[2:]


def gram_kernel(plus, left_ref, right_ref, *refs):
    total = dot_tn(left_ref[...], right_ref[...])
    if plus:
        total = total + refs[0][...]
    refs[-1][...] = total.astype(refs[-1].dtype)


def gram(left, right, left_cols, right_cols, dtype, plus=None):
    rows = left.shape[0]
    left_at, left_count = left_cols
    right_at, right_count = right_cols
    tall = min(left_count, 256)
    wide = min(right_count, 1024)
    out_spec = pl.BlockSpec((tall, wide), lambda j, i: (i, j))
    return pl.pallas_call(
        functools.partial(gram_kernel, plus is not None),
        out_shape=jax.ShapeDtypeStruct((left_count, right_count), dtype),
        grid=(right_count // wide, left_count // tall),
        in_specs=[
            pl.BlockSpec((rows, tall), lambda j, i: (0, left_at // tall + i)),
            pl.BlockSpec((rows, wide), lambda j, i: (0, right_at // wide + j)),
        ]
        + [out_spec] * (plus is not None),
        out_specs=out_spec,
        compiler_params=params(2, 48),
        cost_estimate=estimate(
            flops=2 * rows * left_count * right_count,
            bytes_accessed=2 * rows * (left_count + right_count) + 4 * left_count * right_count,
            transcendentals=0,
        ),
        name="gram",
    )(left, right, *(() if plus is None else (plus,)))


def project_kernel(plus, core_ref, rows_ref, weights_ref, *refs):
    total = dot_nt(rows_ref[...], weights_ref[...])
    if plus:
        total = total + refs[0][...].astype(f32)
    refs[-1][...] = total.astype(bf16)


def project_back(core, rows, weights, tok_rows, plus=None):
    count, depth = rows.shape
    width = weights.shape[0]
    chips = count // tok_rows // 2
    out_spec = pl.BlockSpec((tok_rows, width), lambda i, s: (i, 0))
    return pl.pallas_call(
        functools.partial(project_kernel, plus is not None),
        out_shape=jax.ShapeDtypeStruct((chips * tok_rows, width), bf16),
        grid_spec=pltpu.PrefetchScalarGridSpec(
            num_scalar_prefetch=1,
            grid=(chips,),
            in_specs=[
                pl.BlockSpec((tok_rows, depth), lambda i, s: (2 * i + s[0], 0)),
                pl.BlockSpec((width, depth), lambda i, s: (0, 0)),
            ]
            + [out_spec] * (plus is not None),
            out_specs=out_spec,
        ),
        compiler_params=params(1, 40),
        cost_estimate=estimate(
            flops=count * depth * width,
            bytes_accessed=2 * width * depth + count * depth + count * width,
            transcendentals=0,
        ),
        name="project_back",
    )(core, rows, weights, *(() if plus is None else (plus,)))


def after(value, *others):
    return lax.optimization_barrier((value,) + others)[0]


def body(
    hidden_in,
    out_cotangent,
    segment_number,
    expert_routes,
    pair_order,
    norm_gain,
    query_weight,
    key_weight,
    value_weight,
    output_weight,
    query_gain,
    key_gain,
    ffn_norm_gain,
    router_weight,
    expert_gate,
    expert_up,
    expert_down,
):
    tok_rows, width = hidden_in.shape
    devices = lax.axis_size(AXIS)
    members = max(1, SEQ_MIN // tok_rows)
    planes = devices // members
    per_plane = members // 2
    expert_count = devices // 2
    capacity = tok_rows * TOPK // expert_count
    heads = width // HD // members
    head_width = heads * HD
    own_rows = norm_gain.shape[0]
    seq = members * tok_rows
    me = lax.axis_index(AXIS)
    plane, member = me // members, me % members
    mine = (me // 2).astype(jnp.int32).reshape(1)
    first = (plane * per_plane).astype(jnp.int32)
    places = (plane ^ jnp.arange(planes, dtype=jnp.int32)).astype(jnp.int32)
    counted = jnp.concatenate([first[None], jnp.arange(planes, dtype=jnp.int32)])
    halfway = -(-planes // 2)
    chunks = [part for part in (range(halfway, planes), range(halfway)) if len(part)]

    def placed(part):
        return jnp.concatenate([first[None], places[part.start : part.stop]])

    plane_groups = [[g * members + j for j in range(members)] for g in range(planes)]
    stack_groups = [[g * members + j for g in range(planes)] for j in range(members)]
    core_groups = [
        [g * members + 2 * c + h for c in range(per_plane)] for g in range(planes) for h in (0, 1)
    ]

    def exchange(value, groups=None):
        return lax.all_to_all(
            value, AXIS, split_axis=0, concat_axis=0, tiled=True, axis_index_groups=groups
        )

    def gather(value, groups=None):
        return lax.all_gather(value, AXIS, axis=0, tiled=True, axis_index_groups=groups)

    def flip(value, bits):
        if bits == 0:
            return value
        return lax.ppermute(value, AXIS, [(i, i ^ bits) for i in range(devices)])

    def to_core(value):
        return flip(value, 1)

    def to_plane(value, d):
        return flip(value, members * d)

    def spread(value):
        found = {0: value}
        for d in range(1, planes):
            lowest = d & -d
            found[d] = to_plane(found[d ^ lowest], lowest)
        return [found[d] for d in range(planes)]

    def fold(sums, *others):
        bit = 1
        while bit < len(sums):
            for d in range(len(sums)):
                if d & bit and not d & (bit - 1):
                    came = to_plane(sums[d].astype(bf16), bit)
                    if d == bit:
                        came = after(came, *others)
                    sums[d ^ bit] = sums[d ^ bit].astype(f32) + came.astype(f32)
            bit *= 2
        return sums[0]

    wire, core_op = [], []

    def on_wire(value, groups):
        came = exchange(after(value, *wire[-1:]), groups)
        wire.append(came)
        return came

    def to_chips(value):
        return on_wire(value, core_groups)

    def in_turn(value):
        return after(value, *core_op[-1:])

    def ran(value):
        core_op.append(value)
        return value

    pieces = (
        router_weight.reshape(-1),
        norm_gain,
        ffn_norm_gain,
        query_gain,
        key_gain,
        segment_number.astype(bf16),
    )
    packed = jnp.concatenate(pieces)
    length = packed.shape[0]
    padded = -(-length // 128) * 128
    packed = jnp.pad(packed, (0, padded - length))
    packed = on_wire(jnp.broadcast_to(packed[None], (devices, padded)), None)
    small = []
    at = 0
    for piece in pieces:
        small.append(packed[:, at : at + piece.shape[0]])
        at += piece.shape[0]
    router_full = small[0].reshape(width, expert_count)
    gain_one = small[1].reshape(1, width).astype(f32)
    gain_two = small[2].reshape(1, width).astype(f32)
    gain_q = small[3].reshape(1, HD).astype(f32)
    gain_k = small[4].reshape(1, HD).astype(f32)
    segments = lax.dynamic_slice_in_dim(small[5], plane * members, members, 0).astype(f32)
    seg_row, seg_col = segments.reshape(1, seq), segments.reshape(seq, 1)
    seg_blocks = segments.reshape(seq // ROWS, ROWS)
    seg_first, seg_last = seg_blocks[:, 0], seg_blocks[:, -1]
    low = jnp.sum((seg_last[None, :] < seg_first[:, None]).astype(jnp.int32), axis=1)
    high = jnp.sum((seg_first[None, :] <= seg_last[:, None]).astype(jnp.int32), axis=1)

    columns = jnp.concatenate(
        [w.reshape(own_rows, members, head_width) for w in (query_weight, key_weight, value_weight)],
        axis=2,
    )
    slots = block_slots(expert_routes, pair_order, expert_count)
    columns = on_wire(
        after(columns, slots).transpose(1, 0, 2).reshape(members * own_rows, 3 * head_width), plane_groups
    )
    stacked = [to_plane(after(output_weight, packed), d) for d in range(planes)]
    weights = spread(after(columns, *stacked))
    slots = [to_plane(after(slots, *weights) if d else slots, d) for d in range(planes)]
    output_rows = jnp.zeros((planes * own_rows, width), bf16)
    for d, rows in enumerate(stacked):
        output_rows = lax.dynamic_update_slice_in_dim(output_rows, rows, places[d] * own_rows, 0)
    rows_all = gather(hidden_in, plane_groups)

    cot_own = dispatch(counted, slots[0][None], out_cotangent[None], per_plane, capacity)
    cot_first = [to_chips(cot_own)]
    output_full = gather(after(output_rows, columns), plane_groups)
    slot_list, slots = slots, jnp.stack(slots)
    cot_rows = {0: out_cotangent}
    top = planes // 2
    early, late = [], []
    if planes > 1:
        cot_rows[top] = to_plane(after(out_cotangent, *weights), top)
        early.append(cot_rows[top])
    for d in range(1, planes):
        if d != top:
            lowest = d & -d
            start = after(out_cotangent, *early) if d == lowest else cot_rows[d ^ lowest]
            cot_rows[d] = to_plane(start, lowest)
            late.append(cot_rows[d])

    halves = lambda w: jnp.concatenate([w, to_core(w)], axis=0)
    wg, wu, wd = halves(expert_gate), halves(expert_up), halves(expert_down)

    cosine, sine = rope_tables(seq)
    act_one, pre, rot, ordered = qkv_project(
        places, rows_all, gain_one, weights, gain_q, gain_k, cosine, sine, heads
    )
    out_wide, out_heads, lse = attention(rot, seg_col, seg_row, low, high, heads)
    out_low = on_wire(after(out_heads, *slot_list, *early), plane_groups)
    if planes > 1:
        rows = after(cot_rows[top], out_heads)
        sent = dispatch(counted, slots[top : top + 1], rows[None], per_plane, capacity)
        cot_first.append(to_chips(sent))
    out_low = out_low.reshape(members, tok_rows, head_width).transpose(1, 0, 2)
    out_low = out_low.reshape(tok_rows, planes, members, own_rows).transpose(0, 2, 1, 3)
    out_low = out_low.reshape(tok_rows, width)
    tokens = hidden_in.astype(f32)
    cotangent = out_cotangent.astype(f32)
    middle = tokens + dot_nn(out_low, output_full)
    inverse_two = lax.rsqrt(jnp.mean(middle * middle, axis=-1, keepdims=True) + norm_eps)
    act_two = (middle * inverse_two * gain_two).astype(bf16)

    logits = dot_nn(act_two, router_full)
    expert_ids = jnp.arange(expert_count, dtype=jnp.int32)
    routed = jnp.any(expert_routes[:, :, None] == expert_ids[None, None, :], axis=1)
    logits = jnp.where(routed, logits, masked_score)
    gates = jnp.where(routed, jnp.exp(logits - jnp.max(logits, axis=1, keepdims=True)), 0.0)
    gates = gates / jnp.sum(gates, axis=1, keepdims=True)
    coarse = lax.reduce_precision(gates, 8, 7)
    extra = -(-2 * expert_count // 128) * 128
    act_wide = jnp.concatenate(
        [
            act_two,
            coarse.astype(bf16),
            (gates - coarse).astype(bf16),
            jnp.zeros((tok_rows, extra - 2 * expert_count), bf16),
        ],
        axis=1,
    )

    act_wide = after(act_wide, *late, *cot_first)
    act_all = gather(act_wide, stack_groups).reshape(planes, tok_rows, -1)
    others = [d for d in range(1, planes) if d != top]
    cot_far = cot_first[0]
    if others:
        far = jnp.stack([after(cot_rows[d], act_wide) for d in others])
        far_slots = jnp.stack([slots[d] for d in others])
        cot_far = to_chips(
            ran(dispatch(counted[: len(others) + 1], far_slots, far, per_plane, capacity))
        )

    act = []
    for part in chunks:
        own_slots = slots[part.start : part.stop]
        rows = after(in_turn(act_all), wg, wu, wd)
        sent = dispatch(placed(part), own_slots, rows, per_plane, capacity)
        act.append(to_chips(ran(sent)))
    kept, back, outs = None, [], []
    for part, rows in zip(chunks, act):
        sent, out, kept = experts(
            mine,
            in_turn(rows),
            cot_first[0 if part.start == 0 else 1],
            cot_far,
            wg,
            wu,
            wd,
            part.start,
            planes,
            expert_count,
            kept,
        )
        back.append(to_chips(ran(sent)))
        outs.append(out)
    x_all, c_all, hid_all, gp_all, up_all = kept

    hidden = expert_gate.shape[2]
    flat = lambda value: value.reshape(-1, value.shape[3])
    sides = (
        (flat(x_all), flat(gp_all), 1),
        (flat(x_all), flat(up_all), 1),
        (flat(hid_all), flat(c_all), 0),
    )

    def half(side, which, plus=None):
        left, right, split = side
        cut, whole = (which * hidden, hidden), (0, width)
        cols = (whole, cut) if split else (cut, whole)
        return ran(gram(in_turn(left), right, *cols, f32, plus))

    passed = []

    def home(part, rows):
        sums = {}
        for d in sorted(part, key=lambda d: (-(d & 1), d)):
            sums[d] = ran(combine(first[None], slots[d], in_turn(rows), d - part.start))
        bit = 1
        while bit < len(part):
            for d in part:
                if d & bit and not d & (bit - 1):
                    came = to_plane(sums[d].astype(bf16), bit)
                    passed.append(came)
                    sums[d ^ bit] = sums[d ^ bit].astype(f32) + came.astype(f32)
            bit *= 2
        return sums[part.start]

    back_sum = home(chunks[0], back[0])
    theirs = [half(side, 1) for side in sides[:2]]
    if len(chunks) > 1:
        back_sum = ran(in_turn(back_sum.astype(bf16)))
        back_sum = to_plane(back_sum, top)
    theirs.append(half(sides[2], 1))
    if len(chunks) > 1:
        back_sum = back_sum.astype(f32) + home(chunks[1], back[1])
    outs[0] = to_chips(outs[0])

    expert_in_grad = back_sum[:, :width]
    gate_grad = (
        back_sum[:, width : width + expert_count]
        + back_sum[:, width + expert_count : width + 2 * expert_count]
    )
    select_grad = gates * (gate_grad - jnp.sum(gates * gate_grad, axis=1, keepdims=True))
    logit_grad = select_grad.astype(bf16)
    grad_router = dot_tn(act_two, logit_grad)
    act_two_grad = expert_in_grad + dot_nt(logit_grad, router_full)
    weighted = act_two_grad * gain_two
    grad_gain_two = jnp.sum(act_two_grad * middle * inverse_two, axis=0)
    middle_grad = (
        cotangent
        + inverse_two * weighted
        - middle * inverse_two**3 * jnp.mean(weighted * middle, axis=-1, keepdims=True)
    )
    middle_low = middle_grad.astype(bf16)

    out_grad = dot_nt(middle_low, output_full).astype(bf16)
    out_grad = out_grad.reshape(tok_rows, members, planes, own_rows).transpose(0, 2, 1, 3)
    out_grad = out_grad.reshape(tok_rows, members, head_width).transpose(1, 0, 2)
    out_grad = out_grad.reshape(seq, head_width)
    ran(out_grad)
    theirs = [to_core(after(grad, out_grad)) for grad in theirs]
    out_grad = on_wire(out_grad, plane_groups)
    mixture = home(chunks[0], outs[0]).astype(bf16)
    dqkv, grad_gains = attention_back(
        rot,
        in_turn(out_grad),
        out_wide,
        lse,
        seg_col,
        seg_row,
        low,
        high,
        pre,
        gain_q,
        gain_k,
        cosine,
        sine,
        heads,
    )
    ran(dqkv)
    if len(chunks) > 1:
        near_sum = home(chunks[1], to_chips(outs[1]))
        done = (*core_op[-2:], mixture, *theirs)
        dqkv, grad_gains = after(dqkv, *done), after(grad_gains, *done)
    middle_all = gather(after(middle_low, dqkv), plane_groups)

    sums = (
        grad_router.reshape(devices, -1),
        grad_gain_two.reshape(devices, -1),
        grad_gains[0].reshape(devices, -1),
        grad_gains[1].reshape(devices, -1),
    )
    packed = jnp.concatenate(sums, axis=1)
    length = packed.shape[1]
    padded = -(-length // 128) * 128
    packed = jnp.pad(packed, ((0, 0), (0, padded - length)))

    core = (me % 2).astype(jnp.int32).reshape(1)
    given = project_back(1 - core, dqkv, ordered, tok_rows)
    part = gram(after(act_one, given), dqkv, (0, width), (0, 3 * head_width), bf16)
    part = part.reshape(planes, members * own_rows, 3 * head_width)
    shares = [lax.dynamic_index_in_dim(part, places[d], 0, False) for d in range(planes)]
    mixture = to_plane(mixture, top) if len(chunks) > 1 else mixture
    given = after(to_core(given), *shares, mixture, *passed[-1:])
    act_one_grad = project_back(core, dqkv, ordered, tok_rows, given)
    ran(act_one_grad)
    output_part = ran(gram(out_heads, in_turn(middle_all), (0, head_width), (0, width), bf16))
    grad_gate, grad_up, grad_down = (
        half(side, 0, other) for side, other in zip(sides, theirs)
    )
    shares = [after(share, act_one_grad) for share in shares]
    taken = fold(shares, grad_gate, grad_up, grad_down).astype(bf16)
    act_one_grad = on_wire(act_one_grad, core_groups)

    output_part = lax.psum_scatter(
        output_part, AXIS, scatter_dimension=0, tiled=True, axis_index_groups=stack_groups
    )
    to_owner = [
        (g * members + j, j * planes + g) for g in range(planes) for j in range(members)
    ]
    grad_output = lax.ppermute(output_part, AXIS, to_owner)
    mixture = mixture.astype(f32)
    if len(chunks) > 1:
        mixture = mixture + near_sum
    packed, act_one_grad, mixture, grad_gate, grad_up, grad_down = lax.optimization_barrier(
        (packed, act_one_grad, mixture, grad_gate, grad_up, grad_down)
    )
    layer_out = (middle + mixture).astype(bf16)
    packed = exchange(packed)
    taken, packed, grad_output = lax.optimization_barrier((taken, packed, grad_output))
    part = exchange(taken, plane_groups).reshape(members, own_rows, 3, head_width)
    part = part.transpose(2, 1, 0, 3).reshape(3, own_rows, width).astype(f32)
    grad_query, grad_key, grad_value = part[0], part[1], part[2]
    act_one_grad = act_one_grad.reshape(per_plane, tok_rows, width)
    act_one_grad = jnp.sum(act_one_grad.astype(f32), axis=0)

    inverse_one = lax.rsqrt(jnp.mean(tokens * tokens, axis=-1, keepdims=True) + norm_eps)
    weighted = act_one_grad * gain_one
    grad_hidden = (
        middle_grad
        + inverse_one * weighted
        - tokens * inverse_one**3 * jnp.mean(weighted * tokens, axis=-1, keepdims=True)
    )
    grad_gain_one = (
        jnp.sum(
            grad_query * query_weight.astype(f32)
            + grad_key * key_weight.astype(f32)
            + grad_value * value_weight.astype(f32),
            axis=1,
        )
        / norm_gain.astype(f32)
    )

    summed = jnp.sum(packed, axis=0)
    at, tiny = 0, []
    for piece in sums:
        tiny.append(summed[at : at + piece.shape[1]])
        at += piece.shape[1]

    return (
        layer_out,
        grad_hidden,
        grad_gain_one,
        grad_query,
        grad_key,
        grad_value,
        grad_output.astype(f32),
        tiny[2],
        tiny[3],
        tiny[1],
        tiny[0].reshape(own_rows, expert_count),
        grad_gate[None],
        grad_up[None],
        grad_down[None],
    )


def solution(mesh):
    row, mat, cube = P(AXIS), P(AXIS, None), P(AXIS, None, None)
    return jax.shard_map(
        body,
        mesh=mesh,
        in_specs=(mat, mat, row, mat, mat, row, mat, mat, mat, mat, row, row, row, mat)
        + (cube,) * 3,
        out_specs=(mat, mat, row, mat, mat, mat, mat, row, row, row, mat) + (cube,) * 3,
        check_vma=False,
    )
```

```python
import functools
import math

import jax
import jax.numpy as jnp
from jax import lax
from jax.experimental import pallas as pl
from jax.experimental.pallas import tpu as pltpu
from jax.sharding import PartitionSpec as P

HD = 128
TOPK = 8
SEQ_MIN = 2048
ROWS = 256
SHARE = 32

norm_eps = 1e-05
head_eps = 1e-06
rope_base = 10000.0
masked_score = -1e30
absent_slot = 4096.0

AXIS = "fsdp"
f32 = jnp.float32
bf16 = jnp.bfloat16
MIB = 1 << 20


def dot_nt(left, right):
    return lax.dot_general(left, right, (((1,), (1,)), ((), ())), preferred_element_type=f32)


def dot_tn(left, right):
    return lax.dot_general(left, right, (((0,), (0,)), ((), ())), preferred_element_type=f32)


def dot_nn(left, right):
    return lax.dot_general(left, right, (((1,), (0,)), ((), ())), preferred_element_type=f32)


def params(steps, mib):
    return pltpu.CompilerParams(
        dimension_semantics=("arbitrary",) * steps, vmem_limit_bytes=mib * MIB
    )


def estimate(flops, bytes_accessed, transcendentals):
    return pl.CostEstimate(
        flops=flops // SHARE, bytes_accessed=bytes_accessed // SHARE, transcendentals=transcendentals // SHARE
    )


def rope_tables(count):
    half_width = HD // 2
    frequency = jnp.exp(-math.log(rope_base) * 2.0 * jnp.arange(half_width, dtype=f32) / HD)
    angles = jnp.arange(count, dtype=f32)[:, None] * frequency[None, :]
    cosine, sine = jnp.cos(angles), jnp.sin(angles)
    return jnp.concatenate([cosine, cosine], axis=-1), jnp.concatenate([-sine, sine], axis=-1)


def slots_kernel(expert_count, routes_ref, order_ref, slots_ref):
    tok_rows = routes_ref.shape[0]
    pair_count = order_ref.shape[1]
    order = order_ref[...]
    shift = TOPK.bit_length() - 1
    token_of = lax.shift_right_logical(order, jnp.full_like(order, shift))
    route_of = order & (TOPK - 1)
    token_iota = lax.broadcasted_iota(jnp.int32, (tok_rows, pair_count), 0)
    token_hot = jnp.where(token_iota == token_of, 1.0, 0.0).astype(bf16)
    place = lax.broadcasted_iota(jnp.int32, (TOPK, pair_count), 1)
    chosen = lax.broadcasted_iota(jnp.int32, (TOPK, pair_count), 0) == route_of
    high = lax.shift_right_logical(place, jnp.full_like(place, 8)).astype(f32)
    low = (place & 255).astype(f32)
    digits = jnp.concatenate([jnp.where(chosen, high, 0.0), jnp.where(chosen, low, 0.0)], axis=0)
    found = dot_nt(token_hot, digits.astype(bf16))
    rank = found[:, :TOPK] * 256.0 + found[:, TOPK:]
    routes = routes_ref[...]
    lanes = -(-expert_count // 128) * 128
    expert_iota = lax.broadcasted_iota(jnp.int32, (tok_rows, lanes), 1)
    never = 1e9
    by_expert = jnp.full((tok_rows, lanes), never, f32)
    for k in range(TOPK):
        by_expert = jnp.where(expert_iota == routes[:, k : k + 1], rank[:, k : k + 1], by_expert)
    turned = by_expert.T
    for e in range(expert_count):
        mine = turned[e : e + 1, :]
        earlier = jnp.where(by_expert[:, e : e + 1] < mine, 1.0, 0.0)
        count = jnp.sum(earlier, axis=0, keepdims=True)
        slots_ref[e : e + 1, :] = jnp.where(mine < never, count, absent_slot)


def block_slots(routes, order, expert_count):
    tok_rows = routes.shape[0]
    return pl.pallas_call(
        functools.partial(slots_kernel, expert_count),
        out_shape=jax.ShapeDtypeStruct((expert_count, tok_rows), f32),
        compiler_params=pltpu.CompilerParams(vmem_limit_bytes=32 * MIB),
        name="block_slots",
    )(routes, order)


def slot_hot(slots_ref, expert, capacity):
    slot_row = slots_ref[pl.ds(expert, 1), :]
    slot_iota = lax.broadcasted_iota(jnp.int32, (capacity, slot_row.shape[1]), 0).astype(f32)
    return jnp.where(slot_iota == slot_row, 1.0, 0.0).astype(bf16)


def plane_hot(slots_ref, first, shape):
    return jnp.concatenate([slot_hot(slots_ref, first + r, shape[1]) for r in range(shape[0])])


def dispatch_kernel(at_ref, slots_ref, rows_ref, out_ref):
    hot = plane_hot(slots_ref, at_ref[0], out_ref.shape)
    out_ref[...] = dot_nn(hot, rows_ref[...]).astype(bf16).reshape(out_ref.shape)


def dispatch(at, slots, rows, per_plane, capacity):
    blocks, experts, tok_rows = slots.shape
    width = rows.shape[2]
    slot_rows = per_plane * capacity
    return pl.pallas_call(
        dispatch_kernel,
        out_shape=jax.ShapeDtypeStruct((per_plane, blocks, capacity, width), bf16),
        grid_spec=pltpu.PrefetchScalarGridSpec(
            num_scalar_prefetch=1,
            grid=(blocks,),
            in_specs=[
                pl.BlockSpec((None, experts, tok_rows), lambda i, s: (i, 0, 0)),
                pl.BlockSpec((None, tok_rows, width), lambda i, s: (s[1 + i], 0, 0)),
            ],
            out_specs=pl.BlockSpec((per_plane, None, capacity, width), lambda i, s: (0, i, 0, 0)),
        ),
        compiler_params=params(1, 40),
        cost_estimate=estimate(
            flops=2 * blocks * slot_rows * tok_rows * width,
            bytes_accessed=2 * blocks * (slot_rows + tok_rows) * width,
            transcendentals=0,
        ),
        name="dispatch",
    )(at, slots, rows)


def combine_kernel(first_ref, slots_ref, rows_ref, out_ref):
    hot = plane_hot(slots_ref, first_ref[0], rows_ref.shape)
    rows = rows_ref[...].reshape(hot.shape[0], rows_ref.shape[2])
    out_ref[...] = dot_tn(hot, rows).astype(bf16)


def combine(first, slots, rows, block):
    experts, tok_rows = slots.shape
    per_plane, _, capacity, width = rows.shape
    slot_rows = per_plane * capacity
    return pl.pallas_call(
        combine_kernel,
        out_shape=jax.ShapeDtypeStruct((tok_rows, width), bf16),
        grid_spec=pltpu.PrefetchScalarGridSpec(
            num_scalar_prefetch=1,
            grid=(1,),
            in_specs=[
                pl.BlockSpec((experts, tok_rows), lambda i, s: (0, 0)),
                pl.BlockSpec((per_plane, None, capacity, width), lambda i, s: (0, block, 0, 0)),
            ],
            out_specs=pl.BlockSpec((tok_rows, width), lambda i, s: (0, 0)),
        ),
        compiler_params=params(1, 40),
        cost_estimate=estimate(
            flops=2 * slot_rows * tok_rows * width,
            bytes_accessed=2 * (slot_rows + tok_rows) * width,
            transcendentals=0,
        ),
        name="combine",
    )(first, slots, rows)


def qkv_kernel(heads, planes, at_ref, x_ref, gain_ref, *refs):
    w_refs = refs[:planes]
    gq_ref, gk_ref, cos_ref, sin_ref, act_ref, pre_ref, rot_ref, all_ref = refs[planes:]
    depth = w_refs[0].shape[0]

    @pl.when(pl.program_id(0) == 0)
    def _():
        for d in range(planes):
            place = pl.ds(pl.multiple_of(at_ref[d] * depth, depth), depth)
            all_ref[place, :] = w_refs[d][...]

    x = x_ref[...].astype(f32)
    inverse = lax.rsqrt(jnp.mean(x * x, axis=-1, keepdims=True) + norm_eps)
    act = (x * inverse * gain_ref[...]).astype(bf16)
    act_ref[...] = act
    y = None
    for d in range(planes):
        columns = pl.ds(pl.multiple_of(at_ref[d] * depth, depth), depth)
        term = dot_nn(act_ref[:, columns], w_refs[d][...])
        y = term if y is None else y + term
    cosine, sine = cos_ref[...], sin_ref[...]
    for part, gain in enumerate((gq_ref[...], gk_ref[...])):
        for h in range(heads):
            at = (part * heads + h) * HD
            u = y[:, at : at + HD]
            pre_ref[:, at : at + HD] = u
            n = u * lax.rsqrt(jnp.mean(u * u, axis=-1, keepdims=True) + head_eps) * gain
            rot_ref[:, at : at + HD] = (n * cosine + pltpu.roll(n, HD // 2, 1) * sine).astype(bf16)
    at = 2 * heads * HD
    rot_ref[:, at:] = y[:, at:].astype(bf16)


def qkv_project(places, rows, gain, weights, gain_q, gain_k, cosine, sine, heads):
    count, width = rows.shape
    planes = len(weights)
    depth, out_width = weights[0].shape
    pre_width = 2 * heads * HD
    whole = lambda i, s: (0, 0)
    block = lambda i, s: (i, 0)
    return pl.pallas_call(
        functools.partial(qkv_kernel, heads, planes),
        out_shape=(
            jax.ShapeDtypeStruct((count, width), bf16),
            jax.ShapeDtypeStruct((count, pre_width), f32),
            jax.ShapeDtypeStruct((count, out_width), bf16),
            jax.ShapeDtypeStruct((width, out_width), bf16),
        ),
        grid_spec=pltpu.PrefetchScalarGridSpec(
            num_scalar_prefetch=1,
            grid=(count // ROWS,),
            in_specs=[
                pl.BlockSpec((ROWS, width), block),
                pl.BlockSpec((1, width), whole),
            ]
            + [pl.BlockSpec((depth, out_width), whole)] * planes
            + [
                pl.BlockSpec((1, HD), whole),
                pl.BlockSpec((1, HD), whole),
                pl.BlockSpec((ROWS, HD), block),
                pl.BlockSpec((ROWS, HD), block),
            ],
            out_specs=(
                pl.BlockSpec((ROWS, width), block),
                pl.BlockSpec((ROWS, pre_width), block),
                pl.BlockSpec((ROWS, out_width), block),
                pl.BlockSpec((width, out_width), whole),
            ),
        ),
        compiler_params=params(1, 56),
        cost_estimate=estimate(
            flops=2 * count * width * out_width,
            bytes_accessed=4 * count * width + 2 * width * out_width + 6 * count * out_width,
            transcendentals=0,
        ),
        name="qkv_project",
    )(places, rows, gain, *weights, gain_q, gain_k, cosine, sine)


def attn_kernel(
    scale, low_ref, high_ref, q_ref, k_ref, v_ref, sq_ref, sk_ref, o_ref, ol_ref, lse_ref, s_scr
):
    block = pl.program_id(1)
    low, high = low_ref[block], high_ref[block]
    q = q_ref[...]
    seg_q = sq_ref[...]
    half = ROWS // 2

    def scores(kb, top):
        at = pl.ds(pl.multiple_of(kb * ROWS, ROWS), ROWS)
        s = dot_nt(q, k_ref[at, :]) * scale
        s = jnp.where(seg_q == sk_ref[:, at], s, masked_score)
        s_scr[:, at] = s
        return jnp.maximum(top, jnp.maximum(s[:, :half], s[:, half:]))

    top = lax.fori_loop(low, high, scores, jnp.full((ROWS, half), masked_score, f32))
    top = jnp.max(top, axis=-1, keepdims=True)

    def weigh(kb, carry):
        total, acc = carry
        at = pl.ds(pl.multiple_of(kb * ROWS, ROWS), ROWS)
        p = jnp.exp(s_scr[:, at] - top)
        acc = acc + dot_nn(p.astype(bf16), v_ref[at, :])
        return total + (p[:, :half] + p[:, half:]), acc

    total, acc = lax.fori_loop(
        low, high, weigh, (jnp.zeros((ROWS, half), f32), jnp.zeros((ROWS, HD), f32))
    )
    total = jnp.sum(total, axis=-1, keepdims=True)
    out = acc / total
    o_ref[...] = out
    ol_ref[...] = out.astype(bf16)
    lse = jnp.broadcast_to(top + jnp.log(total), (ROWS, HD)).T
    lse_ref[0] = lse[0:1, :]


def attention(rot, seg_col, seg_row, low, high, heads):
    count = rot.shape[0]
    blocks = count // ROWS
    scale = HD ** (-0.5)
    return pl.pallas_call(
        functools.partial(attn_kernel, scale),
        out_shape=(
            jax.ShapeDtypeStruct((count, heads * HD), f32),
            jax.ShapeDtypeStruct((count, heads * HD), bf16),
            jax.ShapeDtypeStruct((heads * blocks, 1, ROWS), f32),
        ),
        grid_spec=pltpu.PrefetchScalarGridSpec(
            num_scalar_prefetch=2,
            grid=(heads, blocks),
            in_specs=[
                pl.BlockSpec((ROWS, HD), lambda h, i, *s: (i, h)),
                pl.BlockSpec((count, HD), lambda h, i, *s: (0, heads + h)),
                pl.BlockSpec((count, HD), lambda h, i, *s: (0, 2 * heads + h)),
                pl.BlockSpec((ROWS, 1), lambda h, i, *s: (i, 0)),
                pl.BlockSpec((1, count), lambda h, i, *s: (0, 0)),
            ],
            out_specs=(
                pl.BlockSpec((ROWS, HD), lambda h, i, *s: (i, h)),
                pl.BlockSpec((ROWS, HD), lambda h, i, *s: (i, h)),
                pl.BlockSpec((1, 1, ROWS), lambda h, i, *s: (h * blocks + i, 0, 0)),
            ),
            scratch_shapes=[pltpu.VMEM((ROWS, count), f32)],
        ),
        compiler_params=params(2, 32),
        cost_estimate=estimate(
            flops=2 * heads * count * count * HD,
            bytes_accessed=12 * heads * count * HD,
            transcendentals=heads * count * count // 2,
        ),
        name="attention",
    )(low, high, rot, rot, rot, seg_col, seg_row)


def head_back(grad, pre, gain, cosine, sine):
    n = grad * cosine - pltpu.roll(grad, HD // 2, 1) * sine
    inverse = lax.rsqrt(jnp.mean(pre * pre, axis=-1, keepdims=True) + head_eps)
    w = n * gain
    back = inverse * w - pre * inverse**3 * jnp.mean(w * pre, axis=-1, keepdims=True)
    return back, jnp.sum(n * pre * inverse, axis=0, keepdims=True)


def attn_back_kernel(
    scale,
    low_ref,
    high_ref,
    q_ref,
    k_ref,
    v_ref,
    do_ref,
    o_ref,
    lse_ref,
    sq_ref,
    sk_ref,
    qpre_ref,
    kpre_ref,
    gq_ref,
    gk_ref,
    cosq_ref,
    sinq_ref,
    cosk_ref,
    sink_ref,
    grad_ref,
    gain_ref,
    dk_scr,
    dv_scr,
):
    head, block = pl.program_id(0), pl.program_id(1)
    heads = pl.num_programs(0)

    def columns(part):
        return pl.ds(pl.multiple_of((part * heads + head) * HD, HD), HD)

    low, high = low_ref[block], high_ref[block]

    @pl.when(block == 0)
    def _():
        dk_scr[...] = jnp.zeros_like(dk_scr)
        dv_scr[...] = jnp.zeros_like(dv_scr)

    @pl.when((block == 0) & (head == 0))
    def _():
        gain_ref[...] = jnp.zeros_like(gain_ref)

    q, do = q_ref[...], do_ref[...]
    row_dot = jnp.sum((do.astype(f32) * o_ref[...]).T, axis=0, keepdims=True)
    lse = lse_ref[0]
    seg_q = sq_ref[...]

    def tile(kb, dq):
        at = pl.ds(pl.multiple_of(kb * ROWS, ROWS), ROWS)
        k, v = k_ref[at, :], v_ref[at, :]
        s = dot_nt(k, q) * scale
        p = jnp.where(sk_ref[at, :] == seg_q, jnp.exp(s - lse), 0.0)
        dp = dot_nt(v, do)
        ds = (p * (dp - row_dot)).astype(bf16)
        dv_scr[at, :] += dot_nn(p.astype(bf16), do)
        dk_scr[at, :] += dot_nn(ds, q)
        return dq + dot_tn(ds, k)

    dq = lax.fori_loop(low, high, tile, jnp.zeros((ROWS, HD), f32))
    back, gain_q = head_back(dq * scale, qpre_ref[...], gq_ref[...], cosq_ref[...], sinq_ref[...])
    grad_ref[pl.ds(pl.multiple_of(block * ROWS, ROWS), ROWS), columns(0)] = back.astype(bf16)
    gain_ref[0:1, :] += gain_q

    @pl.when(block == pl.num_programs(1) - 1)
    def _():
        @pl.loop(0, dk_scr.shape[0] // ROWS)
        def _(i):
            at = pl.ds(pl.multiple_of(i * ROWS, ROWS), ROWS)
            back, gain_k = head_back(
                dk_scr[at, :] * scale, kpre_ref[at, :], gk_ref[...], cosk_ref[at, :], sink_ref[at, :]
            )
            grad_ref[at, columns(1)] = back.astype(bf16)
            grad_ref[at, columns(2)] = dv_scr[at, :].astype(bf16)
            gain_ref[1:2, :] += gain_k


def attention_back(
    rot, grad, out, lse, seg_col, seg_row, low, high, pre, gain_q, gain_k, cosine, sine, heads
):
    count = rot.shape[0]
    blocks = count // ROWS
    scale = HD ** (-0.5)
    mine = lambda h, i, *s: (i, h)
    whole = lambda h, i, *s: (0, 0)
    return pl.pallas_call(
        functools.partial(attn_back_kernel, scale),
        out_shape=(
            jax.ShapeDtypeStruct((count, 3 * heads * HD), bf16),
            jax.ShapeDtypeStruct((8, HD), f32),
        ),
        grid_spec=pltpu.PrefetchScalarGridSpec(
            num_scalar_prefetch=2,
            grid=(heads, blocks),
            in_specs=[
                pl.BlockSpec((ROWS, HD), mine),
                pl.BlockSpec((count, HD), lambda h, i, *s: (0, heads + h)),
                pl.BlockSpec((count, HD), lambda h, i, *s: (0, 2 * heads + h)),
                pl.BlockSpec((ROWS, HD), mine),
                pl.BlockSpec((ROWS, HD), mine),
                pl.BlockSpec((1, 1, ROWS), lambda h, i, *s: (h * blocks + i, 0, 0)),
                pl.BlockSpec((1, ROWS), lambda h, i, *s: (0, i)),
                pl.BlockSpec((count, 1), whole),
                pl.BlockSpec((ROWS, HD), mine),
                pl.BlockSpec((count, HD), lambda h, i, *s: (0, heads + h)),
                pl.BlockSpec((1, HD), whole),
                pl.BlockSpec((1, HD), whole),
                pl.BlockSpec((ROWS, HD), lambda h, i, *s: (i, 0)),
                pl.BlockSpec((ROWS, HD), lambda h, i, *s: (i, 0)),
                pl.BlockSpec((count, HD), whole),
                pl.BlockSpec((count, HD), whole),
            ],
            out_specs=(
                pl.BlockSpec((count, 3 * heads * HD), whole),
                pl.BlockSpec((8, HD), whole),
            ),
            scratch_shapes=[pltpu.VMEM((count, HD), f32), pltpu.VMEM((count, HD), f32)],
        ),
        compiler_params=params(2, 48),
        cost_estimate=estimate(
            flops=5 * heads * count * count * HD,
            bytes_accessed=30 * heads * count * HD,
            transcendentals=heads * count * count // 2,
        ),
        name="attention_back",
    )(
        low,
        high,
        rot,
        rot,
        rot,
        grad,
        out,
        lse,
        seg_row,
        seg_col,
        pre,
        pre,
        gain_q,
        gain_k,
        cosine,
        sine,
        cosine,
        sine,
    )


def expert_kernel(count, carried, mine_ref, x_ref, near_ref, far_ref, *refs):
    wg_ref, wu_ref, wd_ref = refs[:3]
    refs = refs[3 + carried :]
    back_ref, out_ref, xs_ref, c_ref, hid_ref, gp_ref, up_ref = refs[:7]
    out_acc, back_acc, gate_scr, dot_scr = refs[7:]
    step = pl.program_id(1)
    per_plane, capacity, width = c_ref.shape
    rows = per_plane * capacity
    extra = x_ref.shape[2] - width
    lane = lax.broadcasted_iota(jnp.int32, (rows, extra), 1)
    high, low = lane == mine_ref[0], lane == mine_ref[0] + count

    @pl.when(step == 0)
    def _():
        xs_ref[...] = x_ref[:, :, :width]

        @pl.when(pl.program_id(0) == 0)
        def _():
            c_ref[...] = near_ref[...]

        @pl.when(pl.program_id(0) > 0)
        def _():
            c_ref[...] = far_ref[...]
        gates = x_ref[:, :, width:].reshape(rows, extra).astype(f32)
        gate_scr[...] = jnp.sum(jnp.where(high | low, gates, 0.0), axis=-1, keepdims=True)
        out_acc[...] = jnp.zeros_like(out_acc)
        back_acc[...] = jnp.zeros_like(back_acc)
        dot_scr[...] = jnp.zeros_like(dot_scr)

    x = x_ref[:, :, :width].reshape(rows, width)
    c = c_ref[...].reshape(rows, width)
    gate = gate_scr[...]
    wg, wu, wd = wg_ref[...], wu_ref[...], wd_ref[...]
    gate_pre, up_pre = dot_nn(x, wg), dot_nn(x, wu)
    sig = jax.nn.sigmoid(gate_pre)
    hidden = (gate_pre * sig * up_pre).astype(bf16)
    out_acc[...] += dot_nn(hidden, wd)
    plain = dot_nt(c, wd)
    wide = hidden.astype(f32)
    dot_scr[...] += jnp.sum(wide * plain, axis=-1, keepdims=True)
    hid_ref[...] = (wide * gate).astype(bf16).reshape(hid_ref.shape)
    hidden_grad = plain * gate
    gate_grad = (hidden_grad * up_pre * sig * (1.0 + gate_pre * (1.0 - sig))).astype(bf16)
    up_grad = (hidden_grad * gate_pre * sig).astype(bf16)
    gp_ref[...] = gate_grad.reshape(gp_ref.shape)
    up_ref[...] = up_grad.reshape(up_ref.shape)
    back_acc[...] += dot_nt(gate_grad, wg) + dot_nt(up_grad, wu)

    @pl.when(step == pl.num_programs(1) - 1)
    def _():
        dots = dot_scr[...]
        coarse = dots.astype(bf16).astype(f32)
        lanes = jnp.where(high, coarse, jnp.where(low, dots - coarse, 0.0)).astype(bf16)
        back_ref[:, :, :width] = back_acc[...].astype(bf16).reshape(c_ref.shape)
        back_ref[:, :, width:] = lanes.reshape(per_plane, capacity, extra)
        out_ref[...] = (out_acc[...] * gate).astype(bf16).reshape(out_ref.shape)


def experts(mine, x, near, far, wg, wu, wd, base, planes, count, kept):
    per_plane, blocks, capacity, wide = x.shape
    width = near.shape[3]
    halves, _, hidden = wg.shape
    rows = per_plane * capacity
    saved = jax.ShapeDtypeStruct((per_plane, planes, capacity, width), bf16)
    thin = jax.ShapeDtypeStruct((per_plane, planes, capacity, halves * hidden), bf16)
    moved = pl.BlockSpec((per_plane, None, capacity, wide), lambda i, f, s: (0, i, 0, 0))
    saved_spec = pl.BlockSpec((per_plane, None, capacity, width), lambda i, f, s: (0, base + i, 0, 0))
    thin_spec = pl.BlockSpec((per_plane, None, capacity, hidden), lambda i, f, s: (0, base + i, 0, f))
    carried = 0 if kept is None else len(kept)
    skip = base - 1 if base else 0
    cot_specs = [
        pl.BlockSpec((per_plane, None, capacity, width), lambda i, f, s: (0, 0, 0, 0)),
        pl.BlockSpec(
            (per_plane, None, capacity, width),
            lambda i, f, s: (0, jnp.maximum(skip + i - 1, 0), 0, 0),
        ),
    ]
    result = pl.pallas_call(
        functools.partial(expert_kernel, count, carried),
        out_shape=(
            jax.ShapeDtypeStruct(x.shape, bf16),
            jax.ShapeDtypeStruct((per_plane, blocks, capacity, width), bf16),
            saved,
            saved,
            thin,
            thin,
            thin,
        ),
        grid_spec=pltpu.PrefetchScalarGridSpec(
            num_scalar_prefetch=1,
            grid=(blocks, halves),
            in_specs=[
                moved,
                *cot_specs,
                pl.BlockSpec((None, width, hidden), lambda i, f, s: (f, 0, 0)),
                pl.BlockSpec((None, width, hidden), lambda i, f, s: (f, 0, 0)),
                pl.BlockSpec((None, hidden, width), lambda i, f, s: (f, 0, 0)),
            ]
            + [pl.BlockSpec(memory_space=pl.ANY)] * carried,
            out_specs=(
                moved,
                pl.BlockSpec((per_plane, None, capacity, width), lambda i, f, s: (0, i, 0, 0)),
                saved_spec,
                saved_spec,
                thin_spec,
                thin_spec,
                thin_spec,
            ),
            scratch_shapes=[
                pltpu.VMEM((rows, width), f32),
                pltpu.VMEM((rows, width), f32),
                pltpu.VMEM((rows, 1), f32),
                pltpu.VMEM((rows, 1), f32),
            ],
        ),
        input_output_aliases={7 + i: 2 + i for i in range(carried)},
        compiler_params=params(2, 60),
        cost_estimate=estimate(
            flops=12 * blocks * rows * width * hidden * halves,
            bytes_accessed=10 * blocks * rows * width + 6 * blocks * width * hidden * halves,
            transcendentals=blocks * rows * hidden * halves,
        ),
        name="experts",
    )(mine, x, near, far, wg, wu, wd, *(kept or ()))
    return result[0], result[1], result[2:]


def gram_kernel(plus, left_ref, right_ref, *refs):
    total = dot_tn(left_ref[...], right_ref[...])
    if plus:
        total = total + refs[0][...]
    refs[-1][...] = total.astype(refs[-1].dtype)


def gram(left, right, left_cols, right_cols, dtype, plus=None):
    rows = left.shape[0]
    left_at, left_count = left_cols
    right_at, right_count = right_cols
    tall = min(left_count, 256)
    wide = min(right_count, 1024)
    out_spec = pl.BlockSpec((tall, wide), lambda j, i: (i, j))
    return pl.pallas_call(
        functools.partial(gram_kernel, plus is not None),
        out_shape=jax.ShapeDtypeStruct((left_count, right_count), dtype),
        grid=(right_count // wide, left_count // tall),
        in_specs=[
            pl.BlockSpec((rows, tall), lambda j, i: (0, left_at // tall + i)),
            pl.BlockSpec((rows, wide), lambda j, i: (0, right_at // wide + j)),
        ]
        + [out_spec] * (plus is not None),
        out_specs=out_spec,
        compiler_params=params(2, 48),
        cost_estimate=estimate(
            flops=2 * rows * left_count * right_count,
            bytes_accessed=2 * rows * (left_count + right_count) + 4 * left_count * right_count,
            transcendentals=0,
        ),
        name="gram",
    )(left, right, *(() if plus is None else (plus,)))


def project_kernel(plus, core_ref, rows_ref, weights_ref, *refs):
    total = dot_nt(rows_ref[...], weights_ref[...])
    if plus:
        total = total + refs[0][...].astype(f32)
    refs[-1][...] = total.astype(bf16)


def project_back(core, rows, weights, tok_rows, plus=None):
    count, depth = rows.shape
    width = weights.shape[0]
    chips = count // tok_rows // 2
    out_spec = pl.BlockSpec((tok_rows, width), lambda i, s: (i, 0))
    return pl.pallas_call(
        functools.partial(project_kernel, plus is not None),
        out_shape=jax.ShapeDtypeStruct((chips * tok_rows, width), bf16),
        grid_spec=pltpu.PrefetchScalarGridSpec(
            num_scalar_prefetch=1,
            grid=(chips,),
            in_specs=[
                pl.BlockSpec((tok_rows, depth), lambda i, s: (2 * i + s[0], 0)),
                pl.BlockSpec((width, depth), lambda i, s: (0, 0)),
            ]
            + [out_spec] * (plus is not None),
            out_specs=out_spec,
        ),
        compiler_params=params(1, 40),
        cost_estimate=estimate(
            flops=count * depth * width,
            bytes_accessed=2 * width * depth + count * depth + count * width,
            transcendentals=0,
        ),
        name="project_back",
    )(core, rows, weights, *(() if plus is None else (plus,)))


def after(value, *others):
    return lax.optimization_barrier((value,) + others)[0]


def body(
    hidden_in,
    out_cotangent,
    segment_number,
    expert_routes,
    pair_order,
    norm_gain,
    query_weight,
    key_weight,
    value_weight,
    output_weight,
    query_gain,
    key_gain,
    ffn_norm_gain,
    router_weight,
    expert_gate,
    expert_up,
    expert_down,
):
    tok_rows, width = hidden_in.shape
    devices = lax.axis_size(AXIS)
    members = max(1, SEQ_MIN // tok_rows)
    planes = devices // members
    per_plane = members // 2
    expert_count = devices // 2
    capacity = tok_rows * TOPK // expert_count
    heads = width // HD // members
    head_width = heads * HD
    own_rows = norm_gain.shape[0]
    seq = members * tok_rows
    me = lax.axis_index(AXIS)
    plane, member = me // members, me % members
    mine = (me // 2).astype(jnp.int32).reshape(1)
    first = (plane * per_plane).astype(jnp.int32)
    places = (plane ^ jnp.arange(planes, dtype=jnp.int32)).astype(jnp.int32)
    counted = jnp.concatenate([first[None], jnp.arange(planes, dtype=jnp.int32)])
    halfway = -(-planes // 2)
    chunks = [part for part in (range(halfway, planes), range(halfway)) if len(part)]

    def placed(part):
        return jnp.concatenate([first[None], places[part.start : part.stop]])

    plane_groups = [[g * members + j for j in range(members)] for g in range(planes)]
    stack_groups = [[g * members + j for g in range(planes)] for j in range(members)]
    core_groups = [
        [g * members + 2 * c + h for c in range(per_plane)] for g in range(planes) for h in (0, 1)
    ]

    def exchange(value, groups=None):
        return lax.all_to_all(
            value, AXIS, split_axis=0, concat_axis=0, tiled=True, axis_index_groups=groups
        )

    def gather(value, groups=None):
        return lax.all_gather(value, AXIS, axis=0, tiled=True, axis_index_groups=groups)

    def flip(value, bits):
        if bits == 0:
            return value
        return lax.ppermute(value, AXIS, [(i, i ^ bits) for i in range(devices)])

    def to_core(value):
        return flip(value, 1)

    def to_plane(value, d):
        return flip(value, members * d)

    def spread(value):
        found = {0: value}
        for d in range(1, planes):
            lowest = d & -d
            found[d] = to_plane(found[d ^ lowest], lowest)
        return [found[d] for d in range(planes)]

    def fold(sums, *others):
        bit = 1
        while bit < len(sums):
            for d in range(len(sums)):
                if d & bit and not d & (bit - 1):
                    came = to_plane(sums[d].astype(bf16), bit)
                    if d == bit:
                        came = after(came, *others)
                    sums[d ^ bit] = sums[d ^ bit].astype(f32) + came.astype(f32)
            bit *= 2
        return sums[0]

    wire, core_op = [], []

    def on_wire(value, groups):
        came = exchange(after(value, *wire[-1:]), groups)
        wire.append(came)
        return came

    def to_chips(value):
        return on_wire(value, core_groups)

    def in_turn(value):
        return after(value, *core_op[-1:])

    def ran(value):
        core_op.append(value)
        return value

    columns = jnp.concatenate(
        [w.reshape(own_rows, members, head_width) for w in (query_weight, key_weight, value_weight)],
        axis=2,
    )
    slots = block_slots(expert_routes, pair_order, expert_count)
    columns = on_wire(
        after(columns, slots).transpose(1, 0, 2).reshape(members * own_rows, 3 * head_width), plane_groups
    )
    stacked = [to_plane(after(output_weight, slots), d) for d in range(planes)]
    weights = spread(after(columns, *stacked))
    slots = [to_plane(after(slots, *weights) if d else slots, d) for d in range(planes)]
    output_rows = jnp.zeros((planes * own_rows, width), bf16)
    for d, rows in enumerate(stacked):
        output_rows = lax.dynamic_update_slice_in_dim(output_rows, rows, places[d] * own_rows, 0)
    rows_all = gather(hidden_in, plane_groups)

    pieces = (
        router_weight.reshape(-1),
        norm_gain,
        ffn_norm_gain,
        query_gain,
        key_gain,
        segment_number.astype(bf16),
    )
    packed = jnp.concatenate(pieces)
    length = packed.shape[0]
    padded = -(-length // 128) * 128
    packed = jnp.pad(packed, (0, padded - length))
    packed = on_wire(jnp.broadcast_to(packed[None], (devices, padded)), None)
    small = []
    at = 0
    for piece in pieces:
        small.append(packed[:, at : at + piece.shape[0]])
        at += piece.shape[0]
    router_full = small[0].reshape(width, expert_count)
    gain_one = small[1].reshape(1, width).astype(f32)
    gain_two = small[2].reshape(1, width).astype(f32)
    gain_q = small[3].reshape(1, HD).astype(f32)
    gain_k = small[4].reshape(1, HD).astype(f32)
    segments = lax.dynamic_slice_in_dim(small[5], plane * members, members, 0).astype(f32)
    seg_row, seg_col = segments.reshape(1, seq), segments.reshape(seq, 1)
    seg_blocks = segments.reshape(seq // ROWS, ROWS)
    seg_first, seg_last = seg_blocks[:, 0], seg_blocks[:, -1]
    low = jnp.sum((seg_last[None, :] < seg_first[:, None]).astype(jnp.int32), axis=1)
    high = jnp.sum((seg_first[None, :] <= seg_last[:, None]).astype(jnp.int32), axis=1)

    cot_own = dispatch(counted, slots[0][None], out_cotangent[None], per_plane, capacity)
    cot_first = [to_chips(cot_own)]
    output_full = gather(after(output_rows, columns), plane_groups)
    slot_list, slots = slots, jnp.stack(slots)
    cot_rows = {0: out_cotangent}
    top = planes // 2
    early, late = [], []
    if planes > 1:
        cot_rows[top] = to_plane(after(out_cotangent, *weights), top)
        early.append(cot_rows[top])
    for d in range(1, planes):
        if d != top:
            lowest = d & -d
            start = after(out_cotangent, *early) if d == lowest else cot_rows[d ^ lowest]
            cot_rows[d] = to_plane(start, lowest)
            late.append(cot_rows[d])

    halves = lambda w: jnp.concatenate([w, to_core(w)], axis=0)
    wg, wu, wd = halves(expert_gate), halves(expert_up), halves(expert_down)

    cosine, sine = rope_tables(seq)
    act_one, pre, rot, ordered = qkv_project(
        places, rows_all, gain_one, weights, gain_q, gain_k, cosine, sine, heads
    )
    out_wide, out_heads, lse = attention(rot, seg_col, seg_row, low, high, heads)
    out_low = on_wire(after(out_heads, *slot_list, *early), plane_groups)
    if planes > 1:
        rows = after(cot_rows[top], out_heads)
        sent = dispatch(counted, slots[top : top + 1], rows[None], per_plane, capacity)
        cot_first.append(to_chips(sent))
    out_low = out_low.reshape(members, tok_rows, head_width).transpose(1, 0, 2)
    out_low = out_low.reshape(tok_rows, planes, members, own_rows).transpose(0, 2, 1, 3)
    out_low = out_low.reshape(tok_rows, width)
    tokens = hidden_in.astype(f32)
    cotangent = out_cotangent.astype(f32)
    middle = tokens + dot_nn(out_low, output_full)
    inverse_two = lax.rsqrt(jnp.mean(middle * middle, axis=-1, keepdims=True) + norm_eps)
    act_two = (middle * inverse_two * gain_two).astype(bf16)

    logits = dot_nn(act_two, router_full)
    expert_ids = jnp.arange(expert_count, dtype=jnp.int32)
    routed = jnp.any(expert_routes[:, :, None] == expert_ids[None, None, :], axis=1)
    logits = jnp.where(routed, logits, masked_score)
    gates = jnp.where(routed, jnp.exp(logits - jnp.max(logits, axis=1, keepdims=True)), 0.0)
    gates = gates / jnp.sum(gates, axis=1, keepdims=True)
    coarse = lax.reduce_precision(gates, 8, 7)
    extra = -(-2 * expert_count // 128) * 128
    act_wide = jnp.concatenate(
        [
            act_two,
            coarse.astype(bf16),
            (gates - coarse).astype(bf16),
            jnp.zeros((tok_rows, extra - 2 * expert_count), bf16),
        ],
        axis=1,
    )

    act_wide = after(act_wide, *late, *cot_first)
    act_all = gather(act_wide, stack_groups).reshape(planes, tok_rows, -1)
    others = [d for d in range(1, planes) if d != top]
    cot_far = cot_first[0]
    if others:
        far = jnp.stack([after(cot_rows[d], act_wide) for d in others])
        far_slots = jnp.stack([slots[d] for d in others])
        cot_far = to_chips(
            ran(dispatch(counted[: len(others) + 1], far_slots, far, per_plane, capacity))
        )

    act = []
    for part in chunks:
        own_slots = slots[part.start : part.stop]
        rows = after(in_turn(act_all), wg, wu, wd)
        sent = dispatch(placed(part), own_slots, rows, per_plane, capacity)
        act.append(to_chips(ran(sent)))
    kept, back, outs = None, [], []
    for part, rows in zip(chunks, act):
        sent, out, kept = experts(
            mine,
            in_turn(rows),
            cot_first[0 if part.start == 0 else 1],
            cot_far,
            wg,
            wu,
            wd,
            part.start,
            planes,
            expert_count,
            kept,
        )
        back.append(to_chips(ran(sent)))
        outs.append(out)
    x_all, c_all, hid_all, gp_all, up_all = kept

    hidden = expert_gate.shape[2]
    flat = lambda value: value.reshape(-1, value.shape[3])
    sides = (
        (flat(x_all), flat(gp_all), 1),
        (flat(x_all), flat(up_all), 1),
        (flat(hid_all), flat(c_all), 0),
    )

    def half(side, which, plus=None):
        left, right, split = side
        cut, whole = (which * hidden, hidden), (0, width)
        cols = (whole, cut) if split else (cut, whole)
        return ran(gram(in_turn(left), right, *cols, f32, plus))

    passed = []

    def home(part, rows):
        sums = {}
        for d in sorted(part, key=lambda d: (-(d & 1), d)):
            sums[d] = ran(combine(first[None], slots[d], in_turn(rows), d - part.start))
        bit = 1
        while bit < len(part):
            for d in part:
                if d & bit and not d & (bit - 1):
                    came = to_plane(sums[d].astype(bf16), bit)
                    passed.append(came)
                    sums[d ^ bit] = sums[d ^ bit].astype(f32) + came.astype(f32)
            bit *= 2
        return sums[part.start]

    back_sum = home(chunks[0], back[0])
    theirs = [half(side, 1) for side in sides[:2]]
    if len(chunks) > 1:
        back_sum = ran(in_turn(back_sum.astype(bf16)))
        back_sum = to_plane(back_sum, top)
    theirs.append(half(sides[2], 1))
    if len(chunks) > 1:
        back_sum = back_sum.astype(f32) + home(chunks[1], back[1])
    outs[0] = to_chips(outs[0])

    expert_in_grad = back_sum[:, :width]
    gate_grad = (
        back_sum[:, width : width + expert_count]
        + back_sum[:, width + expert_count : width + 2 * expert_count]
    )
    select_grad = gates * (gate_grad - jnp.sum(gates * gate_grad, axis=1, keepdims=True))
    logit_grad = select_grad.astype(bf16)
    grad_router = dot_tn(act_two, logit_grad)
    act_two_grad = expert_in_grad + dot_nt(logit_grad, router_full)
    weighted = act_two_grad * gain_two
    grad_gain_two = jnp.sum(act_two_grad * middle * inverse_two, axis=0)
    middle_grad = (
        cotangent
        + inverse_two * weighted
        - middle * inverse_two**3 * jnp.mean(weighted * middle, axis=-1, keepdims=True)
    )
    middle_low = middle_grad.astype(bf16)

    out_grad = dot_nt(middle_low, output_full).astype(bf16)
    out_grad = out_grad.reshape(tok_rows, members, planes, own_rows).transpose(0, 2, 1, 3)
    out_grad = out_grad.reshape(tok_rows, members, head_width).transpose(1, 0, 2)
    out_grad = out_grad.reshape(seq, head_width)
    ran(out_grad)
    theirs = [to_core(after(grad, out_grad)) for grad in theirs]
    out_grad = on_wire(out_grad, plane_groups)
    mixture = home(chunks[0], outs[0]).astype(bf16)
    dqkv, grad_gains = attention_back(
        rot,
        in_turn(out_grad),
        out_wide,
        lse,
        seg_col,
        seg_row,
        low,
        high,
        pre,
        gain_q,
        gain_k,
        cosine,
        sine,
        heads,
    )
    ran(dqkv)
    if len(chunks) > 1:
        near_sum = home(chunks[1], to_chips(outs[1]))
        done = (*core_op[-2:], mixture, *theirs)
        dqkv, grad_gains = after(dqkv, *done), after(grad_gains, *done)
    middle_all = gather(after(middle_low, dqkv), plane_groups)

    sums = (
        grad_router.reshape(devices, -1),
        grad_gain_two.reshape(devices, -1),
        grad_gains[0].reshape(devices, -1),
        grad_gains[1].reshape(devices, -1),
    )
    packed = jnp.concatenate(sums, axis=1)
    length = packed.shape[1]
    padded = -(-length // 128) * 128
    packed = jnp.pad(packed, ((0, 0), (0, padded - length)))

    core = (me % 2).astype(jnp.int32).reshape(1)
    given = project_back(1 - core, dqkv, ordered, tok_rows)
    part = gram(after(act_one, given), dqkv, (0, width), (0, 3 * head_width), bf16)
    part = part.reshape(planes, members * own_rows, 3 * head_width)
    shares = [lax.dynamic_index_in_dim(part, places[d], 0, False) for d in range(planes)]
    mixture = to_plane(mixture, top) if len(chunks) > 1 else mixture
    given = after(to_core(given), *shares, mixture, *passed[-1:])
    act_one_grad = project_back(core, dqkv, ordered, tok_rows, given)
    ran(act_one_grad)
    output_part = ran(gram(out_heads, in_turn(middle_all), (0, head_width), (0, width), bf16))
    grad_gate, grad_up, grad_down = (
        half(side, 0, other) for side, other in zip(sides, theirs)
    )
    shares = [after(share, act_one_grad) for share in shares]
    taken = fold(shares, grad_gate, grad_up, grad_down).astype(bf16)
    act_one_grad = on_wire(act_one_grad, core_groups)

    output_part = lax.psum_scatter(
        output_part, AXIS, scatter_dimension=0, tiled=True, axis_index_groups=stack_groups
    )
    to_owner = [
        (g * members + j, j * planes + g) for g in range(planes) for j in range(members)
    ]
    grad_output = lax.ppermute(output_part, AXIS, to_owner)
    mixture = mixture.astype(f32)
    if len(chunks) > 1:
        mixture = mixture + near_sum
    packed, act_one_grad, mixture, grad_gate, grad_up, grad_down = lax.optimization_barrier(
        (packed, act_one_grad, mixture, grad_gate, grad_up, grad_down)
    )
    layer_out = (middle + mixture).astype(bf16)
    packed = exchange(packed)
    taken, packed, grad_output = lax.optimization_barrier((taken, packed, grad_output))
    part = exchange(taken, plane_groups).reshape(members, own_rows, 3, head_width)
    part = part.transpose(2, 1, 0, 3).reshape(3, own_rows, width).astype(f32)
    grad_query, grad_key, grad_value = part[0], part[1], part[2]
    act_one_grad = act_one_grad.reshape(per_plane, tok_rows, width)
    act_one_grad = jnp.sum(act_one_grad.astype(f32), axis=0)

    inverse_one = lax.rsqrt(jnp.mean(tokens * tokens, axis=-1, keepdims=True) + norm_eps)
    weighted = act_one_grad * gain_one
    grad_hidden = (
        middle_grad
        + inverse_one * weighted
        - tokens * inverse_one**3 * jnp.mean(weighted * tokens, axis=-1, keepdims=True)
    )
    grad_gain_one = (
        jnp.sum(
            grad_query * query_weight.astype(f32)
            + grad_key * key_weight.astype(f32)
            + grad_value * value_weight.astype(f32),
            axis=1,
        )
        / norm_gain.astype(f32)
    )

    summed = jnp.sum(packed, axis=0)
    at, tiny = 0, []
    for piece in sums:
        tiny.append(summed[at : at + piece.shape[1]])
        at += piece.shape[1]

    return (
        layer_out,
        grad_hidden,
        grad_gain_one,
        grad_query,
        grad_key,
        grad_value,
        grad_output.astype(f32),
        tiny[2],
        tiny[3],
        tiny[1],
        tiny[0].reshape(own_rows, expert_count),
        grad_gate[None],
        grad_up[None],
        grad_down[None],
    )


def solution(mesh):
    row, mat, cube = P(AXIS), P(AXIS, None), P(AXIS, None, None)
    return jax.shard_map(
        body,
        mesh=mesh,
        in_specs=(mat, mat, row, mat, mat, row, mat, mat, mat, mat, row, row, row, mat)
        + (cube,) * 3,
        out_specs=(mat, mat, row, mat, mat, mat, mat, row, row, row, mat) + (cube,) * 3,
        check_vma=False,
    )
```

```python
import functools
import math

import jax
import jax.numpy as jnp
from jax import lax
from jax.experimental import pallas as pl
from jax.experimental.pallas import tpu as pltpu
from jax.sharding import PartitionSpec as P

HD = 128
TOPK = 8
SEQ_MIN = 2048
ROWS = 256
SHARE = 32

norm_eps = 1e-05
head_eps = 1e-06
rope_base = 10000.0
masked_score = -1e30
absent_slot = 4096.0

AXIS = "fsdp"
f32 = jnp.float32
bf16 = jnp.bfloat16
MIB = 1 << 20


def dot_nt(left, right):
    return lax.dot_general(left, right, (((1,), (1,)), ((), ())), preferred_element_type=f32)


def dot_tn(left, right):
    return lax.dot_general(left, right, (((0,), (0,)), ((), ())), preferred_element_type=f32)


def dot_nn(left, right):
    return lax.dot_general(left, right, (((1,), (0,)), ((), ())), preferred_element_type=f32)


def params(steps, mib):
    return pltpu.CompilerParams(
        dimension_semantics=("arbitrary",) * steps, vmem_limit_bytes=mib * MIB
    )


def estimate(flops, bytes_accessed, transcendentals):
    return pl.CostEstimate(
        flops=flops // SHARE, bytes_accessed=bytes_accessed // SHARE, transcendentals=transcendentals // SHARE
    )


def rope_tables(count):
    half_width = HD // 2
    frequency = jnp.exp(-math.log(rope_base) * 2.0 * jnp.arange(half_width, dtype=f32) / HD)
    angles = jnp.arange(count, dtype=f32)[:, None] * frequency[None, :]
    cosine, sine = jnp.cos(angles), jnp.sin(angles)
    return jnp.concatenate([cosine, cosine], axis=-1), jnp.concatenate([-sine, sine], axis=-1)


def slots_kernel(expert_count, routes_ref, order_ref, slots_ref):
    tok_rows = routes_ref.shape[0]
    pair_count = order_ref.shape[1]
    order = order_ref[...]
    shift = TOPK.bit_length() - 1
    token_of = lax.shift_right_logical(order, jnp.full_like(order, shift))
    route_of = order & (TOPK - 1)
    token_iota = lax.broadcasted_iota(jnp.int32, (tok_rows, pair_count), 0)
    token_hot = jnp.where(token_iota == token_of, 1.0, 0.0).astype(bf16)
    place = lax.broadcasted_iota(jnp.int32, (TOPK, pair_count), 1)
    chosen = lax.broadcasted_iota(jnp.int32, (TOPK, pair_count), 0) == route_of
    high = lax.shift_right_logical(place, jnp.full_like(place, 8)).astype(f32)
    low = (place & 255).astype(f32)
    digits = jnp.concatenate([jnp.where(chosen, high, 0.0), jnp.where(chosen, low, 0.0)], axis=0)
    found = dot_nt(token_hot, digits.astype(bf16))
    rank = found[:, :TOPK] * 256.0 + found[:, TOPK:]
    routes = routes_ref[...]
    lanes = -(-expert_count // 128) * 128
    expert_iota = lax.broadcasted_iota(jnp.int32, (tok_rows, lanes), 1)
    never = 1e9
    by_expert = jnp.full((tok_rows, lanes), never, f32)
    for k in range(TOPK):
        by_expert = jnp.where(expert_iota == routes[:, k : k + 1], rank[:, k : k + 1], by_expert)
    turned = by_expert.T
    for e in range(expert_count):
        mine = turned[e : e + 1, :]
        earlier = jnp.where(by_expert[:, e : e + 1] < mine, 1.0, 0.0)
        count = jnp.sum(earlier, axis=0, keepdims=True)
        slots_ref[e : e + 1, :] = jnp.where(mine < never, count, absent_slot)


def block_slots(routes, order, expert_count):
    tok_rows = routes.shape[0]
    return pl.pallas_call(
        functools.partial(slots_kernel, expert_count),
        out_shape=jax.ShapeDtypeStruct((expert_count, tok_rows), f32),
        compiler_params=pltpu.CompilerParams(vmem_limit_bytes=32 * MIB),
        name="block_slots",
    )(routes, order)


def slot_hot(slots_ref, expert, capacity):
    slot_row = slots_ref[pl.ds(expert, 1), :]
    slot_iota = lax.broadcasted_iota(jnp.int32, (capacity, slot_row.shape[1]), 0).astype(f32)
    return jnp.where(slot_iota == slot_row, 1.0, 0.0).astype(bf16)


def plane_hot(slots_ref, first, shape):
    return jnp.concatenate([slot_hot(slots_ref, first + r, shape[1]) for r in range(shape[0])])


def dispatch_kernel(at_ref, slots_ref, rows_ref, out_ref):
    hot = plane_hot(slots_ref, at_ref[0], out_ref.shape)
    out_ref[...] = dot_nn(hot, rows_ref[...]).astype(bf16).reshape(out_ref.shape)


def dispatch(at, slots, rows, per_plane, capacity):
    blocks, experts, tok_rows = slots.shape
    width = rows.shape[2]
    slot_rows = per_plane * capacity
    return pl.pallas_call(
        dispatch_kernel,
        out_shape=jax.ShapeDtypeStruct((per_plane, blocks, capacity, width), bf16),
        grid_spec=pltpu.PrefetchScalarGridSpec(
            num_scalar_prefetch=1,
            grid=(blocks,),
            in_specs=[
                pl.BlockSpec((None, experts, tok_rows), lambda i, s: (i, 0, 0)),
                pl.BlockSpec((None, tok_rows, width), lambda i, s: (s[1 + i], 0, 0)),
            ],
            out_specs=pl.BlockSpec((per_plane, None, capacity, width), lambda i, s: (0, i, 0, 0)),
        ),
        compiler_params=params(1, 40),
        cost_estimate=estimate(
            flops=2 * blocks * slot_rows * tok_rows * width,
            bytes_accessed=2 * blocks * (slot_rows + tok_rows) * width,
            transcendentals=0,
        ),
        name="dispatch",
    )(at, slots, rows)


def combine_kernel(first_ref, slots_ref, rows_ref, out_ref):
    hot = plane_hot(slots_ref, first_ref[0], rows_ref.shape)
    rows = rows_ref[...].reshape(hot.shape[0], rows_ref.shape[2])
    out_ref[...] = dot_tn(hot, rows).astype(bf16)


def combine(first, slots, rows, block):
    experts, tok_rows = slots.shape
    per_plane, _, capacity, width = rows.shape
    slot_rows = per_plane * capacity
    return pl.pallas_call(
        combine_kernel,
        out_shape=jax.ShapeDtypeStruct((tok_rows, width), bf16),
        grid_spec=pltpu.PrefetchScalarGridSpec(
            num_scalar_prefetch=1,
            grid=(1,),
            in_specs=[
                pl.BlockSpec((experts, tok_rows), lambda i, s: (0, 0)),
                pl.BlockSpec((per_plane, None, capacity, width), lambda i, s: (0, block, 0, 0)),
            ],
            out_specs=pl.BlockSpec((tok_rows, width), lambda i, s: (0, 0)),
        ),
        compiler_params=params(1, 40),
        cost_estimate=estimate(
            flops=2 * slot_rows * tok_rows * width,
            bytes_accessed=2 * (slot_rows + tok_rows) * width,
            transcendentals=0,
        ),
        name="combine",
    )(first, slots, rows)


def qkv_kernel(heads, planes, at_ref, x_ref, gain_ref, *refs):
    w_refs = refs[:planes]
    gq_ref, gk_ref, cos_ref, sin_ref, act_ref, pre_ref, rot_ref, all_ref = refs[planes:]
    depth = w_refs[0].shape[0]

    @pl.when(pl.program_id(0) == 0)
    def _():
        for d in range(planes):
            place = pl.ds(pl.multiple_of(at_ref[d] * depth, depth), depth)
            all_ref[place, :] = w_refs[d][...]

    x = x_ref[...].astype(f32)
    inverse = lax.rsqrt(jnp.mean(x * x, axis=-1, keepdims=True) + norm_eps)
    act = (x * inverse * gain_ref[...]).astype(bf16)
    act_ref[...] = act
    y = None
    for d in range(planes):
        columns = pl.ds(pl.multiple_of(at_ref[d] * depth, depth), depth)
        term = dot_nn(act_ref[:, columns], w_refs[d][...])
        y = term if y is None else y + term
    cosine, sine = cos_ref[...], sin_ref[...]
    for part, gain in enumerate((gq_ref[...], gk_ref[...])):
        for h in range(heads):
            at = (part * heads + h) * HD
            u = y[:, at : at + HD]
            pre_ref[:, at : at + HD] = u
            n = u * lax.rsqrt(jnp.mean(u * u, axis=-1, keepdims=True) + head_eps) * gain
            rot_ref[:, at : at + HD] = (n * cosine + pltpu.roll(n, HD // 2, 1) * sine).astype(bf16)
    at = 2 * heads * HD
    rot_ref[:, at:] = y[:, at:].astype(bf16)


def qkv_project(places, rows, gain, weights, gain_q, gain_k, cosine, sine, heads):
    count, width = rows.shape
    planes = len(weights)
    depth, out_width = weights[0].shape
    pre_width = 2 * heads * HD
    whole = lambda i, s: (0, 0)
    block = lambda i, s: (i, 0)
    return pl.pallas_call(
        functools.partial(qkv_kernel, heads, planes),
        out_shape=(
            jax.ShapeDtypeStruct((count, width), bf16),
            jax.ShapeDtypeStruct((count, pre_width), f32),
            jax.ShapeDtypeStruct((count, out_width), bf16),
            jax.ShapeDtypeStruct((width, out_width), bf16),
        ),
        grid_spec=pltpu.PrefetchScalarGridSpec(
            num_scalar_prefetch=1,
            grid=(count // ROWS,),
            in_specs=[
                pl.BlockSpec((ROWS, width), block),
                pl.BlockSpec((1, width), whole),
            ]
            + [pl.BlockSpec((depth, out_width), whole)] * planes
            + [
                pl.BlockSpec((1, HD), whole),
                pl.BlockSpec((1, HD), whole),
                pl.BlockSpec((ROWS, HD), block),
                pl.BlockSpec((ROWS, HD), block),
            ],
            out_specs=(
                pl.BlockSpec((ROWS, width), block),
                pl.BlockSpec((ROWS, pre_width), block),
                pl.BlockSpec((ROWS, out_width), block),
                pl.BlockSpec((width, out_width), whole),
            ),
        ),
        compiler_params=params(1, 56),
        cost_estimate=estimate(
            flops=2 * count * width * out_width,
            bytes_accessed=4 * count * width + 2 * width * out_width + 6 * count * out_width,
            transcendentals=0,
        ),
        name="qkv_project",
    )(places, rows, gain, *weights, gain_q, gain_k, cosine, sine)


def head_columns(heads):
    return [slice(h * HD, (h + 1) * HD) for h in range(heads)]


def attn_kernel(
    scale, low_ref, high_ref, q_ref, k_ref, v_ref, sq_ref, sk_ref, o_ref, ol_ref, lse_ref, s_scr
):
    block = pl.program_id(0)
    low, high = low_ref[block], high_ref[block]
    columns = head_columns(lse_ref.shape[1])
    seg_q = sq_ref[...]
    half = ROWS // 2

    def scores(kb, tops):
        at = pl.ds(pl.multiple_of(kb * ROWS, ROWS), ROWS)
        same = seg_q == sk_ref[:, at]
        found = []
        for h, cut in enumerate(columns):
            s = dot_nt(q_ref[:, cut], k_ref[at, cut]) * scale
            s = jnp.where(same, s, masked_score)
            s_scr[h, :, at] = s
            found.append(jnp.maximum(tops[h], jnp.maximum(s[:, :half], s[:, half:])))
        return tuple(found)

    lowest = jnp.full((ROWS, half), masked_score, f32)
    tops = lax.fori_loop(low, high, scores, (lowest,) * len(columns))
    tops = [jnp.max(top, axis=-1, keepdims=True) for top in tops]

    def weigh(kb, carry):
        at = pl.ds(pl.multiple_of(kb * ROWS, ROWS), ROWS)
        found = []
        for h, cut in enumerate(columns):
            total, acc = carry[h]
            p = jnp.exp(s_scr[h, :, at] - tops[h])
            acc = acc + dot_nn(p.astype(bf16), v_ref[at, cut])
            found.append((total + (p[:, :half] + p[:, half:]), acc))
        return tuple(found)

    start = (jnp.zeros((ROWS, half), f32), jnp.zeros((ROWS, HD), f32))
    sums = lax.fori_loop(low, high, weigh, (start,) * len(columns))
    for h, cut in enumerate(columns):
        total = jnp.sum(sums[h][0], axis=-1, keepdims=True)
        out = sums[h][1] / total
        o_ref[:, cut] = out
        ol_ref[:, cut] = out.astype(bf16)
        lse = jnp.broadcast_to(tops[h] + jnp.log(total), (ROWS, HD)).T
        lse_ref[0, h : h + 1, :] = lse[0:1, :]


def attention(rot, seg_col, seg_row, low, high, heads):
    count = rot.shape[0]
    blocks = count // ROWS
    wide = heads * HD
    scale = HD ** (-0.5)
    mine = lambda i, *s: (i, 0)
    return pl.pallas_call(
        functools.partial(attn_kernel, scale),
        out_shape=(
            jax.ShapeDtypeStruct((count, wide), f32),
            jax.ShapeDtypeStruct((count, wide), bf16),
            jax.ShapeDtypeStruct((blocks, heads, ROWS), f32),
        ),
        grid_spec=pltpu.PrefetchScalarGridSpec(
            num_scalar_prefetch=2,
            grid=(blocks,),
            in_specs=[
                pl.BlockSpec((ROWS, wide), mine),
                pl.BlockSpec((count, wide), lambda i, *s: (0, 1)),
                pl.BlockSpec((count, wide), lambda i, *s: (0, 2)),
                pl.BlockSpec((ROWS, 1), mine),
                pl.BlockSpec((1, count), lambda i, *s: (0, 0)),
            ],
            out_specs=(
                pl.BlockSpec((ROWS, wide), mine),
                pl.BlockSpec((ROWS, wide), mine),
                pl.BlockSpec((1, heads, ROWS), lambda i, *s: (i, 0, 0)),
            ),
            scratch_shapes=[pltpu.VMEM((heads, ROWS, count), f32)],
        ),
        compiler_params=params(1, 40),
        cost_estimate=estimate(
            flops=2 * heads * count * count * HD,
            bytes_accessed=12 * heads * count * HD,
            transcendentals=heads * count * count // 2,
        ),
        name="attention",
    )(low, high, rot, rot, rot, seg_col, seg_row)


def head_back(grad, pre, gain, cosine, sine):
    n = grad * cosine - pltpu.roll(grad, HD // 2, 1) * sine
    inverse = lax.rsqrt(jnp.mean(pre * pre, axis=-1, keepdims=True) + head_eps)
    w = n * gain
    back = inverse * w - pre * inverse**3 * jnp.mean(w * pre, axis=-1, keepdims=True)
    return back, jnp.sum(n * pre * inverse, axis=0, keepdims=True)


def attn_back_kernel(
    scale,
    low_ref,
    high_ref,
    q_ref,
    k_ref,
    v_ref,
    do_ref,
    o_ref,
    lse_ref,
    sq_ref,
    sk_ref,
    qpre_ref,
    kpre_ref,
    gq_ref,
    gk_ref,
    cosq_ref,
    sinq_ref,
    cosk_ref,
    sink_ref,
    grad_ref,
    gain_ref,
    dk_scr,
    dv_scr,
):
    block = pl.program_id(0)
    low, high = low_ref[block], high_ref[block]
    heads = lse_ref.shape[1]
    columns = head_columns(heads)
    wide = heads * HD

    @pl.when(block == 0)
    def _():
        dk_scr[...] = jnp.zeros_like(dk_scr)
        dv_scr[...] = jnp.zeros_like(dv_scr)
        gain_ref[...] = jnp.zeros_like(gain_ref)

    seg_q = sq_ref[...]
    row_dots = [
        jnp.sum((do_ref[:, cut].astype(f32) * o_ref[:, cut]).T, axis=0, keepdims=True)
        for cut in columns
    ]

    def tile(kb, sums):
        at = pl.ds(pl.multiple_of(kb * ROWS, ROWS), ROWS)
        same = sk_ref[at, :] == seg_q
        found = []
        for h, cut in enumerate(columns):
            k, v, q, do = k_ref[at, cut], v_ref[at, cut], q_ref[:, cut], do_ref[:, cut]
            s = dot_nt(k, q) * scale
            p = jnp.where(same, jnp.exp(s - lse_ref[0, h : h + 1, :]), 0.0)
            dp = dot_nt(v, do)
            ds = (p * (dp - row_dots[h])).astype(bf16)
            dv_scr[at, cut] += dot_nn(p.astype(bf16), do)
            dk_scr[at, cut] += dot_nn(ds, q)
            found.append(sums[h] + dot_tn(ds, k))
        return tuple(found)

    sums = lax.fori_loop(low, high, tile, (jnp.zeros((ROWS, HD), f32),) * heads)
    rows = pl.ds(pl.multiple_of(block * ROWS, ROWS), ROWS)
    for h, cut in enumerate(columns):
        back, gain_q = head_back(
            sums[h] * scale, qpre_ref[:, cut], gq_ref[...], cosq_ref[...], sinq_ref[...]
        )
        grad_ref[rows, cut] = back.astype(bf16)
        gain_ref[0:1, :] += gain_q

    @pl.when(block == pl.num_programs(0) - 1)
    def _():
        @pl.loop(0, dk_scr.shape[0] // ROWS)
        def _(i):
            at = pl.ds(pl.multiple_of(i * ROWS, ROWS), ROWS)
            for h, cut in enumerate(columns):
                back, gain_k = head_back(
                    dk_scr[at, cut] * scale,
                    kpre_ref[at, cut],
                    gk_ref[...],
                    cosk_ref[at, :],
                    sink_ref[at, :],
                )
                grad_ref[at, wide + h * HD : wide + (h + 1) * HD] = back.astype(bf16)
                gain_ref[1:2, :] += gain_k
            grad_ref[at, 2 * wide :] = dv_scr[at, :].astype(bf16)


def attention_back(
    rot, grad, out, lse, seg_col, seg_row, low, high, pre, gain_q, gain_k, cosine, sine, heads
):
    count = rot.shape[0]
    blocks = count // ROWS
    scale = HD ** (-0.5)
    wide = heads * HD
    mine = lambda i, *s: (i, 0)
    whole = lambda i, *s: (0, 0)
    return pl.pallas_call(
        functools.partial(attn_back_kernel, scale),
        out_shape=(
            jax.ShapeDtypeStruct((count, 3 * wide), bf16),
            jax.ShapeDtypeStruct((8, HD), f32),
        ),
        grid_spec=pltpu.PrefetchScalarGridSpec(
            num_scalar_prefetch=2,
            grid=(blocks,),
            in_specs=[
                pl.BlockSpec((ROWS, wide), mine),
                pl.BlockSpec((count, wide), lambda i, *s: (0, 1)),
                pl.BlockSpec((count, wide), lambda i, *s: (0, 2)),
                pl.BlockSpec((ROWS, wide), mine),
                pl.BlockSpec((ROWS, wide), mine),
                pl.BlockSpec((1, heads, ROWS), lambda i, *s: (i, 0, 0)),
                pl.BlockSpec((1, ROWS), lambda i, *s: (0, i)),
                pl.BlockSpec((count, 1), whole),
                pl.BlockSpec((ROWS, wide), mine),
                pl.BlockSpec((count, wide), lambda i, *s: (0, 1)),
                pl.BlockSpec((1, HD), whole),
                pl.BlockSpec((1, HD), whole),
                pl.BlockSpec((ROWS, HD), mine),
                pl.BlockSpec((ROWS, HD), mine),
                pl.BlockSpec((count, HD), whole),
                pl.BlockSpec((count, HD), whole),
            ],
            out_specs=(
                pl.BlockSpec((count, 3 * wide), whole),
                pl.BlockSpec((8, HD), whole),
            ),
            scratch_shapes=[pltpu.VMEM((count, wide), f32), pltpu.VMEM((count, wide), f32)],
        ),
        compiler_params=params(1, 56),
        cost_estimate=estimate(
            flops=5 * heads * count * count * HD,
            bytes_accessed=30 * heads * count * HD,
            transcendentals=heads * count * count // 2,
        ),
        name="attention_back",
    )(
        low,
        high,
        rot,
        rot,
        rot,
        grad,
        out,
        lse,
        seg_row,
        seg_col,
        pre,
        pre,
        gain_q,
        gain_k,
        cosine,
        sine,
        cosine,
        sine,
    )


def expert_kernel(count, carried, mine_ref, x_ref, near_ref, far_ref, *refs):
    wg_ref, wu_ref, wd_ref = refs[:3]
    refs = refs[3 + carried :]
    back_ref, out_ref, xs_ref, c_ref, hid_ref, gp_ref, up_ref = refs[:7]
    out_acc, back_acc, gate_scr, dot_scr = refs[7:]
    step = pl.program_id(1)
    per_plane, capacity, width = c_ref.shape
    rows = per_plane * capacity
    extra = x_ref.shape[2] - width
    lane = lax.broadcasted_iota(jnp.int32, (rows, extra), 1)
    high, low = lane == mine_ref[0], lane == mine_ref[0] + count

    @pl.when(step == 0)
    def _():
        xs_ref[...] = x_ref[:, :, :width]

        @pl.when(pl.program_id(0) == 0)
        def _():
            c_ref[...] = near_ref[...]

        @pl.when(pl.program_id(0) > 0)
        def _():
            c_ref[...] = far_ref[...]
        gates = x_ref[:, :, width:].reshape(rows, extra).astype(f32)
        gate_scr[...] = jnp.sum(jnp.where(high | low, gates, 0.0), axis=-1, keepdims=True)
        out_acc[...] = jnp.zeros_like(out_acc)
        back_acc[...] = jnp.zeros_like(back_acc)
        dot_scr[...] = jnp.zeros_like(dot_scr)

    x = x_ref[:, :, :width].reshape(rows, width)
    c = c_ref[...].reshape(rows, width)
    gate = gate_scr[...]
    wg, wu, wd = wg_ref[...], wu_ref[...], wd_ref[...]
    gate_pre, up_pre = dot_nn(x, wg), dot_nn(x, wu)
    sig = jax.nn.sigmoid(gate_pre)
    hidden = (gate_pre * sig * up_pre).astype(bf16)
    out_acc[...] += dot_nn(hidden, wd)
    plain = dot_nt(c, wd)
    wide = hidden.astype(f32)
    dot_scr[...] += jnp.sum(wide * plain, axis=-1, keepdims=True)
    hid_ref[...] = (wide * gate).astype(bf16).reshape(hid_ref.shape)
    hidden_grad = plain * gate
    gate_grad = (hidden_grad * up_pre * sig * (1.0 + gate_pre * (1.0 - sig))).astype(bf16)
    up_grad = (hidden_grad * gate_pre * sig).astype(bf16)
    gp_ref[...] = gate_grad.reshape(gp_ref.shape)
    up_ref[...] = up_grad.reshape(up_ref.shape)
    back_acc[...] += dot_nt(gate_grad, wg) + dot_nt(up_grad, wu)

    @pl.when(step == pl.num_programs(1) - 1)
    def _():
        dots = dot_scr[...]
        coarse = dots.astype(bf16).astype(f32)
        lanes = jnp.where(high, coarse, jnp.where(low, dots - coarse, 0.0)).astype(bf16)
        back_ref[:, :, :width] = back_acc[...].astype(bf16).reshape(c_ref.shape)
        back_ref[:, :, width:] = lanes.reshape(per_plane, capacity, extra)
        out_ref[...] = (out_acc[...] * gate).astype(bf16).reshape(out_ref.shape)


def experts(mine, x, near, far, wg, wu, wd, base, planes, count, kept):
    per_plane, blocks, capacity, wide = x.shape
    width = near.shape[3]
    halves, _, hidden = wg.shape
    rows = per_plane * capacity
    saved = jax.ShapeDtypeStruct((per_plane, planes, capacity, width), bf16)
    thin = jax.ShapeDtypeStruct((per_plane, planes, capacity, halves * hidden), bf16)
    moved = pl.BlockSpec((per_plane, None, capacity, wide), lambda i, f, s: (0, i, 0, 0))
    saved_spec = pl.BlockSpec((per_plane, None, capacity, width), lambda i, f, s: (0, base + i, 0, 0))
    thin_spec = pl.BlockSpec((per_plane, None, capacity, hidden), lambda i, f, s: (0, base + i, 0, f))
    carried = 0 if kept is None else len(kept)
    skip = base - 1 if base else 0
    cot_specs = [
        pl.BlockSpec((per_plane, None, capacity, width), lambda i, f, s: (0, 0, 0, 0)),
        pl.BlockSpec(
            (per_plane, None, capacity, width),
            lambda i, f, s: (0, jnp.maximum(skip + i - 1, 0), 0, 0),
        ),
    ]
    result = pl.pallas_call(
        functools.partial(expert_kernel, count, carried),
        out_shape=(
            jax.ShapeDtypeStruct(x.shape, bf16),
            jax.ShapeDtypeStruct((per_plane, blocks, capacity, width), bf16),
            saved,
            saved,
            thin,
            thin,
            thin,
        ),
        grid_spec=pltpu.PrefetchScalarGridSpec(
            num_scalar_prefetch=1,
            grid=(blocks, halves),
            in_specs=[
                moved,
                *cot_specs,
                pl.BlockSpec((None, width, hidden), lambda i, f, s: (f, 0, 0)),
                pl.BlockSpec((None, width, hidden), lambda i, f, s: (f, 0, 0)),
                pl.BlockSpec((None, hidden, width), lambda i, f, s: (f, 0, 0)),
            ]
            + [pl.BlockSpec(memory_space=pl.ANY)] * carried,
            out_specs=(
                moved,
                pl.BlockSpec((per_plane, None, capacity, width), lambda i, f, s: (0, i, 0, 0)),
                saved_spec,
                saved_spec,
                thin_spec,
                thin_spec,
                thin_spec,
            ),
            scratch_shapes=[
                pltpu.VMEM((rows, width), f32),
                pltpu.VMEM((rows, width), f32),
                pltpu.VMEM((rows, 1), f32),
                pltpu.VMEM((rows, 1), f32),
            ],
        ),
        input_output_aliases={7 + i: 2 + i for i in range(carried)},
        compiler_params=params(2, 60),
        cost_estimate=estimate(
            flops=12 * blocks * rows * width * hidden * halves,
            bytes_accessed=10 * blocks * rows * width + 6 * blocks * width * hidden * halves,
            transcendentals=blocks * rows * hidden * halves,
        ),
        name="experts",
    )(mine, x, near, far, wg, wu, wd, *(kept or ()))
    return result[0], result[1], result[2:]


def gram_kernel(plus, left_ref, right_ref, *refs):
    total = dot_tn(left_ref[...], right_ref[...])
    if plus:
        total = total + refs[0][...]
    refs[-1][...] = total.astype(refs[-1].dtype)


def gram(left, right, left_cols, right_cols, dtype, plus=None):
    rows = left.shape[0]
    left_at, left_count = left_cols
    right_at, right_count = right_cols
    tall = min(left_count, 256)
    wide = min(right_count, 1024)
    out_spec = pl.BlockSpec((tall, wide), lambda j, i: (i, j))
    return pl.pallas_call(
        functools.partial(gram_kernel, plus is not None),
        out_shape=jax.ShapeDtypeStruct((left_count, right_count), dtype),
        grid=(right_count // wide, left_count // tall),
        in_specs=[
            pl.BlockSpec((rows, tall), lambda j, i: (0, left_at // tall + i)),
            pl.BlockSpec((rows, wide), lambda j, i: (0, right_at // wide + j)),
        ]
        + [out_spec] * (plus is not None),
        out_specs=out_spec,
        compiler_params=params(2, 48),
        cost_estimate=estimate(
            flops=2 * rows * left_count * right_count,
            bytes_accessed=2 * rows * (left_count + right_count) + 4 * left_count * right_count,
            transcendentals=0,
        ),
        name="gram",
    )(left, right, *(() if plus is None else (plus,)))


def project_kernel(plus, core_ref, rows_ref, weights_ref, *refs):
    total = dot_nt(rows_ref[...], weights_ref[...])
    if plus:
        total = total + refs[0][...].astype(f32)
    refs[-1][...] = total.astype(bf16)


def project_back(core, rows, weights, tok_rows, plus=None):
    count, depth = rows.shape
    width = weights.shape[0]
    chips = count // tok_rows // 2
    out_spec = pl.BlockSpec((tok_rows, width), lambda i, s: (i, 0))
    return pl.pallas_call(
        functools.partial(project_kernel, plus is not None),
        out_shape=jax.ShapeDtypeStruct((chips * tok_rows, width), bf16),
        grid_spec=pltpu.PrefetchScalarGridSpec(
            num_scalar_prefetch=1,
            grid=(chips,),
            in_specs=[
                pl.BlockSpec((tok_rows, depth), lambda i, s: (2 * i + s[0], 0)),
                pl.BlockSpec((width, depth), lambda i, s: (0, 0)),
            ]
            + [out_spec] * (plus is not None),
            out_specs=out_spec,
        ),
        compiler_params=params(1, 40),
        cost_estimate=estimate(
            flops=count * depth * width,
            bytes_accessed=2 * width * depth + count * depth + count * width,
            transcendentals=0,
        ),
        name="project_back",
    )(core, rows, weights, *(() if plus is None else (plus,)))


def after(value, *others):
    return lax.optimization_barrier((value,) + others)[0]


def body(
    hidden_in,
    out_cotangent,
    segment_number,
    expert_routes,
    pair_order,
    norm_gain,
    query_weight,
    key_weight,
    value_weight,
    output_weight,
    query_gain,
    key_gain,
    ffn_norm_gain,
    router_weight,
    expert_gate,
    expert_up,
    expert_down,
):
    tok_rows, width = hidden_in.shape
    devices = lax.axis_size(AXIS)
    members = max(1, SEQ_MIN // tok_rows)
    planes = devices // members
    per_plane = members // 2
    expert_count = devices // 2
    capacity = tok_rows * TOPK // expert_count
    heads = width // HD // members
    head_width = heads * HD
    own_rows = norm_gain.shape[0]
    seq = members * tok_rows
    me = lax.axis_index(AXIS)
    plane, member = me // members, me % members
    mine = (me // 2).astype(jnp.int32).reshape(1)
    first = (plane * per_plane).astype(jnp.int32)
    places = (plane ^ jnp.arange(planes, dtype=jnp.int32)).astype(jnp.int32)
    counted = jnp.concatenate([first[None], jnp.arange(planes, dtype=jnp.int32)])
    halfway = -(-planes // 2)
    chunks = [part for part in (range(halfway, planes), range(halfway)) if len(part)]

    def placed(part):
        return jnp.concatenate([first[None], places[part.start : part.stop]])

    plane_groups = [[g * members + j for j in range(members)] for g in range(planes)]
    stack_groups = [[g * members + j for g in range(planes)] for j in range(members)]
    core_groups = [
        [g * members + 2 * c + h for c in range(per_plane)] for g in range(planes) for h in (0, 1)
    ]

    def exchange(value, groups=None):
        return lax.all_to_all(
            value, AXIS, split_axis=0, concat_axis=0, tiled=True, axis_index_groups=groups
        )

    def gather(value, groups=None):
        return lax.all_gather(value, AXIS, axis=0, tiled=True, axis_index_groups=groups)

    def flip(value, bits):
        if bits == 0:
            return value
        return lax.ppermute(value, AXIS, [(i, i ^ bits) for i in range(devices)])

    def to_core(value):
        return flip(value, 1)

    def to_plane(value, d):
        return flip(value, members * d)

    def spread(value, *others):
        found = {0: value}
        for d in range(1, planes):
            lowest = d & -d
            source = found[d ^ lowest]
            found[d] = to_plane(source if d == lowest else after(source, *others), lowest)
        return [found[d] for d in range(planes)]

    def fold(sums, *others):
        bit = 1
        while bit < len(sums):
            for d in range(len(sums)):
                if d & bit and not d & (bit - 1):
                    came = to_plane(sums[d].astype(bf16), bit)
                    if d == bit:
                        came = after(came, *others)
                    sums[d ^ bit] = sums[d ^ bit].astype(f32) + came.astype(f32)
            bit *= 2
        return sums[0]

    wire, core_op = [], []

    def on_wire(value, groups):
        came = exchange(after(value, *wire[-1:]), groups)
        wire.append(came)
        return came

    def to_chips(value):
        return on_wire(value, core_groups)

    def in_turn(value):
        return after(value, *core_op[-1:])

    def ran(value):
        core_op.append(value)
        return value

    columns = jnp.concatenate(
        [w.reshape(own_rows, members, head_width) for w in (query_weight, key_weight, value_weight)],
        axis=2,
    )
    slots = block_slots(expert_routes, pair_order, expert_count)
    columns = on_wire(
        after(columns, slots).transpose(1, 0, 2).reshape(members * own_rows, 3 * head_width), plane_groups
    )
    stacked = [to_plane(after(output_weight, slots), d) for d in range(planes)]
    cosine, sine = rope_tables(seq)
    weights = spread(after(columns, *stacked), cosine, sine)
    slots = [to_plane(after(slots, *weights) if d else slots, d) for d in range(planes)]
    output_rows = jnp.zeros((planes * own_rows, width), bf16)
    for d, rows in enumerate(stacked):
        output_rows = lax.dynamic_update_slice_in_dim(output_rows, rows, places[d] * own_rows, 0)
    rows_all = gather(hidden_in, plane_groups)

    pieces = (
        router_weight.reshape(-1),
        norm_gain,
        ffn_norm_gain,
        query_gain,
        key_gain,
        segment_number.astype(bf16),
    )
    packed = jnp.concatenate(pieces)
    length = packed.shape[0]
    padded = -(-length // 128) * 128
    packed = jnp.pad(packed, (0, padded - length))
    packed = on_wire(jnp.broadcast_to(packed[None], (devices, padded)), None)
    small = []
    at = 0
    for piece in pieces:
        small.append(packed[:, at : at + piece.shape[0]])
        at += piece.shape[0]
    router_full = small[0].reshape(width, expert_count)
    gain_one = small[1].reshape(1, width).astype(f32)
    gain_two = small[2].reshape(1, width).astype(f32)
    gain_q = small[3].reshape(1, HD).astype(f32)
    gain_k = small[4].reshape(1, HD).astype(f32)
    segments = lax.dynamic_slice_in_dim(small[5], plane * members, members, 0).astype(f32)
    seg_row, seg_col = segments.reshape(1, seq), segments.reshape(seq, 1)
    seg_blocks = segments.reshape(seq // ROWS, ROWS)
    seg_first, seg_last = seg_blocks[:, 0], seg_blocks[:, -1]
    low = jnp.sum((seg_last[None, :] < seg_first[:, None]).astype(jnp.int32), axis=1)
    high = jnp.sum((seg_first[None, :] <= seg_last[:, None]).astype(jnp.int32), axis=1)

    cot_own = dispatch(counted, slots[0][None], out_cotangent[None], per_plane, capacity)
    cot_first = [to_chips(cot_own)]
    output_full = gather(after(output_rows, columns), plane_groups)
    slot_list, slots = slots, jnp.stack(slots)
    cot_rows = {0: out_cotangent}
    top = planes // 2
    early, late = [], []
    if planes > 1:
        cot_rows[top] = to_plane(after(out_cotangent, *weights), top)
        early.append(cot_rows[top])
    for d in range(1, planes):
        if d != top:
            lowest = d & -d
            start = after(out_cotangent, *early) if d == lowest else cot_rows[d ^ lowest]
            cot_rows[d] = to_plane(start, lowest)
            late.append(cot_rows[d])

    halves = lambda w: jnp.concatenate([w, to_core(w)], axis=0)
    wg, wu, wd = halves(expert_gate), halves(expert_up), halves(expert_down)

    act_one, pre, rot, ordered = qkv_project(
        places, rows_all, gain_one, weights, gain_q, gain_k, cosine, sine, heads
    )
    out_wide, out_heads, lse = attention(rot, seg_col, seg_row, low, high, heads)
    out_low = on_wire(after(out_heads, *slot_list, *early), plane_groups)
    if planes > 1:
        rows = after(cot_rows[top], out_heads)
        sent = dispatch(counted, slots[top : top + 1], rows[None], per_plane, capacity)
        cot_first.append(to_chips(sent))
    out_low = out_low.reshape(members, tok_rows, head_width).transpose(1, 0, 2)
    out_low = out_low.reshape(tok_rows, planes, members, own_rows).transpose(0, 2, 1, 3)
    out_low = out_low.reshape(tok_rows, width)
    tokens = hidden_in.astype(f32)
    cotangent = out_cotangent.astype(f32)
    middle = tokens + dot_nn(out_low, output_full)
    inverse_two = lax.rsqrt(jnp.mean(middle * middle, axis=-1, keepdims=True) + norm_eps)
    act_two = (middle * inverse_two * gain_two).astype(bf16)

    logits = dot_nn(act_two, router_full)
    expert_ids = jnp.arange(expert_count, dtype=jnp.int32)
    routed = jnp.any(expert_routes[:, :, None] == expert_ids[None, None, :], axis=1)
    logits = jnp.where(routed, logits, masked_score)
    gates = jnp.where(routed, jnp.exp(logits - jnp.max(logits, axis=1, keepdims=True)), 0.0)
    gates = gates / jnp.sum(gates, axis=1, keepdims=True)
    coarse = lax.reduce_precision(gates, 8, 7)
    extra = -(-2 * expert_count // 128) * 128
    act_wide = jnp.concatenate(
        [
            act_two,
            coarse.astype(bf16),
            (gates - coarse).astype(bf16),
            jnp.zeros((tok_rows, extra - 2 * expert_count), bf16),
        ],
        axis=1,
    )

    act_wide = after(act_wide, *late, *cot_first)
    act_all = gather(act_wide, stack_groups).reshape(planes, tok_rows, -1)
    others = [d for d in range(1, planes) if d != top]
    cot_far = cot_first[0]
    if others:
        far = jnp.stack([after(cot_rows[d], act_wide) for d in others])
        far_slots = jnp.stack([slots[d] for d in others])
        cot_far = to_chips(
            ran(dispatch(counted[: len(others) + 1], far_slots, far, per_plane, capacity))
        )

    act = []
    for part in chunks:
        own_slots = slots[part.start : part.stop]
        rows = after(in_turn(act_all), wg, wu, wd)
        sent = dispatch(placed(part), own_slots, rows, per_plane, capacity)
        act.append(to_chips(ran(sent)))
    kept, back, outs = None, [], []
    for part, rows in zip(chunks, act):
        sent, out, kept = experts(
            mine,
            in_turn(rows),
            cot_first[0 if part.start == 0 else 1],
            cot_far,
            wg,
            wu,
            wd,
            part.start,
            planes,
            expert_count,
            kept,
        )
        back.append(to_chips(ran(sent)))
        outs.append(out)
    x_all, c_all, hid_all, gp_all, up_all = kept

    hidden = expert_gate.shape[2]
    flat = lambda value: value.reshape(-1, value.shape[3])
    sides = (
        (flat(x_all), flat(gp_all), 1),
        (flat(x_all), flat(up_all), 1),
        (flat(hid_all), flat(c_all), 0),
    )

    def half(side, which, plus=None):
        left, right, split = side
        cut, whole = (which * hidden, hidden), (0, width)
        cols = (whole, cut) if split else (cut, whole)
        return ran(gram(in_turn(left), right, *cols, f32, plus))

    passed = []

    def home(part, rows):
        sums = {}
        for d in sorted(part, key=lambda d: (-(d & 1), d)):
            sums[d] = ran(combine(first[None], slots[d], in_turn(rows), d - part.start))
        bit = 1
        while bit < len(part):
            for d in part:
                if d & bit and not d & (bit - 1):
                    came = to_plane(sums[d].astype(bf16), bit)
                    passed.append(came)
                    sums[d ^ bit] = sums[d ^ bit].astype(f32) + came.astype(f32)
            bit *= 2
        return sums[part.start]

    back_sum = home(chunks[0], back[0])
    theirs = [half(side, 1) for side in sides[:2]]
    if len(chunks) > 1:
        back_sum = ran(in_turn(back_sum.astype(bf16)))
        back_sum = to_plane(back_sum, top)
    theirs.append(half(sides[2], 1))
    if len(chunks) > 1:
        back_sum = back_sum.astype(f32) + home(chunks[1], back[1])
    outs[0] = to_chips(outs[0])

    expert_in_grad = back_sum[:, :width]
    gate_grad = (
        back_sum[:, width : width + expert_count]
        + back_sum[:, width + expert_count : width + 2 * expert_count]
    )
    select_grad = gates * (gate_grad - jnp.sum(gates * gate_grad, axis=1, keepdims=True))
    logit_grad = select_grad.astype(bf16)
    grad_router = dot_tn(act_two, logit_grad)
    act_two_grad = expert_in_grad + dot_nt(logit_grad, router_full)
    weighted = act_two_grad * gain_two
    grad_gain_two = jnp.sum(act_two_grad * middle * inverse_two, axis=0)
    middle_grad = (
        cotangent
        + inverse_two * weighted
        - middle * inverse_two**3 * jnp.mean(weighted * middle, axis=-1, keepdims=True)
    )
    middle_low = middle_grad.astype(bf16)

    out_grad = dot_nt(middle_low, output_full).astype(bf16)
    out_grad = out_grad.reshape(tok_rows, members, planes, own_rows).transpose(0, 2, 1, 3)
    out_grad = out_grad.reshape(tok_rows, members, head_width).transpose(1, 0, 2)
    out_grad = out_grad.reshape(seq, head_width)
    ran(out_grad)
    theirs = [to_core(after(grad, out_grad)) for grad in theirs]
    out_grad = on_wire(out_grad, plane_groups)
    mixture = home(chunks[0], outs[0]).astype(bf16)
    dqkv, grad_gains = attention_back(
        rot,
        in_turn(out_grad),
        out_wide,
        lse,
        seg_col,
        seg_row,
        low,
        high,
        pre,
        gain_q,
        gain_k,
        cosine,
        sine,
        heads,
    )
    ran(dqkv)
    if len(chunks) > 1:
        near_sum = home(chunks[1], to_chips(outs[1]))
        done = (*core_op[-2:], mixture, *theirs)
        dqkv, grad_gains = after(dqkv, *done), after(grad_gains, *done)
    middle_all = gather(after(middle_low, dqkv), plane_groups)

    sums = (
        grad_router.reshape(devices, -1),
        grad_gain_two.reshape(devices, -1),
        grad_gains[0].reshape(devices, -1),
        grad_gains[1].reshape(devices, -1),
    )
    packed = jnp.concatenate(sums, axis=1)
    length = packed.shape[1]
    padded = -(-length // 128) * 128
    packed = jnp.pad(packed, ((0, 0), (0, padded - length)))

    core = (me % 2).astype(jnp.int32).reshape(1)
    given = project_back(1 - core, dqkv, ordered, tok_rows)
    part = gram(after(act_one, given), dqkv, (0, width), (0, 3 * head_width), bf16)
    part = part.reshape(planes, members * own_rows, 3 * head_width)
    shares = [lax.dynamic_index_in_dim(part, places[d], 0, False) for d in range(planes)]
    mixture = to_plane(mixture, top) if len(chunks) > 1 else mixture
    given = after(to_core(given), *shares, mixture, *passed[-1:])
    act_one_grad = project_back(core, dqkv, ordered, tok_rows, given)
    ran(act_one_grad)
    output_part = ran(gram(out_heads, in_turn(middle_all), (0, head_width), (0, width), bf16))
    grad_gate, grad_up, grad_down = (
        half(side, 0, other) for side, other in zip(sides, theirs)
    )
    shares = [after(share, act_one_grad) for share in shares]
    taken = fold(shares, grad_gate, grad_up, grad_down).astype(bf16)
    act_one_grad = on_wire(act_one_grad, core_groups)

    output_part = lax.psum_scatter(
        output_part, AXIS, scatter_dimension=0, tiled=True, axis_index_groups=stack_groups
    )
    to_owner = [
        (g * members + j, j * planes + g) for g in range(planes) for j in range(members)
    ]
    mixture = mixture.astype(f32)
    if len(chunks) > 1:
        mixture = mixture + near_sum
    packed, act_one_grad, mixture, grad_gate, grad_up, grad_down = lax.optimization_barrier(
        (packed, act_one_grad, mixture, grad_gate, grad_up, grad_down)
    )
    layer_out = (middle + mixture).astype(bf16)
    packed = exchange(packed)
    taken, packed, output_part = lax.optimization_barrier((taken, packed, output_part))
    grad_output = lax.ppermute(output_part, AXIS, to_owner)
    part = exchange(taken, plane_groups).reshape(members, own_rows, 3, head_width)
    part = part.transpose(2, 1, 0, 3).reshape(3, own_rows, width).astype(f32)
    grad_query, grad_key, grad_value = part[0], part[1], part[2]
    act_one_grad = act_one_grad.reshape(per_plane, tok_rows, width)
    act_one_grad = jnp.sum(act_one_grad.astype(f32), axis=0)

    inverse_one = lax.rsqrt(jnp.mean(tokens * tokens, axis=-1, keepdims=True) + norm_eps)
    weighted = act_one_grad * gain_one
    grad_hidden = (
        middle_grad
        + inverse_one * weighted
        - tokens * inverse_one**3 * jnp.mean(weighted * tokens, axis=-1, keepdims=True)
    )
    grad_gain_one = (
        jnp.sum(
            grad_query * query_weight.astype(f32)
            + grad_key * key_weight.astype(f32)
            + grad_value * value_weight.astype(f32),
            axis=1,
        )
        / norm_gain.astype(f32)
    )

    summed = jnp.sum(packed, axis=0)
    at, tiny = 0, []
    for piece in sums:
        tiny.append(summed[at : at + piece.shape[1]])
        at += piece.shape[1]

    return (
        layer_out,
        grad_hidden,
        grad_gain_one,
        grad_query,
        grad_key,
        grad_value,
        grad_output.astype(f32),
        tiny[2],
        tiny[3],
        tiny[1],
        tiny[0].reshape(own_rows, expert_count),
        grad_gate[None],
        grad_up[None],
        grad_down[None],
    )


def solution(mesh):
    row, mat, cube = P(AXIS), P(AXIS, None), P(AXIS, None, None)
    return jax.shard_map(
        body,
        mesh=mesh,
        in_specs=(mat, mat, row, mat, mat, row, mat, mat, mat, mat, row, row, row, mat)
        + (cube,) * 3,
        out_specs=(mat, mat, row, mat, mat, mat, mat, row, row, row, mat) + (cube,) * 3,
        check_vma=False,
    )
```

```python
import functools
import math

import jax
import jax.numpy as jnp
from jax import lax
from jax.experimental import pallas as pl
from jax.experimental.pallas import tpu as pltpu
from jax.sharding import PartitionSpec as P

HD = 128
TOPK = 8
SEQ_MIN = 2048
ROWS = 256
SHARE = 32

norm_eps = 1e-05
head_eps = 1e-06
rope_base = 10000.0
masked_score = -1e30
absent_slot = 4096.0

AXIS = "fsdp"
f32 = jnp.float32
bf16 = jnp.bfloat16
MIB = 1 << 20


def dot_nt(left, right):
    return lax.dot_general(left, right, (((1,), (1,)), ((), ())), preferred_element_type=f32)


def dot_tn(left, right):
    return lax.dot_general(left, right, (((0,), (0,)), ((), ())), preferred_element_type=f32)


def dot_nn(left, right):
    return lax.dot_general(left, right, (((1,), (0,)), ((), ())), preferred_element_type=f32)


def params(steps, mib):
    return pltpu.CompilerParams(
        dimension_semantics=("arbitrary",) * steps, vmem_limit_bytes=mib * MIB
    )


def estimate(flops, bytes_accessed, transcendentals):
    return pl.CostEstimate(
        flops=flops // SHARE, bytes_accessed=bytes_accessed // SHARE, transcendentals=transcendentals // SHARE
    )


def rope_tables(count):
    half_width = HD // 2
    frequency = jnp.exp(-math.log(rope_base) * 2.0 * jnp.arange(half_width, dtype=f32) / HD)
    angles = jnp.arange(count, dtype=f32)[:, None] * frequency[None, :]
    cosine, sine = jnp.cos(angles), jnp.sin(angles)
    return jnp.concatenate([cosine, cosine], axis=-1), jnp.concatenate([-sine, sine], axis=-1)


def slots_kernel(expert_count, routes_ref, order_ref, slots_ref):
    tok_rows = routes_ref.shape[0]
    pair_count = order_ref.shape[1]
    order = order_ref[...]
    shift = TOPK.bit_length() - 1
    token_of = lax.shift_right_logical(order, jnp.full_like(order, shift))
    route_of = order & (TOPK - 1)
    token_iota = lax.broadcasted_iota(jnp.int32, (tok_rows, pair_count), 0)
    token_hot = jnp.where(token_iota == token_of, 1.0, 0.0).astype(bf16)
    place = lax.broadcasted_iota(jnp.int32, (TOPK, pair_count), 1)
    chosen = lax.broadcasted_iota(jnp.int32, (TOPK, pair_count), 0) == route_of
    high = lax.shift_right_logical(place, jnp.full_like(place, 8)).astype(f32)
    low = (place & 255).astype(f32)
    digits = jnp.concatenate([jnp.where(chosen, high, 0.0), jnp.where(chosen, low, 0.0)], axis=0)
    found = dot_nt(token_hot, digits.astype(bf16))
    rank = found[:, :TOPK] * 256.0 + found[:, TOPK:]
    routes = routes_ref[...]
    lanes = -(-expert_count // 128) * 128
    expert_iota = lax.broadcasted_iota(jnp.int32, (tok_rows, lanes), 1)
    never = 1e9
    by_expert = jnp.full((tok_rows, lanes), never, f32)
    for k in range(TOPK):
        by_expert = jnp.where(expert_iota == routes[:, k : k + 1], rank[:, k : k + 1], by_expert)
    turned = by_expert.T
    for e in range(expert_count):
        mine = turned[e : e + 1, :]
        earlier = jnp.where(by_expert[:, e : e + 1] < mine, 1.0, 0.0)
        count = jnp.sum(earlier, axis=0, keepdims=True)
        slots_ref[e : e + 1, :] = jnp.where(mine < never, count, absent_slot)


def block_slots(routes, order, expert_count):
    tok_rows = routes.shape[0]
    return pl.pallas_call(
        functools.partial(slots_kernel, expert_count),
        out_shape=jax.ShapeDtypeStruct((expert_count, tok_rows), f32),
        compiler_params=pltpu.CompilerParams(vmem_limit_bytes=32 * MIB),
        name="block_slots",
    )(routes, order)


def slot_hot(slots_ref, expert, capacity):
    slot_row = slots_ref[pl.ds(expert, 1), :]
    slot_iota = lax.broadcasted_iota(jnp.int32, (capacity, slot_row.shape[1]), 0).astype(f32)
    return jnp.where(slot_iota == slot_row, 1.0, 0.0).astype(bf16)


def plane_hot(slots_ref, first, shape):
    return jnp.concatenate([slot_hot(slots_ref, first + r, shape[1]) for r in range(shape[0])])


def dispatch_kernel(at_ref, slots_ref, rows_ref, out_ref):
    hot = plane_hot(slots_ref, at_ref[0], out_ref.shape)
    out_ref[...] = dot_nn(hot, rows_ref[...]).astype(bf16).reshape(out_ref.shape)


def dispatch(at, slots, rows, per_plane, capacity):
    blocks, experts, tok_rows = slots.shape
    width = rows.shape[2]
    slot_rows = per_plane * capacity
    return pl.pallas_call(
        dispatch_kernel,
        out_shape=jax.ShapeDtypeStruct((per_plane, blocks, capacity, width), bf16),
        grid_spec=pltpu.PrefetchScalarGridSpec(
            num_scalar_prefetch=1,
            grid=(blocks,),
            in_specs=[
                pl.BlockSpec((None, experts, tok_rows), lambda i, s: (i, 0, 0)),
                pl.BlockSpec((None, tok_rows, width), lambda i, s: (s[1 + i], 0, 0)),
            ],
            out_specs=pl.BlockSpec((per_plane, None, capacity, width), lambda i, s: (0, i, 0, 0)),
        ),
        compiler_params=params(1, 40),
        cost_estimate=estimate(
            flops=2 * blocks * slot_rows * tok_rows * width,
            bytes_accessed=2 * blocks * (slot_rows + tok_rows) * width,
            transcendentals=0,
        ),
        name="dispatch",
    )(at, slots, rows)


def combine_kernel(first_ref, slots_ref, rows_ref, out_ref):
    hot = plane_hot(slots_ref, first_ref[0], rows_ref.shape)
    rows = rows_ref[...].reshape(hot.shape[0], rows_ref.shape[2])
    out_ref[...] = dot_tn(hot, rows).astype(bf16)


def combine(first, slots, rows, block):
    experts, tok_rows = slots.shape
    per_plane, _, capacity, width = rows.shape
    slot_rows = per_plane * capacity
    return pl.pallas_call(
        combine_kernel,
        out_shape=jax.ShapeDtypeStruct((tok_rows, width), bf16),
        grid_spec=pltpu.PrefetchScalarGridSpec(
            num_scalar_prefetch=1,
            grid=(1,),
            in_specs=[
                pl.BlockSpec((experts, tok_rows), lambda i, s: (0, 0)),
                pl.BlockSpec((per_plane, None, capacity, width), lambda i, s: (0, block, 0, 0)),
            ],
            out_specs=pl.BlockSpec((tok_rows, width), lambda i, s: (0, 0)),
        ),
        compiler_params=params(1, 40),
        cost_estimate=estimate(
            flops=2 * slot_rows * tok_rows * width,
            bytes_accessed=2 * (slot_rows + tok_rows) * width,
            transcendentals=0,
        ),
        name="combine",
    )(first, slots, rows)


def qkv_kernel(heads, planes, at_ref, x_ref, gain_ref, *refs):
    w_refs = refs[:planes]
    gq_ref, gk_ref, cos_ref, sin_ref, act_ref, pre_ref, rot_ref, all_ref = refs[planes:]
    depth = w_refs[0].shape[0]

    @pl.when(pl.program_id(0) == 0)
    def _():
        for d in range(planes):
            place = pl.ds(pl.multiple_of(at_ref[d] * depth, depth), depth)
            all_ref[place, :] = w_refs[d][...]

    x = x_ref[...].astype(f32)
    inverse = lax.rsqrt(jnp.mean(x * x, axis=-1, keepdims=True) + norm_eps)
    act = (x * inverse * gain_ref[...]).astype(bf16)
    act_ref[...] = act
    y = dot_nn(act, all_ref[...])
    cosine, sine = cos_ref[...], sin_ref[...]
    for part, gain in enumerate((gq_ref[...], gk_ref[...])):
        for h in range(heads):
            at = (part * heads + h) * HD
            u = y[:, at : at + HD]
            pre_ref[:, at : at + HD] = u
            n = u * lax.rsqrt(jnp.mean(u * u, axis=-1, keepdims=True) + head_eps) * gain
            rot_ref[:, at : at + HD] = (n * cosine + pltpu.roll(n, HD // 2, 1) * sine).astype(bf16)
    at = 2 * heads * HD
    rot_ref[:, at:] = y[:, at:].astype(bf16)


def qkv_project(places, rows, gain, weights, gain_q, gain_k, cosine, sine, heads):
    count, width = rows.shape
    planes = len(weights)
    depth, out_width = weights[0].shape
    pre_width = 2 * heads * HD
    whole = lambda i, s: (0, 0)
    block = lambda i, s: (i, 0)
    return pl.pallas_call(
        functools.partial(qkv_kernel, heads, planes),
        out_shape=(
            jax.ShapeDtypeStruct((count, width), bf16),
            jax.ShapeDtypeStruct((count, pre_width), f32),
            jax.ShapeDtypeStruct((count, out_width), bf16),
            jax.ShapeDtypeStruct((width, out_width), bf16),
        ),
        grid_spec=pltpu.PrefetchScalarGridSpec(
            num_scalar_prefetch=1,
            grid=(count // ROWS,),
            in_specs=[
                pl.BlockSpec((ROWS, width), block),
                pl.BlockSpec((1, width), whole),
            ]
            + [pl.BlockSpec((depth, out_width), whole)] * planes
            + [
                pl.BlockSpec((1, HD), whole),
                pl.BlockSpec((1, HD), whole),
                pl.BlockSpec((ROWS, HD), block),
                pl.BlockSpec((ROWS, HD), block),
            ],
            out_specs=(
                pl.BlockSpec((ROWS, width), block),
                pl.BlockSpec((ROWS, pre_width), block),
                pl.BlockSpec((ROWS, out_width), block),
                pl.BlockSpec((width, out_width), whole),
            ),
        ),
        compiler_params=params(1, 56),
        cost_estimate=estimate(
            flops=2 * count * width * out_width,
            bytes_accessed=4 * count * width + 2 * width * out_width + 6 * count * out_width,
            transcendentals=0,
        ),
        name="qkv_project",
    )(places, rows, gain, *weights, gain_q, gain_k, cosine, sine)


def head_columns(heads):
    return [slice(h * HD, (h + 1) * HD) for h in range(heads)]


def attn_kernel(
    scale, low_ref, high_ref, q_ref, k_ref, v_ref, sq_ref, sk_ref, o_ref, ol_ref, lse_ref, s_scr
):
    block = pl.program_id(0)
    low, high = low_ref[block], high_ref[block]
    columns = head_columns(lse_ref.shape[1])
    seg_q = sq_ref[...]
    half = ROWS // 2

    def scores(kb, tops):
        at = pl.ds(pl.multiple_of(kb * ROWS, ROWS), ROWS)
        same = seg_q == sk_ref[:, at]
        found = []
        for h, cut in enumerate(columns):
            s = dot_nt(q_ref[:, cut], k_ref[at, cut]) * scale
            s = jnp.where(same, s, masked_score)
            s_scr[h, :, at] = s
            found.append(jnp.maximum(tops[h], jnp.maximum(s[:, :half], s[:, half:])))
        return tuple(found)

    lowest = jnp.full((ROWS, half), masked_score, f32)
    tops = lax.fori_loop(low, high, scores, (lowest,) * len(columns))
    tops = [jnp.max(top, axis=-1, keepdims=True) for top in tops]

    def weigh(kb, carry):
        at = pl.ds(pl.multiple_of(kb * ROWS, ROWS), ROWS)
        found = []
        for h, cut in enumerate(columns):
            total, acc = carry[h]
            p = jnp.exp(s_scr[h, :, at] - tops[h])
            acc = acc + dot_nn(p.astype(bf16), v_ref[at, cut])
            found.append((total + (p[:, :half] + p[:, half:]), acc))
        return tuple(found)

    start = (jnp.zeros((ROWS, half), f32), jnp.zeros((ROWS, HD), f32))
    sums = lax.fori_loop(low, high, weigh, (start,) * len(columns))
    for h, cut in enumerate(columns):
        total = jnp.sum(sums[h][0], axis=-1, keepdims=True)
        out = sums[h][1] / total
        o_ref[:, cut] = out
        ol_ref[:, cut] = out.astype(bf16)
        lse = jnp.broadcast_to(tops[h] + jnp.log(total), (ROWS, HD)).T
        lse_ref[0, h : h + 1, :] = lse[0:1, :]


def attention(rot, seg_col, seg_row, low, high, heads):
    count = rot.shape[0]
    blocks = count // ROWS
    wide = heads * HD
    scale = HD ** (-0.5)
    mine = lambda i, *s: (i, 0)
    return pl.pallas_call(
        functools.partial(attn_kernel, scale),
        out_shape=(
            jax.ShapeDtypeStruct((count, wide), f32),
            jax.ShapeDtypeStruct((count, wide), bf16),
            jax.ShapeDtypeStruct((blocks, heads, ROWS), f32),
        ),
        grid_spec=pltpu.PrefetchScalarGridSpec(
            num_scalar_prefetch=2,
            grid=(blocks,),
            in_specs=[
                pl.BlockSpec((ROWS, wide), mine),
                pl.BlockSpec((count, wide), lambda i, *s: (0, 1)),
                pl.BlockSpec((count, wide), lambda i, *s: (0, 2)),
                pl.BlockSpec((ROWS, 1), mine),
                pl.BlockSpec((1, count), lambda i, *s: (0, 0)),
            ],
            out_specs=(
                pl.BlockSpec((ROWS, wide), mine),
                pl.BlockSpec((ROWS, wide), mine),
                pl.BlockSpec((1, heads, ROWS), lambda i, *s: (i, 0, 0)),
            ),
            scratch_shapes=[pltpu.VMEM((heads, ROWS, count), f32)],
        ),
        compiler_params=params(1, 40),
        cost_estimate=estimate(
            flops=2 * heads * count * count * HD,
            bytes_accessed=12 * heads * count * HD,
            transcendentals=heads * count * count // 2,
        ),
        name="attention",
    )(low, high, rot, rot, rot, seg_col, seg_row)


def head_back(grad, pre, gain, cosine, sine):
    n = grad * cosine - pltpu.roll(grad, HD // 2, 1) * sine
    inverse = lax.rsqrt(jnp.mean(pre * pre, axis=-1, keepdims=True) + head_eps)
    w = n * gain
    back = inverse * w - pre * inverse**3 * jnp.mean(w * pre, axis=-1, keepdims=True)
    return back, jnp.sum(n * pre * inverse, axis=0, keepdims=True)


def attn_back_kernel(
    scale,
    low_ref,
    high_ref,
    q_ref,
    k_ref,
    v_ref,
    do_ref,
    o_ref,
    lse_ref,
    sq_ref,
    sk_ref,
    qpre_ref,
    kpre_ref,
    gq_ref,
    gk_ref,
    cosq_ref,
    sinq_ref,
    cosk_ref,
    sink_ref,
    grad_ref,
    gain_ref,
    dk_scr,
    dv_scr,
):
    block = pl.program_id(0)
    low, high = low_ref[block], high_ref[block]
    heads = lse_ref.shape[1]
    columns = head_columns(heads)
    wide = heads * HD

    @pl.when(block == 0)
    def _():
        dk_scr[...] = jnp.zeros_like(dk_scr)
        dv_scr[...] = jnp.zeros_like(dv_scr)
        gain_ref[...] = jnp.zeros_like(gain_ref)

    seg_q = sq_ref[...]
    row_dots = [
        jnp.sum((do_ref[:, cut].astype(f32) * o_ref[:, cut]).T, axis=0, keepdims=True)
        for cut in columns
    ]

    def tile(kb, sums):
        at = pl.ds(pl.multiple_of(kb * ROWS, ROWS), ROWS)
        same = sk_ref[at, :] == seg_q
        found = []
        for h, cut in enumerate(columns):
            k, v, q, do = k_ref[at, cut], v_ref[at, cut], q_ref[:, cut], do_ref[:, cut]
            s = dot_nt(k, q) * scale
            p = jnp.where(same, jnp.exp(s - lse_ref[0, h : h + 1, :]), 0.0)
            dp = dot_nt(v, do)
            ds = (p * (dp - row_dots[h])).astype(bf16)
            dv_scr[at, cut] += dot_nn(p.astype(bf16), do)
            dk_scr[at, cut] += dot_nn(ds, q)
            found.append(sums[h] + dot_tn(ds, k))
        return tuple(found)

    sums = lax.fori_loop(low, high, tile, (jnp.zeros((ROWS, HD), f32),) * heads)
    rows = pl.ds(pl.multiple_of(block * ROWS, ROWS), ROWS)
    for h, cut in enumerate(columns):
        back, gain_q = head_back(
            sums[h] * scale, qpre_ref[:, cut], gq_ref[...], cosq_ref[...], sinq_ref[...]
        )
        grad_ref[rows, cut] = back.astype(bf16)
        gain_ref[0:1, :] += gain_q

    @pl.when(block == pl.num_programs(0) - 1)
    def _():
        @pl.loop(0, dk_scr.shape[0] // ROWS)
        def _(i):
            at = pl.ds(pl.multiple_of(i * ROWS, ROWS), ROWS)
            for h, cut in enumerate(columns):
                back, gain_k = head_back(
                    dk_scr[at, cut] * scale,
                    kpre_ref[at, cut],
                    gk_ref[...],
                    cosk_ref[at, :],
                    sink_ref[at, :],
                )
                grad_ref[at, wide + h * HD : wide + (h + 1) * HD] = back.astype(bf16)
                gain_ref[1:2, :] += gain_k
            grad_ref[at, 2 * wide :] = dv_scr[at, :].astype(bf16)


def attention_back(
    rot, grad, out, lse, seg_col, seg_row, low, high, pre, gain_q, gain_k, cosine, sine, heads
):
    count = rot.shape[0]
    blocks = count // ROWS
    scale = HD ** (-0.5)
    wide = heads * HD
    mine = lambda i, *s: (i, 0)
    whole = lambda i, *s: (0, 0)
    return pl.pallas_call(
        functools.partial(attn_back_kernel, scale),
        out_shape=(
            jax.ShapeDtypeStruct((count, 3 * wide), bf16),
            jax.ShapeDtypeStruct((8, HD), f32),
        ),
        grid_spec=pltpu.PrefetchScalarGridSpec(
            num_scalar_prefetch=2,
            grid=(blocks,),
            in_specs=[
                pl.BlockSpec((ROWS, wide), mine),
                pl.BlockSpec((count, wide), lambda i, *s: (0, 1)),
                pl.BlockSpec((count, wide), lambda i, *s: (0, 2)),
                pl.BlockSpec((ROWS, wide), mine),
                pl.BlockSpec((ROWS, wide), mine),
                pl.BlockSpec((1, heads, ROWS), lambda i, *s: (i, 0, 0)),
                pl.BlockSpec((1, ROWS), lambda i, *s: (0, i)),
                pl.BlockSpec((count, 1), whole),
                pl.BlockSpec((ROWS, wide), mine),
                pl.BlockSpec((count, wide), lambda i, *s: (0, 1)),
                pl.BlockSpec((1, HD), whole),
                pl.BlockSpec((1, HD), whole),
                pl.BlockSpec((ROWS, HD), mine),
                pl.BlockSpec((ROWS, HD), mine),
                pl.BlockSpec((count, HD), whole),
                pl.BlockSpec((count, HD), whole),
            ],
            out_specs=(
                pl.BlockSpec((count, 3 * wide), whole),
                pl.BlockSpec((8, HD), whole),
            ),
            scratch_shapes=[pltpu.VMEM((count, wide), f32), pltpu.VMEM((count, wide), f32)],
        ),
        compiler_params=params(1, 56),
        cost_estimate=estimate(
            flops=5 * heads * count * count * HD,
            bytes_accessed=30 * heads * count * HD,
            transcendentals=heads * count * count // 2,
        ),
        name="attention_back",
    )(
        low,
        high,
        rot,
        rot,
        rot,
        grad,
        out,
        lse,
        seg_row,
        seg_col,
        pre,
        pre,
        gain_q,
        gain_k,
        cosine,
        sine,
        cosine,
        sine,
    )


def expert_kernel(count, carried, mine_ref, x_ref, near_ref, far_ref, *refs):
    wg_ref, wu_ref, wd_ref = refs[:3]
    refs = refs[3 + carried :]
    back_ref, out_ref, xs_ref, c_ref, hid_ref, gp_ref, up_ref = refs[:7]
    out_acc, back_acc, gate_scr, dot_scr = refs[7:]
    step = pl.program_id(1)
    per_plane, capacity, width = c_ref.shape
    rows = per_plane * capacity
    extra = x_ref.shape[2] - width
    lane = lax.broadcasted_iota(jnp.int32, (rows, extra), 1)
    high, low = lane == mine_ref[0], lane == mine_ref[0] + count

    @pl.when(step == 0)
    def _():
        xs_ref[...] = x_ref[:, :, :width]

        @pl.when(pl.program_id(0) == 0)
        def _():
            c_ref[...] = near_ref[...]

        @pl.when(pl.program_id(0) > 0)
        def _():
            c_ref[...] = far_ref[...]
        gates = x_ref[:, :, width:].reshape(rows, extra).astype(f32)
        gate_scr[...] = jnp.sum(jnp.where(high | low, gates, 0.0), axis=-1, keepdims=True)
        out_acc[...] = jnp.zeros_like(out_acc)
        back_acc[...] = jnp.zeros_like(back_acc)
        dot_scr[...] = jnp.zeros_like(dot_scr)

    x = x_ref[:, :, :width].reshape(rows, width)
    c = c_ref[...].reshape(rows, width)
    gate = gate_scr[...]
    wg, wu, wd = wg_ref[...], wu_ref[...], wd_ref[...]
    gate_pre, up_pre = dot_nn(x, wg), dot_nn(x, wu)
    sig = jax.nn.sigmoid(gate_pre)
    hidden = (gate_pre * sig * up_pre).astype(bf16)
    out_acc[...] += dot_nn(hidden, wd)
    plain = dot_nt(c, wd)
    wide = hidden.astype(f32)
    dot_scr[...] += jnp.sum(wide * plain, axis=-1, keepdims=True)
    hid_ref[...] = (wide * gate).astype(bf16).reshape(hid_ref.shape)
    hidden_grad = plain * gate
    gate_grad = (hidden_grad * up_pre * sig * (1.0 + gate_pre * (1.0 - sig))).astype(bf16)
    up_grad = (hidden_grad * gate_pre * sig).astype(bf16)
    gp_ref[...] = gate_grad.reshape(gp_ref.shape)
    up_ref[...] = up_grad.reshape(up_ref.shape)
    back_acc[...] += dot_nt(gate_grad, wg) + dot_nt(up_grad, wu)

    @pl.when(step == pl.num_programs(1) - 1)
    def _():
        dots = dot_scr[...]
        coarse = dots.astype(bf16).astype(f32)
        lanes = jnp.where(high, coarse, jnp.where(low, dots - coarse, 0.0)).astype(bf16)
        back_ref[:, :, :width] = back_acc[...].astype(bf16).reshape(c_ref.shape)
        back_ref[:, :, width:] = lanes.reshape(per_plane, capacity, extra)
        out_ref[...] = (out_acc[...] * gate).astype(bf16).reshape(out_ref.shape)


def experts(mine, x, near, far, wg, wu, wd, base, planes, count, kept):
    per_plane, blocks, capacity, wide = x.shape
    width = near.shape[3]
    halves, _, hidden = wg.shape
    rows = per_plane * capacity
    saved = jax.ShapeDtypeStruct((per_plane, planes, capacity, width), bf16)
    thin = jax.ShapeDtypeStruct((per_plane, planes, capacity, halves * hidden), bf16)
    moved = pl.BlockSpec((per_plane, None, capacity, wide), lambda i, f, s: (0, i, 0, 0))
    saved_spec = pl.BlockSpec((per_plane, None, capacity, width), lambda i, f, s: (0, base + i, 0, 0))
    thin_spec = pl.BlockSpec((per_plane, None, capacity, hidden), lambda i, f, s: (0, base + i, 0, f))
    carried = 0 if kept is None else len(kept)
    skip = base - 1 if base else 0
    cot_specs = [
        pl.BlockSpec((per_plane, None, capacity, width), lambda i, f, s: (0, 0, 0, 0)),
        pl.BlockSpec(
            (per_plane, None, capacity, width),
            lambda i, f, s: (0, jnp.maximum(skip + i - 1, 0), 0, 0),
        ),
    ]
    result = pl.pallas_call(
        functools.partial(expert_kernel, count, carried),
        out_shape=(
            jax.ShapeDtypeStruct(x.shape, bf16),
            jax.ShapeDtypeStruct((per_plane, blocks, capacity, width), bf16),
            saved,
            saved,
            thin,
            thin,
            thin,
        ),
        grid_spec=pltpu.PrefetchScalarGridSpec(
            num_scalar_prefetch=1,
            grid=(blocks, halves),
            in_specs=[
                moved,
                *cot_specs,
                pl.BlockSpec((None, width, hidden), lambda i, f, s: (f, 0, 0)),
                pl.BlockSpec((None, width, hidden), lambda i, f, s: (f, 0, 0)),
                pl.BlockSpec((None, hidden, width), lambda i, f, s: (f, 0, 0)),
            ]
            + [pl.BlockSpec(memory_space=pl.ANY)] * carried,
            out_specs=(
                moved,
                pl.BlockSpec((per_plane, None, capacity, width), lambda i, f, s: (0, i, 0, 0)),
                saved_spec,
                saved_spec,
                thin_spec,
                thin_spec,
                thin_spec,
            ),
            scratch_shapes=[
                pltpu.VMEM((rows, width), f32),
                pltpu.VMEM((rows, width), f32),
                pltpu.VMEM((rows, 1), f32),
                pltpu.VMEM((rows, 1), f32),
            ],
        ),
        input_output_aliases={7 + i: 2 + i for i in range(carried)},
        compiler_params=params(2, 60),
        cost_estimate=estimate(
            flops=12 * blocks * rows * width * hidden * halves,
            bytes_accessed=10 * blocks * rows * width + 6 * blocks * width * hidden * halves,
            transcendentals=blocks * rows * hidden * halves,
        ),
        name="experts",
    )(mine, x, near, far, wg, wu, wd, *(kept or ()))
    return result[0], result[1], result[2:]


def gram_kernel(plus, left_ref, right_ref, *refs):
    total = dot_tn(left_ref[...], right_ref[...])
    if plus:
        total = total + refs[0][...]
    refs[-1][...] = total.astype(refs[-1].dtype)


def gram(left, right, left_cols, right_cols, dtype, plus=None):
    rows = left.shape[0]
    left_at, left_count = left_cols
    right_at, right_count = right_cols
    tall = min(left_count, 256)
    wide = min(right_count, 1024)
    out_spec = pl.BlockSpec((tall, wide), lambda j, i: (i, j))
    return pl.pallas_call(
        functools.partial(gram_kernel, plus is not None),
        out_shape=jax.ShapeDtypeStruct((left_count, right_count), dtype),
        grid=(right_count // wide, left_count // tall),
        in_specs=[
            pl.BlockSpec((rows, tall), lambda j, i: (0, left_at // tall + i)),
            pl.BlockSpec((rows, wide), lambda j, i: (0, right_at // wide + j)),
        ]
        + [out_spec] * (plus is not None),
        out_specs=out_spec,
        compiler_params=params(2, 48),
        cost_estimate=estimate(
            flops=2 * rows * left_count * right_count,
            bytes_accessed=2 * rows * (left_count + right_count) + 4 * left_count * right_count,
            transcendentals=0,
        ),
        name="gram",
    )(left, right, *(() if plus is None else (plus,)))


def project_kernel(plus, core_ref, rows_ref, weights_ref, *refs):
    total = dot_nt(rows_ref[...], weights_ref[...])
    if plus:
        total = total + refs[0][...].astype(f32)
    refs[-1][...] = total.astype(bf16)


def project_back(core, rows, weights, tok_rows, plus=None):
    count, depth = rows.shape
    width = weights.shape[0]
    chips = count // tok_rows // 2
    out_spec = pl.BlockSpec((tok_rows, width), lambda i, s: (i, 0))
    return pl.pallas_call(
        functools.partial(project_kernel, plus is not None),
        out_shape=jax.ShapeDtypeStruct((chips * tok_rows, width), bf16),
        grid_spec=pltpu.PrefetchScalarGridSpec(
            num_scalar_prefetch=1,
            grid=(chips,),
            in_specs=[
                pl.BlockSpec((tok_rows, depth), lambda i, s: (2 * i + s[0], 0)),
                pl.BlockSpec((width, depth), lambda i, s: (0, 0)),
            ]
            + [out_spec] * (plus is not None),
            out_specs=out_spec,
        ),
        compiler_params=params(1, 40),
        cost_estimate=estimate(
            flops=count * depth * width,
            bytes_accessed=2 * width * depth + count * depth + count * width,
            transcendentals=0,
        ),
        name="project_back",
    )(core, rows, weights, *(() if plus is None else (plus,)))


def after(value, *others):
    return lax.optimization_barrier((value,) + others)[0]


def body(
    hidden_in,
    out_cotangent,
    segment_number,
    expert_routes,
    pair_order,
    norm_gain,
    query_weight,
    key_weight,
    value_weight,
    output_weight,
    query_gain,
    key_gain,
    ffn_norm_gain,
    router_weight,
    expert_gate,
    expert_up,
    expert_down,
):
    tok_rows, width = hidden_in.shape
    devices = lax.axis_size(AXIS)
    members = max(1, SEQ_MIN // tok_rows)
    planes = devices // members
    per_plane = members // 2
    expert_count = devices // 2
    capacity = tok_rows * TOPK // expert_count
    heads = width // HD // members
    head_width = heads * HD
    own_rows = norm_gain.shape[0]
    seq = members * tok_rows
    me = lax.axis_index(AXIS)
    plane, member = me // members, me % members
    mine = (me // 2).astype(jnp.int32).reshape(1)
    first = (plane * per_plane).astype(jnp.int32)
    places = (plane ^ jnp.arange(planes, dtype=jnp.int32)).astype(jnp.int32)
    counted = jnp.concatenate([first[None], jnp.arange(planes, dtype=jnp.int32)])
    halfway = -(-planes // 2)
    chunks = [part for part in (range(halfway, planes), range(halfway)) if len(part)]

    def placed(part):
        return jnp.concatenate([first[None], places[part.start : part.stop]])

    plane_groups = [[g * members + j for j in range(members)] for g in range(planes)]
    stack_groups = [[g * members + j for g in range(planes)] for j in range(members)]
    core_groups = [
        [g * members + 2 * c + h for c in range(per_plane)] for g in range(planes) for h in (0, 1)
    ]

    def exchange(value, groups=None):
        return lax.all_to_all(
            value, AXIS, split_axis=0, concat_axis=0, tiled=True, axis_index_groups=groups
        )

    def gather(value, groups=None):
        return lax.all_gather(value, AXIS, axis=0, tiled=True, axis_index_groups=groups)

    def flip(value, bits):
        if bits == 0:
            return value
        return lax.ppermute(value, AXIS, [(i, i ^ bits) for i in range(devices)])

    def to_core(value):
        return flip(value, 1)

    def to_plane(value, d):
        return flip(value, members * d)

    def spread(value, *others):
        found = {0: value}
        for d in range(1, planes):
            lowest = d & -d
            source = found[d ^ lowest]
            found[d] = to_plane(source if d == lowest else after(source, *others), lowest)
        return [found[d] for d in range(planes)]

    def fold(sums, *others):
        bit = 1
        while bit < len(sums):
            for d in range(len(sums)):
                if d & bit and not d & (bit - 1):
                    came = to_plane(sums[d].astype(bf16), bit)
                    if d == bit:
                        came = after(came, *others)
                    sums[d ^ bit] = sums[d ^ bit].astype(f32) + came.astype(f32)
            bit *= 2
        return sums[0]

    wire, core_op = [], []

    def on_wire(value, groups):
        came = exchange(after(value, *wire[-1:]), groups)
        wire.append(came)
        return came

    def to_chips(value):
        return on_wire(value, core_groups)

    def in_turn(value):
        return after(value, *core_op[-1:])

    def ran(value):
        core_op.append(value)
        return value

    columns = jnp.concatenate(
        [w.reshape(own_rows, members, head_width) for w in (query_weight, key_weight, value_weight)],
        axis=2,
    )
    slots = block_slots(expert_routes, pair_order, expert_count)
    columns = on_wire(
        after(columns, slots).transpose(1, 0, 2).reshape(members * own_rows, 3 * head_width), plane_groups
    )
    stacked = [to_plane(after(output_weight, slots), d) for d in range(planes)]
    cosine, sine = rope_tables(seq)
    weights = spread(after(columns, *stacked), cosine, sine)
    slots = [to_plane(after(slots, *weights) if d else slots, d) for d in range(planes)]
    output_rows = jnp.zeros((planes * own_rows, width), bf16)
    for d, rows in enumerate(stacked):
        output_rows = lax.dynamic_update_slice_in_dim(output_rows, rows, places[d] * own_rows, 0)
    rows_all = gather(hidden_in, plane_groups)

    pieces = (
        router_weight.reshape(-1),
        norm_gain,
        ffn_norm_gain,
        query_gain,
        key_gain,
        segment_number.astype(bf16),
    )
    packed = jnp.concatenate(pieces)
    length = packed.shape[0]
    padded = -(-length // 128) * 128
    packed = jnp.pad(packed, (0, padded - length))
    packed = on_wire(jnp.broadcast_to(packed[None], (devices, padded)), None)
    small = []
    at = 0
    for piece in pieces:
        small.append(packed[:, at : at + piece.shape[0]])
        at += piece.shape[0]
    router_full = small[0].reshape(width, expert_count)
    gain_one = small[1].reshape(1, width).astype(f32)
    gain_two = small[2].reshape(1, width).astype(f32)
    gain_q = small[3].reshape(1, HD).astype(f32)
    gain_k = small[4].reshape(1, HD).astype(f32)
    segments = lax.dynamic_slice_in_dim(small[5], plane * members, members, 0).astype(f32)
    seg_row, seg_col = segments.reshape(1, seq), segments.reshape(seq, 1)
    seg_blocks = segments.reshape(seq // ROWS, ROWS)
    seg_first, seg_last = seg_blocks[:, 0], seg_blocks[:, -1]
    low = jnp.sum((seg_last[None, :] < seg_first[:, None]).astype(jnp.int32), axis=1)
    high = jnp.sum((seg_first[None, :] <= seg_last[:, None]).astype(jnp.int32), axis=1)

    cot_own = dispatch(counted, slots[0][None], out_cotangent[None], per_plane, capacity)
    cot_first = [to_chips(cot_own)]
    output_full = gather(after(output_rows, columns), plane_groups)
    slot_list, slots = slots, jnp.stack(slots)
    cot_rows = {0: out_cotangent}
    top = planes // 2
    early, late = [], []
    if planes > 1:
        cot_rows[top] = to_plane(after(out_cotangent, *weights), top)
        early.append(cot_rows[top])
    for d in range(1, planes):
        if d != top:
            lowest = d & -d
            start = after(out_cotangent, *early) if d == lowest else cot_rows[d ^ lowest]
            cot_rows[d] = to_plane(start, lowest)
            late.append(cot_rows[d])

    halves = lambda w: jnp.concatenate([w, to_core(w)], axis=0)
    wg, wu, wd = halves(expert_gate), halves(expert_up), halves(expert_down)

    act_one, pre, rot, ordered = qkv_project(
        places, rows_all, gain_one, weights, gain_q, gain_k, cosine, sine, heads
    )
    out_wide, out_heads, lse = attention(rot, seg_col, seg_row, low, high, heads)
    out_low = on_wire(after(out_heads, *slot_list, *early), plane_groups)
    if planes > 1:
        rows = after(cot_rows[top], out_heads)
        sent = dispatch(counted, slots[top : top + 1], rows[None], per_plane, capacity)
        cot_first.append(to_chips(sent))
    out_low = out_low.reshape(members, tok_rows, head_width).transpose(1, 0, 2)
    out_low = out_low.reshape(tok_rows, planes, members, own_rows).transpose(0, 2, 1, 3)
    out_low = out_low.reshape(tok_rows, width)
    tokens = hidden_in.astype(f32)
    cotangent = out_cotangent.astype(f32)
    middle = tokens + dot_nn(out_low, output_full)
    inverse_two = lax.rsqrt(jnp.mean(middle * middle, axis=-1, keepdims=True) + norm_eps)
    act_two = (middle * inverse_two * gain_two).astype(bf16)

    logits = dot_nn(act_two, router_full)
    expert_ids = jnp.arange(expert_count, dtype=jnp.int32)
    routed = jnp.any(expert_routes[:, :, None] == expert_ids[None, None, :], axis=1)
    logits = jnp.where(routed, logits, masked_score)
    gates = jnp.where(routed, jnp.exp(logits - jnp.max(logits, axis=1, keepdims=True)), 0.0)
    gates = gates / jnp.sum(gates, axis=1, keepdims=True)
    coarse = lax.reduce_precision(gates, 8, 7)
    extra = -(-2 * expert_count // 128) * 128
    act_wide = jnp.concatenate(
        [
            act_two,
            coarse.astype(bf16),
            (gates - coarse).astype(bf16),
            jnp.zeros((tok_rows, extra - 2 * expert_count), bf16),
        ],
        axis=1,
    )

    act_wide = after(act_wide, *late, *cot_first)
    act_all = gather(act_wide, stack_groups).reshape(planes, tok_rows, -1)
    others = [d for d in range(1, planes) if d != top]
    cot_far = cot_first[0]
    if others:
        far = jnp.stack([after(cot_rows[d], act_wide) for d in others])
        far_slots = jnp.stack([slots[d] for d in others])
        cot_far = to_chips(
            ran(dispatch(counted[: len(others) + 1], far_slots, far, per_plane, capacity))
        )

    act = []
    for part in chunks:
        own_slots = slots[part.start : part.stop]
        rows = after(in_turn(act_all), wg, wu, wd)
        sent = dispatch(placed(part), own_slots, rows, per_plane, capacity)
        act.append(to_chips(ran(sent)))
    kept, back, outs = None, [], []
    for part, rows in zip(chunks, act):
        sent, out, kept = experts(
            mine,
            in_turn(rows),
            cot_first[0 if part.start == 0 else 1],
            cot_far,
            wg,
            wu,
            wd,
            part.start,
            planes,
            expert_count,
            kept,
        )
        back.append(to_chips(ran(sent)))
        outs.append(out)
    x_all, c_all, hid_all, gp_all, up_all = kept

    hidden = expert_gate.shape[2]
    flat = lambda value: value.reshape(-1, value.shape[3])
    sides = (
        (flat(x_all), flat(gp_all), 1),
        (flat(x_all), flat(up_all), 1),
        (flat(hid_all), flat(c_all), 0),
    )

    def half(side, which, plus=None):
        left, right, split = side
        cut, whole = (which * hidden, hidden), (0, width)
        cols = (whole, cut) if split else (cut, whole)
        return ran(gram(in_turn(left), right, *cols, f32, plus))

    passed = []

    def home(part, rows):
        sums = {}
        for d in sorted(part, key=lambda d: (-(d & 1), d)):
            sums[d] = ran(combine(first[None], slots[d], in_turn(rows), d - part.start))
        bit = 1
        while bit < len(part):
            for d in part:
                if d & bit and not d & (bit - 1):
                    came = to_plane(sums[d].astype(bf16), bit)
                    passed.append(came)
                    sums[d ^ bit] = sums[d ^ bit].astype(f32) + came.astype(f32)
            bit *= 2
        return sums[part.start]

    back_sum = home(chunks[0], back[0])
    theirs = [half(side, 1) for side in sides[:2]]
    if len(chunks) > 1:
        back_sum = ran(in_turn(back_sum.astype(bf16)))
        back_sum = to_plane(back_sum, top)
    theirs.append(half(sides[2], 1))
    if len(chunks) > 1:
        back_sum = back_sum.astype(f32) + home(chunks[1], back[1])
    outs[0] = to_chips(outs[0])

    expert_in_grad = back_sum[:, :width]
    gate_grad = (
        back_sum[:, width : width + expert_count]
        + back_sum[:, width + expert_count : width + 2 * expert_count]
    )
    select_grad = gates * (gate_grad - jnp.sum(gates * gate_grad, axis=1, keepdims=True))
    logit_grad = select_grad.astype(bf16)
    grad_router = dot_tn(act_two, logit_grad)
    act_two_grad = expert_in_grad + dot_nt(logit_grad, router_full)
    weighted = act_two_grad * gain_two
    grad_gain_two = jnp.sum(act_two_grad * middle * inverse_two, axis=0)
    middle_grad = (
        cotangent
        + inverse_two * weighted
        - middle * inverse_two**3 * jnp.mean(weighted * middle, axis=-1, keepdims=True)
    )
    middle_low = middle_grad.astype(bf16)

    out_grad = dot_nt(middle_low, output_full).astype(bf16)
    out_grad = out_grad.reshape(tok_rows, members, planes, own_rows).transpose(0, 2, 1, 3)
    out_grad = out_grad.reshape(tok_rows, members, head_width).transpose(1, 0, 2)
    out_grad = out_grad.reshape(seq, head_width)
    ran(out_grad)
    theirs = [to_core(after(grad, out_grad)) for grad in theirs]
    out_grad = on_wire(out_grad, plane_groups)
    mixture = home(chunks[0], outs[0]).astype(bf16)
    dqkv, grad_gains = attention_back(
        rot,
        in_turn(out_grad),
        out_wide,
        lse,
        seg_col,
        seg_row,
        low,
        high,
        pre,
        gain_q,
        gain_k,
        cosine,
        sine,
        heads,
    )
    ran(dqkv)
    if len(chunks) > 1:
        near_sum = home(chunks[1], to_chips(outs[1]))
        done = (*core_op[-2:], mixture, *theirs)
        dqkv, grad_gains = after(dqkv, *done), after(grad_gains, *done)
    middle_all = gather(after(middle_low, dqkv), plane_groups)

    sums = (
        grad_router.reshape(devices, -1),
        grad_gain_two.reshape(devices, -1),
        grad_gains[0].reshape(devices, -1),
        grad_gains[1].reshape(devices, -1),
    )
    packed = jnp.concatenate(sums, axis=1)
    length = packed.shape[1]
    padded = -(-length // 128) * 128
    packed = jnp.pad(packed, ((0, 0), (0, padded - length)))

    core = (me % 2).astype(jnp.int32).reshape(1)
    given = project_back(1 - core, dqkv, ordered, tok_rows)
    part = gram(after(act_one, given), dqkv, (0, width), (0, 3 * head_width), bf16)
    part = part.reshape(planes, members * own_rows, 3 * head_width)
    shares = [lax.dynamic_index_in_dim(part, places[d], 0, False) for d in range(planes)]
    mixture = to_plane(mixture, top) if len(chunks) > 1 else mixture
    given = after(to_core(given), *shares, mixture, *passed[-1:])
    act_one_grad = project_back(core, dqkv, ordered, tok_rows, given)
    ran(act_one_grad)
    output_part = ran(gram(out_heads, in_turn(middle_all), (0, head_width), (0, width), bf16))
    grad_gate, grad_up, grad_down = (
        half(side, 0, other) for side, other in zip(sides, theirs)
    )
    shares = [after(share, act_one_grad) for share in shares]
    taken = fold(shares, grad_gate, grad_up, grad_down).astype(bf16)
    act_one_grad = on_wire(act_one_grad, core_groups)

    output_part = lax.psum_scatter(
        output_part, AXIS, scatter_dimension=0, tiled=True, axis_index_groups=stack_groups
    )
    to_owner = [
        (g * members + j, j * planes + g) for g in range(planes) for j in range(members)
    ]
    mixture = mixture.astype(f32)
    if len(chunks) > 1:
        mixture = mixture + near_sum
    packed, act_one_grad, mixture, grad_gate, grad_up, grad_down = lax.optimization_barrier(
        (packed, act_one_grad, mixture, grad_gate, grad_up, grad_down)
    )
    layer_out = (middle + mixture).astype(bf16)
    packed = exchange(packed)
    taken, packed, output_part = lax.optimization_barrier((taken, packed, output_part))
    grad_output = lax.ppermute(output_part, AXIS, to_owner)
    part = exchange(taken, plane_groups).reshape(members, own_rows, 3, head_width)
    part = part.transpose(2, 1, 0, 3).reshape(3, own_rows, width).astype(f32)
    grad_query, grad_key, grad_value = part[0], part[1], part[2]
    act_one_grad = act_one_grad.reshape(per_plane, tok_rows, width)
    act_one_grad = jnp.sum(act_one_grad.astype(f32), axis=0)

    inverse_one = lax.rsqrt(jnp.mean(tokens * tokens, axis=-1, keepdims=True) + norm_eps)
    weighted = act_one_grad * gain_one
    grad_hidden = (
        middle_grad
        + inverse_one * weighted
        - tokens * inverse_one**3 * jnp.mean(weighted * tokens, axis=-1, keepdims=True)
    )
    grad_gain_one = (
        jnp.sum(
            grad_query * query_weight.astype(f32)
            + grad_key * key_weight.astype(f32)
            + grad_value * value_weight.astype(f32),
            axis=1,
        )
        / norm_gain.astype(f32)
    )

    summed = jnp.sum(packed, axis=0)
    at, tiny = 0, []
    for piece in sums:
        tiny.append(summed[at : at + piece.shape[1]])
        at += piece.shape[1]

    return (
        layer_out,
        grad_hidden,
        grad_gain_one,
        grad_query,
        grad_key,
        grad_value,
        grad_output.astype(f32),
        tiny[2],
        tiny[3],
        tiny[1],
        tiny[0].reshape(own_rows, expert_count),
        grad_gate[None],
        grad_up[None],
        grad_down[None],
    )


def solution(mesh):
    row, mat, cube = P(AXIS), P(AXIS, None), P(AXIS, None, None)
    return jax.shard_map(
        body,
        mesh=mesh,
        in_specs=(mat, mat, row, mat, mat, row, mat, mat, mat, mat, row, row, row, mat)
        + (cube,) * 3,
        out_specs=(mat, mat, row, mat, mat, mat, mat, row, row, row, mat) + (cube,) * 3,
        check_vma=False,
    )
```

```python
import functools
import math

import jax
import jax.numpy as jnp
from jax import lax
from jax.experimental import pallas as pl
from jax.experimental.pallas import tpu as pltpu
from jax.sharding import PartitionSpec as P

HD = 128
TOPK = 8
SEQ_MIN = 2048
ROWS = 256
SHARE = 32

norm_eps = 1e-05
head_eps = 1e-06
rope_base = 10000.0
masked_score = -1e30
absent_slot = 4096.0

AXIS = "fsdp"
f32 = jnp.float32
bf16 = jnp.bfloat16
MIB = 1 << 20


def dot_nt(left, right):
    return lax.dot_general(left, right, (((1,), (1,)), ((), ())), preferred_element_type=f32)


def dot_tn(left, right):
    return lax.dot_general(left, right, (((0,), (0,)), ((), ())), preferred_element_type=f32)


def dot_nn(left, right):
    return lax.dot_general(left, right, (((1,), (0,)), ((), ())), preferred_element_type=f32)


def params(steps, mib):
    return pltpu.CompilerParams(
        dimension_semantics=("arbitrary",) * steps, vmem_limit_bytes=mib * MIB
    )


def estimate(flops, bytes_accessed, transcendentals):
    return pl.CostEstimate(
        flops=flops // SHARE, bytes_accessed=bytes_accessed // SHARE, transcendentals=transcendentals // SHARE
    )


def rope_tables(count):
    half_width = HD // 2
    frequency = jnp.exp(-math.log(rope_base) * 2.0 * jnp.arange(half_width, dtype=f32) / HD)
    angles = jnp.arange(count, dtype=f32)[:, None] * frequency[None, :]
    cosine, sine = jnp.cos(angles), jnp.sin(angles)
    return jnp.concatenate([cosine, cosine], axis=-1), jnp.concatenate([-sine, sine], axis=-1)


def slots_kernel(expert_count, routes_ref, order_ref, slots_ref):
    tok_rows = routes_ref.shape[0]
    pair_count = order_ref.shape[1]
    order = order_ref[...]
    shift = TOPK.bit_length() - 1
    token_of = lax.shift_right_logical(order, jnp.full_like(order, shift))
    route_of = order & (TOPK - 1)
    token_iota = lax.broadcasted_iota(jnp.int32, (tok_rows, pair_count), 0)
    token_hot = jnp.where(token_iota == token_of, 1.0, 0.0).astype(bf16)
    place = lax.broadcasted_iota(jnp.int32, (TOPK, pair_count), 1)
    chosen = lax.broadcasted_iota(jnp.int32, (TOPK, pair_count), 0) == route_of
    high = lax.shift_right_logical(place, jnp.full_like(place, 8)).astype(f32)
    low = (place & 255).astype(f32)
    digits = jnp.concatenate([jnp.where(chosen, high, 0.0), jnp.where(chosen, low, 0.0)], axis=0)
    found = dot_nt(token_hot, digits.astype(bf16))
    rank = found[:, :TOPK] * 256.0 + found[:, TOPK:]
    routes = routes_ref[...]
    lanes = -(-expert_count // 128) * 128
    expert_iota = lax.broadcasted_iota(jnp.int32, (tok_rows, lanes), 1)
    never = 1e9
    by_expert = jnp.full((tok_rows, lanes), never, f32)
    for k in range(TOPK):
        by_expert = jnp.where(expert_iota == routes[:, k : k + 1], rank[:, k : k + 1], by_expert)
    turned = by_expert.T
    for e in range(expert_count):
        mine = turned[e : e + 1, :]
        earlier = jnp.where(by_expert[:, e : e + 1] < mine, 1.0, 0.0)
        count = jnp.sum(earlier, axis=0, keepdims=True)
        slots_ref[e : e + 1, :] = jnp.where(mine < never, count, absent_slot)


def block_slots(routes, order, expert_count):
    tok_rows = routes.shape[0]
    return pl.pallas_call(
        functools.partial(slots_kernel, expert_count),
        out_shape=jax.ShapeDtypeStruct((expert_count, tok_rows), f32),
        compiler_params=pltpu.CompilerParams(vmem_limit_bytes=32 * MIB),
        name="block_slots",
    )(routes, order)


def slot_hot(slots_ref, expert, capacity):
    slot_row = slots_ref[pl.ds(expert, 1), :]
    slot_iota = lax.broadcasted_iota(jnp.int32, (capacity, slot_row.shape[1]), 0).astype(f32)
    return jnp.where(slot_iota == slot_row, 1.0, 0.0).astype(bf16)


def plane_hot(slots_ref, first, shape):
    return jnp.concatenate([slot_hot(slots_ref, first + r, shape[1]) for r in range(shape[0])])


def dispatch_kernel(at_ref, slots_ref, rows_ref, out_ref):
    hot = plane_hot(slots_ref, at_ref[0], out_ref.shape)
    out_ref[...] = dot_nn(hot, rows_ref[...]).astype(bf16).reshape(out_ref.shape)


def dispatch(at, slots, rows, per_plane, capacity):
    blocks, experts, tok_rows = slots.shape
    width = rows.shape[2]
    slot_rows = per_plane * capacity
    return pl.pallas_call(
        dispatch_kernel,
        out_shape=jax.ShapeDtypeStruct((per_plane, blocks, capacity, width), bf16),
        grid_spec=pltpu.PrefetchScalarGridSpec(
            num_scalar_prefetch=1,
            grid=(blocks,),
            in_specs=[
                pl.BlockSpec((None, experts, tok_rows), lambda i, s: (i, 0, 0)),
                pl.BlockSpec((None, tok_rows, width), lambda i, s: (s[1 + i], 0, 0)),
            ],
            out_specs=pl.BlockSpec((per_plane, None, capacity, width), lambda i, s: (0, i, 0, 0)),
        ),
        compiler_params=params(1, 40),
        cost_estimate=estimate(
            flops=2 * blocks * slot_rows * tok_rows * width,
            bytes_accessed=2 * blocks * (slot_rows + tok_rows) * width,
            transcendentals=0,
        ),
        name="dispatch",
    )(at, slots, rows)


def combine_kernel(first_ref, slots_ref, rows_ref, out_ref):
    hot = plane_hot(slots_ref, first_ref[0], rows_ref.shape)
    rows = rows_ref[...].reshape(hot.shape[0], rows_ref.shape[2])
    out_ref[...] = dot_tn(hot, rows).astype(bf16)


def combine(first, slots, rows, block):
    experts, tok_rows = slots.shape
    per_plane, _, capacity, width = rows.shape
    slot_rows = per_plane * capacity
    return pl.pallas_call(
        combine_kernel,
        out_shape=jax.ShapeDtypeStruct((tok_rows, width), bf16),
        grid_spec=pltpu.PrefetchScalarGridSpec(
            num_scalar_prefetch=1,
            grid=(1,),
            in_specs=[
                pl.BlockSpec((experts, tok_rows), lambda i, s: (0, 0)),
                pl.BlockSpec((per_plane, None, capacity, width), lambda i, s: (0, block, 0, 0)),
            ],
            out_specs=pl.BlockSpec((tok_rows, width), lambda i, s: (0, 0)),
        ),
        compiler_params=params(1, 40),
        cost_estimate=estimate(
            flops=2 * slot_rows * tok_rows * width,
            bytes_accessed=2 * (slot_rows + tok_rows) * width,
            transcendentals=0,
        ),
        name="combine",
    )(first, slots, rows)


def qkv_kernel(heads, planes, at_ref, x_ref, gain_ref, *refs):
    w_refs = refs[:planes]
    gq_ref, gk_ref, cos_ref, sin_ref, act_ref, pre_ref, rot_ref, all_ref = refs[planes:]
    depth = w_refs[0].shape[0]

    @pl.when(pl.program_id(0) == 0)
    def _():
        for d in range(planes):
            place = pl.ds(pl.multiple_of(at_ref[d] * depth, depth), depth)
            all_ref[place, :] = w_refs[d][...]

    x = x_ref[...].astype(f32)
    inverse = lax.rsqrt(jnp.mean(x * x, axis=-1, keepdims=True) + norm_eps)
    act = (x * inverse * gain_ref[...]).astype(bf16)
    act_ref[...] = act
    y = dot_nn(act, all_ref[...])
    cosine, sine = cos_ref[...], sin_ref[...]
    for part, gain in enumerate((gq_ref[...], gk_ref[...])):
        for h in range(heads):
            at = (part * heads + h) * HD
            u = y[:, at : at + HD]
            pre_ref[:, at : at + HD] = u
            n = u * lax.rsqrt(jnp.mean(u * u, axis=-1, keepdims=True) + head_eps) * gain
            rot_ref[:, at : at + HD] = (n * cosine + pltpu.roll(n, HD // 2, 1) * sine).astype(bf16)
    at = 2 * heads * HD
    rot_ref[:, at:] = y[:, at:].astype(bf16)


def qkv_project(places, rows, gain, weights, gain_q, gain_k, cosine, sine, heads):
    count, width = rows.shape
    planes = len(weights)
    depth, out_width = weights[0].shape
    pre_width = 2 * heads * HD
    tall = min(2 * ROWS, count)
    whole = lambda i, s: (0, 0)
    block = lambda i, s: (i, 0)
    return pl.pallas_call(
        functools.partial(qkv_kernel, heads, planes),
        out_shape=(
            jax.ShapeDtypeStruct((count, width), bf16),
            jax.ShapeDtypeStruct((count, pre_width), f32),
            jax.ShapeDtypeStruct((count, out_width), bf16),
            jax.ShapeDtypeStruct((width, out_width), bf16),
        ),
        grid_spec=pltpu.PrefetchScalarGridSpec(
            num_scalar_prefetch=1,
            grid=(count // tall,),
            in_specs=[
                pl.BlockSpec((tall, width), block),
                pl.BlockSpec((1, width), whole),
            ]
            + [pl.BlockSpec((depth, out_width), whole)] * planes
            + [
                pl.BlockSpec((1, HD), whole),
                pl.BlockSpec((1, HD), whole),
                pl.BlockSpec((tall, HD), block),
                pl.BlockSpec((tall, HD), block),
            ],
            out_specs=(
                pl.BlockSpec((tall, width), block),
                pl.BlockSpec((tall, pre_width), block),
                pl.BlockSpec((tall, out_width), block),
                pl.BlockSpec((width, out_width), whole),
            ),
        ),
        compiler_params=params(1, 56),
        cost_estimate=estimate(
            flops=2 * count * width * out_width,
            bytes_accessed=4 * count * width + 2 * width * out_width + 6 * count * out_width,
            transcendentals=0,
        ),
        name="qkv_project",
    )(places, rows, gain, *weights, gain_q, gain_k, cosine, sine)


def head_columns(heads):
    return [slice(h * HD, (h + 1) * HD) for h in range(heads)]


def attn_kernel(
    scale, low_ref, high_ref, q_ref, k_ref, v_ref, sq_ref, sk_ref, o_ref, ol_ref, lse_ref, s_scr
):
    block = pl.program_id(0)
    low, high = low_ref[block], high_ref[block]
    columns = head_columns(lse_ref.shape[1])
    seg_q = sq_ref[...]
    half = ROWS // 2

    def scores(kb, tops):
        at = pl.ds(pl.multiple_of(kb * ROWS, ROWS), ROWS)
        same = seg_q == sk_ref[:, at]
        found = []
        for h, cut in enumerate(columns):
            s = dot_nt(q_ref[:, cut], k_ref[at, cut]) * scale
            s = jnp.where(same, s, masked_score)
            s_scr[h, :, at] = s
            found.append(jnp.maximum(tops[h], jnp.maximum(s[:, :half], s[:, half:])))
        return tuple(found)

    lowest = jnp.full((ROWS, half), masked_score, f32)
    tops = lax.fori_loop(low, high, scores, (lowest,) * len(columns))
    tops = [jnp.max(top, axis=-1, keepdims=True) for top in tops]

    def weigh(kb, carry):
        at = pl.ds(pl.multiple_of(kb * ROWS, ROWS), ROWS)
        found = []
        for h, cut in enumerate(columns):
            total, acc = carry[h]
            p = jnp.exp(s_scr[h, :, at] - tops[h])
            acc = acc + dot_nn(p.astype(bf16), v_ref[at, cut])
            found.append((total + (p[:, :half] + p[:, half:]), acc))
        return tuple(found)

    start = (jnp.zeros((ROWS, half), f32), jnp.zeros((ROWS, HD), f32))
    sums = lax.fori_loop(low, high, weigh, (start,) * len(columns))
    for h, cut in enumerate(columns):
        total = jnp.sum(sums[h][0], axis=-1, keepdims=True)
        out = sums[h][1] / total
        o_ref[:, cut] = out
        ol_ref[:, cut] = out.astype(bf16)
        lse = jnp.broadcast_to(tops[h] + jnp.log(total), (ROWS, HD)).T
        lse_ref[0, h : h + 1, :] = lse[0:1, :]


def attention(rot, seg_col, seg_row, low, high, heads):
    count = rot.shape[0]
    blocks = count // ROWS
    wide = heads * HD
    scale = HD ** (-0.5)
    mine = lambda i, *s: (i, 0)
    return pl.pallas_call(
        functools.partial(attn_kernel, scale),
        out_shape=(
            jax.ShapeDtypeStruct((count, wide), f32),
            jax.ShapeDtypeStruct((count, wide), bf16),
            jax.ShapeDtypeStruct((blocks, heads, ROWS), f32),
        ),
        grid_spec=pltpu.PrefetchScalarGridSpec(
            num_scalar_prefetch=2,
            grid=(blocks,),
            in_specs=[
                pl.BlockSpec((ROWS, wide), mine),
                pl.BlockSpec((count, wide), lambda i, *s: (0, 1)),
                pl.BlockSpec((count, wide), lambda i, *s: (0, 2)),
                pl.BlockSpec((ROWS, 1), mine),
                pl.BlockSpec((1, count), lambda i, *s: (0, 0)),
            ],
            out_specs=(
                pl.BlockSpec((ROWS, wide), mine),
                pl.BlockSpec((ROWS, wide), mine),
                pl.BlockSpec((1, heads, ROWS), lambda i, *s: (i, 0, 0)),
            ),
            scratch_shapes=[pltpu.VMEM((heads, ROWS, count), f32)],
        ),
        compiler_params=params(1, 40),
        cost_estimate=estimate(
            flops=2 * heads * count * count * HD,
            bytes_accessed=12 * heads * count * HD,
            transcendentals=heads * count * count // 2,
        ),
        name="attention",
    )(low, high, rot, rot, rot, seg_col, seg_row)


def head_back(grad, pre, gain, cosine, sine):
    n = grad * cosine - pltpu.roll(grad, HD // 2, 1) * sine
    inverse = lax.rsqrt(jnp.mean(pre * pre, axis=-1, keepdims=True) + head_eps)
    w = n * gain
    back = inverse * w - pre * inverse**3 * jnp.mean(w * pre, axis=-1, keepdims=True)
    return back, jnp.sum(n * pre * inverse, axis=0, keepdims=True)


def attn_back_kernel(
    scale,
    low_ref,
    high_ref,
    q_ref,
    k_ref,
    v_ref,
    do_ref,
    o_ref,
    lse_ref,
    sq_ref,
    sk_ref,
    qpre_ref,
    kpre_ref,
    gq_ref,
    gk_ref,
    cosq_ref,
    sinq_ref,
    cosk_ref,
    sink_ref,
    grad_ref,
    gain_ref,
    dk_scr,
    dv_scr,
):
    block = pl.program_id(0)
    low, high = low_ref[block], high_ref[block]
    heads = lse_ref.shape[1]
    columns = head_columns(heads)
    wide = heads * HD

    @pl.when(block == 0)
    def _():
        dk_scr[...] = jnp.zeros_like(dk_scr)
        dv_scr[...] = jnp.zeros_like(dv_scr)
        gain_ref[...] = jnp.zeros_like(gain_ref)

    seg_q = sq_ref[...]
    row_dots = [
        jnp.sum((do_ref[:, cut].astype(f32) * o_ref[:, cut]).T, axis=0, keepdims=True)
        for cut in columns
    ]

    def tile(kb, sums):
        at = pl.ds(pl.multiple_of(kb * ROWS, ROWS), ROWS)
        same = sk_ref[at, :] == seg_q
        found = []
        for h, cut in enumerate(columns):
            k, v, q, do = k_ref[at, cut], v_ref[at, cut], q_ref[:, cut], do_ref[:, cut]
            s = dot_nt(k, q) * scale
            p = jnp.where(same, jnp.exp(s - lse_ref[0, h : h + 1, :]), 0.0)
            dp = dot_nt(v, do)
            ds = (p * (dp - row_dots[h])).astype(bf16)
            dv_scr[at, cut] += dot_nn(p.astype(bf16), do)
            dk_scr[at, cut] += dot_nn(ds, q)
            found.append(sums[h] + dot_tn(ds, k))
        return tuple(found)

    sums = lax.fori_loop(low, high, tile, (jnp.zeros((ROWS, HD), f32),) * heads)
    rows = pl.ds(pl.multiple_of(block * ROWS, ROWS), ROWS)
    for h, cut in enumerate(columns):
        back, gain_q = head_back(
            sums[h] * scale, qpre_ref[:, cut], gq_ref[...], cosq_ref[...], sinq_ref[...]
        )
        grad_ref[rows, cut] = back.astype(bf16)
        gain_ref[0:1, :] += gain_q

    @pl.when(block == pl.num_programs(0) - 1)
    def _():
        @pl.loop(0, dk_scr.shape[0] // ROWS)
        def _(i):
            at = pl.ds(pl.multiple_of(i * ROWS, ROWS), ROWS)
            for h, cut in enumerate(columns):
                back, gain_k = head_back(
                    dk_scr[at, cut] * scale,
                    kpre_ref[at, cut],
                    gk_ref[...],
                    cosk_ref[at, :],
                    sink_ref[at, :],
                )
                grad_ref[at, wide + h * HD : wide + (h + 1) * HD] = back.astype(bf16)
                gain_ref[1:2, :] += gain_k
            grad_ref[at, 2 * wide :] = dv_scr[at, :].astype(bf16)


def attention_back(
    rot, grad, out, lse, seg_col, seg_row, low, high, pre, gain_q, gain_k, cosine, sine, heads
):
    count = rot.shape[0]
    blocks = count // ROWS
    scale = HD ** (-0.5)
    wide = heads * HD
    mine = lambda i, *s: (i, 0)
    whole = lambda i, *s: (0, 0)
    return pl.pallas_call(
        functools.partial(attn_back_kernel, scale),
        out_shape=(
            jax.ShapeDtypeStruct((count, 3 * wide), bf16),
            jax.ShapeDtypeStruct((8, HD), f32),
        ),
        grid_spec=pltpu.PrefetchScalarGridSpec(
            num_scalar_prefetch=2,
            grid=(blocks,),
            in_specs=[
                pl.BlockSpec((ROWS, wide), mine),
                pl.BlockSpec((count, wide), lambda i, *s: (0, 1)),
                pl.BlockSpec((count, wide), lambda i, *s: (0, 2)),
                pl.BlockSpec((ROWS, wide), mine),
                pl.BlockSpec((ROWS, wide), mine),
                pl.BlockSpec((1, heads, ROWS), lambda i, *s: (i, 0, 0)),
                pl.BlockSpec((1, ROWS), lambda i, *s: (0, i)),
                pl.BlockSpec((count, 1), whole),
                pl.BlockSpec((ROWS, wide), mine),
                pl.BlockSpec((count, wide), lambda i, *s: (0, 1)),
                pl.BlockSpec((1, HD), whole),
                pl.BlockSpec((1, HD), whole),
                pl.BlockSpec((ROWS, HD), mine),
                pl.BlockSpec((ROWS, HD), mine),
                pl.BlockSpec((count, HD), whole),
                pl.BlockSpec((count, HD), whole),
            ],
            out_specs=(
                pl.BlockSpec((count, 3 * wide), whole),
                pl.BlockSpec((8, HD), whole),
            ),
            scratch_shapes=[pltpu.VMEM((count, wide), f32), pltpu.VMEM((count, wide), f32)],
        ),
        compiler_params=params(1, 56),
        cost_estimate=estimate(
            flops=5 * heads * count * count * HD,
            bytes_accessed=30 * heads * count * HD,
            transcendentals=heads * count * count // 2,
        ),
        name="attention_back",
    )(
        low,
        high,
        rot,
        rot,
        rot,
        grad,
        out,
        lse,
        seg_row,
        seg_col,
        pre,
        pre,
        gain_q,
        gain_k,
        cosine,
        sine,
        cosine,
        sine,
    )


def expert_kernel(count, carried, mine_ref, x_ref, near_ref, far_ref, *refs):
    wg_ref, wu_ref, wd_ref = refs[:3]
    refs = refs[3 + carried :]
    back_ref, out_ref, xs_ref, c_ref, hid_ref, gp_ref, up_ref = refs[:7]
    out_acc, back_acc, gate_scr, dot_scr = refs[7:]
    step = pl.program_id(1)
    per_plane, capacity, width = c_ref.shape
    rows = per_plane * capacity
    extra = x_ref.shape[2] - width
    lane = lax.broadcasted_iota(jnp.int32, (rows, extra), 1)
    high, low = lane == mine_ref[0], lane == mine_ref[0] + count

    @pl.when(step == 0)
    def _():
        xs_ref[...] = x_ref[:, :, :width]

        @pl.when(pl.program_id(0) == 0)
        def _():
            c_ref[...] = near_ref[...]

        @pl.when(pl.program_id(0) > 0)
        def _():
            c_ref[...] = far_ref[...]
        gates = x_ref[:, :, width:].reshape(rows, extra).astype(f32)
        gate_scr[...] = jnp.sum(jnp.where(high | low, gates, 0.0), axis=-1, keepdims=True)
        out_acc[...] = jnp.zeros_like(out_acc)
        back_acc[...] = jnp.zeros_like(back_acc)
        dot_scr[...] = jnp.zeros_like(dot_scr)

    x = x_ref[:, :, :width].reshape(rows, width)
    c = c_ref[...].reshape(rows, width)
    gate = gate_scr[...]
    wg, wu, wd = wg_ref[...], wu_ref[...], wd_ref[...]
    gate_pre, up_pre = dot_nn(x, wg), dot_nn(x, wu)
    sig = jax.nn.sigmoid(gate_pre)
    hidden = (gate_pre * sig * up_pre).astype(bf16)
    out_acc[...] += dot_nn(hidden, wd)
    plain = dot_nt(c, wd)
    wide = hidden.astype(f32)
    dot_scr[...] += jnp.sum(wide * plain, axis=-1, keepdims=True)
    hid_ref[...] = (wide * gate).astype(bf16).reshape(hid_ref.shape)
    hidden_grad = plain * gate
    gate_grad = (hidden_grad * up_pre * sig * (1.0 + gate_pre * (1.0 - sig))).astype(bf16)
    up_grad = (hidden_grad * gate_pre * sig).astype(bf16)
    gp_ref[...] = gate_grad.reshape(gp_ref.shape)
    up_ref[...] = up_grad.reshape(up_ref.shape)
    back_acc[...] += dot_nt(gate_grad, wg) + dot_nt(up_grad, wu)

    @pl.when(step == pl.num_programs(1) - 1)
    def _():
        dots = dot_scr[...]
        coarse = dots.astype(bf16).astype(f32)
        lanes = jnp.where(high, coarse, jnp.where(low, dots - coarse, 0.0)).astype(bf16)
        back_ref[:, :, :width] = back_acc[...].astype(bf16).reshape(c_ref.shape)
        back_ref[:, :, width:] = lanes.reshape(per_plane, capacity, extra)
        out_ref[...] = (out_acc[...] * gate).astype(bf16).reshape(out_ref.shape)


def experts(mine, x, near, far, wg, wu, wd, base, planes, count, kept):
    per_plane, blocks, capacity, wide = x.shape
    width = near.shape[3]
    halves, _, hidden = wg.shape
    rows = per_plane * capacity
    saved = jax.ShapeDtypeStruct((per_plane, planes, capacity, width), bf16)
    thin = jax.ShapeDtypeStruct((per_plane, planes, capacity, halves * hidden), bf16)
    moved = pl.BlockSpec((per_plane, None, capacity, wide), lambda i, f, s: (0, i, 0, 0))
    saved_spec = pl.BlockSpec((per_plane, None, capacity, width), lambda i, f, s: (0, base + i, 0, 0))
    thin_spec = pl.BlockSpec((per_plane, None, capacity, hidden), lambda i, f, s: (0, base + i, 0, f))
    carried = 0 if kept is None else len(kept)
    skip = base - 1 if base else 0
    cot_specs = [
        pl.BlockSpec((per_plane, None, capacity, width), lambda i, f, s: (0, 0, 0, 0)),
        pl.BlockSpec(
            (per_plane, None, capacity, width),
            lambda i, f, s: (0, jnp.maximum(skip + i - 1, 0), 0, 0),
        ),
    ]
    result = pl.pallas_call(
        functools.partial(expert_kernel, count, carried),
        out_shape=(
            jax.ShapeDtypeStruct(x.shape, bf16),
            jax.ShapeDtypeStruct((per_plane, blocks, capacity, width), bf16),
            saved,
            saved,
            thin,
            thin,
            thin,
        ),
        grid_spec=pltpu.PrefetchScalarGridSpec(
            num_scalar_prefetch=1,
            grid=(blocks, halves),
            in_specs=[
                moved,
                *cot_specs,
                pl.BlockSpec((None, width, hidden), lambda i, f, s: (f, 0, 0)),
                pl.BlockSpec((None, width, hidden), lambda i, f, s: (f, 0, 0)),
                pl.BlockSpec((None, hidden, width), lambda i, f, s: (f, 0, 0)),
            ]
            + [pl.BlockSpec(memory_space=pl.ANY)] * carried,
            out_specs=(
                moved,
                pl.BlockSpec((per_plane, None, capacity, width), lambda i, f, s: (0, i, 0, 0)),
                saved_spec,
                saved_spec,
                thin_spec,
                thin_spec,
                thin_spec,
            ),
            scratch_shapes=[
                pltpu.VMEM((rows, width), f32),
                pltpu.VMEM((rows, width), f32),
                pltpu.VMEM((rows, 1), f32),
                pltpu.VMEM((rows, 1), f32),
            ],
        ),
        input_output_aliases={7 + i: 2 + i for i in range(carried)},
        compiler_params=params(2, 60),
        cost_estimate=estimate(
            flops=12 * blocks * rows * width * hidden * halves,
            bytes_accessed=10 * blocks * rows * width + 6 * blocks * width * hidden * halves,
            transcendentals=blocks * rows * hidden * halves,
        ),
        name="experts",
    )(mine, x, near, far, wg, wu, wd, *(kept or ()))
    return result[0], result[1], result[2:]


def gram_kernel(plus, left_ref, right_ref, *refs):
    total = dot_tn(left_ref[...], right_ref[...])
    if plus:
        total = total + refs[0][...]
    refs[-1][...] = total.astype(refs[-1].dtype)


def gram(left, right, left_cols, right_cols, dtype, plus=None):
    rows = left.shape[0]
    left_at, left_count = left_cols
    right_at, right_count = right_cols
    tall = min(left_count, 256)
    wide = min(right_count, 1024)
    out_spec = pl.BlockSpec((tall, wide), lambda j, i: (i, j))
    return pl.pallas_call(
        functools.partial(gram_kernel, plus is not None),
        out_shape=jax.ShapeDtypeStruct((left_count, right_count), dtype),
        grid=(right_count // wide, left_count // tall),
        in_specs=[
            pl.BlockSpec((rows, tall), lambda j, i: (0, left_at // tall + i)),
            pl.BlockSpec((rows, wide), lambda j, i: (0, right_at // wide + j)),
        ]
        + [out_spec] * (plus is not None),
        out_specs=out_spec,
        compiler_params=params(2, 48),
        cost_estimate=estimate(
            flops=2 * rows * left_count * right_count,
            bytes_accessed=2 * rows * (left_count + right_count) + 4 * left_count * right_count,
            transcendentals=0,
        ),
        name="gram",
    )(left, right, *(() if plus is None else (plus,)))


def project_kernel(plus, core_ref, rows_ref, weights_ref, *refs):
    total = dot_nt(rows_ref[...], weights_ref[...])
    if plus:
        total = total + refs[0][...].astype(f32)
    refs[-1][...] = total.astype(bf16)


def project_back(core, rows, weights, tok_rows, plus=None):
    count, depth = rows.shape
    width = weights.shape[0]
    chips = count // tok_rows // 2
    out_spec = pl.BlockSpec((tok_rows, width), lambda i, s: (i, 0))
    return pl.pallas_call(
        functools.partial(project_kernel, plus is not None),
        out_shape=jax.ShapeDtypeStruct((chips * tok_rows, width), bf16),
        grid_spec=pltpu.PrefetchScalarGridSpec(
            num_scalar_prefetch=1,
            grid=(chips,),
            in_specs=[
                pl.BlockSpec((tok_rows, depth), lambda i, s: (2 * i + s[0], 0)),
                pl.BlockSpec((width, depth), lambda i, s: (0, 0)),
            ]
            + [out_spec] * (plus is not None),
            out_specs=out_spec,
        ),
        compiler_params=params(1, 40),
        cost_estimate=estimate(
            flops=count * depth * width,
            bytes_accessed=2 * width * depth + count * depth + count * width,
            transcendentals=0,
        ),
        name="project_back",
    )(core, rows, weights, *(() if plus is None else (plus,)))


def after(value, *others):
    return lax.optimization_barrier((value,) + others)[0]


def body(
    hidden_in,
    out_cotangent,
    segment_number,
    expert_routes,
    pair_order,
    norm_gain,
    query_weight,
    key_weight,
    value_weight,
    output_weight,
    query_gain,
    key_gain,
    ffn_norm_gain,
    router_weight,
    expert_gate,
    expert_up,
    expert_down,
):
    tok_rows, width = hidden_in.shape
    devices = lax.axis_size(AXIS)
    members = max(1, SEQ_MIN // tok_rows)
    planes = devices // members
    per_plane = members // 2
    expert_count = devices // 2
    capacity = tok_rows * TOPK // expert_count
    heads = width // HD // members
    head_width = heads * HD
    own_rows = norm_gain.shape[0]
    seq = members * tok_rows
    me = lax.axis_index(AXIS)
    plane, member = me // members, me % members
    mine = (me // 2).astype(jnp.int32).reshape(1)
    first = (plane * per_plane).astype(jnp.int32)
    places = (plane ^ jnp.arange(planes, dtype=jnp.int32)).astype(jnp.int32)
    counted = jnp.concatenate([first[None], jnp.arange(planes, dtype=jnp.int32)])
    halfway = -(-planes // 2)
    chunks = [part for part in (range(halfway, planes), range(halfway)) if len(part)]

    def placed(part):
        return jnp.concatenate([first[None], places[part.start : part.stop]])

    plane_groups = [[g * members + j for j in range(members)] for g in range(planes)]
    stack_groups = [[g * members + j for g in range(planes)] for j in range(members)]
    core_groups = [
        [g * members + 2 * c + h for c in range(per_plane)] for g in range(planes) for h in (0, 1)
    ]

    def exchange(value, groups=None):
        return lax.all_to_all(
            value, AXIS, split_axis=0, concat_axis=0, tiled=True, axis_index_groups=groups
        )

    def gather(value, groups=None):
        return lax.all_gather(value, AXIS, axis=0, tiled=True, axis_index_groups=groups)

    def flip(value, bits):
        if bits == 0:
            return value
        return lax.ppermute(value, AXIS, [(i, i ^ bits) for i in range(devices)])

    def to_core(value):
        return flip(value, 1)

    def to_plane(value, d):
        return flip(value, members * d)

    def spread(value, *others):
        found = {0: value}
        for d in range(1, planes):
            lowest = d & -d
            source = found[d ^ lowest]
            found[d] = to_plane(source if d == lowest else after(source, *others), lowest)
        return [found[d] for d in range(planes)]

    def fold(sums, *others):
        bit = 1
        while bit < len(sums):
            for d in range(len(sums)):
                if d & bit and not d & (bit - 1):
                    came = to_plane(sums[d].astype(bf16), bit)
                    if d == bit:
                        came = after(came, *others)
                    sums[d ^ bit] = sums[d ^ bit].astype(f32) + came.astype(f32)
            bit *= 2
        return sums[0]

    wire, core_op = [], []

    def on_wire(value, groups):
        came = exchange(after(value, *wire[-1:]), groups)
        wire.append(came)
        return came

    def to_chips(value):
        return on_wire(value, core_groups)

    def in_turn(value):
        return after(value, *core_op[-1:])

    def ran(value):
        core_op.append(value)
        return value

    columns = jnp.concatenate(
        [w.reshape(own_rows, members, head_width) for w in (query_weight, key_weight, value_weight)],
        axis=2,
    )
    slots = block_slots(expert_routes, pair_order, expert_count)
    columns = on_wire(
        after(columns, slots).transpose(1, 0, 2).reshape(members * own_rows, 3 * head_width), plane_groups
    )
    stacked = [to_plane(after(output_weight, slots), d) for d in range(planes)]
    cosine, sine = rope_tables(seq)
    weights = spread(after(columns, *stacked), cosine, sine)
    slots = [to_plane(after(slots, *weights) if d else slots, d) for d in range(planes)]
    output_rows = jnp.zeros((planes * own_rows, width), bf16)
    for d, rows in enumerate(stacked):
        output_rows = lax.dynamic_update_slice_in_dim(output_rows, rows, places[d] * own_rows, 0)
    rows_all = gather(hidden_in, plane_groups)

    pieces = (
        router_weight.reshape(-1),
        norm_gain,
        ffn_norm_gain,
        query_gain,
        key_gain,
        segment_number.astype(bf16),
    )
    packed = jnp.concatenate(pieces)
    length = packed.shape[0]
    padded = -(-length // 128) * 128
    packed = jnp.pad(packed, (0, padded - length))
    packed = on_wire(jnp.broadcast_to(packed[None], (devices, padded)), None)
    small = []
    at = 0
    for piece in pieces:
        small.append(packed[:, at : at + piece.shape[0]])
        at += piece.shape[0]
    router_full = small[0].reshape(width, expert_count)
    gain_one = small[1].reshape(1, width).astype(f32)
    gain_two = small[2].reshape(1, width).astype(f32)
    gain_q = small[3].reshape(1, HD).astype(f32)
    gain_k = small[4].reshape(1, HD).astype(f32)
    segments = lax.dynamic_slice_in_dim(small[5], plane * members, members, 0).astype(f32)
    seg_row, seg_col = segments.reshape(1, seq), segments.reshape(seq, 1)
    seg_blocks = segments.reshape(seq // ROWS, ROWS)
    seg_first, seg_last = seg_blocks[:, 0], seg_blocks[:, -1]
    low = jnp.sum((seg_last[None, :] < seg_first[:, None]).astype(jnp.int32), axis=1)
    high = jnp.sum((seg_first[None, :] <= seg_last[:, None]).astype(jnp.int32), axis=1)

    cot_own = dispatch(counted, slots[0][None], out_cotangent[None], per_plane, capacity)
    cot_first = [to_chips(cot_own)]
    output_full = gather(after(output_rows, columns), plane_groups)
    slot_list, slots = slots, jnp.stack(slots)
    cot_rows = {0: out_cotangent}
    top = planes // 2
    early, late = [], []
    if planes > 1:
        cot_rows[top] = to_plane(after(out_cotangent, *weights), top)
        early.append(cot_rows[top])
    for d in range(1, planes):
        if d != top:
            lowest = d & -d
            start = after(out_cotangent, *early) if d == lowest else cot_rows[d ^ lowest]
            cot_rows[d] = to_plane(start, lowest)
            late.append(cot_rows[d])

    halves = lambda w: jnp.concatenate([w, to_core(w)], axis=0)
    wg, wu, wd = halves(expert_gate), halves(expert_up), halves(expert_down)

    act_one, pre, rot, ordered = qkv_project(
        places, rows_all, gain_one, weights, gain_q, gain_k, cosine, sine, heads
    )
    out_wide, out_heads, lse = attention(rot, seg_col, seg_row, low, high, heads)
    out_low = on_wire(after(out_heads, *slot_list, *early), plane_groups)
    if planes > 1:
        rows = after(cot_rows[top], out_heads)
        sent = dispatch(counted, slots[top : top + 1], rows[None], per_plane, capacity)
        cot_first.append(to_chips(sent))
    out_low = out_low.reshape(members, tok_rows, head_width).transpose(1, 0, 2)
    out_low = out_low.reshape(tok_rows, planes, members, own_rows).transpose(0, 2, 1, 3)
    out_low = out_low.reshape(tok_rows, width)
    tokens = hidden_in.astype(f32)
    cotangent = out_cotangent.astype(f32)
    middle = tokens + dot_nn(out_low, output_full)
    inverse_two = lax.rsqrt(jnp.mean(middle * middle, axis=-1, keepdims=True) + norm_eps)
    act_two = (middle * inverse_two * gain_two).astype(bf16)

    logits = dot_nn(act_two, router_full)
    expert_ids = jnp.arange(expert_count, dtype=jnp.int32)
    routed = jnp.any(expert_routes[:, :, None] == expert_ids[None, None, :], axis=1)
    logits = jnp.where(routed, logits, masked_score)
    gates = jnp.where(routed, jnp.exp(logits - jnp.max(logits, axis=1, keepdims=True)), 0.0)
    gates = gates / jnp.sum(gates, axis=1, keepdims=True)
    coarse = lax.reduce_precision(gates, 8, 7)
    extra = -(-2 * expert_count // 128) * 128
    act_wide = jnp.concatenate(
        [
            act_two,
            coarse.astype(bf16),
            (gates - coarse).astype(bf16),
            jnp.zeros((tok_rows, extra - 2 * expert_count), bf16),
        ],
        axis=1,
    )

    act_wide = after(act_wide, *late, *cot_first)
    act_all = gather(act_wide, stack_groups).reshape(planes, tok_rows, -1)
    others = [d for d in range(1, planes) if d != top]
    cot_far = cot_first[0]
    if others:
        far = jnp.stack([after(cot_rows[d], act_wide) for d in others])
        far_slots = jnp.stack([slots[d] for d in others])
        cot_far = to_chips(
            ran(dispatch(counted[: len(others) + 1], far_slots, far, per_plane, capacity))
        )

    act = []
    for part in chunks:
        own_slots = slots[part.start : part.stop]
        rows = after(in_turn(act_all), wg, wu, wd)
        sent = dispatch(placed(part), own_slots, rows, per_plane, capacity)
        act.append(to_chips(ran(sent)))
    kept, back, outs = None, [], []
    for part, rows in zip(chunks, act):
        sent, out, kept = experts(
            mine,
            in_turn(rows),
            cot_first[0 if part.start == 0 else 1],
            cot_far,
            wg,
            wu,
            wd,
            part.start,
            planes,
            expert_count,
            kept,
        )
        back.append(to_chips(ran(sent)))
        outs.append(out)
    x_all, c_all, hid_all, gp_all, up_all = kept

    hidden = expert_gate.shape[2]
    flat = lambda value: value.reshape(-1, value.shape[3])
    sides = (
        (flat(x_all), flat(gp_all), 1),
        (flat(x_all), flat(up_all), 1),
        (flat(hid_all), flat(c_all), 0),
    )

    def half(side, which, plus=None):
        left, right, split = side
        cut, whole = (which * hidden, hidden), (0, width)
        cols = (whole, cut) if split else (cut, whole)
        return ran(gram(in_turn(left), right, *cols, f32, plus))

    passed = []

    def home(part, rows):
        sums = {}
        for d in sorted(part, key=lambda d: (-(d & 1), d)):
            sums[d] = ran(combine(first[None], slots[d], in_turn(rows), d - part.start))
        bit = 1
        while bit < len(part):
            for d in part:
                if d & bit and not d & (bit - 1):
                    came = to_plane(sums[d].astype(bf16), bit)
                    passed.append(came)
                    sums[d ^ bit] = sums[d ^ bit].astype(f32) + came.astype(f32)
            bit *= 2
        return sums[part.start]

    back_sum = home(chunks[0], back[0])
    theirs = [half(side, 1) for side in sides[:2]]
    if len(chunks) > 1:
        back_sum = ran(in_turn(back_sum.astype(bf16)))
        back_sum = to_plane(back_sum, top)
    theirs.append(half(sides[2], 1))
    if len(chunks) > 1:
        back_sum = back_sum.astype(f32) + home(chunks[1], back[1])
    outs[0] = to_chips(outs[0])

    expert_in_grad = back_sum[:, :width]
    gate_grad = (
        back_sum[:, width : width + expert_count]
        + back_sum[:, width + expert_count : width + 2 * expert_count]
    )
    select_grad = gates * (gate_grad - jnp.sum(gates * gate_grad, axis=1, keepdims=True))
    logit_grad = select_grad.astype(bf16)
    grad_router = dot_tn(act_two, logit_grad)
    act_two_grad = expert_in_grad + dot_nt(logit_grad, router_full)
    weighted = act_two_grad * gain_two
    grad_gain_two = jnp.sum(act_two_grad * middle * inverse_two, axis=0)
    middle_grad = (
        cotangent
        + inverse_two * weighted
        - middle * inverse_two**3 * jnp.mean(weighted * middle, axis=-1, keepdims=True)
    )
    middle_low = middle_grad.astype(bf16)

    out_grad = dot_nt(middle_low, output_full).astype(bf16)
    out_grad = out_grad.reshape(tok_rows, members, planes, own_rows).transpose(0, 2, 1, 3)
    out_grad = out_grad.reshape(tok_rows, members, head_width).transpose(1, 0, 2)
    out_grad = out_grad.reshape(seq, head_width)
    ran(out_grad)
    theirs = [to_core(after(grad, out_grad)) for grad in theirs]
    out_grad = on_wire(out_grad, plane_groups)
    mixture = home(chunks[0], outs[0]).astype(bf16)
    dqkv, grad_gains = attention_back(
        rot,
        in_turn(out_grad),
        out_wide,
        lse,
        seg_col,
        seg_row,
        low,
        high,
        pre,
        gain_q,
        gain_k,
        cosine,
        sine,
        heads,
    )
    ran(dqkv)
    if len(chunks) > 1:
        near_sum = home(chunks[1], to_chips(outs[1]))
        done = (*core_op[-2:], mixture, *theirs)
        dqkv, grad_gains = after(dqkv, *done), after(grad_gains, *done)
    middle_all = gather(after(middle_low, dqkv), plane_groups)

    sums = (
        grad_router.reshape(devices, -1),
        grad_gain_two.reshape(devices, -1),
        grad_gains[0].reshape(devices, -1),
        grad_gains[1].reshape(devices, -1),
    )
    packed = jnp.concatenate(sums, axis=1)
    length = packed.shape[1]
    padded = -(-length // 128) * 128
    packed = jnp.pad(packed, ((0, 0), (0, padded - length)))

    core = (me % 2).astype(jnp.int32).reshape(1)
    given = project_back(1 - core, dqkv, ordered, tok_rows)
    part = gram(after(act_one, given), dqkv, (0, width), (0, 3 * head_width), bf16)
    part = part.reshape(planes, members * own_rows, 3 * head_width)
    shares = [lax.dynamic_index_in_dim(part, places[d], 0, False) for d in range(planes)]
    mixture = to_plane(mixture, top) if len(chunks) > 1 else mixture
    given = after(to_core(given), *shares, mixture, *passed[-1:])
    act_one_grad = project_back(core, dqkv, ordered, tok_rows, given)
    ran(act_one_grad)
    output_part = ran(gram(out_heads, in_turn(middle_all), (0, head_width), (0, width), bf16))
    grad_gate, grad_up, grad_down = (
        half(side, 0, other) for side, other in zip(sides, theirs)
    )
    shares = [after(share, act_one_grad) for share in shares]
    taken = fold(shares, grad_gate, grad_up, grad_down).astype(bf16)
    act_one_grad = on_wire(act_one_grad, core_groups)

    output_part = lax.psum_scatter(
        output_part, AXIS, scatter_dimension=0, tiled=True, axis_index_groups=stack_groups
    )
    to_owner = [
        (g * members + j, j * planes + g) for g in range(planes) for j in range(members)
    ]
    mixture = mixture.astype(f32)
    if len(chunks) > 1:
        mixture = mixture + near_sum
    packed, act_one_grad, mixture, grad_gate, grad_up, grad_down = lax.optimization_barrier(
        (packed, act_one_grad, mixture, grad_gate, grad_up, grad_down)
    )
    layer_out = (middle + mixture).astype(bf16)
    packed = exchange(packed)
    taken, packed, output_part = lax.optimization_barrier((taken, packed, output_part))
    grad_output = lax.ppermute(output_part, AXIS, to_owner)
    part = exchange(taken, plane_groups).reshape(members, own_rows, 3, head_width)
    part = part.transpose(2, 1, 0, 3).reshape(3, own_rows, width).astype(f32)
    grad_query, grad_key, grad_value = part[0], part[1], part[2]
    act_one_grad = act_one_grad.reshape(per_plane, tok_rows, width)
    act_one_grad = jnp.sum(act_one_grad.astype(f32), axis=0)

    inverse_one = lax.rsqrt(jnp.mean(tokens * tokens, axis=-1, keepdims=True) + norm_eps)
    weighted = act_one_grad * gain_one
    grad_hidden = (
        middle_grad
        + inverse_one * weighted
        - tokens * inverse_one**3 * jnp.mean(weighted * tokens, axis=-1, keepdims=True)
    )
    grad_gain_one = (
        jnp.sum(
            grad_query * query_weight.astype(f32)
            + grad_key * key_weight.astype(f32)
            + grad_value * value_weight.astype(f32),
            axis=1,
        )
        / norm_gain.astype(f32)
    )

    summed = jnp.sum(packed, axis=0)
    at, tiny = 0, []
    for piece in sums:
        tiny.append(summed[at : at + piece.shape[1]])
        at += piece.shape[1]

    return (
        layer_out,
        grad_hidden,
        grad_gain_one,
        grad_query,
        grad_key,
        grad_value,
        grad_output.astype(f32),
        tiny[2],
        tiny[3],
        tiny[1],
        tiny[0].reshape(own_rows, expert_count),
        grad_gate[None],
        grad_up[None],
        grad_down[None],
    )


def solution(mesh):
    row, mat, cube = P(AXIS), P(AXIS, None), P(AXIS, None, None)
    return jax.shard_map(
        body,
        mesh=mesh,
        in_specs=(mat, mat, row, mat, mat, row, mat, mat, mat, mat, row, row, row, mat)
        + (cube,) * 3,
        out_specs=(mat, mat, row, mat, mat, mat, mat, row, row, row, mat) + (cube,) * 3,
        check_vma=False,
    )
```
